32 devices in a mesh: dp: 8 (over z, y), fsdp: 4 (over x, core).
Axes of the slice: x: 2, y: 2, z: 4, core: 2. Of those that a mesh axis runs over, the one named last changes fastest.
Arguments:
- tokens: bfloat16 [3, 4, 2048, 768], P(None, 'fsdp', 'dp'), may hold values from -6 to 6
- seq_lengths: int32 [3, 4, 2], P(None, 'fsdp'), may hold values from 1 to 1920, as said below
- norm_gain: bfloat16 [768], P('fsdp'), may hold values from 0.25 to 1.75
- w_inner: bfloat16 [768, 3072], P('fsdp'), may hold values from -0.21875 to 0.21875
- w_state: bfloat16 [768, 128], P('fsdp'), may hold values from -0.078125 to 0.078125
- w_step: bfloat16 [768, 48], P('fsdp'), may hold values from -0.21875 to 0.21875
- conv_weight: bfloat16 [4, 1664], P(None, 'fsdp'), may hold values from -3 to 3
- conv_bias: bfloat16 [1664], P('fsdp'), may hold values from -3 to 3
- step_bias: bfloat16 [48], P('fsdp'), may hold values from -2 to 1
- decay_log: bfloat16 [24], P('fsdp'), may hold values from -9.1875 to -2.296875
- skip_gain: bfloat16 [24], P('fsdp'), may hold values from 0.5 to 2
- out_gain: bfloat16 [1536], P('fsdp'), may hold values from 0.25 to 1.75
- w_out: bfloat16 [1536, 768], P('fsdp'), may hold values from -0.15625 to 0.15625
- cotangent: bfloat16 [3, 4, 2048, 768], P(None, 'fsdp', 'dp'), may hold values from -6 to 6
Outputs:
- layer_out: bfloat16 [3, 4, 2048, 768], P(None, 'fsdp', 'dp')
- tokens_grad: float32 [3, 4, 2048, 768], P(None, 'fsdp', 'dp')
- norm_gain_grad: float32 [768], P('fsdp')
- w_inner_grad: float32 [768, 3072], P('fsdp')
- w_state_grad: float32 [768, 128], P('fsdp')
- w_step_grad: float32 [768, 48], P('fsdp')
- conv_weight_grad: float32 [4, 1664], P(None, 'fsdp')
- conv_bias_grad: float32 [1664], P('fsdp')
- step_bias_grad: float32 [48], P('fsdp')
- decay_log_grad: float32 [24], P('fsdp')
- skip_gain_grad: float32 [24], P('fsdp')
- out_gain_grad: float32 [1536], P('fsdp')
- w_out_grad: float32 [1536, 768], P('fsdp')
The draws below stay inside these ranges and needn't reach their ends.
Inputs may be any that keep to these rules, and one draw needn't show every extreme that they name: Each row of seq_lengths describes one span of 2048 positions: the first sequence begins at 0, the second at the first multiple of 128 at or after the first one's end, and it ends at or before 2048. For each group, in the span of one of the 3 micro-batches, one of the two sequences begins among the first 256 positions and ends among the last 256; in every other span both sequences have 2048 // 4 tokens or more. Some sequence has exactly 1920 tokens.
All inputs are finite; a program needn't handle non-finite values.
Results may differ from the reference program's by a relative error of at most 0.0045.
The reference program's roundings to bfloat16 on the way (of `hidden` and `normed`) count: a program that leaves them out, or rounds other values in their place, can miss the bound.
Values may be sent and summed in bfloat16 or wider, within the bound.
A program may use at most 576 MiB of HBM per device.

```python
import jax
import jax.numpy as jnp
from jax import lax

D = 768
INNER = 1536
HEADS = 24
HEAD_DIM = 64
STATE = 64
CONV = 4
BLOCK = 128
MB = 3
TOK_DEV = 256
SPAN = 2048
GROUPS = 4


def draw_seq_lengths(key, part):
    subkeys = jax.random.split(key, 8)
    grid_shape = (MB, GROUPS)
    long_later = jax.random.randint(subkeys[0], grid_shape, 0, 2)
    long_later = long_later.at[0, 0].set(1)
    short_first = jax.random.randint(subkeys[1], grid_shape, 1, TOK_DEV - BLOCK + 1)
    start_after = (short_first + BLOCK - 1) // BLOCK * BLOCK
    long_second = SPAN - start_after - jax.random.randint(subkeys[2], grid_shape, 0, TOK_DEV)
    long_first = SPAN - BLOCK - jax.random.randint(subkeys[3], grid_shape, 0, TOK_DEV - BLOCK)
    long_first = long_first.at[0, 0].set(SPAN - BLOCK)
    start_second = (long_first + BLOCK - 1) // BLOCK * BLOCK
    short_second = 1 + jax.random.randint(subkeys[4], grid_shape, 0, 1 << 20) % (SPAN - start_second)
    reach_first = jnp.where(long_later == 0, short_first, long_first)
    reach_second = jnp.where(long_later == 0, long_second, short_second)
    chosen = jax.random.randint(subkeys[5], (GROUPS,), 0, MB)
    chosen = chosen.at[0].set(0)
    reaching = jnp.arange(MB, dtype=jnp.int32)[:, None] == chosen[None, :]
    quarter = SPAN // 4
    mid_first = jax.random.randint(subkeys[6], grid_shape, quarter, SPAN - quarter - BLOCK + 1)
    mid_start = (mid_first + BLOCK - 1) // BLOCK * BLOCK
    mid_second = quarter + jax.random.randint(subkeys[7], grid_shape, 0, 1 << 20) % (SPAN - mid_start - quarter + 1)
    first_lens = jnp.where(reaching, reach_first, mid_first)
    second_lens = jnp.where(reaching, reach_second, mid_second)
    return jnp.stack([first_lens, second_lens], axis=-1).astype(jnp.int32)


def level_of(own_key, shape, pieces, least, high):
    def one(dim, blocks):
        steps = jax.random.uniform(jax.random.fold_in(jax.random.fold_in(own_key, 6), dim), (blocks,), jnp.float32, least / len(pieces), high / len(pieces))
        return jnp.repeat(jnp.exp(steps), shape[dim] // blocks).reshape((-1,) + (1,) * (len(shape) - dim - 1))

    factor_of = one(*pieces[0])
    for cut in pieces[1:]:
        factor_of = factor_of * one(*cut)
    return factor_of


def gaussian(stream_key, shape, width, bound, shards=(), held_as=jnp.bfloat16):
    array = width * jax.random.normal(stream_key, shape, jnp.float32)
    if shards:
        array = array * level_of(stream_key, shape, shards, -0.22, 0.18)
    return jnp.clip(array, -bound, bound).astype(held_as)


def setup_inputs(seed: int = 0) -> dict:
    keys = jax.random.split(jax.random.key(seed), 15)
    tokens = gaussian(keys[0], (MB, GROUPS, SPAN, D), 1.0, 6.0, ((1, 4), (2, 8)))
    seq_lengths = draw_seq_lengths(jax.random.fold_in(keys[14], 71), 0)
    norm_gain = jnp.clip(1.0 + 0.15 * jax.random.normal(keys[2], (D,), jnp.float32), 0.25, 1.75).astype(jnp.bfloat16)
    w_inner = gaussian(keys[3], (D, 2 * INNER), D ** -0.5, 0.21875, ((0, 4),))
    w_state = gaussian(keys[4], (D, 2 * STATE), (9 * D) ** -0.5, 0.078125, ((0, 4),))
    w_step = gaussian(keys[5], (D, 2 * HEADS), D ** -0.5, 0.21875, ((0, 4),))
    conv_weight = gaussian(keys[6], (CONV, INNER + 2 * STATE), CONV ** -0.5, 3.0, ((1, 4),))
    conv_bias = gaussian(keys[7], (INNER + 2 * STATE,), 0.3, 3.0, ((0, 4),))
    step_bias = jnp.clip(-2.0 + 3.0 * jax.random.uniform(keys[8], (2 * HEADS,), jnp.float32) ** level_of(keys[8], (2 * HEADS,), ((0, 4),), -0.2, 0.2), -2.0, 1.0).astype(jnp.bfloat16)
    decay_log = jnp.clip(-9.1875 + 6.890625 * jax.random.uniform(keys[9], (HEADS,), jnp.float32) ** level_of(keys[9], (HEADS,), ((0, 4),), -0.2, 0.2), -9.1875, -2.296875).astype(jnp.bfloat16)
    skip_gain = jnp.clip(0.5 + 1.5 * jax.random.uniform(keys[10], (HEADS,), jnp.float32) ** level_of(keys[10], (HEADS,), ((0, 4),), -0.2, 0.2), 0.5, 2.0).astype(jnp.bfloat16)
    out_gain = jnp.clip(1.0 + 0.15 * jax.random.normal(keys[11], (INNER,), jnp.float32), 0.25, 1.75).astype(jnp.bfloat16)
    w_out = gaussian(keys[12], (INNER, D), INNER ** -0.5, 0.15625, ((0, 4),))
    cotangent = gaussian(keys[13], (MB, GROUPS, SPAN, D), 1.0, 6.0, ((1, 4), (2, 8)))
    return {"tokens": tokens, "seq_lengths": seq_lengths, "norm_gain": norm_gain, "w_inner": w_inner, "w_state": w_state, "w_step": w_step, "conv_weight": conv_weight, "conv_bias": conv_bias, "step_bias": step_bias, "decay_log": decay_log, "skip_gain": skip_gain, "out_gain": out_gain, "w_out": w_out, "cotangent": cotangent}


EPSILON = 1e-05
HIGHEST = lax.Precision.HIGHEST

@jax.custom_vjp
def low(v):
    return lax.optimization_barrier(v.astype(jnp.bfloat16)).astype(jnp.float32)

@jax.custom_vjp
def low_back(v):
    return v

def low_keep(v):
    return (low(v), None)

def low_pass(kept, grad):
    return (grad,)

def back_keep(v):
    return (v, None)

def back_low(kept, grad):
    return (low(grad),)
low.defvjp(low_keep, low_pass)
low_back.defvjp(back_keep, back_low)

def rms_scale(values, norm_gain):
    return values * lax.rsqrt(lax.optimization_barrier(jnp.mean(values * values, axis=-1, keepdims=True)) + EPSILON) * norm_gain

def span_layout(lengths, places, block_first, span_len):
    first_len = lengths[0]
    second_start = (first_len + BLOCK - 1) // BLOCK * BLOCK
    second_end = second_start + lengths[1]
    inside = (places < first_len) | (places >= second_start) & (places < second_end)
    valid_mask = inside.astype(jnp.float32)
    offset = jnp.where(places >= second_start, places - second_start, places)

    def begins(position):
        return ((position == 0) | (position == second_start) | (position >= span_len)).astype(jnp.float32)
    return (valid_mask, offset, 1.0 - begins(block_first), 1.0 - begins(block_first + BLOCK))

def mixer_inputs(conv_in, before, dt_raw, conv_weight, conv_bias, step_bias, decay_log, valid_mask, offset):
    rows_count = conv_in.shape[0]
    padded = jnp.concatenate([before, conv_in], axis=0)
    conv_out = conv_bias + jnp.zeros_like(conv_in)
    for lag_index in range(CONV):
        window = padded[CONV - 1 - lag_index:CONV - 1 - lag_index + rows_count]
        conv_out = conv_out + conv_weight[lag_index] * window * (offset >= lag_index).astype(jnp.float32)[:, None]
    activated = valid_mask[:, None] * jax.nn.silu(conv_out)
    head_vals = activated[:, :INNER].reshape(rows_count, HEADS, HEAD_DIM)
    state_in = activated[:, INNER:INNER + STATE]
    state_out = activated[:, INNER + STATE:]
    step_sizes = jax.nn.softplus(dt_raw + step_bias)
    decay_rates = jnp.exp(decay_log)
    fwd_step = step_sizes[:, :HEADS]
    rev_step = step_sizes[:, HEADS:]
    return (head_vals, state_in, state_out, fwd_step, rev_step, -fwd_step * decay_rates, -rev_step * decay_rates)

def block_sums(fwd_log, rev_log):
    fwd_cum = jnp.cumsum(fwd_log, axis=0)
    rev_cum = jnp.flip(jnp.cumsum(jnp.flip(rev_log, 0), axis=0), 0)
    return (fwd_cum, rev_cum)

def block_states(head_vals, state_in, fwd_step, rev_step, fwd_log, rev_log):
    fwd_cum, rev_cum = block_sums(fwd_log, rev_log)
    fwd_tail = jnp.exp(fwd_cum[-1:] - fwd_cum) * fwd_step
    rev_head = jnp.exp(rev_cum[:1] - rev_cum) * rev_step
    fwd_state = jnp.einsum('sh,sn,shp->hnp', fwd_tail, state_in, head_vals, precision=HIGHEST)
    rev_state = jnp.einsum('sh,sn,shp->hnp', rev_head, state_in, head_vals, precision=HIGHEST)
    return (fwd_state, jnp.exp(fwd_cum[-1]), rev_state, jnp.exp(rev_cum[0]))

def block_output(head_vals, state_in, state_out, fwd_step, rev_step, fwd_log, rev_log, fwd_enter, rev_enter):
    fwd_cum, rev_cum = block_sums(fwd_log, rev_log)
    positions = jnp.arange(head_vals.shape[0], dtype=jnp.int32)
    lower_mask = (positions[:, None] > positions[None, :])[:, :, None]
    upper_mask = (positions[:, None] < positions[None, :])[:, :, None]
    fwd_gap = fwd_cum[:, None, :] - fwd_cum[None, :, :]
    rev_gap = rev_cum[:, None, :] - rev_cum[None, :, :]
    scores = jnp.dot(state_out, state_in.T, precision=HIGHEST)
    mixing = jnp.where(lower_mask, jnp.exp(jnp.where(lower_mask, fwd_gap, 0.0)) * fwd_step[None], 0.0)
    mixing = mixing + jnp.where(upper_mask, jnp.exp(jnp.where(upper_mask, rev_gap, 0.0)) * rev_step[None], 0.0)
    mixing = mixing * scores[:, :, None]
    inner_part = jnp.einsum('tsh,shp->thp', mixing, head_vals, precision=HIGHEST)
    carried = jnp.einsum('tn,hnp->thp', state_out, fwd_enter, precision=HIGHEST) * jnp.exp(fwd_cum)[:, :, None]
    carried = carried + jnp.einsum('tn,hnp->thp', state_out, rev_enter, precision=HIGHEST) * jnp.exp(rev_cum)[:, :, None]
    return inner_part + carried

def output_block(members):
    return block_output(*members)

def walk_block(running, block_item):
    state_part, decay_part, keep_part = block_item
    entering = keep_part * running
    return (decay_part[:, None, None] * entering + state_part, entering)

def layer_span(x_rows, lengths, weights):
    norm_gain, w_inner, w_state, w_step, conv_weight, conv_bias, step_bias, decay_log, skip_gain, out_gain, w_out = weights
    block_count = SPAN // BLOCK
    places = jnp.arange(SPAN, dtype=jnp.int32)
    block_first = jnp.arange(block_count, dtype=jnp.int32) * BLOCK
    valid_mask, offset, keep_fwd, keep_rev = span_layout(lengths, places, block_first, SPAN)
    hidden = low(rms_scale(x_rows, norm_gain))
    proj_zx = low_back(jnp.dot(hidden, w_inner, precision=HIGHEST))
    proj_bc = low_back(jnp.dot(hidden, w_state, precision=HIGHEST))
    dt_raw = low_back(jnp.dot(hidden, w_step, precision=HIGHEST))
    gate_in = proj_zx[:, :INNER]
    conv_in = jnp.concatenate([proj_zx[:, INNER:], proj_bc], axis=1)
    before = jnp.zeros((CONV - 1, conv_in.shape[1]), jnp.float32)
    mixer_parts = mixer_inputs(conv_in, before, dt_raw, conv_weight, conv_bias, step_bias, decay_log, valid_mask, offset)
    blocks = tuple((member.reshape((block_count, BLOCK) + member.shape[1:]) for member in mixer_parts))
    fwd_state, fwd_decay, rev_state, rev_decay = jax.vmap(block_states)(blocks[0], blocks[1], blocks[3], blocks[4], blocks[5], blocks[6])
    zero_state = jnp.zeros((HEADS, STATE, HEAD_DIM), jnp.float32)
    _, fwd_enter = lax.scan(walk_block, zero_state, (fwd_state, fwd_decay, keep_fwd))
    _, rev_enter = lax.scan(walk_block, zero_state, (rev_state, rev_decay, keep_rev), reverse=True)
    mixed = lax.map(jax.checkpoint(output_block), blocks + (fwd_enter, rev_enter))
    mixed = mixed.reshape(SPAN, HEADS, HEAD_DIM) + skip_gain[None, :, None] * mixer_parts[0]
    gated = mixed.reshape(SPAN, INNER) * jax.nn.silu(gate_in)
    normed = low(rms_scale(gated, out_gain))
    branch = jnp.dot(normed, w_out, precision=HIGHEST)
    return valid_mask[:, None] * (x_rows + branch)

def reference(tokens, seq_lengths, norm_gain, w_inner, w_state, w_step, conv_weight, conv_bias, step_bias, decay_log, skip_gain, out_gain, w_out, cotangent):
    weights = tuple((member.astype(jnp.float32) for member in (norm_gain, w_inner, w_state, w_step, conv_weight, conv_bias, step_bias, decay_log, skip_gain, out_gain, w_out)))
    spans = tokens.reshape(MB * GROUPS, SPAN, D).astype(jnp.float32)
    cot_spans = cotangent.reshape(MB * GROUPS, SPAN, D).astype(jnp.float32)
    all_lengths = seq_lengths.reshape(MB * GROUPS, 2)

    def one_span(totals, span_item):
        x_rows, lengths, cot_rows = span_item
        result, pullback = jax.vjp(lambda rows_in, params_in: layer_span(rows_in, lengths, params_in), x_rows, weights)
        d_rows, d_weights = pullback(cot_rows)
        return (jax.tree.map(jnp.add, totals, d_weights), (result.astype(jnp.bfloat16), d_rows))
    initial = jax.tree.map(jnp.zeros_like, weights)
    totals, (out_spans, grad_spans) = lax.scan(one_span, initial, (spans, all_lengths, cot_spans))
    layer_out = out_spans.reshape(tokens.shape)
    tokens_grad = grad_spans.reshape(tokens.shape)
    return (layer_out, tokens_grad, totals[0], totals[1], totals[2], totals[3], totals[4], totals[5], totals[6], totals[7], totals[8], totals[9], totals[10])
```

```python
from functools import partial

import jax
import jax.numpy as jnp
from jax import lax
from jax.experimental import pallas as pl
from jax.experimental.pallas import tpu as pltpu
from jax.sharding import PartitionSpec as P

D = 768
INNER = 1536
HEADS = 24
HEAD_DIM = 64
STATE = 64
CONV = 4
BLOCK = 128
MB = 3
TOK_DEV = 256
HALO = 8
LANES = 128
CONV_COLS = INNER + 2 * STATE
WIDE = 2 * INNER + 2 * LANES
LATE = INNER + 2 * LANES
PAIRS = HEADS // 2
PARTS = 2
CHUNKS = MB * PARTS
EPSILON = 1e-05
HIGHEST = lax.Precision.HIGHEST
F32 = jnp.float32
BF16 = jnp.bfloat16
SENT = F32
ROWS = ((0,), (0,))
COLS = ((1,), (1,))
INNER_DIMS = ((1,), (0,))
VMEM_LIMIT = 48 * 1024 * 1024


def dot(left, right, dims=INNER_DIMS, precision=None):
    return lax.dot_general(left, right, (dims, ((), ())), precision=precision, preferred_element_type=F32)


def halves(value):
    high = value.astype(BF16)
    return high, (value - high.astype(F32)).astype(BF16)


def spread_operand(value):
    high, low = halves(value)
    return jnp.concatenate([high, low], axis=1)


def by_lane(first, second):
    low = iota(first.shape, 1) < STATE
    twice = jnp.where(low, first, second)
    high = twice.astype(BF16).astype(F32)
    return jnp.where(low, high, twice - high)


def twice(value, axis):
    return jnp.concatenate([value, value], axis=axis)


def fold(value):
    return value[:STATE] + value[STATE:]


def head_sums(value, selector):
    high, low = halves(value)
    return dot(high, selector) + dot(low, selector)


def sigmoid(value):
    return 1.0 / (1.0 + jnp.exp(-value))


def softplus(value):
    tail = jnp.exp(-jnp.abs(value))
    series = tail * (1.0 - tail * (0.5 - tail * (1.0 / 3.0 - 0.25 * tail)))
    return jnp.maximum(value, 0.0) + jnp.where(tail < 0.01, series, jnp.log(1.0 + tail))


def iota(shape, dim):
    return lax.broadcasted_iota(jnp.int32, shape, dim)


def span_scalars(info, m):
    first = info[2 * m]
    start = ((first + (BLOCK - 1)) >> 7) << 7
    return first, start, start + info[2 * m + 1], info[2 * MB], info[2 * MB + 1]


def keeps(info, m):
    _, start, _, base, span = span_scalars(info, m)

    def keep(position):
        begins = (position == 0) | (position == start) | (position >= span)
        return jnp.where(begins, 0.0, 1.0).astype(F32)

    forward = [keep(base), keep(base + BLOCK)]
    reverse = [keep(base + BLOCK), keep(base + 2 * BLOCK)]
    return forward, reverse


def row_masks(info, m, shape):
    first, start, end, base, _ = span_scalars(info, m)
    place = iota(shape, 0) + base
    inside = (place < first) | ((place >= start) & (place < end))
    offset = jnp.where(place >= start, place - start, place)
    return inside.astype(F32), [(offset >= k).astype(F32) for k in range(CONV)]


def conv_windows(ref, cols):
    main = ref[0, :TOK_DEV, cols]
    halo = ref[0, TOK_DEV:, cols]
    whole = jnp.concatenate([halo, main], axis=0)
    return [main] + [whole[HALO - k : HALO - k + TOK_DEV] for k in range(1, CONV)]


def conv_value(windows, masks, taps, cols):
    value = taps[CONV : CONV + 1, cols] + taps[0:1, cols] * windows[0]
    for k in range(1, CONV):
        value = value + taps[k : k + 1, cols] * (windows[k] * masks[k])
    return value


def front_kernel(info, vals, bc, dt, taps, steps, spread_f, spread_r, v_out, bc_out, fr_out, frp_out, tot_f, tot_r, kept_f, kept_r, dx_out):
    m = pl.program_id(0)
    valid, masks = row_masks(info, m, (TOK_DEV, LANES))
    for chunk in range(PAIRS + 1):
        cols = pl.ds(chunk * LANES, LANES)
        source, own = (vals, cols) if chunk < PAIRS else (bc, pl.ds(0, LANES))
        value = conv_value(conv_windows(source, own), masks, taps, cols)
        value = valid * (value * sigmoid(value))
        if chunk < PAIRS:
            v_out[0, :, cols] = value.astype(BF16)
        else:
            bc_out[0] = value
    lane = iota((BLOCK, LANES), 1)
    rows = iota((BLOCK, BLOCK), 0)
    columns = iota((BLOCK, BLOCK), 1)
    lower = (rows >= columns).astype(F32)
    upper = (rows <= columns).astype(F32)
    forward, reverse = keeps(info, m)
    ends = []
    tails = []
    inputs = []
    for b in range(2):
        span = pl.ds(b * BLOCK, BLOCK)
        step = softplus(dt[0, span, :] + steps[0:1, :])
        log = -step * steps[1:2, :]
        summed = jnp.where(lane < HEADS, dot(lower, log, precision=HIGHEST), dot(upper, log, precision=HIGHEST))
        shifted = summed - jnp.log(step)
        fr_out[0, span, :] = summed
        frp_out[0, span, :] = shifted
        end = jnp.where(lane[:1] < HEADS, summed[BLOCK - 1 :], summed[:1])
        ends.append(jnp.exp(end))
        tails.append(spread_operand(jnp.where(lane < 2 * HEADS, jnp.exp(end - shifted), 0.0)))
        acts = bc_out[0, span, :]
        inputs.append(twice(jnp.transpose(by_lane(acts, swapped(acts))).astype(BF16), 1))
    ends = spread_operand(jnp.concatenate(ends + [jnp.zeros((6, LANES), F32)], axis=0))
    width = 2 * LANES
    for chunk in range(INNER // width):
        cols = pl.ds(chunk * width, width)
        decay_f = dot(ends, spread_f[:, cols])
        decay_r = dot(ends, spread_r[:, cols])
        parts_f = []
        parts_r = []
        for b in range(2):
            v = v_out[0, pl.ds(b * BLOCK, BLOCK), cols].astype(F32)
            parts_f.append(fold(dot(inputs[b], stacked(dot(tails[b], spread_f[:, cols]) * v))))
            parts_r.append(fold(dot(inputs[b], stacked(dot(tails[b], spread_r[:, cols]) * v))))
        kept_f[0, :, cols] = parts_f[0]
        kept_r[0, :, cols] = parts_r[1]
        tot_f[0, :, cols] = (parts_f[1] + (forward[1] * decay_f[1:2]) * parts_f[0]).astype(SENT)
        tot_r[0, :, cols] = (parts_r[0] + (reverse[0] * decay_r[0:1]) * parts_r[1]).astype(SENT)
        dx_out[0, 0:2, cols] = decay_f[0:2]
        dx_out[0, 2:4, cols] = decay_r[0:2]
        dx_out[0, 4:5, cols] = (forward[0] * forward[1]) * (decay_f[0:1] * decay_f[1:2])
        dx_out[0, 5:6, cols] = (reverse[0] * reverse[1]) * (decay_r[0:1] * decay_r[1:2])
        dx_out[0, 6:8, cols] = jnp.zeros((2, width), F32)


def stacked(value):
    return jnp.concatenate(halves(value), axis=0)


def doubled(value):
    high, low = halves(value)
    return jnp.concatenate([high, high, low, low], axis=0)


def pair_stack(value):
    lane = iota(value.shape, 1)
    zero = jnp.zeros_like(value)
    return jnp.concatenate([jnp.where(lane < HEAD_DIM, value, zero), jnp.where(lane < HEAD_DIM, zero, value)], axis=0)


def swapped(value):
    return pltpu.roll(value, STATE, axis=1)


def intra_kernel(v, bc, fr, frp, skip, y_out):
    rows = iota((BLOCK, BLOCK), 0)
    columns = iota((BLOCK, BLOCK), 1)
    lower = rows > columns
    acts = bc[0]
    outs = jnp.where(columns < STATE, swapped(acts), 0.0)
    scores = jnp.where(rows == columns, 0.0, dot(outs, acts, COLS, HIGHEST))
    cum = fr[0]
    shifted = jnp.transpose(frp[0])
    for pair in range(PAIRS):
        mats = []
        for h in (2 * pair, 2 * pair + 1):
            r = HEADS + h
            gap = jnp.where(lower, cum[:, h : h + 1] - shifted[h : h + 1], cum[:, r : r + 1] - shifted[r : r + 1])
            mats.append((jnp.exp(gap) * scores).astype(BF16))
        cols = pl.ds(pair * LANES, LANES)
        value = v[0, :, cols]
        y = dot(jnp.concatenate(mats, axis=1), pair_stack(value))
        y_out[0, :, cols] = y + skip[0:1, cols] * value.astype(F32)


def entering(b, cols, forward, reverse, enter_f, enter_r, kept_f, kept_r, dx):
    first_f = forward[0] * enter_f[0, :, cols].astype(F32)
    last_r = reverse[1] * enter_r[0, :, cols].astype(F32)
    state_f = jnp.where(b == 0, first_f, forward[1] * (dx[0, 0:1, cols] * first_f + kept_f[0, :, cols]))
    state_r = jnp.where(b == 1, last_r, reverse[0] * (dx[0, 3:4, cols] * last_r + kept_r[0, :, cols]))
    return state_f, state_r


def middle_kernel(
    info, y, gate, d_normed, v, bc, fr, enter_f, enter_r, kept_f, kept_r, dx, gain, spread_f, spread_r, sum_f, sum_r,
    normed, d_mixed, d_gate, back_f, back_r, leave_f, leave_r, d_outs, read_out, d_gain, d_skip, mixed_s, part_f, part_r, exp_f, exp_r,
):
    m, b = pl.program_id(0), pl.program_id(1)
    forward, reverse = keeps(info, m)
    lane = iota((BLOCK, LANES), 1)
    outs = by_lane(swapped(bc[0]), bc[0])
    outs_t = twice(jnp.transpose(outs).astype(BF16), 1)
    outs = twice(outs.astype(BF16), 1)
    grown = spread_operand(jnp.where(lane < 2 * HEADS, jnp.exp(fr[0]), 0.0))
    width = 2 * LANES
    chunks = INNER // width
    squares = jnp.zeros((BLOCK, 1), F32)
    cross = jnp.zeros((BLOCK, 1), F32)
    for chunk in range(chunks):
        cols = pl.ds(chunk * width, width)
        state_f, state_r = entering(b, cols, forward, reverse, enter_f, enter_r, kept_f, kept_r, dx)
        ef = dot(grown, spread_f[:, cols])
        er = dot(grown, spread_r[:, cols])
        carried_f = ef * dot(outs, doubled(state_f))
        carried_r = er * dot(outs, doubled(state_r))
        mixed = y[0, :, cols] + carried_f + carried_r
        exp_f[:, cols] = ef
        exp_r[:, cols] = er
        part_f[:, cols] = carried_f
        part_r[:, cols] = carried_r
        mixed_s[:, cols] = mixed
        g = gate[0, :, cols]
        gated = mixed * (g * sigmoid(g))
        squares = squares + jnp.sum(gated * gated, axis=1, keepdims=True)
        cross = cross + jnp.sum(gated * gain[0:1, cols] * d_normed[0, :, cols], axis=1, keepdims=True)
    scale = lax.rsqrt(squares * (1.0 / INNER) + EPSILON)
    pull = scale * scale * scale * (cross * (1.0 / INNER))
    d_o = jnp.zeros((BLOCK, LANES), F32)
    reads = jnp.zeros((BLOCK, LANES), F32)

    @pl.when((m == 0) & (b == 0))
    def _():
        d_gain[...] = jnp.zeros_like(d_gain)
        d_skip[...] = jnp.zeros_like(d_skip)

    @pl.when(b == 0)
    def _():
        leave_f[...] = jnp.zeros_like(leave_f)
        leave_r[...] = jnp.zeros_like(leave_r)

    for chunk in range(chunks):
        cols = pl.ds(chunk * width, width)
        g = gate[0, :, cols]
        sig = sigmoid(g)
        silu = g * sig
        mixed = mixed_s[:, cols]
        gated = mixed * silu
        dy = d_normed[0, :, cols]
        scaled = gated * scale
        normed[0, :, cols] = (scaled * gain[0:1, cols]).astype(BF16)
        d_gain[0:1, cols] += jnp.sum(dy * scaled, axis=0, keepdims=True)
        d_gated = scale * gain[0:1, cols] * dy - gated * pull
        dm = d_gated * silu
        d_gate[0, :, cols] = (d_gated * mixed * sig * (1.0 + g * (1.0 - sig))).astype(BF16)
        d_mixed[0, :, cols] = dm.astype(BF16)
        d_skip[0:1, cols] += jnp.sum(dm * v[0, :, cols].astype(F32), axis=0, keepdims=True)
        state_f, state_r = entering(b, cols, forward, reverse, enter_f, enter_r, kept_f, kept_r, dx)
        grown_f = exp_f[:, cols] * dm
        grown_r = exp_r[:, cols] * dm
        local_f = fold(dot(outs_t, stacked(grown_f)))
        local_r = fold(dot(outs_t, stacked(grown_r)))
        back_f[0, 0, :, cols] = local_f
        back_r[0, 0, :, cols] = local_r
        weight_f = jnp.where(b == 0, forward[0], (forward[0] * forward[1]) * dx[0, 0:1, cols])
        weight_r = jnp.where(b == 0, (reverse[0] * reverse[1]) * dx[0, 3:4, cols], reverse[1])
        leave_f[0, :, cols] += weight_f * local_f
        leave_r[0, :, cols] += weight_r * local_r
        d_o = d_o + dot(spread_operand(grown_f), twice(stacked(state_f), 1), COLS)
        d_o = d_o + dot(spread_operand(grown_r), twice(stacked(state_r), 1), COLS)
        reads = reads + head_sums(dm * part_f[:, cols], sum_f[cols, :]) + head_sums(dm * part_r[:, cols], sum_r[cols, :])
    d_outs[0] = jnp.where(lane < STATE, 0.0, d_o + swapped(d_o))
    read_out[0] = reads


def intra_back_kernel(v, d_mixed, bc, fr, frp, skip, d_outs, read_out, d_v, d_bc, sums, d_log, row_s):
    rows = iota((BLOCK, BLOCK), 0)
    columns = iota((BLOCK, BLOCK), 1)
    ahead = rows < columns
    acts = bc[0]
    low = columns < STATE
    turned = swapped(acts)
    outs = jnp.where(low, turned, 0.0)
    scores = jnp.where(rows == columns, 0.0, dot(acts, outs, COLS, HIGHEST))
    cum = jnp.transpose(fr[0])
    shifted = frp[0]
    d_scores = jnp.zeros((BLOCK, BLOCK), F32)
    gathered = jnp.zeros((BLOCK, LANES), F32)

    row_s[...] = jnp.zeros_like(row_s)
    for pair in range(PAIRS):
        cols = pl.ds(pair * LANES, LANES)
        value = v[0, :, cols]
        dm = d_mixed[0, :, cols]
        products = dot(pair_stack(value), dm, COLS)
        mats = []
        for side in range(2):
            h = 2 * pair + side
            r = HEADS + h
            gap = jnp.where(ahead, cum[h : h + 1] - shifted[:, h : h + 1], cum[r : r + 1] - shifted[:, r : r + 1])
            weight = jnp.exp(gap)
            mats.append((weight * scores).astype(BF16))
            reach = products[side * BLOCK : (side + 1) * BLOCK] * weight
            d_scores = d_scores + reach
            both = reach * scores
            first = jnp.where(ahead, both, 0.0)
            second = both - first
            gathered = jnp.where(columns == h, jnp.sum(first, axis=1, keepdims=True), gathered)
            gathered = jnp.where(columns == r, jnp.sum(second, axis=1, keepdims=True), gathered)
            row_s[h : h + 1, :] = jnp.sum(first, axis=0, keepdims=True)
            row_s[r : r + 1, :] = jnp.sum(second, axis=0, keepdims=True)
        dmf = dm.astype(F32)
        d_v[0, :, cols] = dot(jnp.concatenate(mats, axis=1), pair_stack(dm)) + skip[0:1, cols] * dmf
    d_scores = jnp.where(rows == columns, 0.0, d_scores)
    ins = jnp.where(low, 0.0, turned)
    d_bc[0] = dot(d_scores, outs, precision=HIGHEST) + dot(jnp.transpose(d_scores), ins, precision=HIGHEST) + d_outs[0]
    sums[0] = gathered
    d_log[0] = jnp.transpose(row_s[...]) - gathered + read_out[0]


def final_kernel(
    info, vals, bc_in, dt, taps, steps, v, bc, fr, frp, enter_f, enter_r, kept_f, kept_r, dx, after_f, after_r, back_f, back_r,
    d_v, d_bc, sums, d_log, spread_f, spread_r, sum_f, sum_r,
    late, before, last, d_taps, d_small, d_acts,
):
    m = pl.program_id(0)
    forward, reverse = keeps(info, m)
    lane = iota((BLOCK, LANES), 1)
    row = iota((BLOCK, LANES), 0)
    rows = iota((BLOCK, BLOCK), 0)
    columns = iota((BLOCK, BLOCK), 1)
    lower = (rows >= columns).astype(F32)
    upper = (rows <= columns).astype(F32)
    width = 2 * LANES

    @pl.when(m == 0)
    def _():
        d_taps[...] = jnp.zeros_like(d_taps)
        d_small[...] = jnp.zeros_like(d_small)

    for b in range(2):
        span = pl.ds(b * BLOCK, BLOCK)
        summed = fr[0, span, :]
        end = jnp.where(lane[:1] < HEADS, summed[BLOCK - 1 :], summed[:1])
        tail = spread_operand(jnp.where(lane < 2 * HEADS, jnp.exp(end - frp[0, span, :]), 0.0))
        acts = bc[0, span, :]
        ins = twice(by_lane(acts, swapped(acts)).astype(BF16), 1)
        d_in = jnp.zeros((BLOCK, LANES), F32)
        used = jnp.zeros((BLOCK, LANES), F32)
        decays = jnp.zeros((8, LANES), F32)
        for chunk in range(INNER // width):
            cols = pl.ds(chunk * width, width)
            grad_f = after_f[0, :, cols].astype(F32)
            grad_r = after_r[0, :, cols].astype(F32)
            if b == 0:
                grad_f = forward[1] * (back_f[0, 1, :, cols] + dx[0, 1:2, cols] * grad_f)
            else:
                grad_r = reverse[0] * (back_r[0, 0, :, cols] + dx[0, 2:3, cols] * grad_r)
            state_f, state_r = entering(b, cols, forward, reverse, enter_f, enter_r, kept_f, kept_r, dx)
            tail_f = dot(tail, spread_f[:, cols])
            tail_r = dot(tail, spread_r[:, cols])
            value = v[0, span, cols].astype(F32)
            pulled_f = tail_f * dot(ins, doubled(grad_f))
            pulled_r = tail_r * dot(ins, doubled(grad_r))
            d_acts[span, cols] = d_v[0, span, cols] + pulled_f + pulled_r
            d_in = d_in + dot(spread_operand(tail_f * value), twice(stacked(grad_f), 1), COLS)
            d_in = d_in + dot(spread_operand(tail_r * value), twice(stacked(grad_r), 1), COLS)
            used = used + head_sums(pulled_f * value, sum_f[cols, :]) + head_sums(pulled_r * value, sum_r[cols, :])
            meet_f = jnp.sum(grad_f * state_f, axis=0, keepdims=True) * dx[0, b : b + 1, cols]
            meet_r = jnp.sum(grad_r * state_r, axis=0, keepdims=True) * dx[0, 2 + b : 3 + b, cols]
            zero = jnp.zeros((7, width), F32)
            decays = decays + head_sums(jnp.concatenate([meet_f, zero], axis=0), sum_f[cols, :])
            decays = decays + head_sums(jnp.concatenate([meet_r, zero], axis=0), sum_r[cols, :])
        d_acts[span, pl.ds(INNER, LANES)] = d_bc[0, span, :] + jnp.where(lane < STATE, d_in + swapped(d_in), 0.0)
        direct = sums[0, span, :] + used
        edge = decays[0:1] + jnp.sum(used, axis=0, keepdims=True)
        at_end = ((lane < HEADS) & (row == BLOCK - 1)) | ((lane >= HEADS) & (row == 0))
        grad = d_log[0, span, :] - used + jnp.where(at_end, edge, 0.0)
        grad = jnp.where(lane < HEADS, dot(upper, grad, precision=HIGHEST), dot(lower, grad, precision=HIGHEST))
        x = dt[0, span, :] + steps[0:1, :]
        step = softplus(x)
        sig = sigmoid(x)
        ratio = jnp.where(x < -17.0, 1.0, sig / step)
        d_x = direct * ratio - steps[1:2, :] * grad * sig
        d_x = jnp.where(lane < 2 * HEADS, d_x, 0.0)
        late[0, span, pl.ds(INNER + LANES, LANES)] = d_x.astype(BF16)
        d_small[0:1, :] += jnp.sum(d_x, axis=0, keepdims=True)
        d_small[1:2, :] -= steps[1:2, :] * jnp.sum(step * grad, axis=0, keepdims=True)
    valid, masks = row_masks(info, m, (TOK_DEV, LANES))
    edge = jnp.zeros((HALO, LANES), F32)
    for chunk in range(PAIRS + 1):
        cols = pl.ds(chunk * LANES, LANES)
        source, own = (vals, cols) if chunk < PAIRS else (bc_in, pl.ds(0, LANES))
        windows = conv_windows(source, own)
        value = conv_value(windows, masks, taps, cols)
        sig = sigmoid(value)
        grad = valid * d_acts[:, cols] * (sig * (1.0 + value * (1.0 - sig)))
        total = jnp.zeros((HALO + TOK_DEV, LANES), F32)
        for k in range(CONV):
            masked = grad if k == 0 else grad * masks[k]
            d_taps[k : k + 1, cols] += jnp.sum(masked * windows[k], axis=0, keepdims=True)
            padded = jnp.concatenate([edge, masked, edge], axis=0)
            total = total + taps[k : k + 1, cols] * padded[k : k + HALO + TOK_DEV]
        d_taps[CONV : CONV + 1, cols] += jnp.sum(grad, axis=0, keepdims=True)
        before[0, :, cols] = total[:HALO]
        last[0, :, cols] = total[TOK_DEV:]
        late[0, :, cols] = total[HALO:].astype(BF16)


def once(shape):
    return pl.BlockSpec(shape, lambda *grid: (0,) * len(shape))


def per_micro(shape, column=0):
    return pl.BlockSpec((1,) + shape, lambda m, *rest: (m,) + (0,) * (len(shape) - 1) + (column,))


def per_block(width, column=0):
    return pl.BlockSpec((1, BLOCK, width), lambda m, b: (m, b, column))


def struct(*shape, dtype=F32):
    return jax.ShapeDtypeStruct(shape, dtype)


SCALARS = pl.BlockSpec(memory_space=pltpu.SMEM)


def call(kernel, grid, in_specs, out_specs, out_shape, scratch=(), flops=0, moved=0):
    return pl.pallas_call(
        kernel,
        grid=grid,
        in_specs=in_specs,
        out_specs=out_specs,
        out_shape=out_shape,
        scratch_shapes=list(scratch),
        compiler_params=pltpu.CompilerParams(vmem_limit_bytes=VMEM_LIMIT),
        cost_estimate=pl.CostEstimate(flops=flops, bytes_accessed=moved, transcendentals=0),
    )


def shift(value, distance):
    count = lax.axis_size("dp")
    route = [(i, i + distance) for i in range(count) if 0 <= i + distance < count]
    return lax.ppermute(value, "dp", route)


def carry_kernel(
    levels, up_row, down_row, up_in, down_in, gains_in, up_out, down_out,
    up_other, down_other, gains_other, up_chain, down_chain, up_next, down_next,
    up_sems, down_sems, gain_sems, up_link, down_link,
):
    me = lax.axis_index("dp")
    side = lax.rem(me, 2)
    level = me // 2
    partner = me + 1 - 2 * side
    above, below = me + 2, me - 2
    has_above, has_below = level < levels - 1, level > 0

    barrier = pltpu.get_barrier_semaphore()
    pl.semaphore_signal(barrier, inc=1, device_id={"dp": partner})

    @pl.when(has_above)
    def _():
        pl.semaphore_signal(barrier, inc=1, device_id={"dp": above})

    @pl.when(has_below)
    def _():
        pl.semaphore_signal(barrier, inc=1, device_id={"dp": below})

    pl.semaphore_wait(barrier, 1 + has_above.astype(jnp.int32) + has_below.astype(jnp.int32))

    def remote(source, target, sems, k, device):
        return pltpu.make_async_remote_copy(
            src_ref=source, dst_ref=target, send_sem=sems.at[0, k], recv_sem=sems.at[1, k], device_id={"dp": device}
        )

    def swap_up(k):
        return remote(up_in.at[k], up_other.at[k], up_sems, k, partner)

    def swap_down(k):
        return remote(down_in.at[k], down_other.at[k], down_sems, k, partner)

    def climb(k):
        return remote(up_next.at[k], up_chain.at[k], up_link, k, above)

    def descend(k):
        return remote(down_next.at[k], down_chain.at[k], down_link, k, below)

    swap_gains = remote(gains_in, gains_other, gain_sems, 0, partner)
    swap_gains.start()

    @pl.loop(0, CHUNKS)
    def _(k):
        swap_up(k).start()
        swap_down(k).start()

    @pl.when(level == 0)
    def _():
        up_chain[...] = jnp.zeros_like(up_chain)

    @pl.when(level == levels - 1)
    def _():
        down_chain[...] = jnp.zeros_like(down_chain)

    swap_gains.wait()
    first = side == 0

    @pl.loop(0, CHUNKS + levels - 1)
    def _(s):
        up, down = s - level, s - (levels - 1 - level)

        @pl.when((up >= 0) & (up < CHUNKS))
        def _():
            swap_up(up).wait()

            @pl.when(has_below)
            def _():
                climb(up).wait_recv()

            m = up // PARTS
            own, other = gains_in[m, up_row : up_row + 1], gains_other[m, up_row : up_row + 1]
            near, far = jnp.where(first, own, other), jnp.where(first, other, own)
            mine, theirs = up_in[up], up_other[up]
            before = up_chain[up]
            middle = jnp.where(first, mine, theirs) + near * before
            up_out[up] = jnp.where(first, before, middle)

            @pl.when(has_above)
            def _():
                up_next[up] = jnp.where(first, theirs, mine) + far * middle
                climb(up).start()

        @pl.when((down >= 0) & (down < CHUNKS))
        def _():
            swap_down(down).wait()

            @pl.when(has_above)
            def _():
                descend(down).wait_recv()

            m = down // PARTS
            own, other = gains_in[m, down_row : down_row + 1], gains_other[m, down_row : down_row + 1]
            near, far = jnp.where(first, other, own), jnp.where(first, own, other)
            mine, theirs = down_in[down], down_other[down]
            before = down_chain[down]
            middle = jnp.where(first, theirs, mine) + near * before
            down_out[down] = jnp.where(first, middle, before)

            @pl.when(has_below)
            def _():
                down_next[down] = jnp.where(first, mine, theirs) + far * middle
                descend(down).start()

    @pl.when(has_above)
    def _():
        @pl.loop(0, CHUNKS)
        def _(k):
            climb(k).wait_send()

    @pl.when(has_below)
    def _():
        @pl.loop(0, CHUNKS)
        def _(k):
            descend(k).wait_send()


def carry(up, down, gains, up_row, down_row, identity):
    levels = lax.axis_size("dp") // 2
    shape = (CHUNKS, STATE // PARTS, INNER)
    buffer = pltpu.VMEM(shape, F32)
    outs = pl.pallas_call(
        partial(carry_kernel, levels, up_row, down_row),
        in_specs=[pl.BlockSpec(memory_space=pltpu.VMEM)] * 3,
        out_specs=[pl.BlockSpec(memory_space=pltpu.VMEM)] * 2,
        out_shape=[struct(*shape), struct(*shape)],
        scratch_shapes=[buffer, buffer, pltpu.VMEM((MB, 8, INNER), F32), buffer, buffer, buffer, buffer]
        + [pltpu.SemaphoreType.DMA((2, CHUNKS))] * 2
        + [pltpu.SemaphoreType.DMA((2, 1))]
        + [pltpu.SemaphoreType.DMA((2, CHUNKS))] * 2,
        compiler_params=pltpu.CompilerParams(vmem_limit_bytes=VMEM_LIMIT, collective_id=identity, has_side_effects=True),
    )(up.reshape(shape), down.reshape(shape), gains)
    return [out.reshape(MB, STATE, INNER) for out in outs]


def total_kernel(
    levels, columns, first_in, second_in, third_in, taps_in, scale_in, skip_in, small_in, norm_in, selector,
    first_out, inner_out, state_out, step_out, norm_out, taps_out, bias_out, steps_out, decay_out, skip_out, scale_out,
    mate_got, cross_put, cross_got, third_sum, fourth_sum,
    put_1y, got_1y, put_1z, got_1z, sum_1, all_1,
    put_2z, got_2z, put_2y, got_2y, sum_2, all_2,
    put_3y, got_3y, put_3z, got_3z, all_3,
    put_4z, got_4z, put_4y, got_4y, all_4, short_sum, short_got, short_sems,
    mate_sems, cross_sems, side_sems, level_sems,
):
    me, part = lax.axis_index("dp"), lax.axis_index("fsdp")
    side, level = lax.rem(me, 2), me // 2
    core, column = lax.rem(part, 2), part // 2
    partner = me + 1 - 2 * side
    mate = part + 1 - 2 * core

    def level_at(d):
        return lax.rem(level + d + levels, levels)

    def column_at(d):
        return lax.rem(column + d + columns, columns)

    def device(at):
        return {"dp": 2 * level_at(at) + side}

    barrier = pltpu.get_barrier_semaphore()
    pl.semaphore_signal(barrier, inc=1, device_id={"dp": partner})
    pl.semaphore_signal(barrier, inc=1, device_id={"fsdp": mate})
    for d in range(1, levels):
        pl.semaphore_signal(barrier, inc=1, device_id=device(d))
    for d in range(1, columns):
        pl.semaphore_signal(barrier, inc=1, device_id={"fsdp": 2 * column_at(d) + core})
    pl.semaphore_wait(barrier, levels + columns)

    def remote(source, target, sems, k, where):
        return pltpu.make_async_remote_copy(
            src_ref=source, dst_ref=target, send_sem=sems.at[0, k], recv_sem=sems.at[1, k], device_id=where
        )

    waiting = []

    def start(copy):
        copy.start()
        waiting.append(copy)

    def beside(source, target, k):
        return remote(source, target, side_sems, k, {"dp": partner})

    def scatter(put, got, k, d):
        return remote(put.at[level_at(d)], got.at[level], level_sems, k * levels + d, device(d))

    def scattered(put, got, k, d):
        return remote(put.at[level_at(d)], got.at[level_at(-d)], level_sems, k * levels + d, device(d))

    def gather(pick, k, d):
        return remote(pick(level), pick(level), level_sems, k * levels + d, device(d))

    def gathered(pick, k, d):
        return remote(pick(level), pick(level_at(-d)), level_sems, k * levels + d, device(d))

    for x in range(columns):
        start(remote(third_in.at[2 * x + 1 - core], mate_got.at[x], mate_sems, x, {"fsdp": mate}))

    lane = iota((8, LANES), 1)
    summed = jnp.where(lane < HEADS, head_sums(skip_in[...], selector[...]), 0.0)
    folded = small_in[...] + pltpu.roll(small_in[...], LANES - HEADS, axis=1)
    short_sum[0, 0:8, :] = taps_in[...]
    short_sum[0, 8:16, :] = jnp.zeros((8, CONV_COLS), F32)
    short_sum[0, 5:6, :INNER] = scale_in[0:1]
    short_sum[0, 6:7, :D] = norm_in[...]
    short_sum[0, 8:9, :LANES] = small_in[0:1]
    short_sum[0, 9:10, :LANES] = folded[1:2]
    short_sum[0, 10:11, :LANES] = summed[0:1]
    routes = [{"fsdp": mate}, {"dp": partner}]
    stride = 1
    while stride < columns:
        routes.append({"fsdp": part + 2 * stride - 4 * stride * lax.rem(column // stride, 2)})
        stride *= 2
    stride = 1
    while stride < levels:
        routes.append({"dp": me + 2 * stride - 4 * stride * lax.rem(level // stride, 2)})
        stride *= 2

    def short(k):
        return remote(short_sum.at[k], short_got.at[k], short_sems, k, routes[k])

    def short_step(k):
        if k > 0:
            short(k - 1).wait_recv()
            short_sum[k] = short_sum[k - 1] + short_got[k - 1]
        if k < len(routes):
            start(short(k))

    short_step(0)
    put_1y[...] = first_in[1 - side].astype(BF16)
    start(beside(put_1y, got_1y, 0))
    half = put_2z.shape[-1]
    for d in range(1, levels):
        target = level_at(d)
        for h in range(2):
            put_2z[target, h] = second_in[target, :, h * half : (h + 1) * half].astype(BF16)
        start(scatter(put_2z, got_2z, 0, d))

    short_step(1)
    rows, width = third_sum.shape[2], third_sum.shape[3]
    for x in range(columns):
        remote(third_in.at[2 * x + 1 - core], mate_got.at[x], mate_sems, x, {"fsdp": mate}).wait_recv()
    for d in range(1, columns):
        x = column_at(d)
        cross_put[x] = (third_in[2 * x + core] + mate_got[x]).astype(BF16)
        start(remote(cross_put.at[x], cross_got.at[column], cross_sems, d, {"fsdp": 2 * x + core}))

    short_step(2)
    beside(put_1y, got_1y, 0).wait_recv()
    sum_1[...] = first_in[side] + got_1y[...].astype(F32)
    for d in range(1, levels):
        target = level_at(d)
        put_1z[target] = sum_1[target].astype(BF16)
        start(scatter(put_1z, got_1z, 1, d))

    short_step(3)
    total = [second_in[level, :, h * half : (h + 1) * half] for h in range(2)]
    for d in range(1, levels):
        scattered(put_2z, got_2z, 0, d).wait_recv()
        for h in range(2):
            total[h] = total[h] + got_2z[level_at(-d), h].astype(F32)
    first = side == 0
    put_2y[...] = jnp.where(first, total[1], total[0]).astype(BF16)
    sum_2[...] = jnp.where(first, total[0], total[1])
    start(beside(put_2y, got_2y, 1))

    for d in range(1, columns):
        remote(cross_put.at[column_at(d)], cross_got.at[column_at(-d)], cross_sems, d, {"fsdp": part}).wait_recv()
    for x in range(2):
        for j in range(levels):
            at = pl.ds((x * levels + j) * rows, rows)
            value = third_in[part, at, :] + mate_got[column, at, :]
            for d in range(1, columns):
                value = value + cross_got[column_at(-d), at, :].astype(F32)
            third_sum[x, j] = value[:, :width]
            place = x * levels + j
            fourth_sum[place // 2, place % 2] = value[:, width:]

    short_step(4)
    put_3y[...] = third_sum[1 - side].astype(BF16)
    start(beside(put_3y, got_3y, 2))
    for d in range(1, levels):
        target = level_at(d)
        put_4z[target] = fourth_sum[target].astype(BF16)
        start(scatter(put_4z, got_4z, 2, d))

    total = sum_1[level]
    for d in range(1, levels):
        scattered(put_1z, got_1z, 1, d).wait_recv()
        total = total + got_1z[level_at(-d)].astype(F32)
    all_1[side, level] = total.astype(BF16)
    for d in range(1, levels):
        start(gather(lambda at: all_1.at[side, at], 3, d))

    for k in range(5, len(routes) + 1):
        short_step(k)
    result = short_sum.at[len(routes)]
    for f in range(2 * columns):

        @pl.when(part == f)
        def _():
            def own(row, rows, width, ref):
                size = width // (2 * columns)
                ref[...] = result[row : row + rows, f * size : (f + 1) * size]

            own(0, CONV, CONV_COLS, taps_out)
            own(4, 1, CONV_COLS, bias_out)
            own(5, 1, INNER, scale_out)
            own(6, 1, D, norm_out)
            own(8, 1, 2 * HEADS, steps_out)
            own(9, 1, HEADS, decay_out)
            own(10, 1, HEADS, skip_out)

    beside(put_2y, got_2y, 1).wait_recv()
    all_2[level, side] = (sum_2[...] + got_2y[...].astype(F32)).astype(BF16)
    start(beside(all_2.at[level, side], all_2.at[level, side], 3))

    beside(put_3y, got_3y, 2).wait_recv()
    third_sum[side] = third_sum[side] + got_3y[...].astype(F32)
    for d in range(1, levels):
        target = level_at(d)
        put_3z[target] = third_sum[side, target].astype(BF16)
        start(scatter(put_3z, got_3z, 4, d))

    total = fourth_sum[level]
    for d in range(1, levels):
        scattered(put_4z, got_4z, 2, d).wait_recv()
        total = total + got_4z[level_at(-d)].astype(F32)
    fourth_sum[level] = total
    put_4y[...] = fourth_sum[level, 1 - side].astype(BF16)
    start(beside(put_4y, got_4y, 4))

    for d in range(1, levels):
        gathered(lambda at: all_1.at[side, at], 3, d).wait_recv()
    start(beside(all_1.at[side], all_1.at[side], 5))
    beside(all_2.at[level, side], all_2.at[level, 1 - side], 3).wait_recv()
    for d in range(1, levels):
        start(gather(lambda at: all_2.at[at], 5, d))

    total = third_sum[side, level]
    for d in range(1, levels):
        scattered(put_3z, got_3z, 4, d).wait_recv()
        total = total + got_3z[level_at(-d)].astype(F32)
    all_3[side, level] = total.astype(BF16)
    for d in range(1, levels):
        start(gather(lambda at: all_3.at[side, at], 6, d))

    beside(put_4y, got_4y, 4).wait_recv()
    all_4[level, side] = (fourth_sum[level, side] + got_4y[...].astype(F32)).astype(BF16)
    start(beside(all_4.at[level, side], all_4.at[level, side], 6))

    beside(all_1.at[side], all_1.at[1 - side], 5).wait_recv()
    first_out[...] = all_1[...].astype(F32)
    for d in range(1, levels):
        gathered(lambda at: all_2.at[at], 5, d).wait_recv()
    for h in range(2):
        for j in range(levels):
            inner_out[j * 2 * rows : (j + 1) * 2 * rows, h * half : (h + 1) * half] = all_2[j, h].astype(F32)

    for d in range(1, levels):
        gathered(lambda at: all_3.at[side, at], 6, d).wait_recv()
    start(beside(all_3.at[side], all_3.at[side], 7))
    beside(all_4.at[level, side], all_4.at[level, 1 - side], 6).wait_recv()
    for d in range(1, levels):
        start(gather(lambda at: all_4.at[at], 7, d))
    beside(all_3.at[side], all_3.at[1 - side], 7).wait_recv()
    for d in range(1, levels):
        gathered(lambda at: all_4.at[at], 7, d).wait_recv()
    for x in range(2):
        for j in range(levels):
            place = x * levels + j
            at = pl.ds(place * rows, rows)
            inner_out[at, INNER : INNER + width] = all_3[x, j].astype(F32)
            value = all_4[place // 2, place % 2].astype(F32)
            inner_out[at, INNER + width :] = value[:, : INNER - width]
            state_out[at, :] = value[:, INNER - width : INNER - width + LANES]
            step_out[at, :] = value[:, INNER - width + LANES : INNER - width + LANES + 2 * HEADS]
    for copy in waiting:
        copy.wait_send()


def total_fits(levels, shards, dp_count):
    rows = D // shards
    return dp_count == 2 * levels and shards % 2 == 0 and rows % (16 * levels) == 0 and 24 % shards == 0


def totals(first, second, third, short, identity):
    dp_count, shards = lax.axis_size("dp"), lax.axis_size("fsdp")
    levels, columns = dp_count // 2, shards // 2
    rows = D // shards
    piece = rows // levels
    small = piece // 2
    width = LATE // 2
    steps = (dp_count * shards).bit_length() - 1

    def low(*shape):
        return pltpu.VMEM(shape, BF16)

    def full(*shape):
        return pltpu.VMEM(shape, F32)

    outs = pl.pallas_call(
        partial(total_kernel, levels, columns),
        in_specs=[pl.BlockSpec(memory_space=pltpu.VMEM)] * 9,
        out_specs=[pl.BlockSpec(memory_space=pltpu.VMEM)] * 11,
        out_shape=[struct(2, levels, piece, D), struct(rows, 2 * INNER), struct(rows, 2 * STATE), struct(rows, 2 * HEADS)]
        + [struct(1, D // shards), struct(CONV, CONV_COLS // shards), struct(1, CONV_COLS // shards)]
        + [struct(1, width // shards) for width in (2 * HEADS, HEADS, HEADS, INNER)],
        scratch_shapes=[
            full(columns, rows, LATE), low(columns, rows, LATE), low(columns, rows, LATE),
            full(2, levels, small, width), full(levels, 2, small, width),
            low(levels, piece, D), low(levels, piece, D), low(levels, piece, D), low(levels, piece, D),
            full(levels, piece, D), low(2, levels, piece, D),
            low(levels, 2, piece, D), low(levels, 2, piece, D), low(piece, D), low(piece, D),
            full(piece, D), low(levels, 2, piece, D),
            low(levels, small, width), low(levels, small, width), low(levels, small, width), low(levels, small, width),
            low(2, levels, small, width),
            low(levels, 2, small, width), low(levels, 2, small, width), low(small, width), low(small, width),
            low(levels, 2, small, width),
            full(steps + 1, 16, CONV_COLS), full(steps, 16, CONV_COLS), pltpu.SemaphoreType.DMA((2, steps)),
            pltpu.SemaphoreType.DMA((2, columns)), pltpu.SemaphoreType.DMA((2, columns)),
            pltpu.SemaphoreType.DMA((2, 8)), pltpu.SemaphoreType.DMA((2, 8 * levels)),
        ],
        compiler_params=pltpu.CompilerParams(vmem_limit_bytes=VMEM_LIMIT, collective_id=identity, has_side_effects=True),
    )(
        first.reshape(2, levels, piece, D), second.reshape(levels, piece, INNER), third.reshape(shards, rows, LATE), *short,
    )
    flat = [out.reshape(-1) for out in outs[6:]]
    return [outs[4].reshape(-1)] + list(outs[1:4]) + [outs[5]] + flat + [outs[0].reshape(2 * rows, D)]


def rms(values):
    return lax.rsqrt(jnp.mean(values * values, axis=-1, keepdims=True) + EPSILON)


def gather_small(parts):
    flat = jnp.concatenate([part.reshape(-1) for part in parts])
    size = flat.shape[0]
    padded = -(-size // LANES) * LANES
    everything = lax.all_gather(jnp.pad(flat, (0, padded - size)).reshape(1, padded), "fsdp", axis=0, tiled=True)
    result = []
    at = 0
    for part in parts:
        piece = everything[:, at : at + part.size].astype(F32)
        at += part.size
        if part.ndim == 2:
            piece = piece.reshape(-1, *part.shape).transpose(1, 0, 2).reshape(part.shape[0], -1)
        else:
            piece = piece.reshape(-1)
        result.append(piece)
    return result


def scatter_small(parts, shards):
    rows = []
    for part in parts:
        if part.ndim == 2:
            rows.append(part.reshape(part.shape[0], shards, -1).transpose(1, 0, 2).reshape(shards, -1))
        else:
            rows.append(part.reshape(shards, -1))
    flat = jnp.concatenate(rows, axis=1)
    size = flat.shape[1]
    padded = -(-size // LANES) * LANES
    return jnp.pad(flat, ((0, 0), (0, padded - size)))


def on_device(
    tokens, seq_lengths, norm_gain, w_inner, w_state, w_step, conv_weight, conv_bias, step_bias, decay_log, skip_gain, out_gain, w_out, cotangent,
):
    dp_count = lax.axis_size("dp")
    shards = lax.axis_size("fsdp")
    base = lax.axis_index("dp") * TOK_DEV
    lengths = seq_lengths[:, 0]
    info = jnp.concatenate([lengths.reshape(-1), jnp.stack([base, jnp.int32(dp_count * TOK_DEV)]).astype(jnp.int32)])
    mine = jnp.concatenate([w_inner, w_state, w_step, jnp.zeros((w_step.shape[0], WIDE - 2 * INNER - 2 * STATE - 2 * HEADS), BF16)], axis=1)
    w_all = lax.all_gather(mine, "fsdp", axis=0, tiled=True)
    gain_in, weight_conv, bias_conv, bias_steps, log_decay, gain_skip, gain_out = gather_small(
        (norm_gain, conv_weight, conv_bias, step_bias, decay_log, skip_gain, out_gain)
    )
    w_all, w_later = lax.optimization_barrier((w_all, w_out))
    w_back = lax.all_gather(w_later, "fsdp", axis=0, tiled=True)

    taps = jnp.concatenate([weight_conv, bias_conv[None], jnp.zeros((3, CONV_COLS), F32)], axis=0)
    rates = jnp.exp(log_decay)
    steps = jnp.zeros((8, LANES), F32).at[0, : 2 * HEADS].set(bias_steps).at[1, : 2 * HEADS].set(jnp.concatenate([rates, rates]))
    skip = jnp.broadcast_to(jnp.repeat(gain_skip, HEAD_DIM)[None], (8, INNER))
    out_scale = jnp.broadcast_to(gain_out[None], (8, INNER))
    head_of = jnp.arange(INNER, dtype=jnp.int32) // HEAD_DIM
    lanes = jnp.arange(LANES, dtype=jnp.int32)
    sum_f = (head_of[:, None] == lanes[None, :]).astype(BF16)
    sum_r = (head_of[:, None] + HEADS == lanes[None, :]).astype(BF16)
    both = jnp.concatenate([lanes, lanes])
    spread_f = (both[:, None] == head_of[None, :]).astype(BF16)
    spread_r = (both[:, None] == head_of[None, :] + HEADS).astype(BF16)

    x = tokens[:, 0]
    halo = shift(x[:, TOK_DEV - HALO :], 1)
    x_all = jnp.concatenate([x, halo], axis=1).astype(F32)
    hidden = (x_all * rms(x_all) * gain_in).astype(BF16)
    rows = TOK_DEV + HALO
    zx = jnp.dot(hidden.reshape(MB * rows, D), w_all, preferred_element_type=F32).reshape(MB, rows, WIDE)

    places = base + jnp.arange(TOK_DEV, dtype=jnp.int32)
    first = lengths[:, :1]
    start = (first + BLOCK - 1) // BLOCK * BLOCK
    valid = (places[None] < first) | (places[None] >= start) & (places[None] < start + lengths[:, 1:])
    valid = valid[..., None]
    cot = cotangent[:, 0]
    d_branch = jnp.where(valid, cot, jnp.zeros_like(cot)).reshape(MB * TOK_DEV, D)
    d_normed = dot(d_branch, w_back, COLS).reshape(MB, TOK_DEV, INNER)

    zx_vals = per_micro((rows, INNER), 1)
    zx_bc = per_micro((rows, LANES), 2 * INNER // LANES)
    zx_dt = per_micro((rows, LANES), 2 * INNER // LANES + 1)
    taps_spec, steps_spec = once((8, CONV_COLS)), once((8, LANES))
    spread_spec, sum_spec = once((2 * LANES, INNER)), once((INNER, LANES))
    state_spec, dx_spec = per_micro((STATE, INNER)), per_micro((8, INNER))
    wide_spec, lane_spec = per_micro((TOK_DEV, INNER)), per_micro((TOK_DEV, LANES))
    v, bc, fr, frp, tot_f, tot_r, kept_f, kept_r, dx = call(
        front_kernel,
        (MB,),
        [SCALARS, zx_vals, zx_bc, zx_dt, taps_spec, steps_spec, spread_spec, spread_spec],
        [wide_spec, lane_spec, lane_spec, lane_spec, state_spec, state_spec, state_spec, state_spec, dx_spec],
        [
            struct(MB, TOK_DEV, INNER, dtype=BF16),
            struct(MB, TOK_DEV, LANES),
            struct(MB, TOK_DEV, LANES),
            struct(MB, TOK_DEV, LANES),
            struct(MB, STATE, INNER, dtype=SENT),
            struct(MB, STATE, INNER, dtype=SENT),
            struct(MB, STATE, INNER),
            struct(MB, STATE, INNER),
            struct(MB, 8, INNER),
        ],
        flops=1_000_000_000,
        moved=20_000_000,
    )(info, zx, zx, zx, taps, steps, spread_f, spread_r)

    enter_f, enter_r = carry(tot_f, tot_r, dx, 4, 5, 0)

    y = call(
        intra_kernel,
        (MB, 2),
        [per_block(INNER), per_block(LANES), per_block(LANES), per_block(LANES), once((8, INNER))],
        per_block(INNER),
        struct(MB, TOK_DEV, INNER),
        flops=20_000_000_000,
        moved=8_000_000,
    )(v, bc, fr, frp, skip)

    back_spec = pl.BlockSpec((1, 1, STATE, INNER), lambda m, b: (m, b, 0, 0))
    normed, d_mixed, d_gate, back_f, back_r, leave_f, leave_r, d_outs, read_out, d_out_gain, d_skip = call(
        middle_kernel,
        (MB, 2),
        [SCALARS, per_block(INNER), per_block(INNER), per_block(INNER), per_block(INNER), per_block(LANES), per_block(LANES)]
        + [state_spec] * 4
        + [dx_spec, once((8, INNER)), spread_spec, spread_spec, sum_spec, sum_spec],
        [per_block(INNER)] * 3 + [back_spec, back_spec, state_spec, state_spec, per_block(LANES), per_block(LANES), once((8, INNER)), once((8, INNER))],
        [
            struct(MB, TOK_DEV, INNER, dtype=BF16),
            struct(MB, TOK_DEV, INNER, dtype=BF16),
            struct(MB, TOK_DEV, INNER, dtype=BF16),
            struct(MB, 2, STATE, INNER),
            struct(MB, 2, STATE, INNER),
            struct(MB, STATE, INNER),
            struct(MB, STATE, INNER),
            struct(MB, TOK_DEV, LANES),
            struct(MB, TOK_DEV, LANES),
            struct(8, INNER),
            struct(8, INNER),
        ],
        scratch=[pltpu.VMEM((BLOCK, INNER), F32)] * 5,
        flops=2_000_000_000,
        moved=30_000_000,
    )(info, y, zx, d_normed, v, bc, fr, enter_f, enter_r, kept_f, kept_r, dx, out_scale, spread_f, spread_r, sum_f, sum_r)

    after_r, after_f = carry(leave_r, leave_f, dx, 5, 4, 1)

    d_v, d_bc, sums, d_log = call(
        intra_back_kernel,
        (MB, 2),
        [per_block(INNER), per_block(INNER), per_block(LANES), per_block(LANES), per_block(LANES), once((8, INNER)), per_block(LANES), per_block(LANES)],
        [per_block(INNER), per_block(LANES), per_block(LANES), per_block(LANES)],
        [struct(MB, TOK_DEV, INNER)] + [struct(MB, TOK_DEV, LANES)] * 3,
        scratch=[pltpu.VMEM((BLOCK, LANES), F32)],
        flops=30_000_000_000,
        moved=10_000_000,
    )(v, d_mixed, bc, fr, frp, skip, d_outs, read_out)

    late, before, last, d_taps, d_small = call(
        final_kernel,
        (MB,),
        [SCALARS, zx_vals, zx_bc, zx_dt, taps_spec, steps_spec, wide_spec, lane_spec, lane_spec, lane_spec]
        + [state_spec] * 4
        + [dx_spec, state_spec, state_spec, per_micro((2, STATE, INNER)), per_micro((2, STATE, INNER))]
        + [wide_spec, lane_spec, lane_spec, lane_spec, spread_spec, spread_spec, sum_spec, sum_spec],
        [per_micro((TOK_DEV, LATE)), per_micro((HALO, CONV_COLS)), per_micro((HALO, CONV_COLS)), once((8, CONV_COLS)), once((8, LANES))],
        [
            struct(MB, TOK_DEV, LATE, dtype=BF16),
            struct(MB, HALO, CONV_COLS),
            struct(MB, HALO, CONV_COLS),
            struct(8, CONV_COLS),
            struct(8, LANES),
        ],
        scratch=[pltpu.VMEM((TOK_DEV, CONV_COLS), F32)],
        flops=2_000_000_000,
        moved=40_000_000,
    )(
        info, zx, zx, zx, taps, steps, v, bc, fr, frp, enter_f, enter_r, kept_f, kept_r, dx, after_f, after_r, back_f, back_r,
        d_v, d_bc, sums, d_log, spread_f, spread_r, sum_f, sum_r,
    )
    ending = (last + shift(before, -1)).astype(BF16)
    late = lax.dynamic_update_slice(late, ending, (0, TOK_DEV - HALO, 0)).reshape(MB * TOK_DEV, LATE)

    hidden_low = hidden[:, :TOK_DEV].reshape(MB * TOK_DEV, D)
    d_gate = d_gate.reshape(MB * TOK_DEV, INNER)
    normed = normed.reshape(MB * TOK_DEV, INNER)
    branch = dot(normed, w_back).reshape(MB, TOK_DEV, D)
    x_rows = x.astype(F32)
    layer_out = jnp.where(valid, x_rows + branch, 0.0).astype(BF16)

    def owned(grad):
        return lax.psum_scatter(grad, "fsdp", scatter_dimension=0, tiled=True)

    first_grad = owned(dot(normed, d_branch, ROWS))
    gate_grad = owned(dot(hidden_low, d_gate, ROWS))
    late_grad = dot(hidden_low, late, ROWS)

    d_hidden = dot(d_gate, w_all[:, :INNER], COLS) + dot(late, w_all[:, INNER:], COLS)
    d_hidden = d_hidden.reshape(MB, TOK_DEV, D)
    scale = rms(x_rows)
    d_norm_gain = jnp.sum(d_hidden * x_rows * scale, axis=(0, 1))
    pulled = d_hidden * gain_in
    d_x = scale * pulled - x_rows * (scale * scale * scale) * jnp.mean(x_rows * pulled, axis=-1, keepdims=True)
    tokens_grad = d_x + jnp.where(valid, cot.astype(F32), 0.0)

    d_norm_gain = d_norm_gain[None]
    if total_fits(dp_count // 2, shards, dp_count):
        grads = totals(first_grad, gate_grad, late_grad, (d_taps, d_out_gain, d_skip, d_small, d_norm_gain, sum_f), 2)
    else:
        d_skip_gain = jnp.sum(d_skip[0].reshape(HEADS, HEAD_DIM), axis=1)
        d_decay = d_small[1, :HEADS] + d_small[1, HEADS : 2 * HEADS]
        small = (d_norm_gain[0], d_taps[:CONV], d_taps[CONV], d_small[0, : 2 * HEADS], d_decay, d_skip_gain, d_out_gain[0])
        w_out_grad, gate_grad, late_grad = lax.psum((first_grad, gate_grad, owned(late_grad)), "dp")
        summed = lax.psum(scatter_small(small, shards), ("dp", "fsdp"))
        own = lax.dynamic_slice_in_dim(summed, lax.axis_index("fsdp"), 1, axis=0)[0]
        pieces = []
        at = 0
        for part in (norm_gain, conv_weight, conv_bias, step_bias, decay_log, skip_gain, out_gain):
            pieces.append(own[at : at + part.size].reshape(part.shape))
            at += part.size
        w_inner_grad = jnp.concatenate([gate_grad, late_grad[:, :INNER]], axis=1)
        w_state_grad = late_grad[:, INNER : INNER + 2 * STATE]
        w_step_grad = late_grad[:, INNER + LANES : INNER + LANES + 2 * HEADS]
        grads = pieces[:1] + [w_inner_grad, w_state_grad, w_step_grad] + pieces[1:] + [w_out_grad]
    return (layer_out[:, None], tokens_grad[:, None], *grads)


def solution(mesh):
    rows, vector, matrix = P(None, "fsdp", "dp", None), P("fsdp"), P("fsdp", None)
    weights = (vector, matrix, matrix, matrix, P(None, "fsdp"), vector, vector, vector, vector, vector, matrix)
    return jax.shard_map(
        on_device,
        mesh=mesh,
        in_specs=(rows, P(None, "fsdp", None)) + weights + (rows,),
        out_specs=(rows, rows) + weights,
        check_vma=False,
    )
```

```python
from functools import partial

import jax
import jax.numpy as jnp
from jax import lax
from jax.experimental import pallas as pl
from jax.experimental.pallas import tpu as pltpu
from jax.sharding import PartitionSpec as P

D = 768
INNER = 1536
HEADS = 24
HEAD_DIM = 64
STATE = 64
CONV = 4
BLOCK = 128
MB = 3
TOK_DEV = 256
HALO = 8
LANES = 128
CONV_COLS = INNER + 2 * STATE
WIDE = 2 * INNER + 2 * LANES
LATE = INNER + 2 * LANES
PAIRS = HEADS // 2
PARTS = 4
CHUNKS = MB * PARTS
LAG = 2
EPSILON = 1e-05
HIGHEST = lax.Precision.HIGHEST
F32 = jnp.float32
BF16 = jnp.bfloat16
SENT = F32
ROWS = ((0,), (0,))
COLS = ((1,), (1,))
INNER_DIMS = ((1,), (0,))
VMEM_LIMIT = 58 * 1024 * 1024


def dot(left, right, dims=INNER_DIMS, precision=None):
    return lax.dot_general(left, right, (dims, ((), ())), precision=precision, preferred_element_type=F32)


def halves(value):
    high = value.astype(BF16)
    return high, (value - high.astype(F32)).astype(BF16)


def spread_operand(value):
    high, low = halves(value)
    return jnp.concatenate([high, low], axis=1)


def by_lane(first, second):
    low = iota(first.shape, 1) < STATE
    twice = jnp.where(low, first, second)
    high = twice.astype(BF16).astype(F32)
    return jnp.where(low, high, twice - high)


def twice(value, axis):
    return jnp.concatenate([value, value], axis=axis)


def fold(value):
    return value[:STATE] + value[STATE:]


def head_sums(value, selector):
    high, low = halves(value)
    return dot(high, selector) + dot(low, selector)


def sigmoid(value):
    return 1.0 / (1.0 + jnp.exp(-value))


def softplus(value):
    tail = jnp.exp(-jnp.abs(value))
    series = tail * (1.0 - tail * (0.5 - tail * (1.0 / 3.0 - 0.25 * tail)))
    return jnp.maximum(value, 0.0) + jnp.where(tail < 0.01, series, jnp.log(1.0 + tail))


def iota(shape, dim):
    return lax.broadcasted_iota(jnp.int32, shape, dim)


def span_scalars(info, m):
    first = info[2 * m]
    start = ((first + (BLOCK - 1)) >> 7) << 7
    return first, start, start + info[2 * m + 1], info[2 * MB], info[2 * MB + 1]


def keeps(info, m):
    _, start, _, base, span = span_scalars(info, m)

    def keep(position):
        begins = (position == 0) | (position == start) | (position >= span)
        return jnp.where(begins, 0.0, 1.0).astype(F32)

    forward = [keep(base), keep(base + BLOCK)]
    reverse = [keep(base + BLOCK), keep(base + 2 * BLOCK)]
    return forward, reverse


def row_masks(info, m, shape):
    first, start, end, base, _ = span_scalars(info, m)
    place = iota(shape, 0) + base
    inside = (place < first) | ((place >= start) & (place < end))
    offset = jnp.where(place >= start, place - start, place)
    return inside.astype(F32), [(offset >= k).astype(F32) for k in range(CONV)]


def conv_windows(ref, cols):
    main = ref[0, :TOK_DEV, cols]
    halo = ref[0, TOK_DEV:, cols]
    whole = jnp.concatenate([halo, main], axis=0)
    return [main] + [whole[HALO - k : HALO - k + TOK_DEV] for k in range(1, CONV)]


def conv_value(windows, masks, taps, cols):
    value = taps[CONV : CONV + 1, cols] + taps[0:1, cols] * windows[0]
    for k in range(1, CONV):
        value = value + taps[k : k + 1, cols] * (windows[k] * masks[k])
    return value


def front_body(m, info, vals, bc, dt, taps, steps, spread_f, spread_r, v_out, bc_out, fr_out, frp_out, tot_f, tot_r, kept_f, kept_r, dx_out):
    valid, masks = row_masks(info, m, (TOK_DEV, LANES))
    for chunk in range(PAIRS + 1):
        cols = pl.ds(chunk * LANES, LANES)
        source, own = (vals, cols) if chunk < PAIRS else (bc, pl.ds(0, LANES))
        value = conv_value(conv_windows(source, own), masks, taps, cols)
        value = valid * (value * sigmoid(value))
        if chunk < PAIRS:
            v_out[m, :, cols] = value.astype(BF16)
        else:
            bc_out[m] = value
    lane = iota((BLOCK, LANES), 1)
    rows = iota((BLOCK, BLOCK), 0)
    columns = iota((BLOCK, BLOCK), 1)
    lower = (rows >= columns).astype(F32)
    upper = (rows <= columns).astype(F32)
    forward, reverse = keeps(info, m)
    ends = []
    tails = []
    inputs = []
    for b in range(2):
        span = pl.ds(b * BLOCK, BLOCK)
        step = softplus(dt[0, span, :] + steps[0:1, :])
        log = -step * steps[1:2, :]
        summed = jnp.where(lane < HEADS, dot(lower, log, precision=HIGHEST), dot(upper, log, precision=HIGHEST))
        shifted = summed - jnp.log(step)
        fr_out[m, span, :] = summed
        frp_out[m, span, :] = shifted
        end = jnp.where(lane[:1] < HEADS, summed[BLOCK - 1 :], summed[:1])
        ends.append(jnp.exp(end))
        tails.append(spread_operand(jnp.where(lane < 2 * HEADS, jnp.exp(end - shifted), 0.0)))
        acts = bc_out[m, span, :]
        inputs.append(twice(jnp.transpose(by_lane(acts, swapped(acts))).astype(BF16), 1))
    ends = spread_operand(jnp.concatenate(ends + [jnp.zeros((6, LANES), F32)], axis=0))
    width = 2 * LANES
    for chunk in range(INNER // width):
        cols = pl.ds(chunk * width, width)
        decay_f = dot(ends, spread_f[:, cols])
        decay_r = dot(ends, spread_r[:, cols])
        parts_f = []
        parts_r = []
        for b in range(2):
            v = v_out[m, pl.ds(b * BLOCK, BLOCK), cols].astype(F32)
            parts_f.append(fold(dot(inputs[b], stacked(dot(tails[b], spread_f[:, cols]) * v))))
            parts_r.append(fold(dot(inputs[b], stacked(dot(tails[b], spread_r[:, cols]) * v))))
        kept_f[0, :, cols] = parts_f[0]
        kept_r[0, :, cols] = parts_r[1]
        total_f = parts_f[1] + (forward[1] * decay_f[1:2]) * parts_f[0]
        total_r = parts_r[0] + (reverse[0] * decay_r[0:1]) * parts_r[1]
        for k in range(PARTS):
            part = slice(k * STATE // PARTS, (k + 1) * STATE // PARTS)
            tot_f[PARTS * m + k, :, cols] = total_f[part]
            tot_r[PARTS * m + k, :, cols] = total_r[part]
        dx_out[m, 0:2, cols] = decay_f[0:2]
        dx_out[m, 2:4, cols] = decay_r[0:2]
        dx_out[m, 4:5, cols] = (forward[0] * forward[1]) * (decay_f[0:1] * decay_f[1:2])
        dx_out[m, 5:6, cols] = (reverse[0] * reverse[1]) * (decay_r[0:1] * decay_r[1:2])
        dx_out[m, 6:8, cols] = jnp.zeros((2, width), F32)


def stacked(value):
    return jnp.concatenate(halves(value), axis=0)


def doubled(value):
    high, low = halves(value)
    return jnp.concatenate([high, high, low, low], axis=0)


def pair_stack(value):
    lane = iota(value.shape, 1)
    zero = jnp.zeros_like(value)
    return jnp.concatenate([jnp.where(lane < HEAD_DIM, value, zero), jnp.where(lane < HEAD_DIM, zero, value)], axis=0)


def swapped(value):
    return pltpu.roll(value, STATE, axis=1)


def intra_body(m, b, v, bc, fr, frp, skip, y_out):
    span = pl.ds(pl.multiple_of(b * BLOCK, BLOCK), BLOCK)
    rows = iota((BLOCK, BLOCK), 0)
    columns = iota((BLOCK, BLOCK), 1)
    lower = rows > columns
    acts = bc[m, span, :]
    outs = jnp.where(columns < STATE, swapped(acts), 0.0)
    scores = jnp.where(rows == columns, 0.0, dot(outs, acts, COLS, HIGHEST))
    cum = fr[m, span, :]
    shifted = jnp.transpose(frp[m, span, :])
    for pair in range(PAIRS):
        mats = []
        for h in (2 * pair, 2 * pair + 1):
            r = HEADS + h
            gap = jnp.where(lower, cum[:, h : h + 1] - shifted[h : h + 1], cum[:, r : r + 1] - shifted[r : r + 1])
            mats.append((jnp.exp(gap) * scores).astype(BF16))
        cols = pl.ds(pair * LANES, LANES)
        value = v[m, span, cols]
        y = dot(jnp.concatenate(mats, axis=1), pair_stack(value))
        y_out[0, :, cols] = y + skip[0:1, cols] * value.astype(F32)


def front_kernel(
    levels, info, vals, bc_in, dt, taps, steps, spread_f, spread_r, skip,
    v, bc, fr, frp, kept_f, kept_r, dx, y, enter_f, enter_r, tot_f, tot_r, *buffers,
):
    s = pl.program_id(0)
    begin, send_gains, send, turns, end = carry_steps(levels, 4, 5, dx, tot_f, tot_r, enter_f, enter_r, buffers)

    @pl.when(s == 0)
    def _():
        begin()

    @pl.when(s < MB)
    def _():
        front_body(s, info, vals, bc_in, dt, taps, steps, spread_f, spread_r, v, bc, fr, frp, tot_f, tot_r, kept_f, kept_r, dx)
        send_gains(s)

        @pl.when(s == 0)
        def _():
            send(0, PARTS)

        @pl.when(s == 1)
        def _():
            send(PARTS, PARTS + 2)

    @pl.when(s >= MB)
    def _():
        slot = s - MB
        intra_body(slot // 2, lax.rem(slot, 2), v, bc, fr, frp, skip, y)
        turns(slot, 2 * MB, PARTS + 2)

    @pl.when(s == 3 * MB - 1)
    def _():
        end()


def entering(b, cols, forward, reverse, enter_f, enter_r, kept_f, kept_r, dx):
    first_f = forward[0] * enter_f[0, :, cols].astype(F32)
    last_r = reverse[1] * enter_r[0, :, cols].astype(F32)
    state_f = jnp.where(b == 0, first_f, forward[1] * (dx[0, 0:1, cols] * first_f + kept_f[0, :, cols]))
    state_r = jnp.where(b == 1, last_r, reverse[0] * (dx[0, 3:4, cols] * last_r + kept_r[0, :, cols]))
    return state_f, state_r


def middle_body(
    slot, info, y, gate, d_normed, v, bc, fr, enter_f, enter_r, kept_f, kept_r, dx, gain, spread_f, spread_r, sum_f, sum_r,
    normed, d_mixed, d_gate, back_f, back_r, leave_f, leave_r, d_outs, read_out, d_gain, d_skip, mixed_s, part_f, part_r, exp_f, exp_r,
):
    m, b = slot // 2, lax.rem(slot, 2)
    span = pl.ds(pl.multiple_of(b * BLOCK, BLOCK), BLOCK)
    forward, reverse = keeps(info, m)
    lane = iota((BLOCK, LANES), 1)
    outs = by_lane(swapped(bc[0]), bc[0])
    outs_t = twice(jnp.transpose(outs).astype(BF16), 1)
    outs = twice(outs.astype(BF16), 1)
    grown = spread_operand(jnp.where(lane < 2 * HEADS, jnp.exp(fr[0]), 0.0))
    width = 2 * LANES
    chunks = INNER // width
    squares = jnp.zeros((BLOCK, 1), F32)
    cross = jnp.zeros((BLOCK, 1), F32)
    for chunk in range(chunks):
        cols = pl.ds(chunk * width, width)
        state_f, state_r = entering(b, cols, forward, reverse, enter_f, enter_r, kept_f, kept_r, dx)
        ef = dot(grown, spread_f[:, cols])
        er = dot(grown, spread_r[:, cols])
        carried_f = ef * dot(outs, doubled(state_f))
        carried_r = er * dot(outs, doubled(state_r))
        mixed = y[0, :, cols] + carried_f + carried_r
        exp_f[:, cols] = ef
        exp_r[:, cols] = er
        part_f[:, cols] = carried_f
        part_r[:, cols] = carried_r
        mixed_s[:, cols] = mixed
        g = gate[0, :, cols]
        gated = mixed * (g * sigmoid(g))
        squares = squares + jnp.sum(gated * gated, axis=1, keepdims=True)
        cross = cross + jnp.sum(gated * gain[0:1, cols] * d_normed[0, :, cols], axis=1, keepdims=True)
    scale = lax.rsqrt(squares * (1.0 / INNER) + EPSILON)
    pull = scale * scale * scale * (cross * (1.0 / INNER))
    d_o = jnp.zeros((BLOCK, LANES), F32)
    reads = jnp.zeros((BLOCK, LANES), F32)

    @pl.when((m == 0) & (b == 0))
    def _():
        d_gain[...] = jnp.zeros_like(d_gain)
        d_skip[...] = jnp.zeros_like(d_skip)

    @pl.when(b == 0)
    def _():
        for k in range(PARTS):
            leave_f[PARTS * m + k] = jnp.zeros(CARRY_SHAPE[1:], F32)
            leave_r[PARTS * m + k] = jnp.zeros(CARRY_SHAPE[1:], F32)

    for chunk in range(chunks):
        cols = pl.ds(chunk * width, width)
        g = gate[0, :, cols]
        sig = sigmoid(g)
        silu = g * sig
        mixed = mixed_s[:, cols]
        gated = mixed * silu
        dy = d_normed[0, :, cols]
        scaled = gated * scale
        normed[m, span, cols] = (scaled * gain[0:1, cols]).astype(BF16)
        d_gain[0:1, cols] += jnp.sum(dy * scaled, axis=0, keepdims=True)
        d_gated = scale * gain[0:1, cols] * dy - gated * pull
        dm = d_gated * silu
        d_gate[m, span, cols] = (d_gated * mixed * sig * (1.0 + g * (1.0 - sig))).astype(BF16)
        d_mixed[slot, :, cols] = dm.astype(BF16)
        d_skip[0:1, cols] += jnp.sum(dm * v[0, :, cols].astype(F32), axis=0, keepdims=True)
        state_f, state_r = entering(b, cols, forward, reverse, enter_f, enter_r, kept_f, kept_r, dx)
        grown_f = exp_f[:, cols] * dm
        grown_r = exp_r[:, cols] * dm
        local_f = fold(dot(outs_t, stacked(grown_f)))
        local_r = fold(dot(outs_t, stacked(grown_r)))
        back_f[0, 0, :, cols] = local_f
        back_r[0, 0, :, cols] = local_r
        weight_f = jnp.where(b == 0, forward[0], (forward[0] * forward[1]) * dx[0, 0:1, cols])
        weight_r = jnp.where(b == 0, (reverse[0] * reverse[1]) * dx[0, 3:4, cols], reverse[1])
        local_f = weight_f * local_f
        local_r = weight_r * local_r
        for k in range(PARTS):
            part = slice(k * STATE // PARTS, (k + 1) * STATE // PARTS)
            leave_f[PARTS * m + k, :, cols] += local_f[part]
            leave_r[PARTS * m + k, :, cols] += local_r[part]
        d_o = d_o + dot(spread_operand(grown_f), twice(stacked(state_f), 1), COLS)
        d_o = d_o + dot(spread_operand(grown_r), twice(stacked(state_r), 1), COLS)
        reads = reads + head_sums(dm * part_f[:, cols], sum_f[cols, :]) + head_sums(dm * part_r[:, cols], sum_r[cols, :])
    d_outs[slot] = jnp.where(lane < STATE, 0.0, d_o + swapped(d_o))
    read_out[slot] = reads


def intra_back_body(slot, v, d_mixed, bc, fr, frp, skip, d_outs, read_out, d_v, d_bc, sums, d_log, row_s):
    rows = iota((BLOCK, BLOCK), 0)
    columns = iota((BLOCK, BLOCK), 1)
    ahead = rows < columns
    acts = bc[0]
    low = columns < STATE
    turned = swapped(acts)
    outs = jnp.where(low, turned, 0.0)
    scores = jnp.where(rows == columns, 0.0, dot(acts, outs, COLS, HIGHEST))
    cum = jnp.transpose(fr[0])
    shifted = frp[0]
    d_scores = jnp.zeros((BLOCK, BLOCK), F32)
    gathered = jnp.zeros((BLOCK, LANES), F32)

    row_s[...] = jnp.zeros_like(row_s)
    for pair in range(PAIRS):
        cols = pl.ds(pair * LANES, LANES)
        value = v[0, :, cols]
        dm = d_mixed[slot, :, cols]
        products = dot(pair_stack(value), dm, COLS)
        mats = []
        for side in range(2):
            h = 2 * pair + side
            r = HEADS + h
            gap = jnp.where(ahead, cum[h : h + 1] - shifted[:, h : h + 1], cum[r : r + 1] - shifted[:, r : r + 1])
            weight = jnp.exp(gap)
            mats.append((weight * scores).astype(BF16))
            reach = products[side * BLOCK : (side + 1) * BLOCK] * weight
            d_scores = d_scores + reach
            both = reach * scores
            first = jnp.where(ahead, both, 0.0)
            second = both - first
            gathered = jnp.where(columns == h, jnp.sum(first, axis=1, keepdims=True), gathered)
            gathered = jnp.where(columns == r, jnp.sum(second, axis=1, keepdims=True), gathered)
            row_s[h : h + 1, :] = jnp.sum(first, axis=0, keepdims=True)
            row_s[r : r + 1, :] = jnp.sum(second, axis=0, keepdims=True)
        dmf = dm.astype(F32)
        d_v[0, :, cols] = dot(jnp.concatenate(mats, axis=1), pair_stack(dm)) + skip[0:1, cols] * dmf
    d_scores = jnp.where(rows == columns, 0.0, d_scores)
    ins = jnp.where(low, 0.0, turned)
    d_bc[0] = dot(d_scores, outs, precision=HIGHEST) + dot(jnp.transpose(d_scores), ins, precision=HIGHEST) + d_outs[slot]
    sums[0] = gathered
    d_log[0] = jnp.transpose(row_s[...]) - gathered + read_out[slot]


def shard_steps(columns, normed, d_branch, hidden_t, d_gate, outs, buffers):
    put, gots, cross_puts, cross_gots, mate_sems, cross_sems = buffers
    part = lax.axis_index("fsdp")
    core, column = lax.rem(part, 2), part // 2
    mate = part + 1 - 2 * core
    rows = put.shape[1]

    def column_at(d):
        return lax.rem(column + d + columns, columns)

    def remote(source, target, sems, k, device):
        return pltpu.make_async_remote_copy(
            src_ref=source, dst_ref=target, send_sem=sems.at[0, k], recv_sem=sems.at[1, k], device_id={"fsdp": device}
        )

    def to_mate(which, x):
        return remote(put.at[x], gots[which].at[x], mate_sems, which * columns + x, mate)

    def across(which, d):
        target = 2 * column_at(d) + core
        return remote(cross_puts[which].at[d], cross_gots[which].at[d], cross_sems, which * columns + d, target)

    def piece(which, owner, h):
        half = rows // 2
        if which == 0:
            at = pl.ds(pl.multiple_of(owner * rows, LANES), rows)
            return sum(dot(normed[m, :, at], d_branch[m, :, h * D // 2 : (h + 1) * D // 2], ROWS) for m in range(MB))
        at = pl.ds(pl.multiple_of(owner * half, 16), half)
        return sum(
            dot(hidden_t[at, m * TOK_DEV : (m + 1) * TOK_DEV], d_gate[m, :, h * D : (h + 1) * D]) for m in range(MB)
        )

    def view(which, h):
        return (slice(None), slice(h * D // 2, (h + 1) * D // 2)) if which == 0 else (slice(h * rows // 2, (h + 1) * rows // 2),)

    def greet(barrier):
        pl.semaphore_signal(barrier, inc=1, device_id={"fsdp": mate})
        for d in range(1, columns):
            pl.semaphore_signal(barrier, inc=1, device_id={"fsdp": 2 * column_at(d) + core})
        return columns

    def foreign(which):
        for x in range(columns):
            if which == 1:
                to_mate(0, x).wait_send()
            for h in range(2):
                put[(x,) + view(which, h)] = piece(which, 2 * x + 1 - core, h).astype(BF16)
            to_mate(which, x).start()

    def local(which):
        for x in range(columns):
            to_mate(which, x).wait_recv()
        for d in list(range(1, columns)) + [0]:
            x = column_at(d)
            for h in range(2):
                at = view(which, h)
                value = piece(which, 2 * x + core, h) + gots[which][(x,) + at].astype(F32)
                if d == 0:
                    outs[which][at] = value
                else:
                    cross_puts[which][(d,) + at] = value.astype(BF16)
            if d > 0:
                across(which, d).start()

    def close():
        for which in range(2):
            for d in range(1, columns):
                across(which, d).wait()
                outs[which][...] += cross_gots[which][d].astype(F32)
        for x in range(columns):
            to_mate(1, x).wait_send()

    return greet, foreign, local, close


def shard_buffers(shards):
    columns, shape = shards // 2, (shards // 2, INNER // shards, D)
    low = pltpu.VMEM(shape, BF16)
    return [low] * 7 + [pltpu.SemaphoreType.DMA((2, 2 * columns))] * 2


def middle_kernel(
    levels, columns, info, y, gate, d_normed, v, bc, fr, frp, enter_f, enter_r, kept_f, kept_r, dx, dx_all, gain, skip, spread_f, spread_r,
    sum_f, sum_r, d_branch, hidden_t,
    normed, d_gate, back_f, back_r, d_gain, d_skip, d_v, d_bc, sums, d_log, after_f, after_r, first_out, second_out,
    mixed_s, part_f, part_r, exp_f, exp_r, row_s, d_mixed, d_outs, read_out, leave_f, leave_r,
    put, got_1, got_2, cross_put_1, cross_put_2, cross_got_1, cross_got_2, mate_sems, cross_sems, *buffers,
):
    s = pl.program_id(0)
    begin, send_gains, send, turns, end = carry_steps(levels, 5, 4, dx_all, leave_r, leave_f, after_r, after_f, buffers)
    greet, foreign, local, close = shard_steps(
        columns, normed, d_branch, hidden_t, d_gate, (first_out, second_out),
        (put, (got_1, got_2), (cross_put_1, cross_put_2), (cross_got_1, cross_got_2), mate_sems, cross_sems),
    )
    half = 2 * MB

    @pl.when(s == 0)
    def _():
        begin(greet)

    @pl.when(s < half)
    def _():
        middle_body(
            s, info, y, gate, d_normed, v, bc, fr, enter_f, enter_r, kept_f, kept_r, dx, gain, spread_f, spread_r, sum_f, sum_r,
            normed, d_mixed, d_gate, back_f, back_r, leave_f, leave_r, d_outs, read_out, d_gain, d_skip, mixed_s, part_f, part_r, exp_f, exp_r,
        )

        @pl.when(s == 1)
        def _():
            @pl.loop(0, MB)
            def _(m):
                send_gains(m)

            send(0, PARTS)

        @pl.when(s == 3)
        def _():
            send(PARTS, 2 * PARTS)

    for k, step in enumerate((foreign, local)):
        for which in range(2):

            @pl.when(s == half + 2 * which + k)
            def _():
                step(which)

    @pl.when(s >= half)
    def _():
        slot = s - half
        intra_back_body(slot, v, d_mixed, bc, fr, frp, skip, d_outs, read_out, d_v, d_bc, sums, d_log, row_s)
        turns(slot, half, 2 * PARTS)

    @pl.when(s == 2 * half - 1)
    def _():
        close()
        end()


def final_kernel(
    levels, info, vals, bc_in, dt, taps, rates, v, bc, fr, frp, enter_f, enter_r, kept_f, kept_r, dx, after_f, after_r, back_f, back_r,
    d_v, d_bc, sums, d_log, spread_f, spread_r, sum_f, sum_r, first_in, second_in,
    late, before, last, d_taps, d_small, first_out, second_out, d_acts, *buffers,
):
    m = pl.program_id(0)
    forward, reverse = keeps(info, m)
    if levels:
        greet, steps = sum_steps(levels, (buffers[:6], buffers[6:12]), *buffers[12:])

    def beside(at, *todo):
        if levels:

            @pl.when(m == at)
            def _():
                for stage, i in todo:
                    steps[stage](i)

    if levels:

        @pl.when(m == 0)
        def _():
            barrier = pltpu.get_barrier_semaphore()
            pl.semaphore_wait(barrier, greet(barrier))
            buffers[0][...] = first_in[...]
            buffers[6][...] = second_in[...]

    beside(0, (0, 0))
    lane = iota((BLOCK, LANES), 1)
    row = iota((BLOCK, LANES), 0)
    rows = iota((BLOCK, BLOCK), 0)
    columns = iota((BLOCK, BLOCK), 1)
    lower = (rows >= columns).astype(F32)
    upper = (rows <= columns).astype(F32)
    width = 2 * LANES

    @pl.when(m == 0)
    def _():
        d_taps[...] = jnp.zeros_like(d_taps)
        d_small[...] = jnp.zeros_like(d_small)

    for b in range(2):
        span = pl.ds(b * BLOCK, BLOCK)
        summed = fr[0, span, :]
        end = jnp.where(lane[:1] < HEADS, summed[BLOCK - 1 :], summed[:1])
        tail = spread_operand(jnp.where(lane < 2 * HEADS, jnp.exp(end - frp[0, span, :]), 0.0))
        acts = bc[0, span, :]
        ins = twice(by_lane(acts, swapped(acts)).astype(BF16), 1)
        d_in = jnp.zeros((BLOCK, LANES), F32)
        used = jnp.zeros((BLOCK, LANES), F32)
        decays = jnp.zeros((8, LANES), F32)
        for chunk in range(INNER // width):
            cols = pl.ds(chunk * width, width)
            grad_f = after_f[0, :, cols].astype(F32)
            grad_r = after_r[0, :, cols].astype(F32)
            if b == 0:
                grad_f = forward[1] * (back_f[0, 1, :, cols] + dx[0, 1:2, cols] * grad_f)
            else:
                grad_r = reverse[0] * (back_r[0, 0, :, cols] + dx[0, 2:3, cols] * grad_r)
            state_f, state_r = entering(b, cols, forward, reverse, enter_f, enter_r, kept_f, kept_r, dx)
            tail_f = dot(tail, spread_f[:, cols])
            tail_r = dot(tail, spread_r[:, cols])
            value = v[0, span, cols].astype(F32)
            pulled_f = tail_f * dot(ins, doubled(grad_f))
            pulled_r = tail_r * dot(ins, doubled(grad_r))
            d_acts[span, cols] = d_v[0, span, cols] + pulled_f + pulled_r
            d_in = d_in + dot(spread_operand(tail_f * value), twice(stacked(grad_f), 1), COLS)
            d_in = d_in + dot(spread_operand(tail_r * value), twice(stacked(grad_r), 1), COLS)
            used = used + head_sums(pulled_f * value, sum_f[cols, :]) + head_sums(pulled_r * value, sum_r[cols, :])
            meet_f = jnp.sum(grad_f * state_f, axis=0, keepdims=True) * dx[0, b : b + 1, cols]
            meet_r = jnp.sum(grad_r * state_r, axis=0, keepdims=True) * dx[0, 2 + b : 3 + b, cols]
            zero = jnp.zeros((7, width), F32)
            decays = decays + head_sums(jnp.concatenate([meet_f, zero], axis=0), sum_f[cols, :])
            decays = decays + head_sums(jnp.concatenate([meet_r, zero], axis=0), sum_r[cols, :])
        d_acts[span, pl.ds(INNER, LANES)] = d_bc[0, span, :] + jnp.where(lane < STATE, d_in + swapped(d_in), 0.0)
        direct = sums[0, span, :] + used
        edge = decays[0:1] + jnp.sum(used, axis=0, keepdims=True)
        at_end = ((lane < HEADS) & (row == BLOCK - 1)) | ((lane >= HEADS) & (row == 0))
        grad = d_log[0, span, :] - used + jnp.where(at_end, edge, 0.0)
        grad = jnp.where(lane < HEADS, dot(upper, grad, precision=HIGHEST), dot(lower, grad, precision=HIGHEST))
        x = dt[0, span, :] + rates[0:1, :]
        step = softplus(x)
        sig = sigmoid(x)
        ratio = jnp.where(x < -17.0, 1.0, sig / step)
        d_x = direct * ratio - rates[1:2, :] * grad * sig
        d_x = jnp.where(lane < 2 * HEADS, d_x, 0.0)
        late[0, span, pl.ds(INNER + LANES, LANES)] = d_x.astype(BF16)
        d_small[0:1, :] += jnp.sum(d_x, axis=0, keepdims=True)
        d_small[1:2, :] -= rates[1:2, :] * jnp.sum(step * grad, axis=0, keepdims=True)
        if b == 0:
            beside(1, (1, 1))
            beside(2, (3, 0))
        else:
            beside(0, (0, 1))
            beside(1, (2, 0))
            beside(2, (3, 1))
    valid, masks = row_masks(info, m, (TOK_DEV, LANES))
    edge = jnp.zeros((HALO, LANES), F32)
    for chunk in range(PAIRS + 1):
        cols = pl.ds(chunk * LANES, LANES)
        source, own = (vals, cols) if chunk < PAIRS else (bc_in, pl.ds(0, LANES))
        windows = conv_windows(source, own)
        value = conv_value(windows, masks, taps, cols)
        sig = sigmoid(value)
        grad = valid * d_acts[:, cols] * (sig * (1.0 + value * (1.0 - sig)))
        total = jnp.zeros((HALO + TOK_DEV, LANES), F32)
        for k in range(CONV):
            masked = grad if k == 0 else grad * masks[k]
            d_taps[k : k + 1, cols] += jnp.sum(masked * windows[k], axis=0, keepdims=True)
            padded = jnp.concatenate([edge, masked, edge], axis=0)
            total = total + taps[k : k + 1, cols] * padded[k : k + HALO + TOK_DEV]
        d_taps[CONV : CONV + 1, cols] += jnp.sum(grad, axis=0, keepdims=True)
        before[0, :, cols] = total[:HALO]
        last[0, :, cols] = total[TOK_DEV:]
        late[0, :, cols] = total[HALO:].astype(BF16)
    beside(0, (1, 0))
    beside(1, (2, 1))
    beside(2, (4, 0), (4, 1), (5, 0), (5, 1))
    if levels:

        @pl.when(m == MB - 1)
        def _():
            first_out[...] = buffers[5][...].astype(F32)
            second_out[...] = buffers[11][...].astype(F32)


def once(shape):
    return pl.BlockSpec(shape, lambda *grid: (0,) * len(shape), pipeline_mode=pl.Buffered(1))


def per_micro(shape, column=0):
    return pl.BlockSpec((1,) + shape, lambda m, *rest: (m,) + (0,) * (len(shape) - 1) + (column,))


def per_block(width, column=0):
    return pl.BlockSpec((1, BLOCK, width), lambda m, b: (m, b, column))


def struct(*shape, dtype=F32):
    return jax.ShapeDtypeStruct(shape, dtype)


SCALARS = pl.BlockSpec(memory_space=pltpu.SMEM)


def call(kernel, grid, in_specs, out_specs, out_shape, scratch=(), flops=0, moved=0, identity=None):
    return pl.pallas_call(
        kernel,
        grid=grid,
        in_specs=in_specs,
        out_specs=out_specs,
        out_shape=out_shape,
        scratch_shapes=list(scratch),
        compiler_params=pltpu.CompilerParams(
            vmem_limit_bytes=VMEM_LIMIT, collective_id=identity, has_side_effects=identity is not None
        ),
        cost_estimate=pl.CostEstimate(flops=flops, bytes_accessed=moved, transcendentals=0),
    )


def shift(value, distance):
    count = lax.axis_size("dp")
    route = [(i, i + distance) for i in range(count) if 0 <= i + distance < count]
    return lax.ppermute(value, "dp", route)


def carry_steps(levels, up_row, down_row, gains, up_in, down_in, up_out, down_out, buffers):
    up_other, down_other, gains_other, up_chain, down_chain, up_next, down_next = buffers[:7]
    up_sems, down_sems, gain_sems, up_link, down_link = buffers[7:]
    me = lax.axis_index("dp")
    side = lax.rem(me, 2)
    level = me // 2
    partner = me + 1 - 2 * side
    above, below = me + 2, me - 2
    has_above, has_below = level < levels - 1, level > 0
    first = side == 0

    def remote(source, target, sems, k, device):
        return pltpu.make_async_remote_copy(
            src_ref=source, dst_ref=target, send_sem=sems.at[0, k], recv_sem=sems.at[1, k], device_id={"dp": device}
        )

    def swap_gains(m):
        return remote(gains.at[m], gains_other.at[m], gain_sems, m, partner)

    def swap_up(k):
        return remote(up_in.at[k], up_other.at[k], up_sems, k, partner)

    def swap_down(k):
        return remote(down_in.at[k], down_other.at[k], down_sems, k, partner)

    def climb(k):
        return remote(up_next.at[k], up_chain.at[k], up_link, k, above)

    def descend(k):
        return remote(down_next.at[k], down_chain.at[k], down_link, k, below)

    def begin(greet=None):
        barrier = pltpu.get_barrier_semaphore()
        others = 0 if greet is None else greet(barrier)
        pl.semaphore_signal(barrier, inc=1, device_id={"dp": partner})

        @pl.when(has_above)
        def _():
            pl.semaphore_signal(barrier, inc=1, device_id={"dp": above})

        @pl.when(has_below)
        def _():
            pl.semaphore_signal(barrier, inc=1, device_id={"dp": below})

        pl.semaphore_wait(barrier, 1 + others + has_above.astype(jnp.int32) + has_below.astype(jnp.int32))

        @pl.when(level == 0)
        def _():
            up_chain[...] = jnp.zeros_like(up_chain)

        @pl.when(level == levels - 1)
        def _():
            down_chain[...] = jnp.zeros_like(down_chain)

    total = CHUNKS + LAG * (levels - 1)

    def places(step):
        return step - LAG * level, step - LAG * (levels - 1 - level)

    def send(low, high):
        @pl.loop(low, high)
        def _(step):
            up, down = places(step)

            @pl.when((up >= 0) & (up < CHUNKS))
            def _():
                swap_up(up).start()

            @pl.when((down >= 0) & (down < CHUNKS))
            def _():
                swap_down(down).start()

    def advance(step):
        up, down = places(step)

        @pl.when((up >= 0) & (up < CHUNKS))
        def _():
            swap_up(up).wait_recv()

            @pl.when(has_below)
            def _():
                climb(up).wait_recv()

            m = up // PARTS
            own, other = gains[m, up_row : up_row + 1], gains_other[m, up_row : up_row + 1]
            near, far = jnp.where(first, own, other), jnp.where(first, other, own)
            mine, theirs = up_in[up], up_other[up]
            before = up_chain[up]
            middle = jnp.where(first, mine, theirs) + near * before
            up_out[up] = jnp.where(first, before, middle)

            @pl.when(has_above)
            def _():
                up_next[up] = jnp.where(first, theirs, mine) + far * middle
                climb(up).start()

        @pl.when((down >= 0) & (down < CHUNKS))
        def _():
            swap_down(down).wait_recv()

            @pl.when(has_above)
            def _():
                descend(down).wait_recv()

            m = down // PARTS
            own, other = gains[m, down_row : down_row + 1], gains_other[m, down_row : down_row + 1]
            near, far = jnp.where(first, other, own), jnp.where(first, own, other)
            mine, theirs = down_in[down], down_other[down]
            before = down_chain[down]
            middle = jnp.where(first, theirs, mine) + near * before
            down_out[down] = jnp.where(first, middle, before)

            @pl.when(has_below)
            def _():
                down_next[down] = jnp.where(first, mine, theirs) + far * middle
                descend(down).start()

    def turns(slot, slots, window):
        each = -(-total // slots)

        @pl.when(slot == 0)
        def _():
            @pl.loop(0, MB)
            def _(m):
                swap_gains(m).wait_recv()

        @pl.loop(0, each)
        def _(k):
            step = slot * each + k
            send(step + window, step + window + 1)
            advance(step)

    def end():
        @pl.loop(0, MB)
        def _(m):
            swap_gains(m).wait_send()

        @pl.loop(0, CHUNKS)
        def _(k):
            swap_up(k).wait_send()
            swap_down(k).wait_send()

        @pl.when(has_above)
        def _():
            @pl.loop(0, CHUNKS)
            def _(k):
                climb(k).wait_send()

        @pl.when(has_below)
        def _():
            @pl.loop(0, CHUNKS)
            def _(k):
                descend(k).wait_send()

    return begin, lambda m: swap_gains(m).start(), send, turns, end


CARRY_SHAPE = (CHUNKS, STATE // PARTS, INNER)


def carry_buffers():
    buffer = pltpu.VMEM(CARRY_SHAPE, F32)
    return (
        [buffer, buffer, pltpu.VMEM((MB, 8, INNER), F32), buffer, buffer, buffer, buffer]
        + [pltpu.SemaphoreType.DMA((2, CHUNKS))] * 2
        + [pltpu.SemaphoreType.DMA((2, MB))]
        + [pltpu.SemaphoreType.DMA((2, CHUNKS))] * 2
    )


def sum_steps(levels, parts, side_sems, level_sems):
    me = lax.axis_index("dp")
    side, level = lax.rem(me, 2), me // 2
    partner = me + 1 - 2 * side

    def level_at(d):
        return lax.rem(level + d + levels, levels)

    def device(d):
        return {"dp": 2 * level_at(d) + side}

    def remote(source, target, sems, k, where):
        return pltpu.make_async_remote_copy(
            src_ref=source, dst_ref=target, send_sem=sems.at[0, k], recv_sem=sems.at[1, k], device_id=where
        )

    def greet(barrier):
        pl.semaphore_signal(barrier, inc=1, device_id={"dp": partner})
        for d in range(1, levels):
            pl.semaphore_signal(barrier, inc=1, device_id=device(d))
        return levels

    def halve(i):
        return remote(parts[i][1], parts[i][2], side_sems, 2 * i, {"dp": partner})

    def join(i, theirs):
        full = parts[i][5]
        return remote(full.at[side], full.at[1 - side if theirs else side], side_sems, 2 * i + 1, {"dp": partner})

    def scatter(i, d, theirs):
        put, got = parts[i][3:5]
        return remote(put.at[level_at(d)], got.at[level_at(-d) if theirs else level], level_sems, 2 * i * levels + d, device(d))

    def gather(i, d, theirs):
        full = parts[i][5]
        target = full.at[side, level_at(-d) if theirs else level]
        return remote(full.at[side, level], target, level_sems, (2 * i + 1) * levels + d, device(d))

    def step_0(i):
        total, put = parts[i][:2]
        put[...] = total[1 - side].astype(BF16)
        halve(i).start()

    def step_1(i):
        total, _, got, put = parts[i][:4]
        halve(i).wait_recv()
        total[side] = total[side] + got[...].astype(F32)
        for d in range(1, levels):
            target = level_at(d)
            put[target] = total[side, target].astype(BF16)
            scatter(i, d, False).start()

    def step_2(i):
        total, _, _, _, got, full = parts[i]
        value = total[side, level]
        for d in range(1, levels):
            scatter(i, d, True).wait_recv()
            value = value + got[level_at(-d)].astype(F32)
        full[side, level] = value.astype(BF16)
        for d in range(1, levels):
            gather(i, d, False).start()

    def step_3(i):
        for d in range(1, levels):
            gather(i, d, True).wait_recv()
        join(i, False).start()

    def step_4(i):
        join(i, True).wait_recv()

    def close(i):
        halve(i).wait_send()
        join(i, False).wait_send()
        for d in range(1, levels):
            scatter(i, d, False).wait_send()
            gather(i, d, False).wait_send()

    return greet, (step_0, step_1, step_2, step_3, step_4, close)


def sum_buffers(levels, piece, width):
    low = pltpu.VMEM((levels, piece, width), BF16)
    both = (2, levels, piece, width)
    return [pltpu.VMEM(both, F32), low, low, low, low, pltpu.VMEM(both, BF16)]


def sum_semaphores(levels, count):
    return [pltpu.SemaphoreType.DMA((2, 2 * count)), pltpu.SemaphoreType.DMA((2, 2 * count * levels))]


PIECES = ((0, 512), (512, 512), (1024, 384), (1408, 384))


def total_kernel(
    levels, columns, third_in, gate_in, taps_in, scale_in, skip_in, small_in, norm_in, selector,
    inner_out, state_out, step_out, norm_out, taps_out, bias_out, steps_out, decay_out, skip_out, scale_out,
    mate_got, cross_put, cross_got, short_sum, short_got, short_sems, mate_sems, cross_sems, side_sems, level_sems, *buffers,
):
    me, part = lax.axis_index("dp"), lax.axis_index("fsdp")
    side, level = lax.rem(me, 2), me // 2
    core, column = lax.rem(part, 2), part // 2
    mate = part + 1 - 2 * core
    count = len(PIECES)
    parts = [buffers[6 * i : 6 * i + 6] for i in range(count)]
    greet, steps = sum_steps(levels, parts, side_sems, level_sems)

    def column_at(d):
        return lax.rem(column + d + columns, columns)

    def remote(source, target, sems, k, where):
        return pltpu.make_async_remote_copy(
            src_ref=source, dst_ref=target, send_sem=sems.at[0, k], recv_sem=sems.at[1, k], device_id=where
        )

    barrier = pltpu.get_barrier_semaphore()
    pl.semaphore_signal(barrier, inc=1, device_id={"fsdp": mate})
    for d in range(1, columns):
        pl.semaphore_signal(barrier, inc=1, device_id={"fsdp": 2 * column_at(d) + core})
    pl.semaphore_wait(barrier, greet(barrier) + columns)

    def to_mate(i, x):
        at = pl.ds(*PIECES[i])
        return remote(third_in.at[2 * x + 1 - core, :, at], mate_got.at[x, :, at], mate_sems, i * columns + x, {"fsdp": mate})

    def across(i, d, theirs):
        at = pl.ds(*PIECES[i])
        where = {"fsdp": 2 * column_at(d) + core}
        slot = column_at(-d) if theirs else column
        return remote(cross_put.at[column_at(d), :, at], cross_got.at[slot, :, at], cross_sems, i * columns + d, where)

    for i in range(count):
        for x in range(columns):
            to_mate(i, x).start()

    lane = iota((8, LANES), 1)
    summed = jnp.where(lane < HEADS, head_sums(skip_in[...], selector[...]), 0.0)
    folded = small_in[...] + pltpu.roll(small_in[...], LANES - HEADS, axis=1)
    short_sum[0, 0:8, :] = taps_in[...]
    short_sum[0, 8:16, :] = jnp.zeros((8, CONV_COLS), F32)
    short_sum[0, 5:6, :INNER] = scale_in[0:1]
    short_sum[0, 6:7, :D] = norm_in[...]
    short_sum[0, 8:9, :LANES] = small_in[0:1]
    short_sum[0, 9:10, :LANES] = folded[1:2]
    short_sum[0, 10:11, :LANES] = summed[0:1]
    routes = [{"fsdp": mate}, {"dp": me + 1 - 2 * side}]
    stride = 1
    while stride < columns:
        routes.append({"fsdp": part + 2 * stride - 4 * stride * lax.rem(column // stride, 2)})
        stride *= 2
    stride = 1
    while stride < levels:
        routes.append({"dp": me + 2 * stride - 4 * stride * lax.rem(level // stride, 2)})
        stride *= 2

    def short(k):
        return remote(short_sum.at[k], short_got.at[k], short_sems, k, routes[k])

    def short_step(k):
        if k > 0:
            short(k - 1).wait_recv()
            short_sum[k] = short_sum[k - 1] + short_got[k - 1]
        if k < len(routes):
            short(k).start()

    short_step(0)
    for i in range(count):
        at = pl.ds(*PIECES[i])
        for x in range(columns):
            to_mate(i, x).wait_recv()
        for d in range(1, columns):
            x = column_at(d)
            cross_put[x, :, at] = (third_in[2 * x + core, :, at] + mate_got[x, :, at]).astype(BF16)
            across(i, d, False).start()
    short_step(1)
    rows = parts[0][0].shape[2]

    def arrive(i):
        at = pl.ds(*PIECES[i])
        for d in range(1, columns):
            across(i, d, True).wait_recv()
        for x in range(2):
            for j in range(levels):
                here = pl.ds((x * levels + j) * rows, rows)
                value = third_in[part, here, at] + mate_got[column, here, at]
                for d in range(1, columns):
                    value = value + cross_got[column_at(-d), here, at].astype(F32)
                parts[i][0][x, j] = value
        steps[0](i)

    last = len(routes)
    for wave in range(count + 4):
        for stage in range(4, 0, -1):
            i = wave - stage
            if 0 <= i < count:
                steps[stage](i)
        if wave < count:
            arrive(wave)
        if wave + 2 <= last:
            short_step(wave + 2)
    for k in range(count + 6, last + 1):
        short_step(k)

    result = short_sum.at[last]
    for f in range(2 * columns):

        @pl.when(part == f)
        def _():
            def own(row, rows, width, ref):
                size = width // (2 * columns)
                ref[...] = result[row : row + rows, f * size : (f + 1) * size]

            own(0, CONV, CONV_COLS, taps_out)
            own(4, 1, CONV_COLS, bias_out)
            own(5, 1, INNER, scale_out)
            own(6, 1, D, norm_out)
            own(8, 1, 2 * HEADS, steps_out)
            own(9, 1, HEADS, decay_out)
            own(10, 1, HEADS, skip_out)

    half = gate_in.shape[0] // 2
    for h in range(2):
        inner_out[:, h * D : (h + 1) * D] = gate_in[h * half : (h + 1) * half]
    for i in range(count):
        start, width = PIECES[i]
        for x in range(2):
            for j in range(levels):
                here = pl.ds((x * levels + j) * rows, rows)
                value = parts[i][5][x, j].astype(F32)
                inside = min(width, INNER - start)
                inner_out[here, INNER + start : INNER + start + inside] = value[:, :inside]
                if inside < width:
                    state_out[here, :] = value[:, inside : inside + LANES]
                    step_out[here, :] = value[:, inside + LANES : inside + LANES + 2 * HEADS]
    for i in range(count):
        steps[5](i)
        for x in range(columns):
            to_mate(i, x).wait_send()
        for d in range(1, columns):
            across(i, d, False).wait_send()
    for k in range(last):
        short(k).wait_send()


def total_fits(levels, shards, dp_count):
    rows = D // shards
    return dp_count == 2 * levels and shards % 2 == 0 and rows % (16 * levels) == 0 and 24 % shards == 0


def totals(third, gate, short, identity):
    dp_count, shards = lax.axis_size("dp"), lax.axis_size("fsdp")
    levels, columns = dp_count // 2, shards // 2
    rows = D // shards
    small = rows // levels // 2
    steps = (dp_count * shards).bit_length() - 1
    count = len(PIECES)

    def low(*shape):
        return pltpu.VMEM(shape, BF16)

    def full(*shape):
        return pltpu.VMEM(shape, F32)

    outs = pl.pallas_call(
        partial(total_kernel, levels, columns),
        in_specs=[pl.BlockSpec(memory_space=pltpu.VMEM)] * 8,
        out_specs=[pl.BlockSpec(memory_space=pltpu.VMEM)] * 10,
        out_shape=[struct(rows, 2 * INNER), struct(rows, 2 * STATE), struct(rows, 2 * HEADS)]
        + [struct(1, D // shards), struct(CONV, CONV_COLS // shards), struct(1, CONV_COLS // shards)]
        + [struct(1, width // shards) for width in (2 * HEADS, HEADS, HEADS, INNER)],
        scratch_shapes=[full(columns, rows, LATE), low(columns, rows, LATE), low(columns, rows, LATE)]
        + [full(steps + 1, 16, CONV_COLS), full(steps, 16, CONV_COLS), pltpu.SemaphoreType.DMA((2, steps))]
        + [pltpu.SemaphoreType.DMA((2, count * columns))] * 2
        + sum_semaphores(levels, count)
        + [buffer for _, width in PIECES for buffer in sum_buffers(levels, small, width)],
        compiler_params=pltpu.CompilerParams(vmem_limit_bytes=VMEM_LIMIT, collective_id=identity, has_side_effects=True),
    )(third.reshape(shards, rows, LATE), gate, *short)
    flat = [out.reshape(-1) for out in outs[5:]]
    return [outs[3].reshape(-1)] + list(outs[:3]) + [outs[4]] + flat


def rms(values):
    return lax.rsqrt(jnp.mean(values * values, axis=-1, keepdims=True) + EPSILON)


def gather_small(parts):
    flat = jnp.concatenate([part.reshape(-1) for part in parts])
    size = flat.shape[0]
    padded = -(-size // LANES) * LANES
    everything = lax.all_gather(jnp.pad(flat, (0, padded - size)).reshape(1, padded), "fsdp", axis=0, tiled=True)
    result = []
    at = 0
    for part in parts:
        piece = everything[:, at : at + part.size].astype(F32)
        at += part.size
        if part.ndim == 2:
            piece = piece.reshape(-1, *part.shape).transpose(1, 0, 2).reshape(part.shape[0], -1)
        else:
            piece = piece.reshape(-1)
        result.append(piece)
    return result


def scatter_small(parts, shards):
    rows = []
    for part in parts:
        if part.ndim == 2:
            rows.append(part.reshape(part.shape[0], shards, -1).transpose(1, 0, 2).reshape(shards, -1))
        else:
            rows.append(part.reshape(shards, -1))
    flat = jnp.concatenate(rows, axis=1)
    size = flat.shape[1]
    padded = -(-size // LANES) * LANES
    return jnp.pad(flat, ((0, 0), (0, padded - size)))


def on_device(
    tokens, seq_lengths, norm_gain, w_inner, w_state, w_step, conv_weight, conv_bias, step_bias, decay_log, skip_gain, out_gain, w_out, cotangent,
):
    dp_count = lax.axis_size("dp")
    shards = lax.axis_size("fsdp")
    base = lax.axis_index("dp") * TOK_DEV
    lengths = seq_lengths[:, 0]
    info = jnp.concatenate([lengths.reshape(-1), jnp.stack([base, jnp.int32(dp_count * TOK_DEV)]).astype(jnp.int32)])
    mine = jnp.concatenate([w_inner, w_state, w_step, jnp.zeros((w_step.shape[0], WIDE - 2 * INNER - 2 * STATE - 2 * HEADS), BF16)], axis=1)
    w_all = lax.all_gather(mine, "fsdp", axis=0, tiled=True)
    gain_in, weight_conv, bias_conv, bias_steps, log_decay, gain_skip, gain_out = gather_small(
        (norm_gain, conv_weight, conv_bias, step_bias, decay_log, skip_gain, out_gain)
    )
    w_all, w_later = lax.optimization_barrier((w_all, w_out))
    w_back = lax.all_gather(w_later, "fsdp", axis=0, tiled=True)

    taps = jnp.concatenate([weight_conv, bias_conv[None], jnp.zeros((3, CONV_COLS), F32)], axis=0)
    rates = jnp.exp(log_decay)
    steps = jnp.zeros((8, LANES), F32).at[0, : 2 * HEADS].set(bias_steps).at[1, : 2 * HEADS].set(jnp.concatenate([rates, rates]))
    skip = jnp.broadcast_to(jnp.repeat(gain_skip, HEAD_DIM)[None], (8, INNER))
    out_scale = jnp.broadcast_to(gain_out[None], (8, INNER))
    head_of = jnp.arange(INNER, dtype=jnp.int32) // HEAD_DIM
    lanes = jnp.arange(LANES, dtype=jnp.int32)
    sum_f = (head_of[:, None] == lanes[None, :]).astype(BF16)
    sum_r = (head_of[:, None] + HEADS == lanes[None, :]).astype(BF16)
    both = jnp.concatenate([lanes, lanes])
    spread_f = (both[:, None] == head_of[None, :]).astype(BF16)
    spread_r = (both[:, None] == head_of[None, :] + HEADS).astype(BF16)

    x = tokens[:, 0]
    halo = shift(x[:, TOK_DEV - HALO :], 1)
    x_all = jnp.concatenate([x, halo], axis=1).astype(F32)
    hidden = (x_all * rms(x_all) * gain_in).astype(BF16)
    rows = TOK_DEV + HALO
    zx = jnp.dot(hidden.reshape(MB * rows, D), w_all, preferred_element_type=F32).reshape(MB, rows, WIDE)

    places = base + jnp.arange(TOK_DEV, dtype=jnp.int32)
    first = lengths[:, :1]
    start = (first + BLOCK - 1) // BLOCK * BLOCK
    valid = (places[None] < first) | (places[None] >= start) & (places[None] < start + lengths[:, 1:])
    valid = valid[..., None]
    cot = cotangent[:, 0]
    d_branch = jnp.where(valid, cot, jnp.zeros_like(cot)).reshape(MB * TOK_DEV, D)
    d_normed = dot(d_branch, w_back, COLS).reshape(MB, TOK_DEV, INNER)

    levels = dp_count // 2
    zx_vals = per_micro((rows, INNER), 1)
    zx_bc = per_micro((rows, LANES), 2 * INNER // LANES)
    zx_dt = per_micro((rows, LANES), 2 * INNER // LANES + 1)
    taps_spec, steps_spec = once((8, CONV_COLS)), once((8, LANES))
    spread_spec, sum_spec = once((2 * LANES, INNER)), once((INNER, LANES))
    state_spec, dx_spec = per_micro((STATE, INNER)), per_micro((8, INNER))
    wide_spec, lane_spec = per_micro((TOK_DEV, INNER)), per_micro((TOK_DEV, LANES))
    row_spec, dx_all_spec, carry_spec = once((8, INNER)), once((MB, 8, INNER)), once(CARRY_SHAPE)

    def early(shape, column=0):
        return pl.BlockSpec((1,) + shape, lambda s: (jnp.minimum(s, MB - 1),) + (0,) * (len(shape) - 1) + (column,))

    def mixing(s):
        slot = jnp.maximum(s - MB, 0)
        return slot // 2, lax.rem(slot, 2), 0

    lanes_all, lanes_struct = once((MB, TOK_DEV, LANES)), struct(MB, TOK_DEV, LANES)
    v, bc, fr, frp, kept_f, kept_r, dx, y, enter_f, enter_r = call(
        partial(front_kernel, levels),
        (3 * MB,),
        [
            SCALARS, early((rows, INNER), 1), early((rows, LANES), 2 * INNER // LANES), early((rows, LANES), 2 * INNER // LANES + 1),
            taps_spec, steps_spec, spread_spec, spread_spec, row_spec,
        ],
        [once((MB, TOK_DEV, INNER)), lanes_all, lanes_all, lanes_all, early((STATE, INNER)), early((STATE, INNER)), dx_all_spec]
        + [pl.BlockSpec((1, BLOCK, INNER), mixing), carry_spec, carry_spec],
        [struct(MB, TOK_DEV, INNER, dtype=BF16), lanes_struct, lanes_struct, lanes_struct]
        + [struct(MB, STATE, INNER), struct(MB, STATE, INNER), struct(MB, 8, INNER), struct(MB, TOK_DEV, INNER)]
        + [struct(*CARRY_SHAPE)] * 2,
        scratch=[pltpu.VMEM(CARRY_SHAPE, F32)] * 2 + carry_buffers(),
        flops=20_000_000_000,
        moved=30_000_000,
        identity=0,
    )(info, zx, zx, zx, taps, steps, spread_f, spread_r, skip)
    enter_f, enter_r = enter_f.reshape(MB, STATE, INNER), enter_r.reshape(MB, STATE, INNER)

    def turning(s):
        return jnp.minimum(s, 2 * MB - 1)

    def backing(s):
        return jnp.maximum(s - 2 * MB, 0)

    def either(s):
        return lax.rem(s, 2 * MB)

    def block_at(pick, width, column=0):
        return pl.BlockSpec((1, BLOCK, width), lambda s: (pick(s) // 2, lax.rem(pick(s), 2), column))

    def state_at(height):
        return pl.BlockSpec((1, height, INNER), lambda s: (turning(s) // 2, 0, 0))

    back_spec = pl.BlockSpec((1, 1, STATE, INNER), lambda s: (turning(s) // 2, lax.rem(turning(s), 2), 0, 0))
    wide_in = block_at(turning, INNER)
    lane_in, lane_out = block_at(either, LANES), block_at(backing, LANES)
    hidden_low = hidden[:, :TOK_DEV]
    hidden_t = jnp.transpose(hidden_low.reshape(MB * TOK_DEV, D))
    shard_rows = INNER // shards
    shard_spec = once((shard_rows, D))
    normed, d_gate, back_f, back_r, d_out_gain, d_skip, d_v, d_bc, sums, d_log, after_f, after_r, first_grad, gate_grad = call(
        partial(middle_kernel, levels, shards // 2),
        (4 * MB,),
        [SCALARS, wide_in, wide_in, wide_in, block_at(either, INNER), lane_in, lane_in, lane_in]
        + [state_at(STATE)] * 4
        + [state_at(8), dx_all_spec, row_spec, row_spec, spread_spec, spread_spec, sum_spec, sum_spec]
        + [once((MB, TOK_DEV, D)), once((D, MB * TOK_DEV))],
        [once((MB, TOK_DEV, INNER))] * 2
        + [back_spec, back_spec, row_spec, row_spec, block_at(backing, INNER)]
        + [lane_out] * 3
        + [carry_spec] * 2
        + [shard_spec] * 2,
        [struct(MB, TOK_DEV, INNER, dtype=BF16)] * 2
        + [struct(MB, 2, STATE, INNER)] * 2
        + [struct(8, INNER)] * 2
        + [struct(MB, TOK_DEV, INNER)]
        + [struct(MB, TOK_DEV, LANES)] * 3
        + [struct(*CARRY_SHAPE)] * 2
        + [struct(shard_rows, D)] * 2,
        scratch=[pltpu.VMEM((BLOCK, INNER), F32)] * 5
        + [pltpu.VMEM((BLOCK, LANES), F32), pltpu.VMEM((2 * MB, BLOCK, INNER), BF16)]
        + [pltpu.VMEM((2 * MB, BLOCK, LANES), F32)] * 2
        + [pltpu.VMEM(CARRY_SHAPE, F32)] * 2
        + shard_buffers(shards)
        + carry_buffers(),
        flops=30_000_000_000,
        moved=40_000_000,
        identity=1,
    )(
        info, y, zx, d_normed, v, bc, fr, frp, enter_f, enter_r, kept_f, kept_r, dx, dx, out_scale, skip, spread_f, spread_r, sum_f, sum_r,
        d_branch.reshape(MB, TOK_DEV, D), hidden_t,
    )
    after_f, after_r = after_f.reshape(MB, STATE, INNER), after_r.reshape(MB, STATE, INNER)

    fits = total_fits(levels, shards, dp_count)
    if fits:
        split = (2, levels, shard_rows // (2 * levels), D)
        first_grad, gate_grad = first_grad.reshape(split), gate_grad.reshape(split)
    else:
        split = (8, LANES)
    unused = jnp.zeros((8, LANES), F32)
    late, before, last, d_taps, d_small, first_sum, gate_sum = call(
        partial(final_kernel, levels if fits else 0),
        (MB,),
        [SCALARS, zx_vals, zx_bc, zx_dt, taps_spec, steps_spec, wide_spec, lane_spec, lane_spec, lane_spec]
        + [state_spec] * 4
        + [dx_spec, state_spec, state_spec, per_micro((2, STATE, INNER)), per_micro((2, STATE, INNER))]
        + [wide_spec, lane_spec, lane_spec, lane_spec, spread_spec, spread_spec, sum_spec, sum_spec, once(split), once(split)],
        [per_micro((TOK_DEV, LATE)), per_micro((HALO, CONV_COLS)), per_micro((HALO, CONV_COLS)), once((8, CONV_COLS)), once((8, LANES)), once(split), once(split)],
        [
            struct(MB, TOK_DEV, LATE, dtype=BF16),
            struct(MB, HALO, CONV_COLS),
            struct(MB, HALO, CONV_COLS),
            struct(8, CONV_COLS),
            struct(8, LANES),
            struct(*split),
            struct(*split),
        ],
        scratch=[pltpu.VMEM((TOK_DEV, CONV_COLS), F32)]
        + (2 * sum_buffers(*split[1:]) + sum_semaphores(levels, 2) if fits else []),
        flops=2_000_000_000,
        moved=40_000_000,
        identity=3 if fits else None,
    )(
        info, zx, zx, zx, taps, steps, v, bc, fr, frp, enter_f, enter_r, kept_f, kept_r, dx, after_f, after_r, back_f, back_r,
        d_v, d_bc, sums, d_log, spread_f, spread_r, sum_f, sum_r, first_grad if fits else unused, gate_grad if fits else unused,
    )
    ending = (last + shift(before, -1)).astype(BF16)
    late = lax.dynamic_update_slice(late, ending, (0, TOK_DEV - HALO, 0)).reshape(MB * TOK_DEV, LATE)

    hidden_low = hidden_low.reshape(MB * TOK_DEV, D)
    d_gate = d_gate.reshape(MB * TOK_DEV, INNER)
    normed = normed.reshape(MB * TOK_DEV, INNER)
    branch = dot(normed, w_back).reshape(MB, TOK_DEV, D)
    x_rows = x.astype(F32)
    layer_out = jnp.where(valid, x_rows + branch, 0.0).astype(BF16)

    def owned(grad):
        return lax.psum_scatter(grad, "fsdp", scatter_dimension=0, tiled=True)

    late_grad = dot(hidden_low, late, ROWS)

    d_hidden = dot(d_gate, w_all[:, :INNER], COLS) + dot(late, w_all[:, INNER:], COLS)
    d_hidden = d_hidden.reshape(MB, TOK_DEV, D)
    scale = rms(x_rows)
    d_norm_gain = jnp.sum(d_hidden * x_rows * scale, axis=(0, 1))
    pulled = d_hidden * gain_in
    d_x = scale * pulled - x_rows * (scale * scale * scale) * jnp.mean(x_rows * pulled, axis=-1, keepdims=True)
    tokens_grad = d_x + jnp.where(valid, cot.astype(F32), 0.0)

    d_norm_gain = d_norm_gain[None]
    if fits:
        gate_sum = gate_sum.reshape(shard_rows, D)
        grads = totals(late_grad, gate_sum, (d_taps, d_out_gain, d_skip, d_small, d_norm_gain, sum_f), 2)
        grads.append(first_sum.reshape(shard_rows, D))
    else:
        d_skip_gain = jnp.sum(d_skip[0].reshape(HEADS, HEAD_DIM), axis=1)
        d_decay = d_small[1, :HEADS] + d_small[1, HEADS : 2 * HEADS]
        small = (d_norm_gain[0], d_taps[:CONV], d_taps[CONV], d_small[0, : 2 * HEADS], d_decay, d_skip_gain, d_out_gain[0])
        w_out_grad, gate_grad, late_grad = lax.psum((first_grad, gate_grad, owned(late_grad)), "dp")
        summed = lax.psum(scatter_small(small, shards), ("dp", "fsdp"))
        own = lax.dynamic_slice_in_dim(summed, lax.axis_index("fsdp"), 1, axis=0)[0]
        pieces = []
        at = 0
        for part in (norm_gain, conv_weight, conv_bias, step_bias, decay_log, skip_gain, out_gain):
            pieces.append(own[at : at + part.size].reshape(part.shape))
            at += part.size
        gate_grad = jnp.concatenate([gate_grad[: shard_rows // 2], gate_grad[shard_rows // 2 :]], axis=1)
        w_inner_grad = jnp.concatenate([gate_grad, late_grad[:, :INNER]], axis=1)
        w_state_grad = late_grad[:, INNER : INNER + 2 * STATE]
        w_step_grad = late_grad[:, INNER + LANES : INNER + LANES + 2 * HEADS]
        grads = pieces[:1] + [w_inner_grad, w_state_grad, w_step_grad] + pieces[1:] + [w_out_grad]
    return (layer_out[:, None], tokens_grad[:, None], *grads)


def solution(mesh):
    rows, vector, matrix = P(None, "fsdp", "dp", None), P("fsdp"), P("fsdp", None)
    weights = (vector, matrix, matrix, matrix, P(None, "fsdp"), vector, vector, vector, vector, vector, matrix)
    return jax.shard_map(
        on_device,
        mesh=mesh,
        in_specs=(rows, P(None, "fsdp", None)) + weights + (rows,),
        out_specs=(rows, rows) + weights,
        check_vma=False,
    )
```

```python
from functools import partial

import jax
import jax.numpy as jnp
from jax import lax
from jax.experimental import pallas as pl
from jax.experimental.pallas import tpu as pltpu
from jax.sharding import PartitionSpec as P

D = 768
INNER = 1536
HEADS = 24
HEAD_DIM = 64
STATE = 64
CONV = 4
BLOCK = 128
MB = 3
TOK_DEV = 256
HALO = 8
LANES = 128
CONV_COLS = INNER + 2 * STATE
WIDE = 2 * INNER + 2 * LANES
LATE = INNER + 2 * LANES
PAIRS = HEADS // 2
PARTS = 4
CHUNKS = MB * PARTS
LAG = 2
CUTS = 3
EPSILON = 1e-05
HIGHEST = lax.Precision.HIGHEST
F32 = jnp.float32
BF16 = jnp.bfloat16
SENT = F32
ROWS = ((0,), (0,))
COLS = ((1,), (1,))
INNER_DIMS = ((1,), (0,))
VMEM_LIMIT = 58 * 1024 * 1024
SCALARS = pl.BlockSpec(memory_space=pltpu.SMEM)


def dot(left, right, dims=INNER_DIMS, precision=None):
    return lax.dot_general(left, right, (dims, ((), ())), precision=precision, preferred_element_type=F32)


def halves(value):
    high = value.astype(BF16)
    return high, (value - high.astype(F32)).astype(BF16)


def spread_operand(value):
    high, low = halves(value)
    return jnp.concatenate([high, low], axis=1)


def by_lane(first, second):
    low = iota(first.shape, 1) < STATE
    twice = jnp.where(low, first, second)
    high = twice.astype(BF16).astype(F32)
    return jnp.where(low, high, twice - high)


def twice(value, axis):
    return jnp.concatenate([value, value], axis=axis)


def fold(value):
    return value[:STATE] + value[STATE:]


def head_sums(value, selector):
    high, low = halves(value)
    return dot(high, selector) + dot(low, selector)


def sigmoid(value):
    return 1.0 / (1.0 + jnp.exp(-value))


def softplus(value):
    tail = jnp.exp(-jnp.abs(value))
    series = tail * (1.0 - tail * (0.5 - tail * (1.0 / 3.0 - 0.25 * tail)))
    return jnp.maximum(value, 0.0) + jnp.where(tail < 0.01, series, jnp.log(1.0 + tail))


def iota(shape, dim):
    return lax.broadcasted_iota(jnp.int32, shape, dim)


def span_scalars(info, m):
    first = info[2 * m]
    start = ((first + (BLOCK - 1)) >> 7) << 7
    return first, start, start + info[2 * m + 1], info[2 * MB], info[2 * MB + 1]


def keeps(info, m):
    _, start, _, base, span = span_scalars(info, m)

    def keep(position):
        begins = (position == 0) | (position == start) | (position >= span)
        return jnp.where(begins, 0.0, 1.0).astype(F32)

    forward = [keep(base), keep(base + BLOCK)]
    reverse = [keep(base + BLOCK), keep(base + 2 * BLOCK)]
    return forward, reverse


def row_masks(info, m, shape, offset=0):
    first, start, end, base, _ = span_scalars(info, m)
    place = iota(shape, 0) + (base + offset)
    inside = (place < first) | ((place >= start) & (place < end))
    offset = jnp.where(place >= start, place - start, place)
    return inside.astype(F32), [(offset >= k).astype(F32) for k in range(CONV)]


def conv_windows(ref, cols):
    main = ref[0, :TOK_DEV, cols]
    halo = ref[0, TOK_DEV:, cols]
    whole = jnp.concatenate([halo, main], axis=0)
    return [main] + [whole[HALO - k : HALO - k + TOK_DEV] for k in range(1, CONV)]


def conv_value(windows, masks, taps, cols):
    value = taps[CONV : CONV + 1, cols] + taps[0:1, cols] * windows[0]
    for k in range(1, CONV):
        value = value + taps[k : k + 1, cols] * (windows[k] * masks[k])
    return value


def gather_kernel(
    count, columns, info, x_in, cot_in, w_inner, w_state, w_step, mine,
    w_all, hidden, hidden_t, d_branch, norm, taps, steps, skip, scale, spread_f, spread_r, sum_f, sum_r,
    halo, small, skip_row, halo_sems, small_sems, x_sems, y_sems, mate_sems, own_sems,
):
    me, part = lax.axis_index("dp"), lax.axis_index("fsdp")
    side, core, column = lax.rem(me, 2), lax.rem(part, 2), part // 2
    partner, mate = me + 1 - 2 * side, part + 1 - 2 * core
    has_next, has_last = me < count - 1, me > 0
    shards = 2 * columns
    rows = w_inner.shape[0]
    chunk = rows // (2 * CUTS)

    barrier = pltpu.get_barrier_semaphore()

    @pl.when(has_next)
    def _():
        pl.semaphore_signal(barrier, inc=1, device_id={"dp": me + 1})

    @pl.when(has_last)
    def _():
        pl.semaphore_signal(barrier, inc=1, device_id={"dp": me - 1})

    def other(d):
        return lax.rem(part + d + shards, shards)

    def column_at(d):
        return lax.rem(column + d + columns, columns)

    for d in range(1, shards):
        pl.semaphore_signal(barrier, inc=1, device_id={"fsdp": other(d)})
    pl.semaphore_wait(barrier, shards - 1 + has_next.astype(jnp.int32) + has_last.astype(jnp.int32))

    def remote(source, target, sems, k, where):
        return pltpu.make_async_remote_copy(
            src_ref=source, dst_ref=target, send_sem=sems.at[0, k], recv_sem=sems.at[1, k], device_id=where
        )

    def rows_of(owner, half, k):
        return w_all.at[pl.ds(pl.multiple_of(owner * rows + half * (rows // 2) + k * chunk, 16), chunk)]

    edge = remote(x_in.at[:, pl.ds(TOK_DEV - 2 * HALO, 2 * HALO)], halo, halo_sems, 0, {"dp": me + 1})

    def small_copy(d, theirs):
        return remote(mine, small.at[other(-d) if theirs else part], small_sems, d, {"fsdp": other(d)})

    def x_copy(k, d):
        at = rows_of(part, side, k)
        return remote(at, at, x_sems, k * columns + d, {"fsdp": 2 * column_at(d) + core})

    def x_arrival(k, d):
        at = rows_of(2 * column_at(-d) + core, side, k)
        return remote(at, at, x_sems, k * columns + d, {"fsdp": part})

    def y_copy(k, d, theirs):
        at = rows_of(2 * column_at(-d) + core, 1 - side if theirs else side, k)
        return remote(at, at, y_sems, k * columns + d, {"dp": partner})

    def mate_copy(k, d, half, theirs):
        at = rows_of(2 * column_at(-d) + (1 - core if theirs else core), half, k)
        return remote(at, at, mate_sems, (k * columns + d) * 2 + half, {"fsdp": mate})

    def own_copy(owner):
        at = w_all.at[pl.ds(pl.multiple_of(owner * rows, 16), rows)]
        return remote(at, at, own_sems, 0, {"fsdp": mate})

    @pl.when(has_next)
    def _():
        edge.start()

    for d in range(1, shards):
        small_copy(d, False).start()
    here = pl.ds(pl.multiple_of(part * rows, 16), rows)
    w_all[here, : 2 * INNER] = w_inner[...]
    w_all[here, 2 * INNER : 2 * INNER + 2 * STATE] = w_state[...]
    w_all[here, 2 * INNER + 2 * STATE :] = jnp.concatenate(
        [w_step[...].astype(F32), jnp.zeros((rows, LANES - 2 * HEADS), F32)], axis=1
    ).astype(BF16)
    for k in range(2):
        for d in range(1, columns):
            x_copy(k, d).start()
    own_copy(part).start()

    @pl.when(me == 0)
    def _():
        halo[...] = jnp.zeros_like(halo)

    def chosen(mask):
        return jnp.where(mask, 1.0, 0.0).astype(BF16)

    shape = (2 * LANES, INNER)
    lane_of, head_of = iota(shape, 0) & (LANES - 1), iota(shape, 1) >> 6
    spread_f[...] = chosen(lane_of == head_of)
    spread_r[...] = chosen(lane_of == head_of + HEADS)
    shape = (INNER, LANES)
    lane_of, head_of = iota(shape, 1), iota(shape, 0) >> 6
    sum_f[...] = chosen(lane_of == head_of)
    sum_r[...] = chosen(lane_of == head_of + HEADS)
    for m in range(MB):
        valid = row_masks(info, m, (TOK_DEV, D))[0]
        d_branch[m] = jnp.where(valid > 0.0, cot_in[m].astype(F32), 0.0).astype(BF16)

    for ref in (norm, taps, steps, skip_row):
        ref[...] = jnp.zeros_like(ref)
    for d in range(1, shards):
        small_copy(d, True).wait_recv()
    small[part] = mine[...]
    wide, heads = CONV_COLS // shards, HEADS // shards
    for f in range(shards):
        value = small[f].astype(F32)
        taps[: CONV + 1, f * wide : (f + 1) * wide] = value[: CONV + 1, :wide]
        gain = value[5:6, : INNER // shards]
        scale[:, f * INNER // shards : (f + 1) * INNER // shards] = jnp.broadcast_to(gain, (8, INNER // shards))
        norm[:, f * rows : (f + 1) * rows] = value[6:7, :rows]
        steps[0:1, 2 * f * heads : 2 * (f + 1) * heads] = value[7:8, : 2 * heads]
        rates = jnp.exp(value[8:9, :heads])
        steps[1:2, f * heads : (f + 1) * heads] = rates
        steps[1:2, HEADS + f * heads : HEADS + (f + 1) * heads] = rates
        skip_row[0:1, f * heads : (f + 1) * heads] = value[9:10, :heads]
    skip[...] = dot(spread_operand(skip_row[...]), spread_f[...])

    @pl.when(has_last)
    def _():
        edge.wait_recv()

    def normalise(values):
        root = lax.rsqrt(jnp.mean(values * values, axis=1, keepdims=True) + EPSILON)
        return values * root * norm[...]

    def hide(m):
        value = normalise(x_in[m].astype(F32))
        hidden[m, :TOK_DEV] = value.astype(BF16)
        hidden_t[:, m * TOK_DEV : (m + 1) * TOK_DEV] = jnp.transpose(value).astype(BF16)
        hidden[m, TOK_DEV:] = normalise(halo[m].astype(F32)[HALO:]).astype(BF16)

    def pass_on(k):
        for d in range(1, columns):
            y_copy(k, d, True).wait_recv()

            @pl.when(side == 0)
            def _():
                mate_copy(k, d, 1, False).start()

            @pl.when(side == 1)
            def _():
                mate_copy(k, d, 0, False).start()

    for k in range(CUTS):
        if k < MB:
            hide(k)
        for d in range(1, columns):
            x_arrival(k, d).wait_recv()
            y_copy(k, d, False).start()

            @pl.when(side == 0)
            def _():
                mate_copy(k, d, 0, False).start()

            @pl.when(side == 1)
            def _():
                mate_copy(k, d, 1, False).start()

            if k + 2 < CUTS:
                x_copy(k + 2, d).start()
        if k > 0:
            pass_on(k - 1)
    for m in range(CUTS, MB):
        hide(m)
    pass_on(CUTS - 1)
    own_copy(mate).wait_recv()
    own_copy(part).wait_send()
    for k in range(CUTS):
        for d in range(1, columns):
            for half in range(2):
                mate_copy(k, d, half, True).wait_recv()
                mate_copy(k, d, half, False).wait_send()
            x_copy(k, d).wait_send()
            y_copy(k, d, False).wait_send()
    for d in range(1, shards):
        small_copy(d, False).wait_send()

    @pl.when(has_next)
    def _():
        edge.wait_send()


def gather_weights(info, x, cot, w_inner, w_state, w_step, mine, identity):
    count, shards = lax.axis_size("dp"), lax.axis_size("fsdp")
    columns = shards // 2
    whole = pl.BlockSpec(memory_space=pltpu.VMEM)
    pairs = CUTS * columns
    return pl.pallas_call(
        partial(gather_kernel, count, columns),
        in_specs=[SCALARS] + [whole] * 6,
        out_specs=[whole] * 13,
        out_shape=[
            struct(D, WIDE, dtype=BF16), struct(MB, TOK_DEV + HALO, D, dtype=BF16), struct(D, MB * TOK_DEV, dtype=BF16),
            struct(MB, TOK_DEV, D, dtype=BF16), struct(1, D), struct(8, CONV_COLS), struct(8, LANES), struct(8, INNER), struct(8, INNER),
            struct(2 * LANES, INNER, dtype=BF16), struct(2 * LANES, INNER, dtype=BF16),
            struct(INNER, LANES, dtype=BF16), struct(INNER, LANES, dtype=BF16),
        ],
        scratch_shapes=[
            pltpu.VMEM((MB, 2 * HALO, D), BF16), pltpu.VMEM((shards,) + mine.shape, BF16), pltpu.VMEM((8, LANES), F32),
            pltpu.SemaphoreType.DMA((2, 1)), pltpu.SemaphoreType.DMA((2, shards)), pltpu.SemaphoreType.DMA((2, pairs)),
            pltpu.SemaphoreType.DMA((2, pairs)), pltpu.SemaphoreType.DMA((2, 2 * pairs)), pltpu.SemaphoreType.DMA((2, 1)),
        ],
        compiler_params=pltpu.CompilerParams(vmem_limit_bytes=VMEM_LIMIT, collective_id=identity, has_side_effects=True),
    )(info, x, cot, w_inner, w_state, w_step, mine)


def front_body(m, info, vals, bc, dt, taps, steps, spread_f, spread_r, v_out, bc_out, fr_out, frp_out, tot_f, tot_r, kept_f, kept_r, dx_out):
    valid, masks = row_masks(info, m, (TOK_DEV, LANES))
    for chunk in range(PAIRS + 1):
        cols = pl.ds(chunk * LANES, LANES)
        source, own = (vals, cols) if chunk < PAIRS else (bc, pl.ds(0, LANES))
        value = conv_value(conv_windows(source, own), masks, taps, cols)
        value = valid * (value * sigmoid(value))
        if chunk < PAIRS:
            v_out[m, :, cols] = value.astype(BF16)
        else:
            bc_out[m] = value
    lane = iota((BLOCK, LANES), 1)
    rows = iota((BLOCK, BLOCK), 0)
    columns = iota((BLOCK, BLOCK), 1)
    lower = (rows >= columns).astype(F32)
    upper = (rows <= columns).astype(F32)
    forward, reverse = keeps(info, m)
    ends = []
    tails = []
    inputs = []
    for b in range(2):
        span = pl.ds(b * BLOCK, BLOCK)
        step = softplus(dt[0, span, :] + steps[0:1, :])
        log = -step * steps[1:2, :]
        summed = jnp.where(lane < HEADS, dot(lower, log, precision=HIGHEST), dot(upper, log, precision=HIGHEST))
        shifted = summed - jnp.log(step)
        fr_out[m, span, :] = summed
        frp_out[m, span, :] = shifted
        end = jnp.where(lane[:1] < HEADS, summed[BLOCK - 1 :], summed[:1])
        ends.append(jnp.exp(end))
        tails.append(spread_operand(jnp.where(lane < 2 * HEADS, jnp.exp(end - shifted), 0.0)))
        acts = bc_out[m, span, :]
        inputs.append(twice(jnp.transpose(by_lane(acts, swapped(acts))).astype(BF16), 1))
    ends = spread_operand(jnp.concatenate(ends + [jnp.zeros((6, LANES), F32)], axis=0))
    width = 2 * LANES
    for chunk in range(INNER // width):
        cols = pl.ds(chunk * width, width)
        decay_f = dot(ends, spread_f[:, cols])
        decay_r = dot(ends, spread_r[:, cols])
        parts_f = []
        parts_r = []
        for b in range(2):
            v = v_out[m, pl.ds(b * BLOCK, BLOCK), cols].astype(F32)
            parts_f.append(fold(dot(inputs[b], stacked(dot(tails[b], spread_f[:, cols]) * v))))
            parts_r.append(fold(dot(inputs[b], stacked(dot(tails[b], spread_r[:, cols]) * v))))
        kept_f[0, :, cols] = parts_f[0]
        kept_r[0, :, cols] = parts_r[1]
        total_f = parts_f[1] + (forward[1] * decay_f[1:2]) * parts_f[0]
        total_r = parts_r[0] + (reverse[0] * decay_r[0:1]) * parts_r[1]
        for k in range(PARTS):
            part = slice(k * STATE // PARTS, (k + 1) * STATE // PARTS)
            tot_f[PARTS * m + k, :, cols] = total_f[part]
            tot_r[PARTS * m + k, :, cols] = total_r[part]
        dx_out[m, 0:2, cols] = decay_f[0:2]
        dx_out[m, 2:4, cols] = decay_r[0:2]
        dx_out[m, 4:5, cols] = (forward[0] * forward[1]) * (decay_f[0:1] * decay_f[1:2])
        dx_out[m, 5:6, cols] = (reverse[0] * reverse[1]) * (decay_r[0:1] * decay_r[1:2])
        dx_out[m, 6:8, cols] = jnp.zeros((2, width), F32)


def stacked(value):
    return jnp.concatenate(halves(value), axis=0)


def doubled(value):
    high, low = halves(value)
    return jnp.concatenate([high, high, low, low], axis=0)


def pair_stack(value):
    lane = iota(value.shape, 1)
    zero = jnp.zeros_like(value)
    return jnp.concatenate([jnp.where(lane < HEAD_DIM, value, zero), jnp.where(lane < HEAD_DIM, zero, value)], axis=0)


def swapped(value):
    return pltpu.roll(value, STATE, axis=1)


def intra_body(m, b, v, bc, fr, frp, skip, y_out):
    span = pl.ds(pl.multiple_of(b * BLOCK, BLOCK), BLOCK)
    rows = iota((BLOCK, BLOCK), 0)
    columns = iota((BLOCK, BLOCK), 1)
    lower = rows > columns
    acts = bc[m, span, :]
    outs = jnp.where(columns < STATE, swapped(acts), 0.0)
    scores = jnp.where(rows == columns, 0.0, dot(outs, acts, COLS, HIGHEST))
    cum = fr[m, span, :]
    shifted = jnp.transpose(frp[m, span, :])
    for pair in range(PAIRS):
        mats = []
        for h in (2 * pair, 2 * pair + 1):
            r = HEADS + h
            gap = jnp.where(lower, cum[:, h : h + 1] - shifted[h : h + 1], cum[:, r : r + 1] - shifted[r : r + 1])
            mats.append((jnp.exp(gap) * scores).astype(BF16))
        cols = pl.ds(pair * LANES, LANES)
        value = v[m, span, cols]
        y = dot(jnp.concatenate(mats, axis=1), pair_stack(value))
        y_out[0, :, cols] = y + skip[0:1, cols] * value.astype(F32)


def front_kernel(
    levels, columns, info, vals, bc_in, dt, taps, steps, spread_f, spread_r, skip, w_out, d_branch,
    v, bc, fr, frp, kept_f, kept_r, dx, y, enter_f, enter_r, w_back_out, d_normed, tot_f, tot_r, w_back, cross_sems, mate_sems, *buffers,
):
    s = pl.program_id(0)
    part = lax.axis_index("fsdp")
    core, column = lax.rem(part, 2), part // 2
    mate = part + 1 - 2 * core
    rows = w_out.shape[0]

    def column_at(d):
        return lax.rem(column + d + columns, columns)

    def shard_copy(sems, k, owner, device):
        at = w_back.at[pl.ds(pl.multiple_of(owner * rows, LANES // 2), rows)]
        return pltpu.make_async_remote_copy(
            src_ref=at, dst_ref=at, send_sem=sems.at[0, k], recv_sem=sems.at[1, k], device_id={"fsdp": device}
        )

    def across(d, theirs):
        return shard_copy(cross_sems, d, 2 * column_at(-d) + core if theirs else part, 2 * column_at(d) + core)

    def to_mate(d, theirs):
        return shard_copy(mate_sems, d, 2 * column_at(-d) + (1 - core if theirs else core), mate)

    def greet(barrier):
        pl.semaphore_signal(barrier, inc=1, device_id={"fsdp": mate})
        for d in range(1, columns):
            pl.semaphore_signal(barrier, inc=1, device_id={"fsdp": 2 * column_at(d) + core})
        return columns

    begin, send_gains, send, turns, end = carry_steps(levels, 4, 5, dx, tot_f, tot_r, enter_f, enter_r, buffers)

    @pl.when(s == 0)
    def _():
        begin(greet)
        w_back[pl.ds(pl.multiple_of(part * rows, LANES // 2), rows)] = w_out[...]
        for d in range(1, columns):
            across(d, False).start()
        to_mate(0, False).start()

    @pl.when(s == MB)
    def _():
        for d in range(1, columns):
            across(d, True).wait_recv()
            to_mate(d, False).start()

    @pl.when(s == MB + 1)
    def _():
        for d in range(columns):
            to_mate(d, True).wait_recv()
        w_back_out[...] = w_back[...]

    for m in range(MB):

        @pl.when(s == MB + 2 + m)
        def _():
            d_normed[m] = dot(d_branch[m], w_back[...], COLS)

    @pl.when(s < MB)
    def _():
        front_body(s, info, vals, bc_in, dt, taps, steps, spread_f, spread_r, v, bc, fr, frp, tot_f, tot_r, kept_f, kept_r, dx)
        send_gains(s)

        @pl.when(s == 0)
        def _():
            send(0, PARTS)

        @pl.when(s == 1)
        def _():
            send(PARTS, PARTS + 2)

    @pl.when(s >= MB)
    def _():
        slot = s - MB
        intra_body(slot // 2, lax.rem(slot, 2), v, bc, fr, frp, skip, y)
        turns(slot, 2 * MB, PARTS + 2)

    @pl.when(s == 3 * MB - 1)
    def _():
        for d in range(columns):
            to_mate(d, False).wait_send()
            if d > 0:
                across(d, False).wait_send()
        end()


def entering(b, cols, forward, reverse, enter_f, enter_r, kept_f, kept_r, dx):
    first_f = forward[0] * enter_f[0, :, cols].astype(F32)
    last_r = reverse[1] * enter_r[0, :, cols].astype(F32)
    state_f = jnp.where(b == 0, first_f, forward[1] * (dx[0, 0:1, cols] * first_f + kept_f[0, :, cols]))
    state_r = jnp.where(b == 1, last_r, reverse[0] * (dx[0, 3:4, cols] * last_r + kept_r[0, :, cols]))
    return state_f, state_r


def middle_body(
    slot, info, y, gate, d_normed, v, bc, fr, enter_f, enter_r, kept_f, kept_r, dx, gain, spread_f, spread_r, sum_f, sum_r,
    normed, d_mixed, d_gate, back_f, back_r, leave_f, leave_r, d_outs, read_out, d_gain, d_skip, mixed_s, part_f, part_r, exp_f, exp_r,
):
    m, b = slot // 2, lax.rem(slot, 2)
    span = pl.ds(pl.multiple_of(b * BLOCK, BLOCK), BLOCK)
    forward, reverse = keeps(info, m)
    lane = iota((BLOCK, LANES), 1)
    outs = by_lane(swapped(bc[0]), bc[0])
    outs_t = twice(jnp.transpose(outs).astype(BF16), 1)
    outs = twice(outs.astype(BF16), 1)
    grown = spread_operand(jnp.where(lane < 2 * HEADS, jnp.exp(fr[0]), 0.0))
    width = 2 * LANES
    chunks = INNER // width
    squares = jnp.zeros((BLOCK, 1), F32)
    cross = jnp.zeros((BLOCK, 1), F32)
    for chunk in range(chunks):
        cols = pl.ds(chunk * width, width)
        state_f, state_r = entering(b, cols, forward, reverse, enter_f, enter_r, kept_f, kept_r, dx)
        ef = dot(grown, spread_f[:, cols])
        er = dot(grown, spread_r[:, cols])
        carried_f = ef * dot(outs, doubled(state_f))
        carried_r = er * dot(outs, doubled(state_r))
        mixed = y[0, :, cols] + carried_f + carried_r
        exp_f[:, cols] = ef
        exp_r[:, cols] = er
        part_f[:, cols] = carried_f
        part_r[:, cols] = carried_r
        mixed_s[:, cols] = mixed
        g = gate[0, :, cols]
        gated = mixed * (g * sigmoid(g))
        squares = squares + jnp.sum(gated * gated, axis=1, keepdims=True)
        cross = cross + jnp.sum(gated * gain[0:1, cols] * d_normed[0, :, cols], axis=1, keepdims=True)
    scale = lax.rsqrt(squares * (1.0 / INNER) + EPSILON)
    pull = scale * scale * scale * (cross * (1.0 / INNER))
    d_o = jnp.zeros((BLOCK, LANES), F32)
    reads = jnp.zeros((BLOCK, LANES), F32)

    @pl.when((m == 0) & (b == 0))
    def _():
        d_gain[...] = jnp.zeros_like(d_gain)
        d_skip[...] = jnp.zeros_like(d_skip)

    @pl.when(b == 0)
    def _():
        for k in range(PARTS):
            leave_f[PARTS * m + k] = jnp.zeros(CARRY_SHAPE[1:], F32)
            leave_r[PARTS * m + k] = jnp.zeros(CARRY_SHAPE[1:], F32)

    for chunk in range(chunks):
        cols = pl.ds(chunk * width, width)
        g = gate[0, :, cols]
        sig = sigmoid(g)
        silu = g * sig
        mixed = mixed_s[:, cols]
        gated = mixed * silu
        dy = d_normed[0, :, cols]
        scaled = gated * scale
        normed[m, span, cols] = (scaled * gain[0:1, cols]).astype(BF16)
        d_gain[0:1, cols] += jnp.sum(dy * scaled, axis=0, keepdims=True)
        d_gated = scale * gain[0:1, cols] * dy - gated * pull
        dm = d_gated * silu
        d_gate[m, span, cols] = (d_gated * mixed * sig * (1.0 + g * (1.0 - sig))).astype(BF16)
        d_mixed[slot, :, cols] = dm.astype(BF16)
        d_skip[0:1, cols] += jnp.sum(dm * v[0, :, cols].astype(F32), axis=0, keepdims=True)
        state_f, state_r = entering(b, cols, forward, reverse, enter_f, enter_r, kept_f, kept_r, dx)
        grown_f = exp_f[:, cols] * dm
        grown_r = exp_r[:, cols] * dm
        local_f = fold(dot(outs_t, stacked(grown_f)))
        local_r = fold(dot(outs_t, stacked(grown_r)))
        back_f[0, 0, :, cols] = local_f
        back_r[0, 0, :, cols] = local_r
        weight_f = jnp.where(b == 0, forward[0], (forward[0] * forward[1]) * dx[0, 0:1, cols])
        weight_r = jnp.where(b == 0, (reverse[0] * reverse[1]) * dx[0, 3:4, cols], reverse[1])
        local_f = weight_f * local_f
        local_r = weight_r * local_r
        for k in range(PARTS):
            part = slice(k * STATE // PARTS, (k + 1) * STATE // PARTS)
            leave_f[PARTS * m + k, :, cols] += local_f[part]
            leave_r[PARTS * m + k, :, cols] += local_r[part]
        d_o = d_o + dot(spread_operand(grown_f), twice(stacked(state_f), 1), COLS)
        d_o = d_o + dot(spread_operand(grown_r), twice(stacked(state_r), 1), COLS)
        reads = reads + head_sums(dm * part_f[:, cols], sum_f[cols, :]) + head_sums(dm * part_r[:, cols], sum_r[cols, :])
    d_outs[slot] = jnp.where(lane < STATE, 0.0, d_o + swapped(d_o))
    read_out[slot] = reads


def intra_back_body(slot, v, d_mixed, bc, fr, frp, skip, d_outs, read_out, d_v, d_bc, sums, d_log, row_s):
    rows = iota((BLOCK, BLOCK), 0)
    columns = iota((BLOCK, BLOCK), 1)
    ahead = rows < columns
    acts = bc[0]
    low = columns < STATE
    turned = swapped(acts)
    outs = jnp.where(low, turned, 0.0)
    scores = jnp.where(rows == columns, 0.0, dot(acts, outs, COLS, HIGHEST))
    cum = jnp.transpose(fr[0])
    shifted = frp[0]
    d_scores = jnp.zeros((BLOCK, BLOCK), F32)
    gathered = jnp.zeros((BLOCK, LANES), F32)

    row_s[...] = jnp.zeros_like(row_s)
    for pair in range(PAIRS):
        cols = pl.ds(pair * LANES, LANES)
        value = v[0, :, cols]
        dm = d_mixed[slot, :, cols]
        products = dot(pair_stack(value), dm, COLS)
        mats = []
        for side in range(2):
            h = 2 * pair + side
            r = HEADS + h
            gap = jnp.where(ahead, cum[h : h + 1] - shifted[:, h : h + 1], cum[r : r + 1] - shifted[:, r : r + 1])
            weight = jnp.exp(gap)
            mats.append((weight * scores).astype(BF16))
            reach = products[side * BLOCK : (side + 1) * BLOCK] * weight
            d_scores = d_scores + reach
            both = reach * scores
            first = jnp.where(ahead, both, 0.0)
            second = both - first
            gathered = jnp.where(columns == h, jnp.sum(first, axis=1, keepdims=True), gathered)
            gathered = jnp.where(columns == r, jnp.sum(second, axis=1, keepdims=True), gathered)
            row_s[h : h + 1, :] = jnp.sum(first, axis=0, keepdims=True)
            row_s[r : r + 1, :] = jnp.sum(second, axis=0, keepdims=True)
        dmf = dm.astype(F32)
        d_v[0, :, cols] = dot(jnp.concatenate(mats, axis=1), pair_stack(dm)) + skip[0:1, cols] * dmf
    d_scores = jnp.where(rows == columns, 0.0, d_scores)
    ins = jnp.where(low, 0.0, turned)
    d_bc[0] = dot(d_scores, outs, precision=HIGHEST) + dot(jnp.transpose(d_scores), ins, precision=HIGHEST) + d_outs[slot]
    sums[0] = gathered
    d_log[0] = jnp.transpose(row_s[...]) - gathered + read_out[slot]


def shard_steps(columns, normed, d_branch, hidden_t, d_gate, outs, buffers):
    put, gots, cross_puts, cross_gots, mate_sems, cross_sems = buffers
    part = lax.axis_index("fsdp")
    core, column = lax.rem(part, 2), part // 2
    mate = part + 1 - 2 * core
    rows = put.shape[1]

    def column_at(d):
        return lax.rem(column + d + columns, columns)

    def remote(source, target, sems, k, device):
        return pltpu.make_async_remote_copy(
            src_ref=source, dst_ref=target, send_sem=sems.at[0, k], recv_sem=sems.at[1, k], device_id={"fsdp": device}
        )

    def to_mate(which, x):
        return remote(put.at[x], gots[which].at[x], mate_sems, which * columns + x, mate)

    def across(which, d):
        target = 2 * column_at(d) + core
        return remote(cross_puts[which].at[d], cross_gots[which].at[d], cross_sems, which * columns + d, target)

    def piece(which, owner, h):
        half = rows // 2
        if which == 0:
            at = pl.ds(pl.multiple_of(owner * rows, LANES), rows)
            return sum(dot(normed[m, :, at], d_branch[m, :, h * D // 2 : (h + 1) * D // 2], ROWS) for m in range(MB))
        at = pl.ds(pl.multiple_of(owner * half, 16), half)
        return sum(
            dot(hidden_t[at, m * TOK_DEV : (m + 1) * TOK_DEV], d_gate[m, :, h * D : (h + 1) * D]) for m in range(MB)
        )

    def view(which, h):
        return (slice(None), slice(h * D // 2, (h + 1) * D // 2)) if which == 0 else (slice(h * rows // 2, (h + 1) * rows // 2),)

    def greet(barrier):
        pl.semaphore_signal(barrier, inc=1, device_id={"fsdp": mate})
        for d in range(1, columns):
            pl.semaphore_signal(barrier, inc=1, device_id={"fsdp": 2 * column_at(d) + core})
        return columns

    def foreign(which):
        for x in range(columns):
            if which == 1:
                to_mate(0, x).wait_send()
            for h in range(2):
                put[(x,) + view(which, h)] = piece(which, 2 * x + 1 - core, h).astype(BF16)
            to_mate(which, x).start()

    def local(which):
        for x in range(columns):
            to_mate(which, x).wait_recv()
        for d in list(range(1, columns)) + [0]:
            x = column_at(d)
            for h in range(2):
                at = view(which, h)
                value = piece(which, 2 * x + core, h) + gots[which][(x,) + at].astype(F32)
                if d == 0:
                    outs[which][at] = value
                else:
                    cross_puts[which][(d,) + at] = value.astype(BF16)
            if d > 0:
                across(which, d).start()

    def close():
        for which in range(2):
            for d in range(1, columns):
                across(which, d).wait()
                outs[which][...] += cross_gots[which][d].astype(F32)
        for x in range(columns):
            to_mate(1, x).wait_send()

    return greet, foreign, local, close


def shard_buffers(shards):
    columns, shape = shards // 2, (shards // 2, INNER // shards, D)
    low = pltpu.VMEM(shape, BF16)
    return [low] * 7 + [pltpu.SemaphoreType.DMA((2, 2 * columns))] * 2


def middle_kernel(
    levels, columns, info, y, gate, d_normed, v, bc, fr, frp, enter_f, enter_r, kept_f, kept_r, dx, dx_all, gain, skip, spread_f, spread_r,
    sum_f, sum_r, d_branch, hidden_t,
    normed, d_gate, back_f, back_r, d_gain, d_skip, d_v, d_bc, sums, d_log, after_f, after_r, first_out, second_out,
    mixed_s, part_f, part_r, exp_f, exp_r, row_s, d_mixed, d_outs, read_out, leave_f, leave_r,
    put, got_1, got_2, cross_put_1, cross_put_2, cross_got_1, cross_got_2, mate_sems, cross_sems, *buffers,
):
    s = pl.program_id(0)
    begin, send_gains, send, turns, end = carry_steps(levels, 5, 4, dx_all, leave_r, leave_f, after_r, after_f, buffers)
    greet, foreign, local, close = shard_steps(
        columns, normed, d_branch, hidden_t, d_gate, (first_out, second_out),
        (put, (got_1, got_2), (cross_put_1, cross_put_2), (cross_got_1, cross_got_2), mate_sems, cross_sems),
    )
    half = 2 * MB

    @pl.when(s == 0)
    def _():
        begin(greet)

    @pl.when(s < half)
    def _():
        middle_body(
            s, info, y, gate, d_normed, v, bc, fr, enter_f, enter_r, kept_f, kept_r, dx, gain, spread_f, spread_r, sum_f, sum_r,
            normed, d_mixed, d_gate, back_f, back_r, leave_f, leave_r, d_outs, read_out, d_gain, d_skip, mixed_s, part_f, part_r, exp_f, exp_r,
        )

        @pl.when(s == 1)
        def _():
            @pl.loop(0, MB)
            def _(m):
                send_gains(m)

            send(0, PARTS)

        @pl.when(s == 3)
        def _():
            send(PARTS, 2 * PARTS)

    for k, step in enumerate((foreign, local)):
        for which in range(2):

            @pl.when(s == half + 2 * which + k)
            def _():
                step(which)

    @pl.when(s >= half)
    def _():
        slot = s - half
        intra_back_body(slot, v, d_mixed, bc, fr, frp, skip, d_outs, read_out, d_v, d_bc, sums, d_log, row_s)
        turns(slot, half, 2 * PARTS)

    @pl.when(s == 2 * half - 1)
    def _():
        close()
        end()


def final_kernel(
    levels, info, vals, bc_in, dt, taps, rates, v, bc, fr, frp, enter_f, enter_r, kept_f, kept_r, dx, after_f, after_r, back_f, back_r,
    d_v, d_bc, sums, d_log, spread_f, spread_r, sum_f, sum_r, first_in, second_in,
    late, before, last, d_taps, d_small, first_out, second_out, d_acts, *buffers,
):
    m = pl.program_id(0)
    forward, reverse = keeps(info, m)
    if levels:
        greet, steps = sum_steps(levels, (buffers[:6], buffers[6:12]), *buffers[12:])

    def beside(at, *todo):
        if levels:

            @pl.when(m == at)
            def _():
                for stage, i in todo:
                    steps[stage](i)

    if levels:

        @pl.when(m == 0)
        def _():
            barrier = pltpu.get_barrier_semaphore()
            pl.semaphore_wait(barrier, greet(barrier))
            buffers[0][...] = first_in[...]
            buffers[6][...] = second_in[...]

    beside(0, (0, 0))
    lane = iota((BLOCK, LANES), 1)
    row = iota((BLOCK, LANES), 0)
    rows = iota((BLOCK, BLOCK), 0)
    columns = iota((BLOCK, BLOCK), 1)
    lower = (rows >= columns).astype(F32)
    upper = (rows <= columns).astype(F32)
    width = 2 * LANES

    @pl.when(m == 0)
    def _():
        d_taps[...] = jnp.zeros_like(d_taps)
        d_small[...] = jnp.zeros_like(d_small)

    for b in range(2):
        span = pl.ds(b * BLOCK, BLOCK)
        summed = fr[0, span, :]
        end = jnp.where(lane[:1] < HEADS, summed[BLOCK - 1 :], summed[:1])
        tail = spread_operand(jnp.where(lane < 2 * HEADS, jnp.exp(end - frp[0, span, :]), 0.0))
        acts = bc[0, span, :]
        ins = twice(by_lane(acts, swapped(acts)).astype(BF16), 1)
        d_in = jnp.zeros((BLOCK, LANES), F32)
        used = jnp.zeros((BLOCK, LANES), F32)
        decays = jnp.zeros((8, LANES), F32)
        for chunk in range(INNER // width):
            cols = pl.ds(chunk * width, width)
            grad_f = after_f[0, :, cols].astype(F32)
            grad_r = after_r[0, :, cols].astype(F32)
            if b == 0:
                grad_f = forward[1] * (back_f[0, 1, :, cols] + dx[0, 1:2, cols] * grad_f)
            else:
                grad_r = reverse[0] * (back_r[0, 0, :, cols] + dx[0, 2:3, cols] * grad_r)
            state_f, state_r = entering(b, cols, forward, reverse, enter_f, enter_r, kept_f, kept_r, dx)
            tail_f = dot(tail, spread_f[:, cols])
            tail_r = dot(tail, spread_r[:, cols])
            value = v[0, span, cols].astype(F32)
            pulled_f = tail_f * dot(ins, doubled(grad_f))
            pulled_r = tail_r * dot(ins, doubled(grad_r))
            d_acts[span, cols] = d_v[0, span, cols] + pulled_f + pulled_r
            d_in = d_in + dot(spread_operand(tail_f * value), twice(stacked(grad_f), 1), COLS)
            d_in = d_in + dot(spread_operand(tail_r * value), twice(stacked(grad_r), 1), COLS)
            used = used + head_sums(pulled_f * value, sum_f[cols, :]) + head_sums(pulled_r * value, sum_r[cols, :])
            meet_f = jnp.sum(grad_f * state_f, axis=0, keepdims=True) * dx[0, b : b + 1, cols]
            meet_r = jnp.sum(grad_r * state_r, axis=0, keepdims=True) * dx[0, 2 + b : 3 + b, cols]
            zero = jnp.zeros((7, width), F32)
            decays = decays + head_sums(jnp.concatenate([meet_f, zero], axis=0), sum_f[cols, :])
            decays = decays + head_sums(jnp.concatenate([meet_r, zero], axis=0), sum_r[cols, :])
        d_acts[span, pl.ds(INNER, LANES)] = d_bc[0, span, :] + jnp.where(lane < STATE, d_in + swapped(d_in), 0.0)
        direct = sums[0, span, :] + used
        edge = decays[0:1] + jnp.sum(used, axis=0, keepdims=True)
        at_end = ((lane < HEADS) & (row == BLOCK - 1)) | ((lane >= HEADS) & (row == 0))
        grad = d_log[0, span, :] - used + jnp.where(at_end, edge, 0.0)
        grad = jnp.where(lane < HEADS, dot(upper, grad, precision=HIGHEST), dot(lower, grad, precision=HIGHEST))
        x = dt[0, span, :] + rates[0:1, :]
        step = softplus(x)
        sig = sigmoid(x)
        ratio = jnp.where(x < -17.0, 1.0, sig / step)
        d_x = direct * ratio - rates[1:2, :] * grad * sig
        d_x = jnp.where(lane < 2 * HEADS, d_x, 0.0)
        late[0, span, pl.ds(INNER + LANES, LANES)] = d_x.astype(BF16)
        d_small[0:1, :] += jnp.sum(d_x, axis=0, keepdims=True)
        d_small[1:2, :] -= rates[1:2, :] * jnp.sum(step * grad, axis=0, keepdims=True)
        if b == 0:
            beside(1, (1, 1))
            beside(2, (3, 0))
        else:
            beside(0, (0, 1))
            beside(1, (2, 0))
            beside(2, (3, 1))
    valid, masks = row_masks(info, m, (TOK_DEV, LANES))
    edge = jnp.zeros((HALO, LANES), F32)
    for chunk in range(PAIRS + 1):
        cols = pl.ds(chunk * LANES, LANES)
        source, own = (vals, cols) if chunk < PAIRS else (bc_in, pl.ds(0, LANES))
        windows = conv_windows(source, own)
        value = conv_value(windows, masks, taps, cols)
        sig = sigmoid(value)
        grad = valid * d_acts[:, cols] * (sig * (1.0 + value * (1.0 - sig)))
        total = jnp.zeros((HALO + TOK_DEV, LANES), F32)
        for k in range(CONV):
            masked = grad if k == 0 else grad * masks[k]
            d_taps[k : k + 1, cols] += jnp.sum(masked * windows[k], axis=0, keepdims=True)
            padded = jnp.concatenate([edge, masked, edge], axis=0)
            total = total + taps[k : k + 1, cols] * padded[k : k + HALO + TOK_DEV]
        d_taps[CONV : CONV + 1, cols] += jnp.sum(grad, axis=0, keepdims=True)
        before[0, :, cols] = total[:HALO]
        last[0, :, cols] = total[TOK_DEV:]
        late[0, :, cols] = total[HALO:].astype(BF16)
    beside(0, (1, 0))
    beside(1, (2, 1))
    beside(2, (4, 0), (4, 1), (5, 0), (5, 1))
    if levels:

        @pl.when(m == MB - 1)
        def _():
            first_out[...] = buffers[5][...].astype(F32)
            second_out[...] = buffers[11][...].astype(F32)


def once(shape):
    return pl.BlockSpec(shape, lambda *grid: (0,) * len(shape), pipeline_mode=pl.Buffered(1))


def per_micro(shape, column=0):
    return pl.BlockSpec((1,) + shape, lambda m, *rest: (m,) + (0,) * (len(shape) - 1) + (column,))


def per_block(width, column=0):
    return pl.BlockSpec((1, BLOCK, width), lambda m, b: (m, b, column))


def struct(*shape, dtype=F32):
    return jax.ShapeDtypeStruct(shape, dtype)


def call(kernel, grid, in_specs, out_specs, out_shape, scratch=(), flops=0, moved=0, identity=None):
    return pl.pallas_call(
        kernel,
        grid=grid,
        in_specs=in_specs,
        out_specs=out_specs,
        out_shape=out_shape,
        scratch_shapes=list(scratch),
        compiler_params=pltpu.CompilerParams(
            vmem_limit_bytes=VMEM_LIMIT, collective_id=identity, has_side_effects=identity is not None
        ),
        cost_estimate=pl.CostEstimate(flops=flops, bytes_accessed=moved, transcendentals=0),
    )


def shift(value, distance):
    count = lax.axis_size("dp")
    route = [(i, i + distance) for i in range(count) if 0 <= i + distance < count]
    return lax.ppermute(value, "dp", route)


def carry_steps(levels, up_row, down_row, gains, up_in, down_in, up_out, down_out, buffers):
    up_other, down_other, gains_other, up_chain, down_chain, up_next, down_next = buffers[:7]
    up_sems, down_sems, gain_sems, up_link, down_link = buffers[7:]
    me = lax.axis_index("dp")
    side = lax.rem(me, 2)
    level = me // 2
    partner = me + 1 - 2 * side
    above, below = me + 2, me - 2
    has_above, has_below = level < levels - 1, level > 0
    first = side == 0

    def remote(source, target, sems, k, device):
        return pltpu.make_async_remote_copy(
            src_ref=source, dst_ref=target, send_sem=sems.at[0, k], recv_sem=sems.at[1, k], device_id={"dp": device}
        )

    def swap_gains(m):
        return remote(gains.at[m], gains_other.at[m], gain_sems, m, partner)

    def swap_up(k):
        return remote(up_in.at[k], up_other.at[k], up_sems, k, partner)

    def swap_down(k):
        return remote(down_in.at[k], down_other.at[k], down_sems, k, partner)

    def climb(k):
        return remote(up_next.at[k], up_chain.at[k], up_link, k, above)

    def descend(k):
        return remote(down_next.at[k], down_chain.at[k], down_link, k, below)

    def begin(greet=None):
        barrier = pltpu.get_barrier_semaphore()
        others = 0 if greet is None else greet(barrier)
        pl.semaphore_signal(barrier, inc=1, device_id={"dp": partner})

        @pl.when(has_above)
        def _():
            pl.semaphore_signal(barrier, inc=1, device_id={"dp": above})

        @pl.when(has_below)
        def _():
            pl.semaphore_signal(barrier, inc=1, device_id={"dp": below})

        pl.semaphore_wait(barrier, 1 + others + has_above.astype(jnp.int32) + has_below.astype(jnp.int32))

        @pl.when(level == 0)
        def _():
            up_chain[...] = jnp.zeros_like(up_chain)

        @pl.when(level == levels - 1)
        def _():
            down_chain[...] = jnp.zeros_like(down_chain)

    total = CHUNKS + LAG * (levels - 1)

    def places(step):
        return step - LAG * level, step - LAG * (levels - 1 - level)

    def send(low, high):
        @pl.loop(low, high)
        def _(step):
            up, down = places(step)

            @pl.when((up >= 0) & (up < CHUNKS))
            def _():
                swap_up(up).start()

            @pl.when((down >= 0) & (down < CHUNKS))
            def _():
                swap_down(down).start()

    def advance(step):
        up, down = places(step)

        @pl.when((up >= 0) & (up < CHUNKS))
        def _():
            swap_up(up).wait_recv()

            @pl.when(has_below)
            def _():
                climb(up).wait_recv()

            m = up // PARTS
            own, other = gains[m, up_row : up_row + 1], gains_other[m, up_row : up_row + 1]
            near, far = jnp.where(first, own, other), jnp.where(first, other, own)
            mine, theirs = up_in[up], up_other[up]
            before = up_chain[up]
            middle = jnp.where(first, mine, theirs) + near * before
            up_out[up] = jnp.where(first, before, middle)

            @pl.when(has_above)
            def _():
                up_next[up] = jnp.where(first, theirs, mine) + far * middle
                climb(up).start()

        @pl.when((down >= 0) & (down < CHUNKS))
        def _():
            swap_down(down).wait_recv()

            @pl.when(has_above)
            def _():
                descend(down).wait_recv()

            m = down // PARTS
            own, other = gains[m, down_row : down_row + 1], gains_other[m, down_row : down_row + 1]
            near, far = jnp.where(first, other, own), jnp.where(first, own, other)
            mine, theirs = down_in[down], down_other[down]
            before = down_chain[down]
            middle = jnp.where(first, theirs, mine) + near * before
            down_out[down] = jnp.where(first, middle, before)

            @pl.when(has_below)
            def _():
                down_next[down] = jnp.where(first, mine, theirs) + far * middle
                descend(down).start()

    def turns(slot, slots, window):
        each = -(-total // slots)

        @pl.when(slot == 0)
        def _():
            @pl.loop(0, MB)
            def _(m):
                swap_gains(m).wait_recv()

        @pl.loop(0, each)
        def _(k):
            step = slot * each + k
            send(step + window, step + window + 1)
            advance(step)

    def end():
        @pl.loop(0, MB)
        def _(m):
            swap_gains(m).wait_send()

        @pl.loop(0, CHUNKS)
        def _(k):
            swap_up(k).wait_send()
            swap_down(k).wait_send()

        @pl.when(has_above)
        def _():
            @pl.loop(0, CHUNKS)
            def _(k):
                climb(k).wait_send()

        @pl.when(has_below)
        def _():
            @pl.loop(0, CHUNKS)
            def _(k):
                descend(k).wait_send()

    return begin, lambda m: swap_gains(m).start(), send, turns, end


CARRY_SHAPE = (CHUNKS, STATE // PARTS, INNER)


def carry_buffers():
    buffer = pltpu.VMEM(CARRY_SHAPE, F32)
    return (
        [buffer, buffer, pltpu.VMEM((MB, 8, INNER), F32), buffer, buffer, buffer, buffer]
        + [pltpu.SemaphoreType.DMA((2, CHUNKS))] * 2
        + [pltpu.SemaphoreType.DMA((2, MB))]
        + [pltpu.SemaphoreType.DMA((2, CHUNKS))] * 2
    )


def sum_steps(levels, parts, side_sems, level_sems):
    me = lax.axis_index("dp")
    side, level = lax.rem(me, 2), me // 2
    partner = me + 1 - 2 * side

    def level_at(d):
        return lax.rem(level + d + levels, levels)

    def device(d):
        return {"dp": 2 * level_at(d) + side}

    def remote(source, target, sems, k, where):
        return pltpu.make_async_remote_copy(
            src_ref=source, dst_ref=target, send_sem=sems.at[0, k], recv_sem=sems.at[1, k], device_id=where
        )

    def greet(barrier):
        pl.semaphore_signal(barrier, inc=1, device_id={"dp": partner})
        for d in range(1, levels):
            pl.semaphore_signal(barrier, inc=1, device_id=device(d))
        return levels

    def halve(i):
        return remote(parts[i][1], parts[i][2], side_sems, 2 * i, {"dp": partner})

    def join(i, theirs):
        full = parts[i][5]
        return remote(full.at[side], full.at[1 - side if theirs else side], side_sems, 2 * i + 1, {"dp": partner})

    def scatter(i, d, theirs):
        put, got = parts[i][3:5]
        return remote(put.at[level_at(d)], got.at[level_at(-d) if theirs else level], level_sems, 2 * i * levels + d, device(d))

    def gather(i, d, theirs):
        full = parts[i][5]
        target = full.at[side, level_at(-d) if theirs else level]
        return remote(full.at[side, level], target, level_sems, (2 * i + 1) * levels + d, device(d))

    def step_0(i):
        total, put = parts[i][:2]
        put[...] = total[1 - side].astype(BF16)
        halve(i).start()

    def step_1(i):
        total, _, got, put = parts[i][:4]
        halve(i).wait_recv()
        total[side] = total[side] + got[...].astype(F32)
        for d in range(1, levels):
            target = level_at(d)
            put[target] = total[side, target].astype(BF16)
            scatter(i, d, False).start()

    def step_2(i):
        total, _, _, _, got, full = parts[i]
        value = total[side, level]
        for d in range(1, levels):
            scatter(i, d, True).wait_recv()
            value = value + got[level_at(-d)].astype(F32)
        full[side, level] = value.astype(BF16)
        for d in range(1, levels):
            gather(i, d, False).start()

    def step_3(i):
        for d in range(1, levels):
            gather(i, d, True).wait_recv()
        join(i, False).start()

    def step_4(i):
        join(i, True).wait_recv()

    def close(i):
        halve(i).wait_send()
        join(i, False).wait_send()
        for d in range(1, levels):
            scatter(i, d, False).wait_send()
            gather(i, d, False).wait_send()

    return greet, (step_0, step_1, step_2, step_3, step_4, close)


def sum_buffers(levels, piece, width):
    low = pltpu.VMEM((levels, piece, width), BF16)
    both = (2, levels, piece, width)
    return [pltpu.VMEM(both, F32), low, low, low, low, pltpu.VMEM(both, BF16)]


def sum_semaphores(levels, count):
    return [pltpu.SemaphoreType.DMA((2, 2 * count)), pltpu.SemaphoreType.DMA((2, 2 * count * levels))]


PIECES = ((0, 512), (512, 512), (1024, 384), (1408, 384))


def total_kernel(
    levels, columns, info, hidden_t, late, d_gate, normed, w_all, w_back, x_in, cot_in, gain_in,
    gate_in, taps_in, scale_in, skip_in, small_in, selector,
    layer_out, tokens_out, inner_out, state_out, step_out, norm_out, taps_out, bias_out, steps_out, decay_out, skip_out, scale_out,
    third_in, norm_sum, mate_got, cross_put, cross_got, short_sum, short_got, short_sems, mate_sems, cross_sems, side_sems, level_sems, *buffers,
):
    me, part = lax.axis_index("dp"), lax.axis_index("fsdp")
    side, level = lax.rem(me, 2), me // 2
    core, column = lax.rem(part, 2), part // 2
    mate = part + 1 - 2 * core
    count = len(PIECES)
    parts = [buffers[6 * i : 6 * i + 6] for i in range(count)]
    greet, steps = sum_steps(levels, parts, side_sems, level_sems)

    def column_at(d):
        return lax.rem(column + d + columns, columns)

    def remote(source, target, sems, k, where):
        return pltpu.make_async_remote_copy(
            src_ref=source, dst_ref=target, send_sem=sems.at[0, k], recv_sem=sems.at[1, k], device_id=where
        )

    barrier = pltpu.get_barrier_semaphore()
    pl.semaphore_signal(barrier, inc=1, device_id={"fsdp": mate})
    for d in range(1, columns):
        pl.semaphore_signal(barrier, inc=1, device_id={"fsdp": 2 * column_at(d) + core})
    pl.semaphore_wait(barrier, greet(barrier) + columns)

    def to_mate(i, x):
        at = pl.ds(*PIECES[i])
        return remote(third_in.at[2 * x + 1 - core, :, at], mate_got.at[x, :, at], mate_sems, i * columns + x, {"fsdp": mate})

    def across(i, d, theirs):
        at = pl.ds(*PIECES[i])
        where = {"fsdp": 2 * column_at(d) + core}
        slot = column_at(-d) if theirs else column
        return remote(cross_put.at[column_at(d), :, at], cross_got.at[slot, :, at], cross_sems, i * columns + d, where)

    block_rows = third_in.shape[1]

    def third(owner, i):
        at = pl.ds(pl.multiple_of(owner * block_rows, 16), block_rows)
        cols = pl.ds(*PIECES[i])
        third_in[owner, :, cols] = dot(hidden_t[at, :], late[:, cols])

    def d_hidden_block(k):
        m, b = divmod(k, 2)
        at = slice(k * BLOCK, (k + 1) * BLOCK)
        grad = dot(d_gate[at], w_all[:, :INNER], COLS) + dot(late[at], w_all[:, INNER:], COLS)
        rows = x_in[at].astype(F32)
        scale = lax.rsqrt(jnp.mean(rows * rows, axis=1, keepdims=True) + EPSILON)
        norm_sum[...] += jnp.sum(grad * rows * scale, axis=0, keepdims=True)
        pulled = grad * gain_in[...]
        pull = (scale * scale * scale) * jnp.mean(rows * pulled, axis=1, keepdims=True)
        valid = row_masks(info, m, (BLOCK, D), b * BLOCK)[0]
        tokens_out[at] = scale * pulled - rows * pull + valid * cot_in[at].astype(F32)

    def layer_block(k):
        m, b = divmod(k, 2)
        at = slice(k * BLOCK, (k + 1) * BLOCK)
        branch = dot(normed[at], w_back[...])
        valid = row_masks(info, m, (BLOCK, D), b * BLOCK)[0]
        layer_out[at] = jnp.where(valid > 0.0, x_in[at].astype(F32) + branch, 0.0).astype(BF16)

    norm_sum[...] = jnp.zeros_like(norm_sum)
    for i in range(count):
        for x in range(columns):
            third(2 * x + 1 - core, i)
            to_mate(i, x).start()
    for i in range(count):
        for x in range(columns):
            third(2 * x + core, i)

    def cross(i):
        at = pl.ds(*PIECES[i])
        for x in range(columns):
            to_mate(i, x).wait_recv()
        for d in range(1, columns):
            x = column_at(d)
            cross_put[x, :, at] = (third_in[2 * x + core, :, at] + mate_got[x, :, at]).astype(BF16)
            across(i, d, False).start()

    cross(0)
    cross(1)
    for k in range(2 * MB - 2):
        d_hidden_block(k)

    lane = iota((8, LANES), 1)
    summed = jnp.where(lane < HEADS, head_sums(skip_in[...], selector[...]), 0.0)
    folded = small_in[...] + pltpu.roll(small_in[...], LANES - HEADS, axis=1)
    short_sum[0, 0:8, :] = taps_in[...]
    short_sum[0, 8:16, :] = jnp.zeros((8, CONV_COLS), F32)
    short_sum[0, 5:6, :INNER] = scale_in[0:1]
    short_sum[0, 8:9, :LANES] = small_in[0:1]
    short_sum[0, 9:10, :LANES] = folded[1:2]
    short_sum[0, 10:11, :LANES] = summed[0:1]
    routes = [{"fsdp": mate}, {"dp": me + 1 - 2 * side}]
    stride = 1
    while stride < columns:
        routes.append({"fsdp": part + 2 * stride - 4 * stride * lax.rem(column // stride, 2)})
        stride *= 2
    stride = 1
    while stride < levels:
        routes.append({"dp": me + 2 * stride - 4 * stride * lax.rem(level // stride, 2)})
        stride *= 2

    def short(k):
        return remote(short_sum.at[k], short_got.at[k], short_sems, k, routes[k])

    def short_step(k):
        if k > 0:
            short(k - 1).wait_recv()
            short_sum[k] = short_sum[k - 1] + short_got[k - 1]
        if k < len(routes):
            short(k).start()

    rows = parts[0][0].shape[2]

    def arrive(i):
        at = pl.ds(*PIECES[i])
        for d in range(1, columns):
            across(i, d, True).wait_recv()
        for x in range(2):
            for j in range(levels):
                here = pl.ds((x * levels + j) * rows, rows)
                value = third_in[part, here, at] + mate_got[column, here, at]
                for d in range(1, columns):
                    value = value + cross_got[column_at(-d), here, at].astype(F32)
                parts[i][0][x, j] = value
        steps[0](i)

    last = len(routes)
    for wave in range(count + 4):
        for stage in range(4, 0, -1):
            i = wave - stage
            if 0 <= i < count:
                steps[stage](i)
        if wave < count:
            arrive(wave)
        if wave + 2 < count:
            cross(wave + 2)
        if wave < 2:
            d_hidden_block(2 * MB - 2 + wave)
        elif wave < 2 + 2 * MB:
            layer_block(wave - 2)
        if wave == 1:
            short_sum[0, 6:7, :D] = norm_sum[...]
        if 1 <= wave <= last + 1:
            short_step(wave - 1)
    for k in range(count + 3, last + 1):
        short_step(k)

    result = short_sum.at[last]
    for f in range(2 * columns):

        @pl.when(part == f)
        def _():
            def own(row, rows, width, ref):
                size = width // (2 * columns)
                ref[...] = result[row : row + rows, f * size : (f + 1) * size]

            own(0, CONV, CONV_COLS, taps_out)
            own(4, 1, CONV_COLS, bias_out)
            own(5, 1, INNER, scale_out)
            own(6, 1, D, norm_out)
            own(8, 1, 2 * HEADS, steps_out)
            own(9, 1, HEADS, decay_out)
            own(10, 1, HEADS, skip_out)

    half = gate_in.shape[0] // 2
    for h in range(2):
        inner_out[:, h * D : (h + 1) * D] = gate_in[h * half : (h + 1) * half]
    for i in range(count):
        start, width = PIECES[i]
        for x in range(2):
            for j in range(levels):
                here = pl.ds((x * levels + j) * rows, rows)
                value = parts[i][5][x, j].astype(F32)
                inside = min(width, INNER - start)
                inner_out[here, INNER + start : INNER + start + inside] = value[:, :inside]
                if inside < width:
                    state_out[here, :] = value[:, inside : inside + LANES]
                    step_out[here, :] = value[:, inside + LANES : inside + LANES + 2 * HEADS]
    for i in range(count):
        steps[5](i)
        for x in range(columns):
            to_mate(i, x).wait_send()
        for d in range(1, columns):
            across(i, d, False).wait_send()
    for k in range(last):
        short(k).wait_send()


def total_fits(levels, shards, dp_count):
    rows = D // shards
    return dp_count == 2 * levels and shards % 2 == 0 and rows % (16 * levels) == 0 and 24 % shards == 0


def totals(operands, identity):
    dp_count, shards = lax.axis_size("dp"), lax.axis_size("fsdp")
    levels, columns = dp_count // 2, shards // 2
    rows = D // shards
    small = rows // levels // 2
    steps = (dp_count * shards).bit_length() - 1
    count = len(PIECES)

    def low(*shape):
        return pltpu.VMEM(shape, BF16)

    def full(*shape):
        return pltpu.VMEM(shape, F32)

    outs = pl.pallas_call(
        partial(total_kernel, levels, columns),
        in_specs=[SCALARS] + [pl.BlockSpec(memory_space=pltpu.VMEM)] * 15,
        out_specs=[pl.BlockSpec(memory_space=pltpu.VMEM)] * 12,
        out_shape=[struct(MB * TOK_DEV, D, dtype=BF16), struct(MB * TOK_DEV, D)]
        + [struct(rows, 2 * INNER), struct(rows, 2 * STATE), struct(rows, 2 * HEADS)]
        + [struct(1, D // shards), struct(CONV, CONV_COLS // shards), struct(1, CONV_COLS // shards)]
        + [struct(1, width // shards) for width in (2 * HEADS, HEADS, HEADS, INNER)],
        scratch_shapes=[full(shards, rows, LATE), full(1, D), full(columns, rows, LATE), low(columns, rows, LATE), low(columns, rows, LATE)]
        + [full(steps + 1, 16, CONV_COLS), full(steps, 16, CONV_COLS), pltpu.SemaphoreType.DMA((2, steps))]
        + [pltpu.SemaphoreType.DMA((2, count * columns))] * 2
        + sum_semaphores(levels, count)
        + [buffer for _, width in PIECES for buffer in sum_buffers(levels, small, width)],
        compiler_params=pltpu.CompilerParams(vmem_limit_bytes=VMEM_LIMIT, collective_id=identity, has_side_effects=True),
    )(*operands)
    heads = [out.reshape(MB, 1, TOK_DEV, D) for out in outs[:2]]
    flat = [out.reshape(-1) for out in outs[7:]]
    return heads + [outs[5].reshape(-1)] + list(outs[2:5]) + [outs[6]] + flat


def rms(values):
    return lax.rsqrt(jnp.mean(values * values, axis=-1, keepdims=True) + EPSILON)


def scatter_small(parts, shards):
    rows = []
    for part in parts:
        if part.ndim == 2:
            rows.append(part.reshape(part.shape[0], shards, -1).transpose(1, 0, 2).reshape(shards, -1))
        else:
            rows.append(part.reshape(shards, -1))
    flat = jnp.concatenate(rows, axis=1)
    size = flat.shape[1]
    padded = -(-size // LANES) * LANES
    return jnp.pad(flat, ((0, 0), (0, padded - size)))


def on_device(
    tokens, seq_lengths, norm_gain, w_inner, w_state, w_step, conv_weight, conv_bias, step_bias, decay_log, skip_gain, out_gain, w_out, cotangent,
):
    dp_count = lax.axis_size("dp")
    shards = lax.axis_size("fsdp")
    base = lax.axis_index("dp") * TOK_DEV
    lengths = seq_lengths[:, 0]
    info = jnp.concatenate([lengths.reshape(-1), jnp.stack([base, jnp.int32(dp_count * TOK_DEV)]).astype(jnp.int32)])
    width = 512

    def padded(part):
        return jnp.pad(part, ((0, 0),) * (part.ndim - 1) + ((0, width - part.shape[-1]),)).reshape(-1)

    small = [padded(part) for part in (conv_weight, conv_bias, out_gain, norm_gain, step_bias, decay_log, skip_gain)]
    mine = jnp.concatenate(small + [jnp.zeros((6 * width,), BF16)]).reshape(16, width)
    x, cot = tokens[:, 0], cotangent[:, 0]
    w_all, hidden, hidden_t, d_branch, gain_in, taps, steps, skip, out_scale, spread_f, spread_r, sum_f, sum_r = gather_weights(
        info, x, cot, w_inner, w_state, w_step, mine, 4
    )
    rows = TOK_DEV + HALO
    zx = jnp.dot(hidden.reshape(MB * rows, D), w_all, preferred_element_type=F32).reshape(MB, rows, WIDE)

    levels = dp_count // 2
    zx_vals = per_micro((rows, INNER), 1)
    zx_bc = per_micro((rows, LANES), 2 * INNER // LANES)
    zx_dt = per_micro((rows, LANES), 2 * INNER // LANES + 1)
    taps_spec, steps_spec = once((8, CONV_COLS)), once((8, LANES))
    spread_spec, sum_spec = once((2 * LANES, INNER)), once((INNER, LANES))
    state_spec, dx_spec = per_micro((STATE, INNER)), per_micro((8, INNER))
    wide_spec, lane_spec = per_micro((TOK_DEV, INNER)), per_micro((TOK_DEV, LANES))
    row_spec, dx_all_spec, carry_spec = once((8, INNER)), once((MB, 8, INNER)), once(CARRY_SHAPE)

    def early(shape, column=0):
        return pl.BlockSpec((1,) + shape, lambda s: (jnp.minimum(s, MB - 1),) + (0,) * (len(shape) - 1) + (column,))

    def mixing(s):
        slot = jnp.maximum(s - MB, 0)
        return slot // 2, lax.rem(slot, 2), 0

    lanes_all, lanes_struct = once((MB, TOK_DEV, LANES)), struct(MB, TOK_DEV, LANES)
    v, bc, fr, frp, kept_f, kept_r, dx, y, enter_f, enter_r, w_back, d_normed = call(
        partial(front_kernel, levels, shards // 2),
        (3 * MB,),
        [
            SCALARS, early((rows, INNER), 1), early((rows, LANES), 2 * INNER // LANES), early((rows, LANES), 2 * INNER // LANES + 1),
            taps_spec, steps_spec, spread_spec, spread_spec, row_spec, once(w_out.shape), once((MB, TOK_DEV, D)),
        ],
        [once((MB, TOK_DEV, INNER)), lanes_all, lanes_all, lanes_all, early((STATE, INNER)), early((STATE, INNER)), dx_all_spec]
        + [pl.BlockSpec((1, BLOCK, INNER), mixing), carry_spec, carry_spec, once((INNER, D)), once((MB, TOK_DEV, INNER))],
        [struct(MB, TOK_DEV, INNER, dtype=BF16), lanes_struct, lanes_struct, lanes_struct]
        + [struct(MB, STATE, INNER), struct(MB, STATE, INNER), struct(MB, 8, INNER), struct(MB, TOK_DEV, INNER)]
        + [struct(*CARRY_SHAPE)] * 2
        + [struct(INNER, D, dtype=BF16), struct(MB, TOK_DEV, INNER)],
        scratch=[pltpu.VMEM(CARRY_SHAPE, F32)] * 2
        + [pltpu.VMEM((INNER, D), BF16)]
        + [pltpu.SemaphoreType.DMA((2, shards // 2))] * 2
        + carry_buffers(),
        flops=20_000_000_000,
        moved=30_000_000,
        identity=0,
    )(info, zx, zx, zx, taps, steps, spread_f, spread_r, skip, w_out, d_branch)
    enter_f, enter_r = enter_f.reshape(MB, STATE, INNER), enter_r.reshape(MB, STATE, INNER)

    def turning(s):
        return jnp.minimum(s, 2 * MB - 1)

    def backing(s):
        return jnp.maximum(s - 2 * MB, 0)

    def either(s):
        return lax.rem(s, 2 * MB)

    def block_at(pick, width, column=0):
        return pl.BlockSpec((1, BLOCK, width), lambda s: (pick(s) // 2, lax.rem(pick(s), 2), column))

    def state_at(height):
        return pl.BlockSpec((1, height, INNER), lambda s: (turning(s) // 2, 0, 0))

    back_spec = pl.BlockSpec((1, 1, STATE, INNER), lambda s: (turning(s) // 2, lax.rem(turning(s), 2), 0, 0))
    wide_in = block_at(turning, INNER)
    lane_in, lane_out = block_at(either, LANES), block_at(backing, LANES)
    shard_rows = INNER // shards
    shard_spec = once((shard_rows, D))
    normed, d_gate, back_f, back_r, d_out_gain, d_skip, d_v, d_bc, sums, d_log, after_f, after_r, first_grad, gate_grad = call(
        partial(middle_kernel, levels, shards // 2),
        (4 * MB,),
        [SCALARS, wide_in, wide_in, wide_in, block_at(either, INNER), lane_in, lane_in, lane_in]
        + [state_at(STATE)] * 4
        + [state_at(8), dx_all_spec, row_spec, row_spec, spread_spec, spread_spec, sum_spec, sum_spec]
        + [once((MB, TOK_DEV, D)), once((D, MB * TOK_DEV))],
        [once((MB, TOK_DEV, INNER))] * 2
        + [back_spec, back_spec, row_spec, row_spec, block_at(backing, INNER)]
        + [lane_out] * 3
        + [carry_spec] * 2
        + [shard_spec] * 2,
        [struct(MB, TOK_DEV, INNER, dtype=BF16)] * 2
        + [struct(MB, 2, STATE, INNER)] * 2
        + [struct(8, INNER)] * 2
        + [struct(MB, TOK_DEV, INNER)]
        + [struct(MB, TOK_DEV, LANES)] * 3
        + [struct(*CARRY_SHAPE)] * 2
        + [struct(shard_rows, D)] * 2,
        scratch=[pltpu.VMEM((BLOCK, INNER), F32)] * 5
        + [pltpu.VMEM((BLOCK, LANES), F32), pltpu.VMEM((2 * MB, BLOCK, INNER), BF16)]
        + [pltpu.VMEM((2 * MB, BLOCK, LANES), F32)] * 2
        + [pltpu.VMEM(CARRY_SHAPE, F32)] * 2
        + shard_buffers(shards)
        + carry_buffers(),
        flops=30_000_000_000,
        moved=40_000_000,
        identity=1,
    )(
        info, y, zx, d_normed, v, bc, fr, frp, enter_f, enter_r, kept_f, kept_r, dx, dx, out_scale, skip, spread_f, spread_r, sum_f, sum_r,
        d_branch, hidden_t,
    )
    after_f, after_r = after_f.reshape(MB, STATE, INNER), after_r.reshape(MB, STATE, INNER)

    fits = total_fits(levels, shards, dp_count)
    if fits:
        split = (2, levels, shard_rows // (2 * levels), D)
        first_grad, gate_grad = first_grad.reshape(split), gate_grad.reshape(split)
    else:
        split = (8, LANES)
    unused = jnp.zeros((8, LANES), F32)
    late, before, last, d_taps, d_small, first_sum, gate_sum = call(
        partial(final_kernel, levels if fits else 0),
        (MB,),
        [SCALARS, zx_vals, zx_bc, zx_dt, taps_spec, steps_spec, wide_spec, lane_spec, lane_spec, lane_spec]
        + [state_spec] * 4
        + [dx_spec, state_spec, state_spec, per_micro((2, STATE, INNER)), per_micro((2, STATE, INNER))]
        + [wide_spec, lane_spec, lane_spec, lane_spec, spread_spec, spread_spec, sum_spec, sum_spec, once(split), once(split)],
        [per_micro((TOK_DEV, LATE)), per_micro((HALO, CONV_COLS)), per_micro((HALO, CONV_COLS)), once((8, CONV_COLS)), once((8, LANES)), once(split), once(split)],
        [
            struct(MB, TOK_DEV, LATE, dtype=BF16),
            struct(MB, HALO, CONV_COLS),
            struct(MB, HALO, CONV_COLS),
            struct(8, CONV_COLS),
            struct(8, LANES),
            struct(*split),
            struct(*split),
        ],
        scratch=[pltpu.VMEM((TOK_DEV, CONV_COLS), F32)]
        + (2 * sum_buffers(*split[1:]) + sum_semaphores(levels, 2) if fits else []),
        flops=2_000_000_000,
        moved=40_000_000,
        identity=3 if fits else None,
    )(
        info, zx, zx, zx, taps, steps, v, bc, fr, frp, enter_f, enter_r, kept_f, kept_r, dx, after_f, after_r, back_f, back_r,
        d_v, d_bc, sums, d_log, spread_f, spread_r, sum_f, sum_r, first_grad if fits else unused, gate_grad if fits else unused,
    )
    ending = (last + shift(before, -1)).astype(BF16)
    late = lax.dynamic_update_slice(late, ending, (0, TOK_DEV - HALO, 0)).reshape(MB * TOK_DEV, LATE)

    d_gate = d_gate.reshape(MB * TOK_DEV, INNER)
    normed = normed.reshape(MB * TOK_DEV, INNER)
    if fits:
        flat = [part.reshape(MB * TOK_DEV, D) for part in (x, cot)]
        grads = totals(
            (info, hidden_t, late, d_gate, normed, w_all, w_back, *flat, gain_in, gate_sum.reshape(shard_rows, D))
            + (d_taps, d_out_gain, d_skip, d_small, sum_f),
            2,
        )
        return (*grads, first_sum.reshape(shard_rows, D))

    def owned(grad):
        return lax.psum_scatter(grad, "fsdp", scatter_dimension=0, tiled=True)

    places = base + jnp.arange(TOK_DEV, dtype=jnp.int32)
    first = lengths[:, :1]
    start = (first + BLOCK - 1) // BLOCK * BLOCK
    valid = (places[None] < first) | (places[None] >= start) & (places[None] < start + lengths[:, 1:])
    valid = valid[..., None]
    branch = dot(normed, w_back).reshape(MB, TOK_DEV, D)
    x_rows = x.astype(F32)
    layer_out = jnp.where(valid, x_rows + branch, 0.0).astype(BF16)
    late_grad = dot(hidden_t, late)
    d_hidden = dot(d_gate, w_all[:, :INNER], COLS) + dot(late, w_all[:, INNER:], COLS)
    d_hidden = d_hidden.reshape(MB, TOK_DEV, D)
    scale = rms(x_rows)
    d_norm_gain = jnp.sum(d_hidden * x_rows * scale, axis=(0, 1))
    pulled = d_hidden * gain_in
    d_x = scale * pulled - x_rows * (scale * scale * scale) * jnp.mean(x_rows * pulled, axis=-1, keepdims=True)
    tokens_grad = d_x + jnp.where(valid, cot.astype(F32), 0.0)
    d_skip_gain = jnp.sum(d_skip[0].reshape(HEADS, HEAD_DIM), axis=1)
    d_decay = d_small[1, :HEADS] + d_small[1, HEADS : 2 * HEADS]
    small = (d_norm_gain, d_taps[:CONV], d_taps[CONV], d_small[0, : 2 * HEADS], d_decay, d_skip_gain, d_out_gain[0])
    w_out_grad, gate_grad, late_grad = lax.psum((first_grad, gate_grad, owned(late_grad)), "dp")
    summed = lax.psum(scatter_small(small, shards), ("dp", "fsdp"))
    own = lax.dynamic_slice_in_dim(summed, lax.axis_index("fsdp"), 1, axis=0)[0]
    pieces = []
    at = 0
    for part in (norm_gain, conv_weight, conv_bias, step_bias, decay_log, skip_gain, out_gain):
        pieces.append(own[at : at + part.size].reshape(part.shape))
        at += part.size
    gate_grad = jnp.concatenate([gate_grad[: shard_rows // 2], gate_grad[shard_rows // 2 :]], axis=1)
    w_inner_grad = jnp.concatenate([gate_grad, late_grad[:, :INNER]], axis=1)
    w_state_grad = late_grad[:, INNER : INNER + 2 * STATE]
    w_step_grad = late_grad[:, INNER + LANES : INNER + LANES + 2 * HEADS]
    grads = pieces[:1] + [w_inner_grad, w_state_grad, w_step_grad] + pieces[1:] + [w_out_grad]
    return (layer_out[:, None], tokens_grad[:, None], *grads)


def solution(mesh):
    rows, vector, matrix = P(None, "fsdp", "dp", None), P("fsdp"), P("fsdp", None)
    weights = (vector, matrix, matrix, matrix, P(None, "fsdp"), vector, vector, vector, vector, vector, matrix)
    return jax.shard_map(
        on_device,
        mesh=mesh,
        in_specs=(rows, P(None, "fsdp", None)) + weights + (rows,),
        out_specs=(rows, rows) + weights,
        check_vma=False,
    )
```

```python
from functools import partial

import jax
import jax.numpy as jnp
from jax import lax
from jax.experimental import pallas as pl
from jax.experimental.pallas import tpu as pltpu
from jax.sharding import PartitionSpec as P

D = 768
INNER = 1536
HEADS = 24
HEAD_DIM = 64
STATE = 64
CONV = 4
BLOCK = 128
MB = 3
TOK_DEV = 256
HALO = 8
LANES = 128
CONV_COLS = INNER + 2 * STATE
WIDE = 2 * INNER + 2 * LANES
LATE = INNER + 2 * LANES
PAIRS = HEADS // 2
PARTS = 4
CHUNKS = MB * PARTS
LAG = 2
TURNS = 3
TURN_PAIRS = PAIRS // TURNS
CUTS = 3
EPSILON = 1e-05
HIGHEST = lax.Precision.HIGHEST
F32 = jnp.float32
BF16 = jnp.bfloat16
SENT = F32
ROWS = ((0,), (0,))
COLS = ((1,), (1,))
INNER_DIMS = ((1,), (0,))
VMEM_LIMIT = 60 * 1024 * 1024
SCALARS = pl.BlockSpec(memory_space=pltpu.SMEM)


def dot(left, right, dims=INNER_DIMS, precision=None):
    return lax.dot_general(left, right, (dims, ((), ())), precision=precision, preferred_element_type=F32)


def halves(value):
    high = value.astype(BF16)
    return high, (value - high.astype(F32)).astype(BF16)


def spread_operand(value):
    high, low = halves(value)
    return jnp.concatenate([high, low], axis=1)


def by_lane(first, second):
    low = iota(first.shape, 1) < STATE
    twice = jnp.where(low, first, second)
    high = twice.astype(BF16).astype(F32)
    return jnp.where(low, high, twice - high)


def twice(value, axis):
    return jnp.concatenate([value, value], axis=axis)


def fold(value):
    return value[:STATE] + value[STATE:]


def head_sums(value, selector):
    high, low = halves(value)
    return dot(high, selector) + dot(low, selector)


def sigmoid(value):
    return 1.0 / (1.0 + jnp.exp(-value))


def softplus(value):
    tail = jnp.exp(-jnp.abs(value))
    series = tail * (1.0 - tail * (0.5 - tail * (1.0 / 3.0 - 0.25 * tail)))
    return jnp.maximum(value, 0.0) + jnp.where(tail < 0.01, series, jnp.log(1.0 + tail))


def iota(shape, dim):
    return lax.broadcasted_iota(jnp.int32, shape, dim)


def span_scalars(info, m):
    first = info[2 * m]
    start = ((first + (BLOCK - 1)) >> 7) << 7
    return first, start, start + info[2 * m + 1], info[2 * MB], info[2 * MB + 1]


def keeps(info, m):
    _, start, _, base, span = span_scalars(info, m)

    def keep(position):
        begins = (position == 0) | (position == start) | (position >= span)
        return jnp.where(begins, 0.0, 1.0).astype(F32)

    forward = [keep(base), keep(base + BLOCK)]
    reverse = [keep(base + BLOCK), keep(base + 2 * BLOCK)]
    return forward, reverse


def row_masks(info, m, shape, offset=0):
    first, start, end, base, _ = span_scalars(info, m)
    place = iota(shape, 0) + (base + offset)
    inside = (place < first) | ((place >= start) & (place < end))
    offset = jnp.where(place >= start, place - start, place)
    return inside.astype(F32), [(offset >= k).astype(F32) for k in range(CONV)]


def conv_windows(ref, cols):
    main = ref[0, :TOK_DEV, cols]
    halo = ref[0, TOK_DEV:, cols]
    whole = jnp.concatenate([halo, main], axis=0)
    return [main] + [whole[HALO - k : HALO - k + TOK_DEV] for k in range(1, CONV)]


def conv_value(windows, masks, taps, cols):
    value = taps[CONV : CONV + 1, cols] + taps[0:1, cols] * windows[0]
    for k in range(1, CONV):
        value = value + taps[k : k + 1, cols] * (windows[k] * masks[k])
    return value


def gather_kernel(
    count, columns, info, x_in, cot_in, w_inner, w_state, w_step, mine,
    w_all, hidden, hidden_t, d_branch, d_branch_t, norm, taps, steps, skip, scale, spread_f, spread_r, sum_f, sum_r,
    halo, small, skip_row, halo_sems, small_sems, x_sems, y_sems, mate_sems, own_sems,
):
    me, part = lax.axis_index("dp"), lax.axis_index("fsdp")
    side, core, column = lax.rem(me, 2), lax.rem(part, 2), part // 2
    partner, mate = me + 1 - 2 * side, part + 1 - 2 * core
    has_next, has_last = me < count - 1, me > 0
    shards = 2 * columns
    rows = w_inner.shape[0]
    chunk = rows // (2 * CUTS)

    barrier = pltpu.get_barrier_semaphore()

    @pl.when(has_next)
    def _():
        pl.semaphore_signal(barrier, inc=1, device_id={"dp": me + 1})

    @pl.when(has_last)
    def _():
        pl.semaphore_signal(barrier, inc=1, device_id={"dp": me - 1})

    def other(d):
        return lax.rem(part + d + shards, shards)

    def column_at(d):
        return lax.rem(column + d + columns, columns)

    for d in range(1, shards):
        pl.semaphore_signal(barrier, inc=1, device_id={"fsdp": other(d)})
    pl.semaphore_wait(barrier, shards - 1 + has_next.astype(jnp.int32) + has_last.astype(jnp.int32))

    def remote(source, target, sems, k, where):
        return pltpu.make_async_remote_copy(
            src_ref=source, dst_ref=target, send_sem=sems.at[0, k], recv_sem=sems.at[1, k], device_id=where
        )

    def rows_of(owner, half, k):
        return w_all.at[pl.ds(pl.multiple_of(owner * rows + half * (rows // 2) + k * chunk, 16), chunk)]

    edge = remote(x_in.at[:, pl.ds(TOK_DEV - 2 * HALO, 2 * HALO)], halo, halo_sems, 0, {"dp": me + 1})

    def small_copy(d, theirs):
        return remote(mine, small.at[other(-d) if theirs else part], small_sems, d, {"fsdp": other(d)})

    def x_copy(k, d):
        at = rows_of(part, side, k)
        return remote(at, at, x_sems, k * columns + d, {"fsdp": 2 * column_at(d) + core})

    def x_arrival(k, d):
        at = rows_of(2 * column_at(-d) + core, side, k)
        return remote(at, at, x_sems, k * columns + d, {"fsdp": part})

    def y_copy(k, d, theirs):
        at = rows_of(2 * column_at(-d) + core, 1 - side if theirs else side, k)
        return remote(at, at, y_sems, k * columns + d, {"dp": partner})

    def mate_copy(k, d, half, theirs):
        at = rows_of(2 * column_at(-d) + (1 - core if theirs else core), half, k)
        return remote(at, at, mate_sems, (k * columns + d) * 2 + half, {"fsdp": mate})

    def own_copy(owner):
        at = w_all.at[pl.ds(pl.multiple_of(owner * rows, 16), rows)]
        return remote(at, at, own_sems, 0, {"fsdp": mate})

    @pl.when(has_next)
    def _():
        edge.start()

    for d in range(1, shards):
        small_copy(d, False).start()
    here = pl.ds(pl.multiple_of(part * rows, 16), rows)
    w_all[here, : 2 * INNER] = w_inner[...]
    w_all[here, 2 * INNER : 2 * INNER + 2 * STATE] = w_state[...]
    w_all[here, 2 * INNER + 2 * STATE :] = jnp.concatenate(
        [w_step[...].astype(F32), jnp.zeros((rows, LANES - 2 * HEADS), F32)], axis=1
    ).astype(BF16)
    for k in range(2):
        for d in range(1, columns):
            x_copy(k, d).start()
    own_copy(part).start()

    @pl.when(me == 0)
    def _():
        halo[...] = jnp.zeros_like(halo)

    def chosen(mask):
        return jnp.where(mask, 1.0, 0.0).astype(BF16)

    shape = (2 * LANES, INNER)
    lane_of, head_of = iota(shape, 0) & (LANES - 1), iota(shape, 1) >> 6
    spread_f[...] = chosen(lane_of == head_of)
    spread_r[...] = chosen(lane_of == head_of + HEADS)
    shape = (INNER, LANES)
    lane_of, head_of = iota(shape, 1), iota(shape, 0) >> 6
    sum_f[...] = chosen(lane_of == head_of)
    sum_r[...] = chosen(lane_of == head_of + HEADS)
    for m in range(MB):
        valid = row_masks(info, m, (TOK_DEV, D))[0]
        value = jnp.where(valid > 0.0, cot_in[m].astype(F32), 0.0)
        d_branch[m] = value.astype(BF16)
        d_branch_t[:, m * TOK_DEV : (m + 1) * TOK_DEV] = jnp.transpose(value).astype(BF16)

    for ref in (norm, taps, steps, skip_row):
        ref[...] = jnp.zeros_like(ref)
    for d in range(1, shards):
        small_copy(d, True).wait_recv()
    small[part] = mine[...]
    wide, heads = CONV_COLS // shards, HEADS // shards
    for f in range(shards):
        value = small[f].astype(F32)
        taps[: CONV + 1, f * wide : (f + 1) * wide] = value[: CONV + 1, :wide]
        gain = value[5:6, : INNER // shards]
        scale[:, f * INNER // shards : (f + 1) * INNER // shards] = jnp.broadcast_to(gain, (8, INNER // shards))
        norm[:, f * rows : (f + 1) * rows] = value[6:7, :rows]
        steps[0:1, 2 * f * heads : 2 * (f + 1) * heads] = value[7:8, : 2 * heads]
        rates = jnp.exp(value[8:9, :heads])
        steps[1:2, f * heads : (f + 1) * heads] = rates
        steps[1:2, HEADS + f * heads : HEADS + (f + 1) * heads] = rates
        skip_row[0:1, f * heads : (f + 1) * heads] = value[9:10, :heads]
    skip[...] = dot(spread_operand(skip_row[...]), spread_f[...])

    @pl.when(has_last)
    def _():
        edge.wait_recv()

    def normalise(values):
        root = lax.rsqrt(jnp.mean(values * values, axis=1, keepdims=True) + EPSILON)
        return values * root * norm[...]

    def hide(m):
        value = normalise(x_in[m].astype(F32))
        hidden[m, :TOK_DEV] = value.astype(BF16)
        hidden_t[:, m * TOK_DEV : (m + 1) * TOK_DEV] = jnp.transpose(value).astype(BF16)
        hidden[m, TOK_DEV:] = normalise(halo[m].astype(F32)[HALO:]).astype(BF16)

    def pass_on(k):
        for d in range(1, columns):
            y_copy(k, d, True).wait_recv()

            @pl.when(side == 0)
            def _():
                mate_copy(k, d, 1, False).start()

            @pl.when(side == 1)
            def _():
                mate_copy(k, d, 0, False).start()

    for k in range(CUTS):
        if k < MB:
            hide(k)
        for d in range(1, columns):
            x_arrival(k, d).wait_recv()
            y_copy(k, d, False).start()

            @pl.when(side == 0)
            def _():
                mate_copy(k, d, 0, False).start()

            @pl.when(side == 1)
            def _():
                mate_copy(k, d, 1, False).start()

            if k + 2 < CUTS:
                x_copy(k + 2, d).start()
        if k > 0:
            pass_on(k - 1)
    for m in range(CUTS, MB):
        hide(m)
    pass_on(CUTS - 1)
    own_copy(mate).wait_recv()
    own_copy(part).wait_send()
    for k in range(CUTS):
        for d in range(1, columns):
            for half in range(2):
                mate_copy(k, d, half, True).wait_recv()
                mate_copy(k, d, half, False).wait_send()
            x_copy(k, d).wait_send()
            y_copy(k, d, False).wait_send()
    for d in range(1, shards):
        small_copy(d, False).wait_send()

    @pl.when(has_next)
    def _():
        edge.wait_send()


def gather_weights(info, x, cot, w_inner, w_state, w_step, mine, identity):
    count, shards = lax.axis_size("dp"), lax.axis_size("fsdp")
    columns = shards // 2
    whole = pl.BlockSpec(memory_space=pltpu.VMEM)
    pairs = CUTS * columns
    return pl.pallas_call(
        partial(gather_kernel, count, columns),
        in_specs=[SCALARS] + [whole] * 6,
        out_specs=[whole] * 14,
        out_shape=[
            struct(D, WIDE, dtype=BF16), struct(MB, TOK_DEV + HALO, D, dtype=BF16), struct(D, MB * TOK_DEV, dtype=BF16),
            struct(MB, TOK_DEV, D, dtype=BF16), struct(D, MB * TOK_DEV, dtype=BF16), struct(1, D), struct(8, CONV_COLS), struct(8, LANES), struct(8, INNER), struct(8, INNER),
            struct(2 * LANES, INNER, dtype=BF16), struct(2 * LANES, INNER, dtype=BF16),
            struct(INNER, LANES, dtype=BF16), struct(INNER, LANES, dtype=BF16),
        ],
        scratch_shapes=[
            pltpu.VMEM((MB, 2 * HALO, D), BF16), pltpu.VMEM((shards,) + mine.shape, BF16), pltpu.VMEM((8, LANES), F32),
            pltpu.SemaphoreType.DMA((2, 1)), pltpu.SemaphoreType.DMA((2, shards)), pltpu.SemaphoreType.DMA((2, pairs)),
            pltpu.SemaphoreType.DMA((2, pairs)), pltpu.SemaphoreType.DMA((2, 2 * pairs)), pltpu.SemaphoreType.DMA((2, 1)),
        ],
        compiler_params=pltpu.CompilerParams(vmem_limit_bytes=VMEM_LIMIT, collective_id=identity, has_side_effects=True),
    )(info, x, cot, w_inner, w_state, w_step, mine)


def front_body(m, info, vals, bc, dt, taps, steps, spread_f, spread_r, v_out, bc_out, fr_out, frp_out, tot_f, tot_r, kept_f, kept_r, dx_out):
    valid, masks = row_masks(info, m, (TOK_DEV, LANES))
    for chunk in range(PAIRS + 1):
        cols = pl.ds(chunk * LANES, LANES)
        source, own = (vals, cols) if chunk < PAIRS else (bc, pl.ds(0, LANES))
        value = conv_value(conv_windows(source, own), masks, taps, cols)
        value = valid * (value * sigmoid(value))
        if chunk < PAIRS:
            v_out[m, :, cols] = value.astype(BF16)
        else:
            bc_out[m] = value
    lane = iota((BLOCK, LANES), 1)
    rows = iota((BLOCK, BLOCK), 0)
    columns = iota((BLOCK, BLOCK), 1)
    lower = (rows >= columns).astype(F32)
    upper = (rows <= columns).astype(F32)
    forward, reverse = keeps(info, m)
    ends = []
    tails = []
    inputs = []
    for b in range(2):
        span = pl.ds(b * BLOCK, BLOCK)
        step = softplus(dt[0, span, :] + steps[0:1, :])
        log = -step * steps[1:2, :]
        summed = jnp.where(lane < HEADS, dot(lower, log, precision=HIGHEST), dot(upper, log, precision=HIGHEST))
        shifted = summed - jnp.log(step)
        fr_out[m, span, :] = summed
        frp_out[m, span, :] = shifted
        end = jnp.where(lane[:1] < HEADS, summed[BLOCK - 1 :], summed[:1])
        ends.append(jnp.exp(end))
        tails.append(spread_operand(jnp.where(lane < 2 * HEADS, jnp.exp(end - shifted), 0.0)))
        acts = bc_out[m, span, :]
        inputs.append(twice(jnp.transpose(by_lane(acts, swapped(acts))).astype(BF16), 1))
    ends = spread_operand(jnp.concatenate(ends + [jnp.zeros((6, LANES), F32)], axis=0))
    width = 2 * LANES
    for chunk in range(INNER // width):
        cols = pl.ds(chunk * width, width)
        decay_f = dot(ends, spread_f[:, cols])
        decay_r = dot(ends, spread_r[:, cols])
        parts_f = []
        parts_r = []
        for b in range(2):
            v = v_out[m, pl.ds(b * BLOCK, BLOCK), cols].astype(F32)
            parts_f.append(fold(dot(inputs[b], stacked(dot(tails[b], spread_f[:, cols]) * v))))
            parts_r.append(fold(dot(inputs[b], stacked(dot(tails[b], spread_r[:, cols]) * v))))
        kept_f[m, :, cols] = parts_f[0]
        kept_r[m, :, cols] = parts_r[1]
        total_f = parts_f[1] + (forward[1] * decay_f[1:2]) * parts_f[0]
        total_r = parts_r[0] + (reverse[0] * decay_r[0:1]) * parts_r[1]
        for k in range(PARTS):
            part = slice(k * STATE // PARTS, (k + 1) * STATE // PARTS)
            tot_f[PARTS * m + k, :, cols] = total_f[part]
            tot_r[PARTS * m + k, :, cols] = total_r[part]
        dx_out[m, 0:2, cols] = decay_f[0:2]
        dx_out[m, 2:4, cols] = decay_r[0:2]
        dx_out[m, 4:5, cols] = (forward[0] * forward[1]) * (decay_f[0:1] * decay_f[1:2])
        dx_out[m, 5:6, cols] = (reverse[0] * reverse[1]) * (decay_r[0:1] * decay_r[1:2])
        dx_out[m, 6:8, cols] = jnp.zeros((2, width), F32)


def stacked(value):
    return jnp.concatenate(halves(value), axis=0)


def doubled(value):
    high, low = halves(value)
    return jnp.concatenate([high, high, low, low], axis=0)


def pair_stack(value):
    lane = iota(value.shape, 1)
    zero = jnp.zeros_like(value)
    return jnp.concatenate([jnp.where(lane < HEAD_DIM, value, zero), jnp.where(lane < HEAD_DIM, zero, value)], axis=0)


def swapped(value):
    return pltpu.roll(value, STATE, axis=1)


def intra_body(m, b, v, bc, fr, frp, skip, y_out):
    span = pl.ds(pl.multiple_of(b * BLOCK, BLOCK), BLOCK)
    rows = iota((BLOCK, BLOCK), 0)
    columns = iota((BLOCK, BLOCK), 1)
    lower = rows > columns
    acts = bc[m, span, :]
    outs = jnp.where(columns < STATE, swapped(acts), 0.0)
    scores = jnp.where(rows == columns, 0.0, dot(outs, acts, COLS, HIGHEST))
    cum = fr[m, span, :]
    shifted = jnp.transpose(frp[m, span, :])
    for pair in range(PAIRS):
        mats = []
        for h in (2 * pair, 2 * pair + 1):
            r = HEADS + h
            gap = jnp.where(lower, cum[:, h : h + 1] - shifted[h : h + 1], cum[:, r : r + 1] - shifted[r : r + 1])
            mats.append((jnp.exp(gap) * scores).astype(BF16))
        cols = pl.ds(pair * LANES, LANES)
        value = v[m, span, cols]
        y = dot(jnp.concatenate(mats, axis=1), pair_stack(value))
        y_out[0, :, cols] = y + skip[0:1, cols] * value.astype(F32)


def entering(m, b, cols, forward, reverse, enter_f, enter_r, kept_f, kept_r, dx):
    first_f = forward[0] * jnp.concatenate([enter_f[PARTS * m + k, :, cols] for k in range(PARTS)], axis=0)
    last_r = reverse[1] * jnp.concatenate([enter_r[PARTS * m + k, :, cols] for k in range(PARTS)], axis=0)
    state_f = jnp.where(b == 0, first_f, forward[1] * (dx[m, 0:1, cols] * first_f + kept_f[m, :, cols]))
    state_r = jnp.where(b == 1, last_r, reverse[0] * (dx[m, 3:4, cols] * last_r + kept_r[m, :, cols]))
    return state_f, state_r


def middle_body(
    slot, info, y, gate, d_normed, v, bc, fr, enter_f, enter_r, kept_f, kept_r, dx, gain, spread_f, spread_r, sum_f, sum_r,
    normed, d_mixed, d_gate, back_f, back_r, leave_f, leave_r, d_outs, read_out, d_gain, d_skip, mixed_s, part_f, part_r, exp_f, exp_r,
):
    m, b = slot // 2, lax.rem(slot, 2)
    span = pl.ds(pl.multiple_of(b * BLOCK, BLOCK), BLOCK)
    forward, reverse = keeps(info, m)
    lane = iota((BLOCK, LANES), 1)
    acts = bc[m, span, :]
    outs = by_lane(swapped(acts), acts)
    outs_t = twice(jnp.transpose(outs).astype(BF16), 1)
    outs = twice(outs.astype(BF16), 1)
    grown = spread_operand(jnp.where(lane < 2 * HEADS, jnp.exp(fr[m, span, :]), 0.0))
    width = 2 * LANES
    chunks = INNER // width
    squares = jnp.zeros((BLOCK, 1), F32)
    cross = jnp.zeros((BLOCK, 1), F32)
    for chunk in range(chunks):
        cols = pl.ds(chunk * width, width)
        state_f, state_r = entering(m, b, cols, forward, reverse, enter_f, enter_r, kept_f, kept_r, dx)
        ef = dot(grown, spread_f[:, cols])
        er = dot(grown, spread_r[:, cols])
        carried_f = ef * dot(outs, doubled(state_f))
        carried_r = er * dot(outs, doubled(state_r))
        mixed = y[0, :, cols] + carried_f + carried_r
        exp_f[:, cols] = ef
        exp_r[:, cols] = er
        part_f[:, cols] = carried_f
        part_r[:, cols] = carried_r
        mixed_s[:, cols] = mixed
        g = gate[0, :, cols]
        gated = mixed * (g * sigmoid(g))
        squares = squares + jnp.sum(gated * gated, axis=1, keepdims=True)
        cross = cross + jnp.sum(gated * gain[0:1, cols] * d_normed[0, :, cols], axis=1, keepdims=True)
    scale = lax.rsqrt(squares * (1.0 / INNER) + EPSILON)
    pull = scale * scale * scale * (cross * (1.0 / INNER))
    d_o = jnp.zeros((BLOCK, LANES), F32)
    reads = jnp.zeros((BLOCK, LANES), F32)

    @pl.when((m == 0) & (b == 0))
    def _():
        d_gain[...] = jnp.zeros_like(d_gain)
        d_skip[...] = jnp.zeros_like(d_skip)

    @pl.when(b == 0)
    def _():
        for k in range(PARTS):
            leave_f[PARTS * m + k] = jnp.zeros(CARRY_SHAPE[1:], F32)
            leave_r[PARTS * m + k] = jnp.zeros(CARRY_SHAPE[1:], F32)

    for chunk in range(chunks):
        cols = pl.ds(chunk * width, width)
        g = gate[0, :, cols]
        sig = sigmoid(g)
        silu = g * sig
        mixed = mixed_s[:, cols]
        gated = mixed * silu
        dy = d_normed[0, :, cols]
        scaled = gated * scale
        normed[m, span, cols] = (scaled * gain[0:1, cols]).astype(BF16)
        d_gain[0:1, cols] += jnp.sum(dy * scaled, axis=0, keepdims=True)
        d_gated = scale * gain[0:1, cols] * dy - gated * pull
        dm = d_gated * silu
        d_gate[m, span, cols] = (d_gated * mixed * sig * (1.0 + g * (1.0 - sig))).astype(BF16)
        d_mixed[slot, :, cols] = dm.astype(BF16)
        d_skip[0:1, cols] += jnp.sum(dm * v[m, span, cols].astype(F32), axis=0, keepdims=True)
        state_f, state_r = entering(m, b, cols, forward, reverse, enter_f, enter_r, kept_f, kept_r, dx)
        grown_f = exp_f[:, cols] * dm
        grown_r = exp_r[:, cols] * dm
        local_f = fold(dot(outs_t, stacked(grown_f)))
        local_r = fold(dot(outs_t, stacked(grown_r)))
        back_f[0, 0, :, cols] = local_f
        back_r[0, 0, :, cols] = local_r
        weight_f = jnp.where(b == 0, forward[0], (forward[0] * forward[1]) * dx[m, 0:1, cols])
        weight_r = jnp.where(b == 0, (reverse[0] * reverse[1]) * dx[m, 3:4, cols], reverse[1])
        local_f = weight_f * local_f
        local_r = weight_r * local_r
        for k in range(PARTS):
            part = slice(k * STATE // PARTS, (k + 1) * STATE // PARTS)
            leave_f[PARTS * m + k, :, cols] += local_f[part]
            leave_r[PARTS * m + k, :, cols] += local_r[part]
        d_o = d_o + dot(spread_operand(grown_f), twice(stacked(state_f), 1), COLS)
        d_o = d_o + dot(spread_operand(grown_r), twice(stacked(state_r), 1), COLS)
        reads = reads + head_sums(dm * part_f[:, cols], sum_f[cols, :]) + head_sums(dm * part_r[:, cols], sum_r[cols, :])
    d_outs[slot] = jnp.where(lane < STATE, 0.0, d_o + swapped(d_o))
    read_out[slot] = reads


def intra_back_body(slot, v, d_mixed, bc, fr, frp, skip, d_outs, read_out, d_v, d_bc, sums, d_log, row_s, turn):
    m, b = slot // 2, lax.rem(slot, 2)
    span = pl.ds(pl.multiple_of(b * BLOCK, BLOCK), BLOCK)
    rows = iota((BLOCK, BLOCK), 0)
    columns = iota((BLOCK, BLOCK), 1)
    ahead = rows < columns
    acts = bc[m, span, :]
    low = columns < STATE
    turned = swapped(acts)
    outs = jnp.where(low, turned, 0.0)
    scores = jnp.where(rows == columns, 0.0, dot(acts, outs, COLS, HIGHEST))
    cum = jnp.transpose(fr[m, span, :])
    shifted = frp[m, span, :]
    d_scores = jnp.zeros((BLOCK, BLOCK), F32)
    gathered = jnp.zeros((BLOCK, LANES), F32)

    row_s[...] = jnp.zeros_like(row_s)
    for pair in range(PAIRS):
        cols = pl.ds(pair * LANES, LANES)
        value = v[m, span, cols]
        dm = d_mixed[slot, :, cols]
        products = dot(pair_stack(value), dm, COLS)
        mats = []
        for side in range(2):
            h = 2 * pair + side
            r = HEADS + h
            gap = jnp.where(ahead, cum[h : h + 1] - shifted[:, h : h + 1], cum[r : r + 1] - shifted[:, r : r + 1])
            weight = jnp.exp(gap)
            mats.append((weight * scores).astype(BF16))
            reach = products[side * BLOCK : (side + 1) * BLOCK] * weight
            d_scores = d_scores + reach
            both = reach * scores
            first = jnp.where(ahead, both, 0.0)
            second = both - first
            gathered = jnp.where(columns == h, jnp.sum(first, axis=1, keepdims=True), gathered)
            gathered = jnp.where(columns == r, jnp.sum(second, axis=1, keepdims=True), gathered)
            row_s[h : h + 1, :] = jnp.sum(first, axis=0, keepdims=True)
            row_s[r : r + 1, :] = jnp.sum(second, axis=0, keepdims=True)
        dmf = dm.astype(F32)
        d_v[0, :, cols] = dot(jnp.concatenate(mats, axis=1), pair_stack(dm)) + skip[0:1, cols] * dmf
        if pair % TURN_PAIRS == TURN_PAIRS - 1:
            turn(pair // TURN_PAIRS)
    d_scores = jnp.where(rows == columns, 0.0, d_scores)
    ins = jnp.where(low, 0.0, turned)
    d_bc[0] = dot(d_scores, outs, precision=HIGHEST) + dot(jnp.transpose(d_scores), ins, precision=HIGHEST) + d_outs[slot]
    sums[0] = gathered
    d_log[0] = jnp.transpose(row_s[...]) - gathered + read_out[slot]


def shard_steps(columns, normed, d_branch_t, hidden_t, d_gate, outs, buffers):
    put, gots, cross_puts, cross_gots, mate_sems, cross_sems = buffers
    part = lax.axis_index("fsdp")
    core, column = lax.rem(part, 2), part // 2
    mate = part + 1 - 2 * core
    rows = put.shape[1]

    def column_at(d):
        return lax.rem(column + d + columns, columns)

    def remote(source, target, sems, k, device):
        return pltpu.make_async_remote_copy(
            src_ref=source, dst_ref=target, send_sem=sems.at[0, k], recv_sem=sems.at[1, k], device_id={"fsdp": device}
        )

    def to_mate(which, x):
        return remote(put.at[x], gots[which].at[x], mate_sems, which * columns + x, mate)

    def across(which, d):
        target = 2 * column_at(d) + core
        return remote(cross_puts[which].at[d - 1], cross_gots[which].at[d - 1], cross_sems, which * columns + d, target)

    def piece(which, owner, h):
        half = rows // 2
        if which == 0:
            group = 1 if rows % LANES == 0 else 2
            at = pl.ds(pl.multiple_of((owner // group) * (group * rows), LANES), group * rows)
            total = sum(
                dot(d_branch_t[h * rows : (h + 1) * rows, m * TOK_DEV : (m + 1) * TOK_DEV], normed[m, :, at]) for m in range(MB)
            )
            return total if group == 1 else jnp.where(lax.rem(owner, 2) == 0, total[:, :rows], total[:, rows:])
        at = pl.ds(pl.multiple_of(owner * half, 16), half)
        return sum(
            dot(hidden_t[at, m * TOK_DEV : (m + 1) * TOK_DEV], d_gate[m, :, h * D : (h + 1) * D]) for m in range(MB)
        )

    def view(which, h):
        return (slice(None), slice(h * rows, (h + 1) * rows)) if which == 0 else (slice(h * rows // 2, (h + 1) * rows // 2),)

    def count(which):
        return D // rows if which == 0 else 2

    def greet(barrier):
        pl.semaphore_signal(barrier, inc=1, device_id={"fsdp": mate})
        for d in range(1, columns):
            pl.semaphore_signal(barrier, inc=1, device_id={"fsdp": 2 * column_at(d) + core})
        return columns

    def foreign(which):
        for x in range(columns):
            if which == 1:
                to_mate(0, x).wait_send()
            for h in range(count(which)):
                put[(x,) + view(which, h)] = piece(which, 2 * x + 1 - core, h).astype(BF16)
            to_mate(which, x).start()

    def local(which):
        for x in range(columns):
            to_mate(which, x).wait_recv()
        for d in list(range(1, columns)) + [0]:
            x = column_at(d)
            for h in range(count(which)):
                at = view(which, h)
                value = piece(which, 2 * x + core, h) + gots[which][(x,) + at].astype(F32)
                if d == 0:
                    outs[which][at] = value
                else:
                    cross_puts[which][(d - 1,) + at] = value.astype(BF16)
            if d > 0:
                across(which, d).start()

    def close():
        for which in range(2):
            for d in range(1, columns):
                across(which, d).wait()
                outs[which][...] += cross_gots[which][d - 1].astype(F32)
        for x in range(columns):
            to_mate(1, x).wait_send()

    return greet, foreign, local, close


def shard_buffers(shards):
    columns, shape = shards // 2, (INNER // shards, D)
    low, few = pltpu.VMEM((columns,) + shape, BF16), pltpu.VMEM((columns - 1,) + shape, BF16)
    return [low] * 3 + [few] * 4 + [pltpu.SemaphoreType.DMA((2, 2 * columns))] * 2


def gather_steps(columns, w_out, w_back, w_back_out, cross_sems, mate_sems, out_sems):
    part = lax.axis_index("fsdp")
    core, column = lax.rem(part, 2), part // 2
    mate = part + 1 - 2 * core
    rows = w_out.shape[0]

    def column_at(d):
        return lax.rem(column + d + columns, columns)

    def copy(sems, k, owner, device):
        at = w_back.at[pl.ds(pl.multiple_of(owner * rows, LANES // 2), rows)]
        return pltpu.make_async_remote_copy(
            src_ref=at, dst_ref=at, send_sem=sems.at[0, k], recv_sem=sems.at[1, k], device_id={"fsdp": device}
        )

    def across(d, theirs):
        return copy(cross_sems, d, 2 * column_at(-d) + core if theirs else part, 2 * column_at(d) + core)

    def to_mate(d, theirs):
        return copy(mate_sems, d, 2 * column_at(-d) + (1 - core if theirs else core), mate)

    def keep():
        return pltpu.make_async_copy(w_back, w_back_out, out_sems.at[0])

    def start():
        here = w_back.at[pl.ds(pl.multiple_of(part * rows, LANES // 2), rows)]
        own = pltpu.make_async_copy(w_out, here, out_sems.at[1])
        own.start()
        own.wait()
        for d in range(1, columns):
            across(d, False).start()
        to_mate(0, False).start()

    def forward():
        for d in range(1, columns):
            across(d, True).wait_recv()
            to_mate(d, False).start()

    def arrive():
        for d in range(columns):
            to_mate(d, True).wait_recv()
        keep().start()

    def close():
        keep().wait()
        for d in range(columns):
            to_mate(d, False).wait_send()
            if d > 0:
                across(d, False).wait_send()

    return start, forward, arrive, close


def mixer_kernel(
    levels, columns, info, vals, bc_in, dt, gate, taps, rates, spread_f, spread_r, sum_f, sum_r, skip, gain, w_out, d_branch_in, d_branch_t_in, hidden_t_in,
    v_out, bc_out, fr_out, frp_out, kept_f_out, kept_r_out, dx_out, normed_out, d_gate_out,
    back_f, back_r, d_gain, d_skip, d_v, d_bc, sums, d_log, first_out, second_out, enter_f, enter_r, after_f, after_r, w_back_out,
    v, bc, fr, frp, kept_f, kept_r, dx, normed, d_gate, d_branch, d_branch_t, hidden_t, load_sems, front_sems, middle_sems, y, d_normed, mixed_s, part_f, part_r, exp_f, exp_r, row_s, d_mixed, d_outs, read_out, w_back, w_cross, w_mate, w_kept,
    put, got_1, got_2, cross_put_1, cross_put_2, cross_got_1, cross_got_2, mate_sems, cross_sems,
    gains_other, gain_sems, tot_f, tot_r, leave_f, leave_r, *buffers,
):
    s = pl.program_id(0)
    half = len(buffers) // 2
    greet_dp, begin, send_gains, gains_here, send, run, end, total = carry_steps(
        levels, 4, 5, dx, gains_other, gain_sems, tot_f, tot_r, enter_f, enter_r, buffers[:half]
    )
    _, begin_back, _, _, send_back, run_back, end_back, _ = carry_steps(
        levels, 5, 4, dx, gains_other, gain_sems, leave_r, leave_f, after_r, after_f, buffers[half:]
    )
    greet, foreign, local, close = shard_steps(
        columns, normed, d_branch_t, hidden_t, d_gate, (first_out, second_out),
        (put, (got_1, got_2), (cross_put_1, cross_put_2), (cross_got_1, cross_got_2), mate_sems, cross_sems),
    )
    w_start, w_forward, w_arrive, w_close = gather_steps(columns, w_out, w_back, w_back_out, w_cross, w_mate, w_kept)
    entered_f, entered_r = buffers[0], buffers[1]
    fronts = ((v, v_out), (bc, bc_out), (fr, fr_out), (frp, frp_out), (kept_f, kept_f_out), (kept_r, kept_r_out), (dx, dx_out))

    def front_copy(i, m):
        return pltpu.make_async_copy(fronts[i][0].at[m], fronts[i][1].at[m], front_sems.at[i, m])

    def middle_copy(i, slot):
        ref, out = ((normed, normed_out), (d_gate, d_gate_out))[i]
        m, span = slot // 2, pl.ds(pl.multiple_of(lax.rem(slot, 2) * BLOCK, BLOCK), BLOCK)
        return pltpu.make_async_copy(ref.at[m, span], out.at[m, span], middle_sems.at[i, slot])

    def load(i):
        return pltpu.make_async_copy(*((d_branch_in, d_branch), (hidden_t_in, hidden_t), (d_branch_t_in, d_branch_t))[i], load_sems.at[i])

    middle, back = MB, 3 * MB
    window = 5

    @pl.when(s == 0)
    def _():
        barrier = pltpu.get_barrier_semaphore()
        pl.semaphore_wait(barrier, greet(barrier) + greet_dp(barrier))
        for i in range(3):
            load(i).start()
        begin()
        begin_back()
        w_start()

    @pl.when(s < middle)
    def _():
        front_body(s, info, vals, bc_in, dt, taps, rates, spread_f, spread_r, v, bc, fr, frp, tot_f, tot_r, kept_f, kept_r, dx)
        send_gains(s)
        for i in range(len(fronts)):
            front_copy(i, s).start()

        for m, (low, high) in enumerate(((0, 2), (2, 4), (4, window))):

            @pl.when(s == m)
            def _():
                send(low, high)

    done = 0
    for slot in range(2 * MB):
        need = min(PARTS + LAG * (levels - 1) + slot * (PARTS // 2), total)

        @pl.when(s == middle + slot)
        def _():
            if slot == 0:
                for m in range(MB):
                    gains_here(m)
                w_forward()
            run(done, need, window)
            if slot == 0:
                for i in range(3):
                    load(i).wait()
                w_arrive()

        done = need

    @pl.when((s >= middle) & (s < back))
    def _():
        slot = s - middle
        m, b = slot // 2, lax.rem(slot, 2)
        intra_body(m, b, v, bc, fr, frp, skip, y)
        d_normed[0] = dot(d_branch[m, pl.ds(pl.multiple_of(b * BLOCK, BLOCK), BLOCK), :], w_back[...], COLS)
        middle_body(
            slot, info, y, gate, d_normed, v, bc, fr, entered_f, entered_r, kept_f, kept_r, dx, gain, spread_f, spread_r, sum_f, sum_r,
            normed, d_mixed, d_gate, back_f, back_r, leave_f, leave_r, d_outs, read_out, d_gain, d_skip, mixed_s, part_f, part_r, exp_f, exp_r,
        )

        middle_copy(0, slot).start()
        middle_copy(1, slot).start()

        @pl.when(b == 1)
        def _():
            send_back(PARTS * m, PARTS * (m + 1))

    for k, step in enumerate((foreign, local)):
        for which in range(2):

            @pl.when(s == back + 2 * which + k)
            def _():
                step(which)

    @pl.when(s >= back)
    def _():
        slot = s - back
        each = -(-total // (2 * MB * TURNS))

        def turn(k):
            at = slot * TURNS + k
            run_back(at * each, (at + 1) * each, 0)

        intra_back_body(slot, v, d_mixed, bc, fr, frp, skip, d_outs, read_out, d_v, d_bc, sums, d_log, row_s, turn)

    @pl.when(s == 5 * MB - 1)
    def _():
        close()
        w_close()
        for m in range(MB):
            for i in range(len(fronts)):
                front_copy(i, m).wait()

        @pl.loop(0, 2 * MB)
        def _(slot):
            middle_copy(0, slot).wait()
            middle_copy(1, slot).wait()

        end(True)
        end_back(False)


def final_kernel(
    levels, info, vals, bc_in, dt, taps, rates, v, bc, fr, frp, enter_f, enter_r, kept_f, kept_r, dx, after_f, after_r, back_f, back_r,
    d_v, d_bc, sums, d_log, spread_f, spread_r, sum_f, sum_r, first_in, second_in,
    late, before, last, d_taps, d_small, first_out, second_out, d_acts, *buffers,
):
    m = pl.program_id(0)
    forward, reverse = keeps(info, m)
    if levels:
        greet, steps = sum_steps(levels, (buffers[:6], buffers[6:12]), *buffers[12:])

    def beside(at, *todo):
        if levels:

            @pl.when(m == at)
            def _():
                for stage, i in todo:
                    steps[stage](i)

    if levels:

        @pl.when(m == 0)
        def _():
            barrier = pltpu.get_barrier_semaphore()
            pl.semaphore_wait(barrier, greet(barrier))
            buffers[0][...] = first_in[...]
            buffers[6][...] = second_in[...]

    beside(0, (0, 0))
    lane = iota((BLOCK, LANES), 1)
    row = iota((BLOCK, LANES), 0)
    rows = iota((BLOCK, BLOCK), 0)
    columns = iota((BLOCK, BLOCK), 1)
    lower = (rows >= columns).astype(F32)
    upper = (rows <= columns).astype(F32)
    width = 2 * LANES

    @pl.when(m == 0)
    def _():
        d_taps[...] = jnp.zeros_like(d_taps)
        d_small[...] = jnp.zeros_like(d_small)

    for b in range(2):
        span = pl.ds(b * BLOCK, BLOCK)
        summed = fr[0, span, :]
        end = jnp.where(lane[:1] < HEADS, summed[BLOCK - 1 :], summed[:1])
        tail = spread_operand(jnp.where(lane < 2 * HEADS, jnp.exp(end - frp[0, span, :]), 0.0))
        acts = bc[0, span, :]
        ins = twice(by_lane(acts, swapped(acts)).astype(BF16), 1)
        d_in = jnp.zeros((BLOCK, LANES), F32)
        used = jnp.zeros((BLOCK, LANES), F32)
        decays = jnp.zeros((8, LANES), F32)
        for chunk in range(INNER // width):
            cols = pl.ds(chunk * width, width)
            grad_f = jnp.concatenate([after_f[k, :, cols] for k in range(PARTS)], axis=0)
            grad_r = jnp.concatenate([after_r[k, :, cols] for k in range(PARTS)], axis=0)
            if b == 0:
                grad_f = forward[1] * (back_f[0, 1, :, cols] + dx[0, 1:2, cols] * grad_f)
            else:
                grad_r = reverse[0] * (back_r[0, 0, :, cols] + dx[0, 2:3, cols] * grad_r)
            state_f, state_r = entering(0, b, cols, forward, reverse, enter_f, enter_r, kept_f, kept_r, dx)
            tail_f = dot(tail, spread_f[:, cols])
            tail_r = dot(tail, spread_r[:, cols])
            value = v[0, span, cols].astype(F32)
            pulled_f = tail_f * dot(ins, doubled(grad_f))
            pulled_r = tail_r * dot(ins, doubled(grad_r))
            d_acts[span, cols] = d_v[0, span, cols] + pulled_f + pulled_r
            d_in = d_in + dot(spread_operand(tail_f * value), twice(stacked(grad_f), 1), COLS)
            d_in = d_in + dot(spread_operand(tail_r * value), twice(stacked(grad_r), 1), COLS)
            used = used + head_sums(pulled_f * value, sum_f[cols, :]) + head_sums(pulled_r * value, sum_r[cols, :])
            meet_f = jnp.sum(grad_f * state_f, axis=0, keepdims=True) * dx[0, b : b + 1, cols]
            meet_r = jnp.sum(grad_r * state_r, axis=0, keepdims=True) * dx[0, 2 + b : 3 + b, cols]
            zero = jnp.zeros((7, width), F32)
            decays = decays + head_sums(jnp.concatenate([meet_f, zero], axis=0), sum_f[cols, :])
            decays = decays + head_sums(jnp.concatenate([meet_r, zero], axis=0), sum_r[cols, :])
        d_acts[span, pl.ds(INNER, LANES)] = d_bc[0, span, :] + jnp.where(lane < STATE, d_in + swapped(d_in), 0.0)
        direct = sums[0, span, :] + used
        edge = decays[0:1] + jnp.sum(used, axis=0, keepdims=True)
        at_end = ((lane < HEADS) & (row == BLOCK - 1)) | ((lane >= HEADS) & (row == 0))
        grad = d_log[0, span, :] - used + jnp.where(at_end, edge, 0.0)
        grad = jnp.where(lane < HEADS, dot(upper, grad, precision=HIGHEST), dot(lower, grad, precision=HIGHEST))
        x = dt[0, span, :] + rates[0:1, :]
        step = softplus(x)
        sig = sigmoid(x)
        ratio = jnp.where(x < -17.0, 1.0, sig / step)
        d_x = direct * ratio - rates[1:2, :] * grad * sig
        d_x = jnp.where(lane < 2 * HEADS, d_x, 0.0)
        late[0, span, pl.ds(INNER + LANES, LANES)] = d_x.astype(BF16)
        d_small[0:1, :] += jnp.sum(d_x, axis=0, keepdims=True)
        d_small[1:2, :] -= rates[1:2, :] * jnp.sum(step * grad, axis=0, keepdims=True)
        if b == 0:
            beside(1, (1, 1))
            beside(2, (3, 0))
        else:
            beside(0, (0, 1))
            beside(1, (2, 0))
            beside(2, (3, 1))
    valid, masks = row_masks(info, m, (TOK_DEV, LANES))
    edge = jnp.zeros((HALO, LANES), F32)
    for chunk in range(PAIRS + 1):
        cols = pl.ds(chunk * LANES, LANES)
        source, own = (vals, cols) if chunk < PAIRS else (bc_in, pl.ds(0, LANES))
        windows = conv_windows(source, own)
        value = conv_value(windows, masks, taps, cols)
        sig = sigmoid(value)
        grad = valid * d_acts[:, cols] * (sig * (1.0 + value * (1.0 - sig)))
        total = jnp.zeros((HALO + TOK_DEV, LANES), F32)
        for k in range(CONV):
            masked = grad if k == 0 else grad * masks[k]
            d_taps[k : k + 1, cols] += jnp.sum(masked * windows[k], axis=0, keepdims=True)
            padded = jnp.concatenate([edge, masked, edge], axis=0)
            total = total + taps[k : k + 1, cols] * padded[k : k + HALO + TOK_DEV]
        d_taps[CONV : CONV + 1, cols] += jnp.sum(grad, axis=0, keepdims=True)
        before[0, :, cols] = total[:HALO]
        last[0, :, cols] = total[TOK_DEV:]
        late[0, :, cols] = total[HALO:].astype(BF16)
    beside(0, (1, 0))
    beside(1, (2, 1))
    beside(2, (4, 0), (4, 1), (5, 0), (5, 1))
    if levels:

        @pl.when(m == MB - 1)
        def _():
            first_out[...] = buffers[5][...].astype(F32)
            second_out[...] = buffers[11][...].astype(F32)


def once(shape):
    return pl.BlockSpec(shape, lambda *grid: (0,) * len(shape), pipeline_mode=pl.Buffered(1))


def per_micro(shape, column=0):
    return pl.BlockSpec((1,) + shape, lambda m, *rest: (m,) + (0,) * (len(shape) - 1) + (column,))


def per_block(width, column=0):
    return pl.BlockSpec((1, BLOCK, width), lambda m, b: (m, b, column))


def struct(*shape, dtype=F32):
    return jax.ShapeDtypeStruct(shape, dtype)


def call(kernel, grid, in_specs, out_specs, out_shape, scratch=(), flops=0, moved=0, identity=None):
    return pl.pallas_call(
        kernel,
        grid=grid,
        in_specs=in_specs,
        out_specs=out_specs,
        out_shape=out_shape,
        scratch_shapes=list(scratch),
        compiler_params=pltpu.CompilerParams(
            vmem_limit_bytes=VMEM_LIMIT, collective_id=identity, has_side_effects=identity is not None
        ),
        cost_estimate=pl.CostEstimate(flops=flops, bytes_accessed=moved, transcendentals=0),
    )


def shift(value, distance):
    count = lax.axis_size("dp")
    route = [(i, i + distance) for i in range(count) if 0 <= i + distance < count]
    return lax.ppermute(value, "dp", route)


def carry_steps(levels, up_row, down_row, gains, gains_other, gain_sems, up_in, down_in, up_out, down_out, buffers):
    up_other, down_other, up_chain, down_chain, up_sems, down_sems, up_link, down_link, out_sems = buffers
    me = lax.axis_index("dp")
    side = lax.rem(me, 2)
    level = me // 2
    partner = me + 1 - 2 * side
    above, below = me + 2, me - 2
    has_above, has_below = level < levels - 1, level > 0
    first = side == 0

    def remote(source, target, sems, k, device):
        return pltpu.make_async_remote_copy(
            src_ref=source, dst_ref=target, send_sem=sems.at[0, k], recv_sem=sems.at[1, k], device_id={"dp": device}
        )

    def swap_gains(m):
        return remote(gains.at[m], gains_other.at[m], gain_sems, m, partner)

    def swap_up(k):
        return remote(up_in.at[k], up_other.at[k], up_sems, k, partner)

    def swap_down(k):
        return remote(down_in.at[k], down_other.at[k], down_sems, k, partner)

    def climb(k):
        return remote(up_in.at[k], up_chain.at[k], up_link, k, above)

    def descend(k):
        return remote(down_in.at[k], down_chain.at[k], down_link, k, below)

    def keep_up(k):
        return pltpu.make_async_copy(up_other.at[k], up_out.at[k], out_sems.at[0, k])

    def keep_down(k):
        return pltpu.make_async_copy(down_other.at[k], down_out.at[k], out_sems.at[1, k])

    def greet(barrier):
        pl.semaphore_signal(barrier, inc=1, device_id={"dp": partner})

        @pl.when(has_above)
        def _():
            pl.semaphore_signal(barrier, inc=1, device_id={"dp": above})

        @pl.when(has_below)
        def _():
            pl.semaphore_signal(barrier, inc=1, device_id={"dp": below})

        return 1 + has_above.astype(jnp.int32) + has_below.astype(jnp.int32)

    def begin():
        @pl.when(level == 0)
        def _():
            up_chain[...] = jnp.zeros_like(up_chain)

        @pl.when(level == levels - 1)
        def _():
            down_chain[...] = jnp.zeros_like(down_chain)

    total = CHUNKS + LAG * (levels - 1)

    def places(step):
        return step - LAG * level, step - LAG * (levels - 1 - level)

    def send(low, high):
        @pl.loop(low, high)
        def _(k):
            @pl.when(k < CHUNKS)
            def _():
                swap_up(k).start()
                swap_down(k).start()

    def advance(step):
        up, down = places(step)

        @pl.when((up >= 0) & (up < CHUNKS))
        def _():
            swap_up(up).wait_recv()

            @pl.when(has_below)
            def _():
                climb(up).wait_recv()

            m = up // PARTS
            own, other = gains[m, up_row : up_row + 1], gains_other[m, up_row : up_row + 1]
            near, far = jnp.where(first, own, other), jnp.where(first, other, own)
            mine, theirs = up_in[up], up_other[up]
            before = up_chain[up]
            middle = jnp.where(first, mine, theirs) + near * before
            up_other[up] = jnp.where(first, before, middle)
            keep_up(up).start()

            @pl.when(has_above)
            def _():
                swap_up(up).wait_send()
                up_in[up] = jnp.where(first, theirs, mine) + far * middle
                climb(up).start()

        @pl.when((down >= 0) & (down < CHUNKS))
        def _():
            swap_down(down).wait_recv()

            @pl.when(has_above)
            def _():
                descend(down).wait_recv()

            m = down // PARTS
            own, other = gains[m, down_row : down_row + 1], gains_other[m, down_row : down_row + 1]
            near, far = jnp.where(first, other, own), jnp.where(first, own, other)
            mine, theirs = down_in[down], down_other[down]
            before = down_chain[down]
            middle = jnp.where(first, theirs, mine) + near * before
            down_other[down] = jnp.where(first, middle, before)
            keep_down(down).start()

            @pl.when(has_below)
            def _():
                swap_down(down).wait_send()
                down_in[down] = jnp.where(first, mine, theirs) + far * middle
                descend(down).start()

    def run(low, high, window):
        @pl.loop(low, high)
        def _(step):
            advance(step)
            if window:
                send(step + window, step + window + 1)

    def gains_here(m):
        swap_gains(m).wait_recv()

    def end(last):
        if last:

            @pl.loop(0, MB)
            def _(m):
                swap_gains(m).wait_send()

        @pl.loop(0, CHUNKS)
        def _(k):
            keep_up(k).wait()
            keep_down(k).wait()

            @pl.when(has_above)
            def _():
                climb(k).wait_send()

            @pl.when(jnp.logical_not(has_above))
            def _():
                swap_up(k).wait_send()

            @pl.when(has_below)
            def _():
                descend(k).wait_send()

            @pl.when(jnp.logical_not(has_below))
            def _():
                swap_down(k).wait_send()

    return greet, begin, lambda m: swap_gains(m).start(), gains_here, send, run, end, total


CARRY_SHAPE = (CHUNKS, STATE // PARTS, INNER)


def carry_buffers():
    return [pltpu.VMEM(CARRY_SHAPE, F32)] * 4 + [pltpu.SemaphoreType.DMA((2, CHUNKS))] * 5


def sum_steps(levels, parts, side_sems, level_sems):
    me = lax.axis_index("dp")
    side, level = lax.rem(me, 2), me // 2
    partner = me + 1 - 2 * side

    def level_at(d):
        return lax.rem(level + d + levels, levels)

    def device(d):
        return {"dp": 2 * level_at(d) + side}

    def remote(source, target, sems, k, where):
        return pltpu.make_async_remote_copy(
            src_ref=source, dst_ref=target, send_sem=sems.at[0, k], recv_sem=sems.at[1, k], device_id=where
        )

    def greet(barrier):
        pl.semaphore_signal(barrier, inc=1, device_id={"dp": partner})
        for d in range(1, levels):
            pl.semaphore_signal(barrier, inc=1, device_id=device(d))
        return levels

    def halve(i):
        return remote(parts[i][1], parts[i][2], side_sems, 2 * i, {"dp": partner})

    def join(i, theirs):
        full = parts[i][5]
        return remote(full.at[side], full.at[1 - side if theirs else side], side_sems, 2 * i + 1, {"dp": partner})

    def scatter(i, d, theirs):
        put, got = parts[i][3:5]
        return remote(put.at[level_at(d)], got.at[level_at(-d) if theirs else level], level_sems, 2 * i * levels + d, device(d))

    def gather(i, d, theirs):
        full = parts[i][5]
        target = full.at[side, level_at(-d) if theirs else level]
        return remote(full.at[side, level], target, level_sems, (2 * i + 1) * levels + d, device(d))

    def step_0(i):
        total, put = parts[i][:2]
        put[...] = total[1 - side].astype(BF16)
        halve(i).start()

    def step_1(i):
        total, _, got, put = parts[i][:4]
        halve(i).wait_recv()
        total[side] = total[side] + got[...].astype(F32)
        for d in range(1, levels):
            target = level_at(d)
            put[target] = total[side, target].astype(BF16)
            scatter(i, d, False).start()

    def step_2(i):
        total, _, _, _, got, full = parts[i]
        value = total[side, level]
        for d in range(1, levels):
            scatter(i, d, True).wait_recv()
            value = value + got[level_at(-d)].astype(F32)
        full[side, level] = value.astype(BF16)
        for d in range(1, levels):
            gather(i, d, False).start()

    def step_3(i):
        for d in range(1, levels):
            gather(i, d, True).wait_recv()
        join(i, False).start()

    def step_4(i):
        join(i, True).wait_recv()

    def close(i):
        halve(i).wait_send()
        join(i, False).wait_send()
        for d in range(1, levels):
            scatter(i, d, False).wait_send()
            gather(i, d, False).wait_send()

    return greet, (step_0, step_1, step_2, step_3, step_4, close)


def sum_buffers(levels, piece, width):
    low = pltpu.VMEM((levels, piece, width), BF16)
    both = (2, levels, piece, width)
    return [pltpu.VMEM(both, F32), low, low, low, low, pltpu.VMEM(both, BF16)]


def sum_semaphores(levels, count):
    return [pltpu.SemaphoreType.DMA((2, 2 * count)), pltpu.SemaphoreType.DMA((2, 2 * count * levels))]


PIECES = ((0, 512), (512, 512), (1024, 384), (1408, 384))


def total_kernel(
    levels, columns, info, hidden_t, late, d_gate, normed, w_all, w_back, x_in, cot_in, gain_in,
    gate_in, taps_in, scale_in, skip_in, small_in, selector,
    layer_out, tokens_out, inner_out, state_out, step_out, norm_out, taps_out, bias_out, steps_out, decay_out, skip_out, scale_out,
    third_in, norm_sum, mate_got, cross_put, cross_got, short_sum, short_got, short_sems, mate_sems, cross_sems, side_sems, level_sems, *buffers,
):
    me, part = lax.axis_index("dp"), lax.axis_index("fsdp")
    side, level = lax.rem(me, 2), me // 2
    core, column = lax.rem(part, 2), part // 2
    mate = part + 1 - 2 * core
    count = len(PIECES)
    parts = [buffers[6 * i : 6 * i + 6] for i in range(count)]
    greet, steps = sum_steps(levels, parts, side_sems, level_sems)

    def column_at(d):
        return lax.rem(column + d + columns, columns)

    def remote(source, target, sems, k, where):
        return pltpu.make_async_remote_copy(
            src_ref=source, dst_ref=target, send_sem=sems.at[0, k], recv_sem=sems.at[1, k], device_id=where
        )

    barrier = pltpu.get_barrier_semaphore()
    pl.semaphore_signal(barrier, inc=1, device_id={"fsdp": mate})
    for d in range(1, columns):
        pl.semaphore_signal(barrier, inc=1, device_id={"fsdp": 2 * column_at(d) + core})
    pl.semaphore_wait(barrier, greet(barrier) + columns)

    def to_mate(i, x):
        at = pl.ds(*PIECES[i])
        return remote(third_in.at[2 * x + 1 - core, :, at], mate_got.at[x, :, at], mate_sems, i * columns + x, {"fsdp": mate})

    def across(i, d, theirs):
        at = pl.ds(*PIECES[i])
        where = {"fsdp": 2 * column_at(d) + core}
        slot = column_at(-d) if theirs else column
        return remote(cross_put.at[column_at(d), :, at], cross_got.at[slot, :, at], cross_sems, i * columns + d, where)

    block_rows = third_in.shape[1]

    def third(owner, i):
        at = pl.ds(pl.multiple_of(owner * block_rows, 16), block_rows)
        cols = pl.ds(*PIECES[i])
        third_in[owner, :, cols] = dot(hidden_t[at, :], late[:, cols])

    def d_hidden_block(k):
        m, b = divmod(k, 2)
        at = slice(k * BLOCK, (k + 1) * BLOCK)
        grad = dot(d_gate[at], w_all[:, :INNER], COLS) + dot(late[at], w_all[:, INNER:], COLS)
        rows = x_in[at].astype(F32)
        scale = lax.rsqrt(jnp.mean(rows * rows, axis=1, keepdims=True) + EPSILON)
        norm_sum[...] += jnp.sum(grad * rows * scale, axis=0, keepdims=True)
        pulled = grad * gain_in[...]
        pull = (scale * scale * scale) * jnp.mean(rows * pulled, axis=1, keepdims=True)
        valid = row_masks(info, m, (BLOCK, D), b * BLOCK)[0]
        tokens_out[at] = scale * pulled - rows * pull + valid * cot_in[at].astype(F32)

    def layer_block(k):
        m, b = divmod(k, 2)
        at = slice(k * BLOCK, (k + 1) * BLOCK)
        branch = dot(normed[at], w_back[...])
        valid = row_masks(info, m, (BLOCK, D), b * BLOCK)[0]
        layer_out[at] = jnp.where(valid > 0.0, x_in[at].astype(F32) + branch, 0.0).astype(BF16)

    norm_sum[...] = jnp.zeros_like(norm_sum)
    for i in range(count):
        for x in range(columns):
            third(2 * x + 1 - core, i)
            to_mate(i, x).start()
    for i in range(count):
        for x in range(columns):
            third(2 * x + core, i)

    def cross(i):
        at = pl.ds(*PIECES[i])
        for x in range(columns):
            to_mate(i, x).wait_recv()
        for d in range(1, columns):
            x = column_at(d)
            cross_put[x, :, at] = (third_in[2 * x + core, :, at] + mate_got[x, :, at]).astype(BF16)
            across(i, d, False).start()

    cross(0)
    cross(1)
    for k in range(2 * MB - 2):
        d_hidden_block(k)

    lane = iota((8, LANES), 1)
    summed = jnp.where(lane < HEADS, head_sums(skip_in[...], selector[...]), 0.0)
    folded = small_in[...] + pltpu.roll(small_in[...], LANES - HEADS, axis=1)
    short_sum[0, 0:8, :] = taps_in[...]
    short_sum[0, 8:16, :] = jnp.zeros((8, CONV_COLS), F32)
    short_sum[0, 5:6, :INNER] = scale_in[0:1]
    short_sum[0, 8:9, :LANES] = small_in[0:1]
    short_sum[0, 9:10, :LANES] = folded[1:2]
    short_sum[0, 10:11, :LANES] = summed[0:1]
    routes = [{"fsdp": mate}, {"dp": me + 1 - 2 * side}]
    stride = 1
    while stride < columns:
        routes.append({"fsdp": part + 2 * stride - 4 * stride * lax.rem(column // stride, 2)})
        stride *= 2
    stride = 1
    while stride < levels:
        routes.append({"dp": me + 2 * stride - 4 * stride * lax.rem(level // stride, 2)})
        stride *= 2

    def short(k):
        return remote(short_sum.at[k], short_got.at[k], short_sems, k, routes[k])

    def short_step(k):
        if k > 0:
            short(k - 1).wait_recv()
            short_sum[k] = short_sum[k - 1] + short_got[k - 1]
        if k < len(routes):
            short(k).start()

    rows = parts[0][0].shape[2]

    def arrive(i):
        at = pl.ds(*PIECES[i])
        for d in range(1, columns):
            across(i, d, True).wait_recv()
        for x in range(2):
            for j in range(levels):
                here = pl.ds((x * levels + j) * rows, rows)
                value = third_in[part, here, at] + mate_got[column, here, at]
                for d in range(1, columns):
                    value = value + cross_got[column_at(-d), here, at].astype(F32)
                parts[i][0][x, j] = value
        steps[0](i)

    last = len(routes)
    for wave in range(count + 4):
        for stage in range(4, 0, -1):
            i = wave - stage
            if 0 <= i < count:
                steps[stage](i)
        if wave < count:
            arrive(wave)
        if wave + 2 < count:
            cross(wave + 2)
        if wave < 2:
            d_hidden_block(2 * MB - 2 + wave)
        elif wave < 2 + 2 * MB:
            layer_block(wave - 2)
        if wave == 1:
            short_sum[0, 6:7, :D] = norm_sum[...]
        if 1 <= wave <= last + 1:
            short_step(wave - 1)
    for k in range(count + 3, last + 1):
        short_step(k)

    result = short_sum.at[last]
    for f in range(2 * columns):

        @pl.when(part == f)
        def _():
            def own(row, rows, width, ref):
                size = width // (2 * columns)
                ref[...] = result[row : row + rows, f * size : (f + 1) * size]

            own(0, CONV, CONV_COLS, taps_out)
            own(4, 1, CONV_COLS, bias_out)
            own(5, 1, INNER, scale_out)
            own(6, 1, D, norm_out)
            own(8, 1, 2 * HEADS, steps_out)
            own(9, 1, HEADS, decay_out)
            own(10, 1, HEADS, skip_out)

    half = gate_in.shape[0] // 2
    for h in range(2):
        inner_out[:, h * D : (h + 1) * D] = gate_in[h * half : (h + 1) * half]
    for i in range(count):
        start, width = PIECES[i]
        for x in range(2):
            for j in range(levels):
                here = pl.ds((x * levels + j) * rows, rows)
                value = parts[i][5][x, j].astype(F32)
                inside = min(width, INNER - start)
                inner_out[here, INNER + start : INNER + start + inside] = value[:, :inside]
                if inside < width:
                    state_out[here, :] = value[:, inside : inside + LANES]
                    step_out[here, :] = value[:, inside + LANES : inside + LANES + 2 * HEADS]
    for i in range(count):
        steps[5](i)
        for x in range(columns):
            to_mate(i, x).wait_send()
        for d in range(1, columns):
            across(i, d, False).wait_send()
    for k in range(last):
        short(k).wait_send()


def total_fits(levels, shards, dp_count):
    rows = D // shards
    return dp_count == 2 * levels and shards % 2 == 0 and rows % (16 * levels) == 0 and 24 % shards == 0


def totals(operands, identity):
    dp_count, shards = lax.axis_size("dp"), lax.axis_size("fsdp")
    levels, columns = dp_count // 2, shards // 2
    rows = D // shards
    small = rows // levels // 2
    steps = (dp_count * shards).bit_length() - 1
    count = len(PIECES)

    def low(*shape):
        return pltpu.VMEM(shape, BF16)

    def full(*shape):
        return pltpu.VMEM(shape, F32)

    outs = pl.pallas_call(
        partial(total_kernel, levels, columns),
        in_specs=[SCALARS] + [pl.BlockSpec(memory_space=pltpu.VMEM)] * 15,
        out_specs=[pl.BlockSpec(memory_space=pltpu.VMEM)] * 12,
        out_shape=[struct(MB * TOK_DEV, D, dtype=BF16), struct(MB * TOK_DEV, D)]
        + [struct(rows, 2 * INNER), struct(rows, 2 * STATE), struct(rows, 2 * HEADS)]
        + [struct(1, D // shards), struct(CONV, CONV_COLS // shards), struct(1, CONV_COLS // shards)]
        + [struct(1, width // shards) for width in (2 * HEADS, HEADS, HEADS, INNER)],
        scratch_shapes=[full(shards, rows, LATE), full(1, D), full(columns, rows, LATE), low(columns, rows, LATE), low(columns, rows, LATE)]
        + [full(steps + 1, 16, CONV_COLS), full(steps, 16, CONV_COLS), pltpu.SemaphoreType.DMA((2, steps))]
        + [pltpu.SemaphoreType.DMA((2, count * columns))] * 2
        + sum_semaphores(levels, count)
        + [buffer for _, width in PIECES for buffer in sum_buffers(levels, small, width)],
        compiler_params=pltpu.CompilerParams(vmem_limit_bytes=VMEM_LIMIT, collective_id=identity, has_side_effects=True),
    )(*operands)
    heads = [out.reshape(MB, 1, TOK_DEV, D) for out in outs[:2]]
    flat = [out.reshape(-1) for out in outs[7:]]
    return heads + [outs[5].reshape(-1)] + list(outs[2:5]) + [outs[6]] + flat


def rms(values):
    return lax.rsqrt(jnp.mean(values * values, axis=-1, keepdims=True) + EPSILON)


def scatter_small(parts, shards):
    rows = []
    for part in parts:
        if part.ndim == 2:
            rows.append(part.reshape(part.shape[0], shards, -1).transpose(1, 0, 2).reshape(shards, -1))
        else:
            rows.append(part.reshape(shards, -1))
    flat = jnp.concatenate(rows, axis=1)
    size = flat.shape[1]
    padded = -(-size // LANES) * LANES
    return jnp.pad(flat, ((0, 0), (0, padded - size)))


def on_device(
    tokens, seq_lengths, norm_gain, w_inner, w_state, w_step, conv_weight, conv_bias, step_bias, decay_log, skip_gain, out_gain, w_out, cotangent,
):
    dp_count = lax.axis_size("dp")
    shards = lax.axis_size("fsdp")
    base = lax.axis_index("dp") * TOK_DEV
    lengths = seq_lengths[:, 0]
    info = jnp.concatenate([lengths.reshape(-1), jnp.stack([base, jnp.int32(dp_count * TOK_DEV)]).astype(jnp.int32)])
    width = 512

    def padded(part):
        return jnp.pad(part, ((0, 0),) * (part.ndim - 1) + ((0, width - part.shape[-1]),)).reshape(-1)

    small = [padded(part) for part in (conv_weight, conv_bias, out_gain, norm_gain, step_bias, decay_log, skip_gain)]
    mine = jnp.concatenate(small + [jnp.zeros((6 * width,), BF16)]).reshape(16, width)
    x, cot = tokens[:, 0], cotangent[:, 0]
    w_all, hidden, hidden_t, d_branch, d_branch_t, gain_in, taps, steps, skip, out_scale, spread_f, spread_r, sum_f, sum_r = gather_weights(
        info, x, cot, w_inner, w_state, w_step, mine, 4
    )
    rows = TOK_DEV + HALO
    zx = jnp.dot(hidden.reshape(MB * rows, D), w_all, preferred_element_type=F32).reshape(MB, rows, WIDE)

    levels = dp_count // 2
    zx_vals = per_micro((rows, INNER), 1)
    zx_bc = per_micro((rows, LANES), 2 * INNER // LANES)
    zx_dt = per_micro((rows, LANES), 2 * INNER // LANES + 1)
    taps_spec, steps_spec = once((8, CONV_COLS)), once((8, LANES))
    spread_spec, sum_spec = once((2 * LANES, INNER)), once((INNER, LANES))
    state_spec, dx_spec = per_micro((STATE, INNER)), per_micro((8, INNER))
    wide_spec, lane_spec = per_micro((TOK_DEV, INNER)), per_micro((TOK_DEV, LANES))
    row_spec, dx_all_spec, carry_spec = once((8, INNER)), once((MB, 8, INNER)), once(CARRY_SHAPE)

    def early(width, column):
        return pl.BlockSpec((1, rows, width), lambda s: (jnp.minimum(s, MB - 1), 0, column))

    def turning(s):
        return jnp.clip(s - MB, 0, 2 * MB - 1)

    def backing(s):
        return jnp.maximum(s - 3 * MB, 0)

    def block_at(pick, width):
        return pl.BlockSpec((1, BLOCK, width), lambda s: (pick(s) // 2, lax.rem(pick(s), 2), 0))

    back_spec = pl.BlockSpec((1, 1, STATE, INNER), lambda s: (turning(s) // 2, lax.rem(turning(s), 2), 0, 0))
    lanes_struct = struct(MB, TOK_DEV, LANES)
    lane_out, anywhere = block_at(backing, LANES), pl.BlockSpec(memory_space=pl.ANY)
    shard_rows = INNER // shards
    shard_spec = once((shard_rows, D))
    pairs = pltpu.SemaphoreType.DMA((2, shards // 2))
    block_scratch = pltpu.VMEM((BLOCK, INNER), F32)
    (
        v, bc, fr, frp, kept_f, kept_r, dx, normed, d_gate, back_f, back_r, d_out_gain, d_skip, d_v, d_bc, sums, d_log,
        first_grad, gate_grad, enter_f, enter_r, after_f, after_r, w_back,
    ) = call(
        partial(mixer_kernel, levels, shards // 2),
        (5 * MB,),
        [SCALARS, early(INNER, 1), early(LANES, 2 * INNER // LANES), early(LANES, 2 * INNER // LANES + 1), block_at(turning, INNER)]
        + [taps_spec, steps_spec, spread_spec, spread_spec, sum_spec, sum_spec, row_spec, row_spec]
        + [anywhere] * 4,
        [anywhere] * 9
        + [back_spec, back_spec]
        + [row_spec, row_spec, block_at(backing, INNER), lane_out, lane_out, lane_out, shard_spec, shard_spec]
        + [anywhere] * 5,
        [struct(MB, TOK_DEV, INNER, dtype=BF16)]
        + [lanes_struct] * 3
        + [struct(MB, STATE, INNER)] * 2
        + [struct(MB, 8, INNER)]
        + [struct(MB, TOK_DEV, INNER, dtype=BF16)] * 2
        + [struct(MB, 2, STATE, INNER)] * 2
        + [struct(8, INNER)] * 2
        + [struct(MB, TOK_DEV, INNER)]
        + [lanes_struct] * 3
        + [struct(shard_rows, D)] * 2
        + [struct(*CARRY_SHAPE)] * 4
        + [struct(INNER, D, dtype=BF16)],
        scratch=[pltpu.VMEM((MB, TOK_DEV, INNER), BF16)]
        + [pltpu.VMEM((MB, TOK_DEV, LANES), F32)] * 3
        + [pltpu.VMEM((MB, STATE, INNER), F32)] * 2
        + [pltpu.VMEM((MB, 8, INNER), F32)]
        + [pltpu.VMEM((MB, TOK_DEV, INNER), BF16)] * 2
        + [pltpu.VMEM((MB, TOK_DEV, D), BF16)]
        + [pltpu.VMEM((D, MB * TOK_DEV), BF16)] * 2
        + [pltpu.SemaphoreType.DMA((3,)), pltpu.SemaphoreType.DMA((7, MB)), pltpu.SemaphoreType.DMA((2, 2 * MB))]
        + [pltpu.VMEM((1, BLOCK, INNER), F32)] * 2
        + [block_scratch] * 5
        + [pltpu.VMEM((BLOCK, LANES), F32), pltpu.VMEM((2 * MB, BLOCK, INNER), BF16)]
        + [pltpu.VMEM((2 * MB, BLOCK, LANES), F32)] * 2
        + [pltpu.VMEM((INNER, D), BF16), pairs, pairs, pltpu.SemaphoreType.DMA((2,))]
        + shard_buffers(shards)
        + [pltpu.VMEM((MB, 8, INNER), F32), pltpu.SemaphoreType.DMA((2, MB))]
        + [pltpu.VMEM(CARRY_SHAPE, F32)] * 4
        + 2 * carry_buffers(),
        flops=50_000_000_000,
        moved=60_000_000,
        identity=0,
    )(
        info, zx, zx, zx, zx, taps, steps, spread_f, spread_r, sum_f, sum_r, skip, out_scale, w_out, d_branch, d_branch_t, hidden_t
    )

    def turned(grad):
        return grad.reshape(shard_rows, D // shard_rows, shard_rows).transpose(2, 1, 0).reshape(shard_rows, D)

    fits = total_fits(levels, shards, dp_count)
    if fits:
        split = (2, levels, shard_rows // (2 * levels), D)
        first_grad, gate_grad = first_grad.reshape(split), gate_grad.reshape(split)
    else:
        split = (8, LANES)
    unused = jnp.zeros((8, LANES), F32)
    chunk_spec = pl.BlockSpec((PARTS,) + CARRY_SHAPE[1:], lambda m: (m, 0, 0))
    late, before, last, d_taps, d_small, first_sum, gate_sum = call(
        partial(final_kernel, levels if fits else 0),
        (MB,),
        [SCALARS, zx_vals, zx_bc, zx_dt, taps_spec, steps_spec, wide_spec, lane_spec, lane_spec, lane_spec]
        + [chunk_spec, chunk_spec, state_spec, state_spec]
        + [dx_spec, chunk_spec, chunk_spec, per_micro((2, STATE, INNER)), per_micro((2, STATE, INNER))]
        + [wide_spec, lane_spec, lane_spec, lane_spec, spread_spec, spread_spec, sum_spec, sum_spec, once(split), once(split)],
        [per_micro((TOK_DEV, LATE)), per_micro((HALO, CONV_COLS)), per_micro((HALO, CONV_COLS)), once((8, CONV_COLS)), once((8, LANES)), once(split), once(split)],
        [
            struct(MB, TOK_DEV, LATE, dtype=BF16),
            struct(MB, HALO, CONV_COLS),
            struct(MB, HALO, CONV_COLS),
            struct(8, CONV_COLS),
            struct(8, LANES),
            struct(*split),
            struct(*split),
        ],
        scratch=[pltpu.VMEM((TOK_DEV, CONV_COLS), F32)]
        + (2 * sum_buffers(*split[1:]) + sum_semaphores(levels, 2) if fits else []),
        flops=2_000_000_000,
        moved=40_000_000,
        identity=3 if fits else None,
    )(
        info, zx, zx, zx, taps, steps, v, bc, fr, frp, enter_f, enter_r, kept_f, kept_r, dx, after_f, after_r, back_f, back_r,
        d_v, d_bc, sums, d_log, spread_f, spread_r, sum_f, sum_r, first_grad if fits else unused, gate_grad if fits else unused,
    )
    ending = (last + shift(before, -1)).astype(BF16)
    late = lax.dynamic_update_slice(late, ending, (0, TOK_DEV - HALO, 0)).reshape(MB * TOK_DEV, LATE)

    d_gate = d_gate.reshape(MB * TOK_DEV, INNER)
    normed = normed.reshape(MB * TOK_DEV, INNER)
    if fits:
        flat = [part.reshape(MB * TOK_DEV, D) for part in (x, cot)]
        grads = totals(
            (info, hidden_t, late, d_gate, normed, w_all, w_back, *flat, gain_in, gate_sum.reshape(shard_rows, D))
            + (d_taps, d_out_gain, d_skip, d_small, sum_f),
            2,
        )
        return (*grads, turned(first_sum))

    def owned(grad):
        return lax.psum_scatter(grad, "fsdp", scatter_dimension=0, tiled=True)

    places = base + jnp.arange(TOK_DEV, dtype=jnp.int32)
    first = lengths[:, :1]
    start = (first + BLOCK - 1) // BLOCK * BLOCK
    valid = (places[None] < first) | (places[None] >= start) & (places[None] < start + lengths[:, 1:])
    valid = valid[..., None]
    branch = dot(normed, w_back).reshape(MB, TOK_DEV, D)
    x_rows = x.astype(F32)
    layer_out = jnp.where(valid, x_rows + branch, 0.0).astype(BF16)
    late_grad = dot(hidden_t, late)
    d_hidden = dot(d_gate, w_all[:, :INNER], COLS) + dot(late, w_all[:, INNER:], COLS)
    d_hidden = d_hidden.reshape(MB, TOK_DEV, D)
    scale = rms(x_rows)
    d_norm_gain = jnp.sum(d_hidden * x_rows * scale, axis=(0, 1))
    pulled = d_hidden * gain_in
    d_x = scale * pulled - x_rows * (scale * scale * scale) * jnp.mean(x_rows * pulled, axis=-1, keepdims=True)
    tokens_grad = d_x + jnp.where(valid, cot.astype(F32), 0.0)
    d_skip_gain = jnp.sum(d_skip[0].reshape(HEADS, HEAD_DIM), axis=1)
    d_decay = d_small[1, :HEADS] + d_small[1, HEADS : 2 * HEADS]
    small = (d_norm_gain, d_taps[:CONV], d_taps[CONV], d_small[0, : 2 * HEADS], d_decay, d_skip_gain, d_out_gain[0])
    w_out_grad, gate_grad, late_grad = lax.psum((first_grad, gate_grad, owned(late_grad)), "dp")
    summed = lax.psum(scatter_small(small, shards), ("dp", "fsdp"))
    own = lax.dynamic_slice_in_dim(summed, lax.axis_index("fsdp"), 1, axis=0)[0]
    pieces = []
    at = 0
    for part in (norm_gain, conv_weight, conv_bias, step_bias, decay_log, skip_gain, out_gain):
        pieces.append(own[at : at + part.size].reshape(part.shape))
        at += part.size
    gate_grad = jnp.concatenate([gate_grad[: shard_rows // 2], gate_grad[shard_rows // 2 :]], axis=1)
    w_inner_grad = jnp.concatenate([gate_grad, late_grad[:, :INNER]], axis=1)
    w_state_grad = late_grad[:, INNER : INNER + 2 * STATE]
    w_step_grad = late_grad[:, INNER + LANES : INNER + LANES + 2 * HEADS]
    grads = pieces[:1] + [w_inner_grad, w_state_grad, w_step_grad] + pieces[1:] + [turned(w_out_grad)]
    return (layer_out[:, None], tokens_grad[:, None], *grads)


def solution(mesh):
    rows, vector, matrix = P(None, "fsdp", "dp", None), P("fsdp"), P("fsdp", None)
    weights = (vector, matrix, matrix, matrix, P(None, "fsdp"), vector, vector, vector, vector, vector, matrix)
    return jax.shard_map(
        on_device,
        mesh=mesh,
        in_specs=(rows, P(None, "fsdp", None)) + weights + (rows,),
        out_specs=(rows, rows) + weights,
        check_vma=False,
    )
```

```python
from functools import partial

import jax
import jax.numpy as jnp
from jax import lax
from jax.experimental import pallas as pl
from jax.experimental.pallas import tpu as pltpu
from jax.sharding import PartitionSpec as P

D = 768
INNER = 1536
HEADS = 24
HEAD_DIM = 64
STATE = 64
CONV = 4
BLOCK = 128
MB = 3
TOK_DEV = 256
HALO = 8
LANES = 128
CONV_COLS = INNER + 2 * STATE
WIDE = 2 * INNER + 2 * LANES
LATE = INNER + 2 * LANES
PAIRS = HEADS // 2
PARTS = 4
CHUNKS = MB * PARTS
LAG = 2
TURNS = 3
TURN_PAIRS = PAIRS // TURNS
CUTS = 3
EPSILON = 1e-05
HIGHEST = lax.Precision.HIGHEST
F32 = jnp.float32
BF16 = jnp.bfloat16
SENT = F32
ROWS = ((0,), (0,))
COLS = ((1,), (1,))
INNER_DIMS = ((1,), (0,))
VMEM_LIMIT = 60 * 1024 * 1024
SCALARS = pl.BlockSpec(memory_space=pltpu.SMEM)


def dot(left, right, dims=INNER_DIMS, precision=None):
    return lax.dot_general(left, right, (dims, ((), ())), precision=precision, preferred_element_type=F32)


def halves(value):
    high = value.astype(BF16)
    return high, (value - high.astype(F32)).astype(BF16)


def spread_operand(value):
    high, low = halves(value)
    return jnp.concatenate([high, low], axis=1)


def by_lane(first, second):
    low = iota(first.shape, 1) < STATE
    twice = jnp.where(low, first, second)
    high = twice.astype(BF16).astype(F32)
    return jnp.where(low, high, twice - high)


def twice(value, axis):
    return jnp.concatenate([value, value], axis=axis)


def fold(value):
    return value[:STATE] + value[STATE:]


def head_sums(value, selector):
    high, low = halves(value)
    return dot(high, selector) + dot(low, selector)


def sigmoid(value):
    return 1.0 / (1.0 + jnp.exp(-value))


def softplus(value):
    tail = jnp.exp(-jnp.abs(value))
    series = tail * (1.0 - tail * (0.5 - tail * (1.0 / 3.0 - 0.25 * tail)))
    return jnp.maximum(value, 0.0) + jnp.where(tail < 0.01, series, jnp.log(1.0 + tail))


def iota(shape, dim):
    return lax.broadcasted_iota(jnp.int32, shape, dim)


def span_scalars(info, m):
    first = info[2 * m]
    start = ((first + (BLOCK - 1)) >> 7) << 7
    return first, start, start + info[2 * m + 1], info[2 * MB], info[2 * MB + 1]


def keeps(info, m):
    _, start, _, base, span = span_scalars(info, m)

    def keep(position):
        begins = (position == 0) | (position == start) | (position >= span)
        return jnp.where(begins, 0.0, 1.0).astype(F32)

    forward = [keep(base), keep(base + BLOCK)]
    reverse = [keep(base + BLOCK), keep(base + 2 * BLOCK)]
    return forward, reverse


def row_masks(info, m, shape, offset=0):
    first, start, end, base, _ = span_scalars(info, m)
    place = iota(shape, 0) + (base + offset)
    inside = (place < first) | ((place >= start) & (place < end))
    offset = jnp.where(place >= start, place - start, place)
    return inside.astype(F32), [(offset >= k).astype(F32) for k in range(CONV)]


def conv_windows(ref, cols):
    main = ref[0, :TOK_DEV, cols]
    halo = ref[0, TOK_DEV:, cols]
    whole = jnp.concatenate([halo, main], axis=0)
    return [main] + [whole[HALO - k : HALO - k + TOK_DEV] for k in range(1, CONV)]


def conv_value(windows, masks, taps, cols):
    value = taps[CONV : CONV + 1, cols] + taps[0:1, cols] * windows[0]
    for k in range(1, CONV):
        value = value + taps[k : k + 1, cols] * (windows[k] * masks[k])
    return value


def gather_kernel(
    count, columns, info, x_in, cot_in, w_inner, w_state, w_step, mine,
    w_all, hidden, hidden_t, d_branch, d_branch_t, norm, taps, steps, skip, scale, spread_f, spread_r, sum_f, sum_r,
    halo, small, skip_row, halo_sems, small_sems, x_sems, y_sems, mate_sems, own_sems,
):
    me, part = lax.axis_index("dp"), lax.axis_index("fsdp")
    side, core, column = lax.rem(me, 2), lax.rem(part, 2), part // 2
    partner, mate = me + 1 - 2 * side, part + 1 - 2 * core
    has_next, has_last = me < count - 1, me > 0
    shards = 2 * columns
    rows = w_inner.shape[0]
    chunk = rows // (2 * CUTS)

    barrier = pltpu.get_barrier_semaphore()

    @pl.when(has_next)
    def _():
        pl.semaphore_signal(barrier, inc=1, device_id={"dp": me + 1})

    @pl.when(has_last)
    def _():
        pl.semaphore_signal(barrier, inc=1, device_id={"dp": me - 1})

    def other(d):
        return lax.rem(part + d + shards, shards)

    def column_at(d):
        return lax.rem(column + d + columns, columns)

    for d in range(1, shards):
        pl.semaphore_signal(barrier, inc=1, device_id={"fsdp": other(d)})
    pl.semaphore_wait(barrier, shards - 1 + has_next.astype(jnp.int32) + has_last.astype(jnp.int32))

    def remote(source, target, sems, k, where):
        return pltpu.make_async_remote_copy(
            src_ref=source, dst_ref=target, send_sem=sems.at[0, k], recv_sem=sems.at[1, k], device_id=where
        )

    def rows_of(owner, half, k):
        return w_all.at[pl.ds(pl.multiple_of(owner * rows + half * (rows // 2) + k * chunk, 16), chunk)]

    edge = remote(x_in.at[:, pl.ds(TOK_DEV - 2 * HALO, 2 * HALO)], halo, halo_sems, 0, {"dp": me + 1})

    def small_copy(d, theirs):
        return remote(mine, small.at[other(-d) if theirs else part], small_sems, d, {"fsdp": other(d)})

    def x_copy(k, d):
        at = rows_of(part, side, k)
        return remote(at, at, x_sems, k * columns + d, {"fsdp": 2 * column_at(d) + core})

    def x_arrival(k, d):
        at = rows_of(2 * column_at(-d) + core, side, k)
        return remote(at, at, x_sems, k * columns + d, {"fsdp": part})

    def y_copy(k, d, theirs):
        at = rows_of(2 * column_at(-d) + core, 1 - side if theirs else side, k)
        return remote(at, at, y_sems, k * columns + d, {"dp": partner})

    def mate_copy(k, d, half, theirs):
        at = rows_of(2 * column_at(-d) + (1 - core if theirs else core), half, k)
        return remote(at, at, mate_sems, (k * columns + d) * 2 + half, {"fsdp": mate})

    def own_copy(owner):
        at = w_all.at[pl.ds(pl.multiple_of(owner * rows, 16), rows)]
        return remote(at, at, own_sems, 0, {"fsdp": mate})

    @pl.when(has_next)
    def _():
        edge.start()

    for d in range(1, shards):
        small_copy(d, False).start()
    here = pl.ds(pl.multiple_of(part * rows, 16), rows)
    w_all[here, : 2 * INNER] = w_inner[...]
    w_all[here, 2 * INNER : 2 * INNER + 2 * STATE] = w_state[...]
    w_all[here, 2 * INNER + 2 * STATE :] = jnp.concatenate(
        [w_step[...].astype(F32), jnp.zeros((rows, LANES - 2 * HEADS), F32)], axis=1
    ).astype(BF16)
    for k in range(2):
        for d in range(1, columns):
            x_copy(k, d).start()
    own_copy(part).start()

    @pl.when(me == 0)
    def _():
        halo[...] = jnp.zeros_like(halo)

    def chosen(mask):
        return jnp.where(mask, 1.0, 0.0).astype(BF16)

    shape = (2 * LANES, INNER)
    lane_of, head_of = iota(shape, 0) & (LANES - 1), iota(shape, 1) >> 6
    spread_f[...] = chosen(lane_of == head_of)
    spread_r[...] = chosen(lane_of == head_of + HEADS)
    shape = (INNER, LANES)
    lane_of, head_of = iota(shape, 1), iota(shape, 0) >> 6
    sum_f[...] = chosen(lane_of == head_of)
    sum_r[...] = chosen(lane_of == head_of + HEADS)
    for m in range(MB):
        valid = row_masks(info, m, (TOK_DEV, D))[0]
        value = jnp.where(valid > 0.0, cot_in[m].astype(F32), 0.0)
        d_branch[m] = value.astype(BF16)
        d_branch_t[:, m * TOK_DEV : (m + 1) * TOK_DEV] = jnp.transpose(value).astype(BF16)

    for ref in (norm, taps, steps, skip_row):
        ref[...] = jnp.zeros_like(ref)
    for d in range(1, shards):
        small_copy(d, True).wait_recv()
    small[part] = mine[...]
    wide, heads = CONV_COLS // shards, HEADS // shards
    at = 0
    fields = [(taps, k, 1, wide) for k in range(CONV + 1)] + [(scale, 0, 8, INNER // shards), (norm, 0, 1, rows)]
    fields += [(steps, 0, 1, 2 * heads), (steps, 1, 1, heads), (skip_row, 0, 1, heads)]
    for ref, row, height, width in fields:
        done = 0
        while done < width:
            line, lane = divmod(at + done, LANES)
            size = min(width - done, LANES - lane)
            for f in range(shards):
                value = small[f, line : line + 1, lane : lane + size].astype(F32)
                if ref is steps and row == 1:
                    value = jnp.exp(value)
                    ref[row : row + 1, HEADS + f * width + done : HEADS + f * width + done + size] = value
                value = jnp.broadcast_to(value, (height, size))
                ref[row : row + height, f * width + done : f * width + done + size] = value
            done += size
        at += width
    skip[...] = dot(spread_operand(skip_row[...]), spread_f[...])

    @pl.when(has_last)
    def _():
        edge.wait_recv()

    def normalise(values):
        root = lax.rsqrt(jnp.mean(values * values, axis=1, keepdims=True) + EPSILON)
        return values * root * norm[...]

    def hide(m):
        value = normalise(x_in[m].astype(F32))
        hidden[m, :TOK_DEV] = value.astype(BF16)
        hidden_t[:, m * TOK_DEV : (m + 1) * TOK_DEV] = jnp.transpose(value).astype(BF16)
        hidden[m, TOK_DEV:] = normalise(halo[m].astype(F32)[HALO:]).astype(BF16)

    def pass_on(k):
        for d in range(1, columns):
            y_copy(k, d, True).wait_recv()

            @pl.when(side == 0)
            def _():
                mate_copy(k, d, 1, False).start()

            @pl.when(side == 1)
            def _():
                mate_copy(k, d, 0, False).start()

    for k in range(CUTS):
        if k < MB:
            hide(k)
        for d in range(1, columns):
            x_arrival(k, d).wait_recv()
            y_copy(k, d, False).start()

            @pl.when(side == 0)
            def _():
                mate_copy(k, d, 0, False).start()

            @pl.when(side == 1)
            def _():
                mate_copy(k, d, 1, False).start()

            if k + 2 < CUTS:
                x_copy(k + 2, d).start()
        if k > 0:
            pass_on(k - 1)
    for m in range(CUTS, MB):
        hide(m)
    pass_on(CUTS - 1)
    own_copy(mate).wait_recv()
    own_copy(part).wait_send()
    for k in range(CUTS):
        for d in range(1, columns):
            for half in range(2):
                mate_copy(k, d, half, True).wait_recv()
                mate_copy(k, d, half, False).wait_send()
            x_copy(k, d).wait_send()
            y_copy(k, d, False).wait_send()
    for d in range(1, shards):
        small_copy(d, False).wait_send()

    @pl.when(has_next)
    def _():
        edge.wait_send()


def gather_weights(info, x, cot, w_inner, w_state, w_step, mine, identity):
    count, shards = lax.axis_size("dp"), lax.axis_size("fsdp")
    columns = shards // 2
    whole = pl.BlockSpec(memory_space=pltpu.VMEM)
    pairs = CUTS * columns
    return pl.pallas_call(
        partial(gather_kernel, count, columns),
        in_specs=[SCALARS] + [whole] * 6,
        out_specs=[whole] * 14,
        out_shape=[
            struct(D, WIDE, dtype=BF16), struct(MB, TOK_DEV + HALO, D, dtype=BF16), struct(D, MB * TOK_DEV, dtype=BF16),
            struct(MB, TOK_DEV, D, dtype=BF16), struct(D, MB * TOK_DEV, dtype=BF16), struct(1, D), struct(8, CONV_COLS), struct(8, LANES), struct(8, INNER), struct(8, INNER),
            struct(2 * LANES, INNER, dtype=BF16), struct(2 * LANES, INNER, dtype=BF16),
            struct(INNER, LANES, dtype=BF16), struct(INNER, LANES, dtype=BF16),
        ],
        scratch_shapes=[
            pltpu.VMEM((MB, 2 * HALO, D), BF16), pltpu.VMEM((shards,) + mine.shape, BF16), pltpu.VMEM((8, LANES), F32),
            pltpu.SemaphoreType.DMA((2, 1)), pltpu.SemaphoreType.DMA((2, shards)), pltpu.SemaphoreType.DMA((2, pairs)),
            pltpu.SemaphoreType.DMA((2, pairs)), pltpu.SemaphoreType.DMA((2, 2 * pairs)), pltpu.SemaphoreType.DMA((2, 1)),
        ],
        compiler_params=pltpu.CompilerParams(vmem_limit_bytes=VMEM_LIMIT, collective_id=identity, has_side_effects=True),
    )(info, x, cot, w_inner, w_state, w_step, mine)


def front_body(m, info, vals, bc, dt, taps, steps, spread_f, spread_r, v_out, bc_out, fr_out, frp_out, tot_f, tot_r, kept_f, kept_r, dx_out):
    valid, masks = row_masks(info, m, (TOK_DEV, LANES))
    for chunk in range(PAIRS + 1):
        cols = pl.ds(chunk * LANES, LANES)
        source, own = (vals, cols) if chunk < PAIRS else (bc, pl.ds(0, LANES))
        value = conv_value(conv_windows(source, own), masks, taps, cols)
        value = valid * (value * sigmoid(value))
        if chunk < PAIRS:
            v_out[m, :, cols] = value.astype(BF16)
        else:
            bc_out[m] = value
    lane = iota((BLOCK, LANES), 1)
    rows = iota((BLOCK, BLOCK), 0)
    columns = iota((BLOCK, BLOCK), 1)
    lower = (rows >= columns).astype(F32)
    upper = (rows <= columns).astype(F32)
    forward, reverse = keeps(info, m)
    ends = []
    tails = []
    inputs = []
    for b in range(2):
        span = pl.ds(b * BLOCK, BLOCK)
        step = softplus(dt[0, span, :] + steps[0:1, :])
        log = -step * steps[1:2, :]
        summed = jnp.where(lane < HEADS, dot(lower, log, precision=HIGHEST), dot(upper, log, precision=HIGHEST))
        shifted = summed - jnp.log(step)
        fr_out[m, span, :] = summed
        frp_out[m, span, :] = shifted
        end = jnp.where(lane[:1] < HEADS, summed[BLOCK - 1 :], summed[:1])
        ends.append(jnp.exp(end))
        tails.append(spread_operand(jnp.where(lane < 2 * HEADS, jnp.exp(end - shifted), 0.0)))
        acts = bc_out[m, span, :]
        inputs.append(twice(jnp.transpose(by_lane(acts, swapped(acts))).astype(BF16), 1))
    ends = spread_operand(jnp.concatenate(ends + [jnp.zeros((6, LANES), F32)], axis=0))
    width = 2 * LANES
    for chunk in range(INNER // width):
        cols = pl.ds(chunk * width, width)
        decay_f = dot(ends, spread_f[:, cols])
        decay_r = dot(ends, spread_r[:, cols])
        parts_f = []
        parts_r = []
        for b in range(2):
            v = v_out[m, pl.ds(b * BLOCK, BLOCK), cols].astype(F32)
            parts_f.append(fold(dot(inputs[b], stacked(dot(tails[b], spread_f[:, cols]) * v))))
            parts_r.append(fold(dot(inputs[b], stacked(dot(tails[b], spread_r[:, cols]) * v))))
        kept_f[m, :, cols] = parts_f[0]
        kept_r[m, :, cols] = parts_r[1]
        total_f = parts_f[1] + (forward[1] * decay_f[1:2]) * parts_f[0]
        total_r = parts_r[0] + (reverse[0] * decay_r[0:1]) * parts_r[1]
        for k in range(PARTS):
            part = slice(k * STATE // PARTS, (k + 1) * STATE // PARTS)
            tot_f[PARTS * m + k, :, cols] = total_f[part]
            tot_r[PARTS * m + k, :, cols] = total_r[part]
        dx_out[m, 0:2, cols] = decay_f[0:2]
        dx_out[m, 2:4, cols] = decay_r[0:2]
        dx_out[m, 4:5, cols] = (forward[0] * forward[1]) * (decay_f[0:1] * decay_f[1:2])
        dx_out[m, 5:6, cols] = (reverse[0] * reverse[1]) * (decay_r[0:1] * decay_r[1:2])
        dx_out[m, 6:8, cols] = jnp.zeros((2, width), F32)


def stacked(value):
    return jnp.concatenate(halves(value), axis=0)


def doubled(value):
    high, low = halves(value)
    return jnp.concatenate([high, high, low, low], axis=0)


def pair_stack(value):
    lane = iota(value.shape, 1)
    zero = jnp.zeros_like(value)
    return jnp.concatenate([jnp.where(lane < HEAD_DIM, value, zero), jnp.where(lane < HEAD_DIM, zero, value)], axis=0)


def swapped(value):
    return pltpu.roll(value, STATE, axis=1)


def intra_body(m, b, v, bc, fr, frp, skip, y_out):
    span = pl.ds(pl.multiple_of(b * BLOCK, BLOCK), BLOCK)
    rows = iota((BLOCK, BLOCK), 0)
    columns = iota((BLOCK, BLOCK), 1)
    lower = rows > columns
    acts = bc[m, span, :]
    outs = jnp.where(columns < STATE, swapped(acts), 0.0)
    scores = jnp.where(rows == columns, 0.0, dot(outs, acts, COLS, HIGHEST))
    cum = fr[m, span, :]
    shifted = jnp.transpose(frp[m, span, :])
    for pair in range(PAIRS):
        mats = []
        for h in (2 * pair, 2 * pair + 1):
            r = HEADS + h
            gap = jnp.where(lower, cum[:, h : h + 1] - shifted[h : h + 1], cum[:, r : r + 1] - shifted[r : r + 1])
            mats.append((jnp.exp(gap) * scores).astype(BF16))
        cols = pl.ds(pair * LANES, LANES)
        value = v[m, span, cols]
        y = dot(jnp.concatenate(mats, axis=1), pair_stack(value))
        y_out[0, :, cols] = y + skip[0:1, cols] * value.astype(F32)


def entering(m, b, cols, forward, reverse, enter_f, enter_r, kept_f, kept_r, dx):
    first_f = forward[0] * jnp.concatenate([enter_f[PARTS * m + k, :, cols] for k in range(PARTS)], axis=0)
    last_r = reverse[1] * jnp.concatenate([enter_r[PARTS * m + k, :, cols] for k in range(PARTS)], axis=0)
    state_f = jnp.where(b == 0, first_f, forward[1] * (dx[m, 0:1, cols] * first_f + kept_f[m, :, cols]))
    state_r = jnp.where(b == 1, last_r, reverse[0] * (dx[m, 3:4, cols] * last_r + kept_r[m, :, cols]))
    return state_f, state_r


def middle_body(
    slot, info, y, gate, d_normed, v, bc, fr, enter_f, enter_r, kept_f, kept_r, dx, gain, spread_f, spread_r, sum_f, sum_r,
    normed, d_mixed, d_gate, back_f, back_r, leave_f, leave_r, d_outs, read_out, d_gain, d_skip, mixed_s, part_f, part_r, exp_f, exp_r,
):
    m, b = slot // 2, lax.rem(slot, 2)
    span = pl.ds(pl.multiple_of(b * BLOCK, BLOCK), BLOCK)
    forward, reverse = keeps(info, m)
    lane = iota((BLOCK, LANES), 1)
    acts = bc[m, span, :]
    outs = by_lane(swapped(acts), acts)
    outs_t = twice(jnp.transpose(outs).astype(BF16), 1)
    outs = twice(outs.astype(BF16), 1)
    grown = spread_operand(jnp.where(lane < 2 * HEADS, jnp.exp(fr[m, span, :]), 0.0))
    width = 2 * LANES
    chunks = INNER // width
    squares = jnp.zeros((BLOCK, 1), F32)
    cross = jnp.zeros((BLOCK, 1), F32)
    for chunk in range(chunks):
        cols = pl.ds(chunk * width, width)
        state_f, state_r = entering(m, b, cols, forward, reverse, enter_f, enter_r, kept_f, kept_r, dx)
        ef = dot(grown, spread_f[:, cols])
        er = dot(grown, spread_r[:, cols])
        carried_f = ef * dot(outs, doubled(state_f))
        carried_r = er * dot(outs, doubled(state_r))
        mixed = y[0, :, cols] + carried_f + carried_r
        exp_f[:, cols] = ef
        exp_r[:, cols] = er
        part_f[:, cols] = carried_f
        part_r[:, cols] = carried_r
        mixed_s[:, cols] = mixed
        g = gate[0, :, cols]
        gated = mixed * (g * sigmoid(g))
        squares = squares + jnp.sum(gated * gated, axis=1, keepdims=True)
        cross = cross + jnp.sum(gated * gain[0:1, cols] * d_normed[0, :, cols], axis=1, keepdims=True)
    scale = lax.rsqrt(squares * (1.0 / INNER) + EPSILON)
    pull = scale * scale * scale * (cross * (1.0 / INNER))
    d_o = jnp.zeros((BLOCK, LANES), F32)
    reads = jnp.zeros((BLOCK, LANES), F32)

    @pl.when((m == 0) & (b == 0))
    def _():
        d_gain[...] = jnp.zeros_like(d_gain)
        d_skip[...] = jnp.zeros_like(d_skip)

    @pl.when(b == 0)
    def _():
        for k in range(PARTS):
            leave_f[PARTS * m + k] = jnp.zeros(CARRY_SHAPE[1:], F32)
            leave_r[PARTS * m + k] = jnp.zeros(CARRY_SHAPE[1:], F32)

    for chunk in range(chunks):
        cols = pl.ds(chunk * width, width)
        g = gate[0, :, cols]
        sig = sigmoid(g)
        silu = g * sig
        mixed = mixed_s[:, cols]
        gated = mixed * silu
        dy = d_normed[0, :, cols]
        scaled = gated * scale
        normed[m, span, cols] = (scaled * gain[0:1, cols]).astype(BF16)
        d_gain[0:1, cols] += jnp.sum(dy * scaled, axis=0, keepdims=True)
        d_gated = scale * gain[0:1, cols] * dy - gated * pull
        dm = d_gated * silu
        d_gate[m, span, cols] = (d_gated * mixed * sig * (1.0 + g * (1.0 - sig))).astype(BF16)
        d_mixed[slot, :, cols] = dm.astype(BF16)
        d_skip[0:1, cols] += jnp.sum(dm * v[m, span, cols].astype(F32), axis=0, keepdims=True)
        state_f, state_r = entering(m, b, cols, forward, reverse, enter_f, enter_r, kept_f, kept_r, dx)
        grown_f = exp_f[:, cols] * dm
        grown_r = exp_r[:, cols] * dm
        local_f = fold(dot(outs_t, stacked(grown_f)))
        local_r = fold(dot(outs_t, stacked(grown_r)))
        back_f[0, 0, :, cols] = local_f
        back_r[0, 0, :, cols] = local_r
        weight_f = jnp.where(b == 0, forward[0], (forward[0] * forward[1]) * dx[m, 0:1, cols])
        weight_r = jnp.where(b == 0, (reverse[0] * reverse[1]) * dx[m, 3:4, cols], reverse[1])
        local_f = weight_f * local_f
        local_r = weight_r * local_r
        for k in range(PARTS):
            part = slice(k * STATE // PARTS, (k + 1) * STATE // PARTS)
            leave_f[PARTS * m + k, :, cols] += local_f[part]
            leave_r[PARTS * m + k, :, cols] += local_r[part]
        d_o = d_o + dot(spread_operand(grown_f), twice(stacked(state_f), 1), COLS)
        d_o = d_o + dot(spread_operand(grown_r), twice(stacked(state_r), 1), COLS)
        reads = reads + head_sums(dm * part_f[:, cols], sum_f[cols, :]) + head_sums(dm * part_r[:, cols], sum_r[cols, :])
    d_outs[slot] = jnp.where(lane < STATE, 0.0, d_o + swapped(d_o))
    read_out[slot] = reads


def intra_back_body(slot, v, d_mixed, bc, fr, frp, skip, d_outs, read_out, d_v, d_bc, sums, d_log, row_s, turn):
    m, b = slot // 2, lax.rem(slot, 2)
    span = pl.ds(pl.multiple_of(b * BLOCK, BLOCK), BLOCK)
    rows = iota((BLOCK, BLOCK), 0)
    columns = iota((BLOCK, BLOCK), 1)
    ahead = rows < columns
    acts = bc[m, span, :]
    low = columns < STATE
    turned = swapped(acts)
    outs = jnp.where(low, turned, 0.0)
    scores = jnp.where(rows == columns, 0.0, dot(acts, outs, COLS, HIGHEST))
    cum = jnp.transpose(fr[m, span, :])
    shifted = frp[m, span, :]
    d_scores = jnp.zeros((BLOCK, BLOCK), F32)
    gathered = jnp.zeros((BLOCK, LANES), F32)

    row_s[...] = jnp.zeros_like(row_s)
    for pair in range(PAIRS):
        cols = pl.ds(pair * LANES, LANES)
        value = v[m, span, cols]
        dm = d_mixed[slot, :, cols]
        products = dot(pair_stack(value), dm, COLS)
        mats = []
        for side in range(2):
            h = 2 * pair + side
            r = HEADS + h
            gap = jnp.where(ahead, cum[h : h + 1] - shifted[:, h : h + 1], cum[r : r + 1] - shifted[:, r : r + 1])
            weight = jnp.exp(gap)
            mats.append((weight * scores).astype(BF16))
            reach = products[side * BLOCK : (side + 1) * BLOCK] * weight
            d_scores = d_scores + reach
            both = reach * scores
            first = jnp.where(ahead, both, 0.0)
            second = both - first
            gathered = jnp.where(columns == h, jnp.sum(first, axis=1, keepdims=True), gathered)
            gathered = jnp.where(columns == r, jnp.sum(second, axis=1, keepdims=True), gathered)
            row_s[h : h + 1, :] = jnp.sum(first, axis=0, keepdims=True)
            row_s[r : r + 1, :] = jnp.sum(second, axis=0, keepdims=True)
        dmf = dm.astype(F32)
        d_v[0, :, cols] = dot(jnp.concatenate(mats, axis=1), pair_stack(dm)) + skip[0:1, cols] * dmf
        if pair % TURN_PAIRS == TURN_PAIRS - 1:
            turn(pair // TURN_PAIRS)
    d_scores = jnp.where(rows == columns, 0.0, d_scores)
    ins = jnp.where(low, 0.0, turned)
    d_bc[0] = dot(d_scores, outs, precision=HIGHEST) + dot(jnp.transpose(d_scores), ins, precision=HIGHEST) + d_outs[slot]
    sums[0] = gathered
    d_log[0] = jnp.transpose(row_s[...]) - gathered + read_out[slot]


def shard_steps(columns, normed, d_branch_t, hidden_t, d_gate, outs, buffers):
    put, gots, cross_puts, cross_gots, mate_sems, cross_sems = buffers
    part = lax.axis_index("fsdp")
    core, column = lax.rem(part, 2), part // 2
    mate = part + 1 - 2 * core
    rows = put.shape[1]

    def column_at(d):
        return lax.rem(column + d + columns, columns)

    def remote(source, target, sems, k, device):
        return pltpu.make_async_remote_copy(
            src_ref=source, dst_ref=target, send_sem=sems.at[0, k], recv_sem=sems.at[1, k], device_id={"fsdp": device}
        )

    def to_mate(which, x):
        return remote(put.at[x], gots[which].at[x], mate_sems, which * columns + x, mate)

    def across(which, d):
        target = 2 * column_at(d) + core
        return remote(cross_puts[which].at[d - 1], cross_gots[which].at[d - 1], cross_sems, which * columns + d, target)

    def piece(which, owner, h):
        half = rows // 2
        if which == 0:
            group = 1 if rows % LANES == 0 else 2
            at = pl.ds(pl.multiple_of((owner // group) * (group * rows), LANES), group * rows)
            total = sum(
                dot(d_branch_t[h * rows : (h + 1) * rows, m * TOK_DEV : (m + 1) * TOK_DEV], normed[m, :, at]) for m in range(MB)
            )
            return total if group == 1 else jnp.where(lax.rem(owner, 2) == 0, total[:, :rows], total[:, rows:])
        at = pl.ds(pl.multiple_of(owner * half, 16), half)
        return sum(
            dot(hidden_t[at, m * TOK_DEV : (m + 1) * TOK_DEV], d_gate[m, :, h * D : (h + 1) * D]) for m in range(MB)
        )

    def view(which, h):
        return (slice(None), slice(h * rows, (h + 1) * rows)) if which == 0 else (slice(h * rows // 2, (h + 1) * rows // 2),)

    def count(which):
        return D // rows if which == 0 else 2

    def greet(barrier):
        pl.semaphore_signal(barrier, inc=1, device_id={"fsdp": mate})
        for d in range(1, columns):
            pl.semaphore_signal(barrier, inc=1, device_id={"fsdp": 2 * column_at(d) + core})
        return columns

    def foreign(which):
        for x in range(columns):
            if which == 1:
                to_mate(0, x).wait_send()
            for h in range(count(which)):
                put[(x,) + view(which, h)] = piece(which, 2 * x + 1 - core, h).astype(BF16)
            to_mate(which, x).start()

    def local(which):
        for x in range(columns):
            to_mate(which, x).wait_recv()
        for d in list(range(1, columns)) + [0]:
            x = column_at(d)
            for h in range(count(which)):
                at = view(which, h)
                value = piece(which, 2 * x + core, h) + gots[which][(x,) + at].astype(F32)
                if d == 0:
                    outs[which][at] = value
                else:
                    cross_puts[which][(d - 1,) + at] = value.astype(BF16)
            if d > 0:
                across(which, d).start()

    def close():
        for which in range(2):
            for d in range(1, columns):
                across(which, d).wait()
                outs[which][...] += cross_gots[which][d - 1].astype(F32)
        for x in range(columns):
            to_mate(1, x).wait_send()

    return greet, foreign, local, close


def shard_buffers(shards):
    columns, shape = shards // 2, (INNER // shards, D)
    low, few = pltpu.VMEM((columns,) + shape, BF16), pltpu.VMEM((columns - 1,) + shape, BF16)
    return [low] * 3 + [few] * 4 + [pltpu.SemaphoreType.DMA((2, 2 * columns))] * 2


def gather_steps(columns, w_out, w_back, w_back_out, cross_sems, mate_sems, out_sems):
    part = lax.axis_index("fsdp")
    core, column = lax.rem(part, 2), part // 2
    mate = part + 1 - 2 * core
    rows = w_out.shape[0]

    def column_at(d):
        return lax.rem(column + d + columns, columns)

    def copy(sems, k, owner, device):
        at = w_back.at[pl.ds(pl.multiple_of(owner * rows, LANES // 2), rows)]
        return pltpu.make_async_remote_copy(
            src_ref=at, dst_ref=at, send_sem=sems.at[0, k], recv_sem=sems.at[1, k], device_id={"fsdp": device}
        )

    def across(d, theirs):
        return copy(cross_sems, d, 2 * column_at(-d) + core if theirs else part, 2 * column_at(d) + core)

    def to_mate(d, theirs):
        return copy(mate_sems, d, 2 * column_at(-d) + (1 - core if theirs else core), mate)

    def keep():
        return pltpu.make_async_copy(w_back, w_back_out, out_sems.at[0])

    def start():
        here = w_back.at[pl.ds(pl.multiple_of(part * rows, LANES // 2), rows)]
        own = pltpu.make_async_copy(w_out, here, out_sems.at[1])
        own.start()
        own.wait()
        for d in range(1, columns):
            across(d, False).start()
        to_mate(0, False).start()

    def forward():
        for d in range(1, columns):
            across(d, True).wait_recv()
            to_mate(d, False).start()

    def arrive():
        for d in range(columns):
            to_mate(d, True).wait_recv()
        keep().start()

    def close():
        keep().wait()
        for d in range(columns):
            to_mate(d, False).wait_send()
            if d > 0:
                across(d, False).wait_send()

    return start, forward, arrive, close


def mixer_kernel(
    levels, columns, info, vals, bc_in, dt, gate, taps, rates, spread_f, spread_r, sum_f, sum_r, skip, gain, w_out, d_branch_in, d_branch_t_in, hidden_t_in,
    v_out, bc_out, fr_out, frp_out, kept_f_out, kept_r_out, dx_out, normed_out, d_gate_out,
    back_f, back_r, d_gain, d_skip, d_v, d_bc, sums, d_log, first_out, second_out, enter_f, enter_r, after_f, after_r, w_back_out,
    v, bc, fr, frp, kept_f, kept_r, dx, normed, d_gate, d_branch, d_branch_t, hidden_t, load_sems, front_sems, middle_sems, y, d_normed, mixed_s, part_f, part_r, exp_f, exp_r, row_s, d_mixed, d_outs, read_out, w_back, w_cross, w_mate, w_kept,
    put, got_1, got_2, cross_put_1, cross_put_2, cross_got_1, cross_got_2, mate_sems, cross_sems,
    gains_other, gain_sems, tot_f, tot_r, leave_f, leave_r, *buffers,
):
    s = pl.program_id(0)
    half = len(buffers) // 2
    greet_dp, begin, send_gains, gains_here, send, run, end, total = carry_steps(
        levels, 4, 5, dx, gains_other, gain_sems, tot_f, tot_r, enter_f, enter_r, buffers[:half]
    )
    _, begin_back, _, _, send_back, run_back, end_back, _ = carry_steps(
        levels, 5, 4, dx, gains_other, gain_sems, leave_r, leave_f, after_r, after_f, buffers[half:]
    )
    greet, foreign, local, close = shard_steps(
        columns, normed, d_branch_t, hidden_t, d_gate, (first_out, second_out),
        (put, (got_1, got_2), (cross_put_1, cross_put_2), (cross_got_1, cross_got_2), mate_sems, cross_sems),
    )
    w_start, w_forward, w_arrive, w_close = gather_steps(columns, w_out, w_back, w_back_out, w_cross, w_mate, w_kept)
    entered_f, entered_r = buffers[0], buffers[1]
    fronts = ((v, v_out), (bc, bc_out), (fr, fr_out), (frp, frp_out), (kept_f, kept_f_out), (kept_r, kept_r_out), (dx, dx_out))

    def front_copy(i, m):
        return pltpu.make_async_copy(fronts[i][0].at[m], fronts[i][1].at[m], front_sems.at[i, m])

    def middle_copy(i, slot):
        ref, out = ((normed, normed_out), (d_gate, d_gate_out))[i]
        m, span = slot // 2, pl.ds(pl.multiple_of(lax.rem(slot, 2) * BLOCK, BLOCK), BLOCK)
        return pltpu.make_async_copy(ref.at[m, span], out.at[m, span], middle_sems.at[i, slot])

    def load(i):
        return pltpu.make_async_copy(*((d_branch_in, d_branch), (hidden_t_in, hidden_t), (d_branch_t_in, d_branch_t))[i], load_sems.at[i])

    middle, back = MB, 3 * MB
    window = 5

    @pl.when(s == 0)
    def _():
        barrier = pltpu.get_barrier_semaphore()
        pl.semaphore_wait(barrier, greet(barrier) + greet_dp(barrier))
        for i in range(3):
            load(i).start()
        begin()
        begin_back()
        w_start()

    @pl.when(s < middle)
    def _():
        front_body(s, info, vals, bc_in, dt, taps, rates, spread_f, spread_r, v, bc, fr, frp, tot_f, tot_r, kept_f, kept_r, dx)
        send_gains(s)
        for i in range(len(fronts)):
            front_copy(i, s).start()

        for m, (low, high) in enumerate(((0, 2), (2, 4), (4, window))):

            @pl.when(s == m)
            def _():
                send(low, high)

    done = 0
    for slot in range(2 * MB):
        need = min(PARTS + LAG * (levels - 1) + slot * (PARTS // 2), total)

        @pl.when(s == middle + slot)
        def _():
            if slot == 0:
                for m in range(MB):
                    gains_here(m)
                w_forward()
            run(done, need, window)
            if slot == 0:
                for i in range(3):
                    load(i).wait()
                w_arrive()

        done = need

    @pl.when((s >= middle) & (s < back))
    def _():
        slot = s - middle
        m, b = slot // 2, lax.rem(slot, 2)
        intra_body(m, b, v, bc, fr, frp, skip, y)
        d_normed[0] = dot(d_branch[m, pl.ds(pl.multiple_of(b * BLOCK, BLOCK), BLOCK), :], w_back[...], COLS)
        middle_body(
            slot, info, y, gate, d_normed, v, bc, fr, entered_f, entered_r, kept_f, kept_r, dx, gain, spread_f, spread_r, sum_f, sum_r,
            normed, d_mixed, d_gate, back_f, back_r, leave_f, leave_r, d_outs, read_out, d_gain, d_skip, mixed_s, part_f, part_r, exp_f, exp_r,
        )

        middle_copy(0, slot).start()
        middle_copy(1, slot).start()

        @pl.when(b == 1)
        def _():
            send_back(PARTS * m, PARTS * (m + 1))

    for k, step in enumerate((foreign, local)):
        for which in range(2):

            @pl.when(s == back + 2 * which + k)
            def _():
                step(which)

    @pl.when(s >= back)
    def _():
        slot = s - back
        each = -(-total // (2 * MB * TURNS))

        def turn(k):
            at = slot * TURNS + k
            run_back(at * each, (at + 1) * each, 0)

        intra_back_body(slot, v, d_mixed, bc, fr, frp, skip, d_outs, read_out, d_v, d_bc, sums, d_log, row_s, turn)

    @pl.when(s == 5 * MB - 1)
    def _():
        close()
        w_close()
        for m in range(MB):
            for i in range(len(fronts)):
                front_copy(i, m).wait()

        @pl.loop(0, 2 * MB)
        def _(slot):
            middle_copy(0, slot).wait()
            middle_copy(1, slot).wait()

        end(True)
        end_back(False)


def final_kernel(
    levels, info, vals, bc_in, dt, taps, rates, v, bc, fr, frp, enter_f, enter_r, kept_f, kept_r, dx, after_f, after_r, back_f, back_r,
    d_v, d_bc, sums, d_log, spread_f, spread_r, sum_f, sum_r, first_in, second_in,
    late, before, last, ending, d_taps, d_small, first_out, second_out, d_acts, *buffers,
):
    m = pl.program_id(0)
    forward, reverse = keeps(info, m)
    if levels:
        greet, steps = sum_steps(levels, (buffers[:6], buffers[6:12]), *buffers[12:14])
        leaving, arriving, kept, edge_sems = buffers[14:]
        me = lax.axis_index("dp")
        side = lax.rem(me, 2)
        neighbour = me - 1 + 2 * side
        paired = (neighbour >= 0) & (neighbour < 2 * levels)

        def edge_copy(k):
            return pltpu.make_async_remote_copy(
                src_ref=leaving.at[k], dst_ref=arriving.at[k], send_sem=edge_sems.at[0, k], recv_sem=edge_sems.at[1, k],
                device_id={"dp": me - 1},
            )

    def beside(at, *todo):
        if levels:

            @pl.when(m == at)
            def _():
                for stage, i in todo:
                    steps[stage](i)

    if levels:

        @pl.when(m == 0)
        def _():
            barrier = pltpu.get_barrier_semaphore()

            @pl.when(paired)
            def _():
                pl.semaphore_signal(barrier, inc=1, device_id={"dp": neighbour})

            pl.semaphore_wait(barrier, greet(barrier) + paired.astype(jnp.int32))

            @pl.when(me == 2 * levels - 1)
            def _():
                arriving[...] = jnp.zeros_like(arriving)

            buffers[0][...] = first_in[...]
            buffers[6][...] = second_in[...]

    beside(0, (0, 0))
    lane = iota((BLOCK, LANES), 1)
    row = iota((BLOCK, LANES), 0)
    rows = iota((BLOCK, BLOCK), 0)
    columns = iota((BLOCK, BLOCK), 1)
    lower = (rows >= columns).astype(F32)
    upper = (rows <= columns).astype(F32)
    width = 2 * LANES

    @pl.when(m == 0)
    def _():
        d_taps[...] = jnp.zeros_like(d_taps)
        d_small[...] = jnp.zeros_like(d_small)

    for b in range(2):
        span = pl.ds(b * BLOCK, BLOCK)
        summed = fr[0, span, :]
        end = jnp.where(lane[:1] < HEADS, summed[BLOCK - 1 :], summed[:1])
        tail = spread_operand(jnp.where(lane < 2 * HEADS, jnp.exp(end - frp[0, span, :]), 0.0))
        acts = bc[0, span, :]
        ins = twice(by_lane(acts, swapped(acts)).astype(BF16), 1)
        d_in = jnp.zeros((BLOCK, LANES), F32)
        used = jnp.zeros((BLOCK, LANES), F32)
        decays = jnp.zeros((8, LANES), F32)
        for chunk in range(INNER // width):
            cols = pl.ds(chunk * width, width)
            grad_f = jnp.concatenate([after_f[k, :, cols] for k in range(PARTS)], axis=0)
            grad_r = jnp.concatenate([after_r[k, :, cols] for k in range(PARTS)], axis=0)
            if b == 0:
                grad_f = forward[1] * (back_f[0, 1, :, cols] + dx[0, 1:2, cols] * grad_f)
            else:
                grad_r = reverse[0] * (back_r[0, 0, :, cols] + dx[0, 2:3, cols] * grad_r)
            state_f, state_r = entering(0, b, cols, forward, reverse, enter_f, enter_r, kept_f, kept_r, dx)
            tail_f = dot(tail, spread_f[:, cols])
            tail_r = dot(tail, spread_r[:, cols])
            value = v[0, span, cols].astype(F32)
            pulled_f = tail_f * dot(ins, doubled(grad_f))
            pulled_r = tail_r * dot(ins, doubled(grad_r))
            d_acts[span, cols] = d_v[0, span, cols] + pulled_f + pulled_r
            d_in = d_in + dot(spread_operand(tail_f * value), twice(stacked(grad_f), 1), COLS)
            d_in = d_in + dot(spread_operand(tail_r * value), twice(stacked(grad_r), 1), COLS)
            used = used + head_sums(pulled_f * value, sum_f[cols, :]) + head_sums(pulled_r * value, sum_r[cols, :])
            meet_f = jnp.sum(grad_f * state_f, axis=0, keepdims=True) * dx[0, b : b + 1, cols]
            meet_r = jnp.sum(grad_r * state_r, axis=0, keepdims=True) * dx[0, 2 + b : 3 + b, cols]
            zero = jnp.zeros((7, width), F32)
            decays = decays + head_sums(jnp.concatenate([meet_f, zero], axis=0), sum_f[cols, :])
            decays = decays + head_sums(jnp.concatenate([meet_r, zero], axis=0), sum_r[cols, :])
        d_acts[span, pl.ds(INNER, LANES)] = d_bc[0, span, :] + jnp.where(lane < STATE, d_in + swapped(d_in), 0.0)
        direct = sums[0, span, :] + used
        edge = decays[0:1] + jnp.sum(used, axis=0, keepdims=True)
        at_end = ((lane < HEADS) & (row == BLOCK - 1)) | ((lane >= HEADS) & (row == 0))
        grad = d_log[0, span, :] - used + jnp.where(at_end, edge, 0.0)
        grad = jnp.where(lane < HEADS, dot(upper, grad, precision=HIGHEST), dot(lower, grad, precision=HIGHEST))
        x = dt[0, span, :] + rates[0:1, :]
        step = softplus(x)
        sig = sigmoid(x)
        ratio = jnp.where(x < -17.0, 1.0, sig / step)
        d_x = direct * ratio - rates[1:2, :] * grad * sig
        d_x = jnp.where(lane < 2 * HEADS, d_x, 0.0)
        late[0, span, pl.ds(INNER + LANES, LANES)] = d_x.astype(BF16)
        d_small[0:1, :] += jnp.sum(d_x, axis=0, keepdims=True)
        d_small[1:2, :] -= rates[1:2, :] * jnp.sum(step * grad, axis=0, keepdims=True)
        if b == 0:
            beside(1, (1, 1))
        else:
            beside(0, (0, 1))
            beside(1, (2, 0))
    valid, masks = row_masks(info, m, (TOK_DEV, LANES))
    edge = jnp.zeros((HALO, LANES), F32)
    for chunk in range(PAIRS + 1):
        cols = pl.ds(chunk * LANES, LANES)
        source, own = (vals, cols) if chunk < PAIRS else (bc_in, pl.ds(0, LANES))
        windows = conv_windows(source, own)
        value = conv_value(windows, masks, taps, cols)
        sig = sigmoid(value)
        grad = valid * d_acts[:, cols] * (sig * (1.0 + value * (1.0 - sig)))
        total = jnp.zeros((HALO + TOK_DEV, LANES), F32)
        for k in range(CONV):
            masked = grad if k == 0 else grad * masks[k]
            d_taps[k : k + 1, cols] += jnp.sum(masked * windows[k], axis=0, keepdims=True)
            padded = jnp.concatenate([edge, masked, edge], axis=0)
            total = total + taps[k : k + 1, cols] * padded[k : k + HALO + TOK_DEV]
        d_taps[CONV : CONV + 1, cols] += jnp.sum(grad, axis=0, keepdims=True)
        before[0, :, cols] = total[:HALO]
        last[0, :, cols] = total[TOK_DEV:]
        if levels:
            leaving[m, :, cols] = total[:HALO]
            kept[m, :, cols] = total[TOK_DEV:]
        late[0, :, cols] = total[HALO:].astype(BF16)
    beside(0, (1, 0))
    beside(1, (2, 1))
    if levels:

        @pl.when(me > 0)
        def _():
            edge_copy(m).start()

        @pl.when(m == MB - 1)
        def _():
            for i, out in ((0, first_out), (1, second_out)):
                steps[3](i, False)
                out[...] = buffers[6 * i + 5][side]
            for i in range(2):
                steps[5](i, False)
            for k in range(MB):

                @pl.when(me < 2 * levels - 1)
                def _():
                    edge_copy(k).wait_recv()

                ending[k] = kept[k] + arriving[k]

                @pl.when(me > 0)
                def _():
                    edge_copy(k).wait_send()


def once(shape):
    return pl.BlockSpec(shape, lambda *grid: (0,) * len(shape), pipeline_mode=pl.Buffered(1))


def per_micro(shape, column=0):
    return pl.BlockSpec((1,) + shape, lambda m, *rest: (m,) + (0,) * (len(shape) - 1) + (column,))


def per_block(width, column=0):
    return pl.BlockSpec((1, BLOCK, width), lambda m, b: (m, b, column))


def struct(*shape, dtype=F32):
    return jax.ShapeDtypeStruct(shape, dtype)


def call(kernel, grid, in_specs, out_specs, out_shape, scratch=(), flops=0, moved=0, identity=None):
    return pl.pallas_call(
        kernel,
        grid=grid,
        in_specs=in_specs,
        out_specs=out_specs,
        out_shape=out_shape,
        scratch_shapes=list(scratch),
        compiler_params=pltpu.CompilerParams(
            vmem_limit_bytes=VMEM_LIMIT, collective_id=identity, has_side_effects=identity is not None
        ),
        cost_estimate=pl.CostEstimate(flops=flops, bytes_accessed=moved, transcendentals=0),
    )


def shift(value, distance):
    count = lax.axis_size("dp")
    route = [(i, i + distance) for i in range(count) if 0 <= i + distance < count]
    return lax.ppermute(value, "dp", route)


def carry_steps(levels, up_row, down_row, gains, gains_other, gain_sems, up_in, down_in, up_out, down_out, buffers):
    up_other, down_other, up_chain, down_chain, up_sems, down_sems, up_link, down_link, out_sems = buffers
    me = lax.axis_index("dp")
    side = lax.rem(me, 2)
    level = me // 2
    partner = me + 1 - 2 * side
    above, below = me + 2, me - 2
    has_above, has_below = level < levels - 1, level > 0
    first = side == 0

    def remote(source, target, sems, k, device):
        return pltpu.make_async_remote_copy(
            src_ref=source, dst_ref=target, send_sem=sems.at[0, k], recv_sem=sems.at[1, k], device_id={"dp": device}
        )

    def swap_gains(m):
        return remote(gains.at[m], gains_other.at[m], gain_sems, m, partner)

    def swap_up(k):
        return remote(up_in.at[k], up_other.at[k], up_sems, k, partner)

    def swap_down(k):
        return remote(down_in.at[k], down_other.at[k], down_sems, k, partner)

    def climb(k):
        return remote(up_in.at[k], up_chain.at[k], up_link, k, above)

    def descend(k):
        return remote(down_in.at[k], down_chain.at[k], down_link, k, below)

    def keep_up(k):
        return pltpu.make_async_copy(up_other.at[k], up_out.at[k], out_sems.at[0, k])

    def keep_down(k):
        return pltpu.make_async_copy(down_other.at[k], down_out.at[k], out_sems.at[1, k])

    def greet(barrier):
        pl.semaphore_signal(barrier, inc=1, device_id={"dp": partner})

        @pl.when(has_above)
        def _():
            pl.semaphore_signal(barrier, inc=1, device_id={"dp": above})

        @pl.when(has_below)
        def _():
            pl.semaphore_signal(barrier, inc=1, device_id={"dp": below})

        return 1 + has_above.astype(jnp.int32) + has_below.astype(jnp.int32)

    def begin():
        @pl.when(level == 0)
        def _():
            up_chain[...] = jnp.zeros_like(up_chain)

        @pl.when(level == levels - 1)
        def _():
            down_chain[...] = jnp.zeros_like(down_chain)

    total = CHUNKS + LAG * (levels - 1)

    def places(step):
        return step - LAG * level, step - LAG * (levels - 1 - level)

    def send(low, high):
        @pl.loop(low, high)
        def _(k):
            @pl.when(k < CHUNKS)
            def _():
                swap_up(k).start()
                swap_down(k).start()

    def advance(step):
        up, down = places(step)

        @pl.when((up >= 0) & (up < CHUNKS))
        def _():
            swap_up(up).wait_recv()

            @pl.when(has_below)
            def _():
                climb(up).wait_recv()

            m = up // PARTS
            own, other = gains[m, up_row : up_row + 1], gains_other[m, up_row : up_row + 1]
            near, far = jnp.where(first, own, other), jnp.where(first, other, own)
            mine, theirs = up_in[up], up_other[up]
            before = up_chain[up]
            middle = jnp.where(first, mine, theirs) + near * before
            up_other[up] = jnp.where(first, before, middle)
            keep_up(up).start()

            @pl.when(has_above)
            def _():
                swap_up(up).wait_send()
                up_in[up] = jnp.where(first, theirs, mine) + far * middle
                climb(up).start()

        @pl.when((down >= 0) & (down < CHUNKS))
        def _():
            swap_down(down).wait_recv()

            @pl.when(has_above)
            def _():
                descend(down).wait_recv()

            m = down // PARTS
            own, other = gains[m, down_row : down_row + 1], gains_other[m, down_row : down_row + 1]
            near, far = jnp.where(first, other, own), jnp.where(first, own, other)
            mine, theirs = down_in[down], down_other[down]
            before = down_chain[down]
            middle = jnp.where(first, theirs, mine) + near * before
            down_other[down] = jnp.where(first, middle, before)
            keep_down(down).start()

            @pl.when(has_below)
            def _():
                swap_down(down).wait_send()
                down_in[down] = jnp.where(first, mine, theirs) + far * middle
                descend(down).start()

    def run(low, high, window):
        @pl.loop(low, high)
        def _(step):
            advance(step)
            if window:
                send(step + window, step + window + 1)

    def gains_here(m):
        swap_gains(m).wait_recv()

    def end(last):
        if last:

            @pl.loop(0, MB)
            def _(m):
                swap_gains(m).wait_send()

        @pl.loop(0, CHUNKS)
        def _(k):
            keep_up(k).wait()
            keep_down(k).wait()

            @pl.when(has_above)
            def _():
                climb(k).wait_send()

            @pl.when(jnp.logical_not(has_above))
            def _():
                swap_up(k).wait_send()

            @pl.when(has_below)
            def _():
                descend(k).wait_send()

            @pl.when(jnp.logical_not(has_below))
            def _():
                swap_down(k).wait_send()

    return greet, begin, lambda m: swap_gains(m).start(), gains_here, send, run, end, total


CARRY_SHAPE = (CHUNKS, STATE // PARTS, INNER)


def carry_buffers():
    return [pltpu.VMEM(CARRY_SHAPE, F32)] * 4 + [pltpu.SemaphoreType.DMA((2, CHUNKS))] * 5


def sum_steps(levels, parts, side_sems, level_sems):
    me = lax.axis_index("dp")
    side, level = lax.rem(me, 2), me // 2
    partner = me + 1 - 2 * side

    def level_at(d):
        return lax.rem(level + d + levels, levels)

    def device(d):
        return {"dp": 2 * level_at(d) + side}

    def remote(source, target, sems, k, where):
        return pltpu.make_async_remote_copy(
            src_ref=source, dst_ref=target, send_sem=sems.at[0, k], recv_sem=sems.at[1, k], device_id=where
        )

    def greet(barrier):
        pl.semaphore_signal(barrier, inc=1, device_id={"dp": partner})
        for d in range(1, levels):
            pl.semaphore_signal(barrier, inc=1, device_id=device(d))
        return levels

    def halve(i):
        return remote(parts[i][1], parts[i][2], side_sems, 2 * i, {"dp": partner})

    def join(i, theirs):
        full = parts[i][5]
        return remote(full.at[side], full.at[1 - side if theirs else side], side_sems, 2 * i + 1, {"dp": partner})

    def scatter(i, d, theirs):
        put, got = parts[i][3:5]
        return remote(put.at[level_at(d)], got.at[level_at(-d) if theirs else level], level_sems, 2 * i * levels + d, device(d))

    def gather(i, d, theirs):
        full = parts[i][5]
        target = full.at[side, level_at(-d) if theirs else level]
        return remote(full.at[side, level], target, level_sems, (2 * i + 1) * levels + d, device(d))

    def step_0(i):
        total, put = parts[i][:2]
        put[...] = total[1 - side].astype(BF16)
        halve(i).start()

    def step_1(i):
        total, _, got, put = parts[i][:4]
        halve(i).wait_recv()
        total[side] = total[side] + got[...].astype(F32)
        for d in range(1, levels):
            target = level_at(d)
            put[target] = total[side, target].astype(BF16)
            scatter(i, d, False).start()

    def step_2(i):
        total, _, _, _, got, full = parts[i]
        value = total[side, level]
        for d in range(1, levels):
            scatter(i, d, True).wait_recv()
            value = value + got[level_at(-d)].astype(F32)
        full[side, level] = value.astype(BF16)
        for d in range(1, levels):
            gather(i, d, False).start()

    def step_3(i, joined=True):
        for d in range(1, levels):
            gather(i, d, True).wait_recv()
        if joined:
            join(i, False).start()

    def step_4(i):
        join(i, True).wait_recv()

    def close(i, joined=True):
        halve(i).wait_send()
        if joined:
            join(i, False).wait_send()
        for d in range(1, levels):
            scatter(i, d, False).wait_send()
            gather(i, d, False).wait_send()

    return greet, (step_0, step_1, step_2, step_3, step_4, close)


def sum_buffers(levels, piece, width):
    low = pltpu.VMEM((levels, piece, width), BF16)
    both = (2, levels, piece, width)
    return [pltpu.VMEM(both, F32), low, low, low, low, pltpu.VMEM(both, BF16)]


def sum_semaphores(levels, count):
    return [pltpu.SemaphoreType.DMA((2, 2 * count)), pltpu.SemaphoreType.DMA((2, 2 * count * levels))]


PIECES = ((0, 512), (512, 512), (1024, 384), (1408, 384))


def total_kernel(
    levels, columns, info, hidden_t_in, late_in, w_all_in, d_gate_in, x_hbm, cot_hbm, w_back_in, normed_in, gain_in,
    first_in, gate_in, ending, taps_in, scale_in, skip_in, small_in, selector,
    layer_hbm, tokens_hbm, first_out, inner_out, state_out, step_out, norm_out, taps_out, bias_out, steps_out, decay_out, skip_out, scale_out,
    hidden_t, late, w_all, d_gate, x_in, cot_in, w_back, normed, layer_out, tokens_out, first_sum, first_full, gate_full, load_sems, keep_sems, join_sems,
    third_in, norm_sum, mate_got, cross_put, cross_got, short_sum, short_got, short_sems, mate_sems, cross_sems, side_sems, level_sems, *buffers,
):
    me, part = lax.axis_index("dp"), lax.axis_index("fsdp")
    side, level = lax.rem(me, 2), me // 2
    core, column = lax.rem(part, 2), part // 2
    mate = part + 1 - 2 * core
    count = len(PIECES)
    parts = [buffers[6 * i : 6 * i + 6] for i in range(count)]
    sources = (hidden_t_in, late_in, w_all_in, d_gate_in, x_hbm, cot_hbm, w_back_in, normed_in)
    places = (hidden_t, late, w_all, d_gate, x_in, cot_in, w_back, normed)

    def load(i):
        return pltpu.make_async_copy(sources[i], places[i], load_sems.at[i])

    def keep(i, k):
        ref, out = ((layer_out, layer_hbm), (tokens_out, tokens_hbm))[i]
        at = pl.ds(k * BLOCK, BLOCK)
        return pltpu.make_async_copy(ref.at[at], out.at[at], keep_sems.at[i, k])

    for i in range(len(sources)):
        load(i).start()
    greet, steps = sum_steps(levels, parts, side_sems, level_sems)

    def column_at(d):
        return lax.rem(column + d + columns, columns)

    def remote(source, target, sems, k, where):
        return pltpu.make_async_remote_copy(
            src_ref=source, dst_ref=target, send_sem=sems.at[0, k], recv_sem=sems.at[1, k], device_id=where
        )

    barrier = pltpu.get_barrier_semaphore()
    pl.semaphore_signal(barrier, inc=1, device_id={"fsdp": mate})
    for d in range(1, columns):
        pl.semaphore_signal(barrier, inc=1, device_id={"fsdp": 2 * column_at(d) + core})
    pl.semaphore_wait(barrier, greet(barrier) + columns)

    def to_mate(i, x):
        at = pl.ds(*PIECES[i])
        return remote(third_in.at[2 * x + 1 - core, :, at], mate_got.at[x, :, at], mate_sems, i * columns + x, {"fsdp": mate})

    def across(i, d, theirs):
        at = pl.ds(*PIECES[i])
        where = {"fsdp": 2 * column_at(d) + core}
        slot = column_at(-d) if theirs else column
        return remote(cross_put.at[column_at(d), :, at], cross_got.at[slot, :, at], cross_sems, i * columns + d, where)

    joins = (first_full, gate_full)

    def join(i, theirs):
        full = joins[i]
        return remote(full.at[side], full.at[1 - side if theirs else side], join_sems, i, {"dp": me + 1 - 2 * side})

    for i, ref in enumerate((first_in, gate_in)):
        joins[i][side] = ref[...]
        join(i, False).start()
    load(0).wait()
    load(1).wait()
    for m in range(MB):
        late[(m + 1) * TOK_DEV - HALO : (m + 1) * TOK_DEV, :CONV_COLS] = ending[m].astype(BF16)

    block_rows = third_in.shape[1]

    def third(owner, i):
        at = pl.ds(pl.multiple_of(owner * block_rows, 16), block_rows)
        cols = pl.ds(*PIECES[i])
        third_in[owner, :, cols] = dot(hidden_t[at, :], late[:, cols])

    def d_hidden_block(k):
        m, b = divmod(k, 2)
        at = slice(k * BLOCK, (k + 1) * BLOCK)
        grad = dot(d_gate[at], w_all[:, :INNER], COLS) + dot(late[at], w_all[:, INNER:], COLS)
        rows = x_in[at].astype(F32)
        scale = lax.rsqrt(jnp.mean(rows * rows, axis=1, keepdims=True) + EPSILON)
        norm_sum[...] += jnp.sum(grad * rows * scale, axis=0, keepdims=True)
        pulled = grad * gain_in[...]
        pull = (scale * scale * scale) * jnp.mean(rows * pulled, axis=1, keepdims=True)
        valid = row_masks(info, m, (BLOCK, D), b * BLOCK)[0]
        tokens_out[at] = scale * pulled - rows * pull + valid * cot_in[at].astype(F32)
        keep(1, k).start()

    def layer_block(k):
        m, b = divmod(k, 2)
        at = slice(k * BLOCK, (k + 1) * BLOCK)
        branch = dot(normed[at], w_back[...])
        valid = row_masks(info, m, (BLOCK, D), b * BLOCK)[0]
        layer_out[at] = jnp.where(valid > 0.0, x_in[at].astype(F32) + branch, 0.0).astype(BF16)
        keep(0, k).start()

    norm_sum[...] = jnp.zeros_like(norm_sum)
    for i in range(count):
        for x in range(columns):
            third(2 * x + 1 - core, i)
            to_mate(i, x).start()
    for i in range(count):
        for x in range(columns):
            third(2 * x + core, i)

    def cross(i):
        at = pl.ds(*PIECES[i])
        for x in range(columns):
            to_mate(i, x).wait_recv()
        for d in range(1, columns):
            x = column_at(d)
            cross_put[x, :, at] = (third_in[2 * x + core, :, at] + mate_got[x, :, at]).astype(BF16)
            across(i, d, False).start()

    cross(0)
    cross(1)
    for i in range(2, 6):
        load(i).wait()
    for k in range(2 * MB - 2):
        d_hidden_block(k)

    lane = iota((8, LANES), 1)
    summed = jnp.where(lane < HEADS, head_sums(skip_in[...], selector[...]), 0.0)
    folded = small_in[...] + pltpu.roll(small_in[...], LANES - HEADS, axis=1)
    short_sum[0, 0:8, :] = taps_in[...]
    short_sum[0, 8:16, :] = jnp.zeros((8, CONV_COLS), F32)
    short_sum[0, 5:6, :INNER] = scale_in[0:1]
    short_sum[0, 8:9, :LANES] = small_in[0:1]
    short_sum[0, 9:10, :LANES] = folded[1:2]
    short_sum[0, 10:11, :LANES] = summed[0:1]
    routes = [{"fsdp": mate}, {"dp": me + 1 - 2 * side}]
    stride = 1
    while stride < columns:
        routes.append({"fsdp": part + 2 * stride - 4 * stride * lax.rem(column // stride, 2)})
        stride *= 2
    stride = 1
    while stride < levels:
        routes.append({"dp": me + 2 * stride - 4 * stride * lax.rem(level // stride, 2)})
        stride *= 2

    def short(k):
        return remote(short_sum.at[k], short_got.at[k], short_sems, k, routes[k])

    def short_step(k):
        if k > 0:
            short(k - 1).wait_recv()
            short_sum[k] = short_sum[k - 1] + short_got[k - 1]
        if k < len(routes):
            short(k).start()

    rows = parts[0][0].shape[2]

    def arrive(i):
        at = pl.ds(*PIECES[i])
        for d in range(1, columns):
            across(i, d, True).wait_recv()
        for x in range(2):
            for j in range(levels):
                here = pl.ds((x * levels + j) * rows, rows)
                value = third_in[part, here, at] + mate_got[column, here, at]
                for d in range(1, columns):
                    value = value + cross_got[column_at(-d), here, at].astype(F32)
                parts[i][0][x, j] = value
        steps[0](i)

    last = len(routes)
    for wave in range(count + 4):
        for stage in range(4, 0, -1):
            i = wave - stage
            if 0 <= i < count:
                steps[stage](i)
        if wave < count:
            arrive(wave)
        if wave + 2 < count:
            cross(wave + 2)
        if wave < 2:
            d_hidden_block(2 * MB - 2 + wave)
        elif wave < 2 + 2 * MB:
            if wave == 2:
                load(6).wait()
                load(7).wait()
            layer_block(wave - 2)
        if wave == 1:
            short_sum[0, 6:7, :D] = norm_sum[...]
        if 1 <= wave <= last + 1:
            short_step(wave - 1)
    for k in range(count + 3, last + 1):
        short_step(k)

    result = short_sum.at[last]
    for f in range(2 * columns):

        @pl.when(part == f)
        def _():
            def own(row, rows, width, ref):
                size = width // (2 * columns)
                ref[...] = result[row : row + rows, f * size : (f + 1) * size]

            own(0, CONV, CONV_COLS, taps_out)
            own(4, 1, CONV_COLS, bias_out)
            own(5, 1, INNER, scale_out)
            own(6, 1, D, norm_out)
            own(8, 1, 2 * HEADS, steps_out)
            own(9, 1, HEADS, decay_out)
            own(10, 1, HEADS, skip_out)

    for i in range(2):
        join(i, True).wait_recv()
    tall = gate_in.shape[1]
    for h in range(2):
        for j in range(levels):
            inner_out[j * tall : (j + 1) * tall, h * D : (h + 1) * D] = gate_full[h, j].astype(F32)
            at = (h * levels + j) * tall
            first_sum[at : at + tall] = first_full[h, j].astype(F32)
    tall = first_sum.shape[0]
    for g in range(D // tall):
        at = slice(g * tall, (g + 1) * tall)
        first_out[:, at] = jnp.transpose(first_sum[:, at])
    for i in range(count):
        start, width = PIECES[i]
        for x in range(2):
            for j in range(levels):
                here = pl.ds((x * levels + j) * rows, rows)
                value = parts[i][5][x, j].astype(F32)
                inside = min(width, INNER - start)
                inner_out[here, INNER + start : INNER + start + inside] = value[:, :inside]
                if inside < width:
                    state_out[here, :] = value[:, inside : inside + LANES]
                    step_out[here, :] = value[:, inside + LANES : inside + LANES + 2 * HEADS]
    for i in range(count):
        steps[5](i)
        for x in range(columns):
            to_mate(i, x).wait_send()
        for d in range(1, columns):
            across(i, d, False).wait_send()
    for k in range(last):
        short(k).wait_send()
    for i in range(2):
        join(i, False).wait_send()
        for k in range(2 * MB):
            keep(i, k).wait()


def total_fits(levels, shards, dp_count):
    rows = D // shards
    return dp_count == 2 * levels and shards % 2 == 0 and rows % (16 * levels) == 0 and 2 * rows % LANES == 0 and 24 % shards == 0


def totals(operands, identity):
    dp_count, shards = lax.axis_size("dp"), lax.axis_size("fsdp")
    levels, columns = dp_count // 2, shards // 2
    rows = D // shards
    small = rows // levels // 2
    steps = (dp_count * shards).bit_length() - 1
    count = len(PIECES)

    def low(*shape):
        return pltpu.VMEM(shape, BF16)

    def full(*shape):
        return pltpu.VMEM(shape, F32)

    outs = pl.pallas_call(
        partial(total_kernel, levels, columns),
        in_specs=[SCALARS] + [pl.BlockSpec(memory_space=pl.ANY)] * 8 + [pl.BlockSpec(memory_space=pltpu.VMEM)] * 9,
        out_specs=[pl.BlockSpec(memory_space=pl.ANY)] * 2 + [pl.BlockSpec(memory_space=pltpu.VMEM)] * 11,
        out_shape=[struct(MB * TOK_DEV, D, dtype=BF16), struct(MB * TOK_DEV, D), struct(2 * rows, D)]
        + [struct(rows, 2 * INNER), struct(rows, 2 * STATE), struct(rows, 2 * HEADS)]
        + [struct(1, D // shards), struct(CONV, CONV_COLS // shards), struct(1, CONV_COLS // shards)]
        + [struct(1, width // shards) for width in (2 * HEADS, HEADS, HEADS, INNER)],
        scratch_shapes=[pltpu.VMEM(operand.shape, BF16) for operand in operands[1:9]]
        + [low(MB * TOK_DEV, D), full(MB * TOK_DEV, D), full(2 * rows, D), low(2, levels, small * 2, D), low(2, levels, small * 2, D)]
        + [pltpu.SemaphoreType.DMA((8,)), pltpu.SemaphoreType.DMA((2, 2 * MB)), pltpu.SemaphoreType.DMA((2, 2))]
        + [full(shards, rows, LATE), full(1, D), full(columns, rows, LATE), low(columns, rows, LATE), low(columns, rows, LATE)]
        + [full(steps + 1, 16, CONV_COLS), full(steps, 16, CONV_COLS), pltpu.SemaphoreType.DMA((2, steps))]
        + [pltpu.SemaphoreType.DMA((2, count * columns))] * 2
        + sum_semaphores(levels, count)
        + [buffer for _, width in PIECES for buffer in sum_buffers(levels, small, width)],
        compiler_params=pltpu.CompilerParams(vmem_limit_bytes=VMEM_LIMIT, collective_id=identity, has_side_effects=True),
    )(*operands)
    heads = [out.reshape(MB, 1, TOK_DEV, D) for out in outs[:2]]
    flat = [out.reshape(-1) for out in outs[8:]]
    return heads + [outs[6].reshape(-1)] + list(outs[3:6]) + [outs[7]] + flat, outs[2]


def rms(values):
    return lax.rsqrt(jnp.mean(values * values, axis=-1, keepdims=True) + EPSILON)


def scatter_small(parts, shards):
    rows = []
    for part in parts:
        if part.ndim == 2:
            rows.append(part.reshape(part.shape[0], shards, -1).transpose(1, 0, 2).reshape(shards, -1))
        else:
            rows.append(part.reshape(shards, -1))
    flat = jnp.concatenate(rows, axis=1)
    size = flat.shape[1]
    padded = -(-size // LANES) * LANES
    return jnp.pad(flat, ((0, 0), (0, padded - size)))


def on_device(
    tokens, seq_lengths, norm_gain, w_inner, w_state, w_step, conv_weight, conv_bias, step_bias, decay_log, skip_gain, out_gain, w_out, cotangent,
):
    dp_count = lax.axis_size("dp")
    shards = lax.axis_size("fsdp")
    base = lax.axis_index("dp") * TOK_DEV
    lengths = seq_lengths[:, 0]
    info = jnp.concatenate([lengths.reshape(-1), jnp.stack([base, jnp.int32(dp_count * TOK_DEV)]).astype(jnp.int32)])
    small = [part.reshape(-1) for part in (conv_weight, conv_bias, out_gain, norm_gain, step_bias, decay_log, skip_gain)]
    flat = jnp.concatenate(small)
    mine = jnp.pad(flat, (0, 32 * LANES - flat.shape[0])).reshape(32, LANES)
    x, cot = tokens[:, 0], cotangent[:, 0]
    w_all, hidden, hidden_t, d_branch, d_branch_t, gain_in, taps, steps, skip, out_scale, spread_f, spread_r, sum_f, sum_r = gather_weights(
        info, x, cot, w_inner, w_state, w_step, mine, 4
    )
    rows = TOK_DEV + HALO
    zx = jnp.dot(hidden.reshape(MB * rows, D), w_all, preferred_element_type=F32).reshape(MB, rows, WIDE)

    levels = dp_count // 2
    zx_vals = per_micro((rows, INNER), 1)
    zx_bc = per_micro((rows, LANES), 2 * INNER // LANES)
    zx_dt = per_micro((rows, LANES), 2 * INNER // LANES + 1)
    taps_spec, steps_spec = once((8, CONV_COLS)), once((8, LANES))
    spread_spec, sum_spec = once((2 * LANES, INNER)), once((INNER, LANES))
    state_spec, dx_spec = per_micro((STATE, INNER)), per_micro((8, INNER))
    wide_spec, lane_spec = per_micro((TOK_DEV, INNER)), per_micro((TOK_DEV, LANES))
    row_spec, dx_all_spec, carry_spec = once((8, INNER)), once((MB, 8, INNER)), once(CARRY_SHAPE)

    def early(width, column):
        return pl.BlockSpec((1, rows, width), lambda s: (jnp.minimum(s, MB - 1), 0, column))

    def turning(s):
        return jnp.clip(s - MB, 0, 2 * MB - 1)

    def backing(s):
        return jnp.maximum(s - 3 * MB, 0)

    def block_at(pick, width):
        return pl.BlockSpec((1, BLOCK, width), lambda s: (pick(s) // 2, lax.rem(pick(s), 2), 0))

    back_spec = pl.BlockSpec((1, 1, STATE, INNER), lambda s: (turning(s) // 2, lax.rem(turning(s), 2), 0, 0))
    lanes_struct = struct(MB, TOK_DEV, LANES)
    lane_out, anywhere = block_at(backing, LANES), pl.BlockSpec(memory_space=pl.ANY)
    shard_rows = INNER // shards
    shard_spec = once((shard_rows, D))
    pairs = pltpu.SemaphoreType.DMA((2, shards // 2))
    block_scratch = pltpu.VMEM((BLOCK, INNER), F32)
    (
        v, bc, fr, frp, kept_f, kept_r, dx, normed, d_gate, back_f, back_r, d_out_gain, d_skip, d_v, d_bc, sums, d_log,
        first_grad, gate_grad, enter_f, enter_r, after_f, after_r, w_back,
    ) = call(
        partial(mixer_kernel, levels, shards // 2),
        (5 * MB,),
        [SCALARS, early(INNER, 1), early(LANES, 2 * INNER // LANES), early(LANES, 2 * INNER // LANES + 1), block_at(turning, INNER)]
        + [taps_spec, steps_spec, spread_spec, spread_spec, sum_spec, sum_spec, row_spec, row_spec]
        + [anywhere] * 4,
        [anywhere] * 9
        + [back_spec, back_spec]
        + [row_spec, row_spec, block_at(backing, INNER), lane_out, lane_out, lane_out, shard_spec, shard_spec]
        + [anywhere] * 5,
        [struct(MB, TOK_DEV, INNER, dtype=BF16)]
        + [lanes_struct] * 3
        + [struct(MB, STATE, INNER)] * 2
        + [struct(MB, 8, INNER)]
        + [struct(MB, TOK_DEV, INNER, dtype=BF16)] * 2
        + [struct(MB, 2, STATE, INNER)] * 2
        + [struct(8, INNER)] * 2
        + [struct(MB, TOK_DEV, INNER)]
        + [lanes_struct] * 3
        + [struct(shard_rows, D)] * 2
        + [struct(*CARRY_SHAPE)] * 4
        + [struct(INNER, D, dtype=BF16)],
        scratch=[pltpu.VMEM((MB, TOK_DEV, INNER), BF16)]
        + [pltpu.VMEM((MB, TOK_DEV, LANES), F32)] * 3
        + [pltpu.VMEM((MB, STATE, INNER), F32)] * 2
        + [pltpu.VMEM((MB, 8, INNER), F32)]
        + [pltpu.VMEM((MB, TOK_DEV, INNER), BF16)] * 2
        + [pltpu.VMEM((MB, TOK_DEV, D), BF16)]
        + [pltpu.VMEM((D, MB * TOK_DEV), BF16)] * 2
        + [pltpu.SemaphoreType.DMA((3,)), pltpu.SemaphoreType.DMA((7, MB)), pltpu.SemaphoreType.DMA((2, 2 * MB))]
        + [pltpu.VMEM((1, BLOCK, INNER), F32)] * 2
        + [block_scratch] * 5
        + [pltpu.VMEM((BLOCK, LANES), F32), pltpu.VMEM((2 * MB, BLOCK, INNER), BF16)]
        + [pltpu.VMEM((2 * MB, BLOCK, LANES), F32)] * 2
        + [pltpu.VMEM((INNER, D), BF16), pairs, pairs, pltpu.SemaphoreType.DMA((2,))]
        + shard_buffers(shards)
        + [pltpu.VMEM((MB, 8, INNER), F32), pltpu.SemaphoreType.DMA((2, MB))]
        + [pltpu.VMEM(CARRY_SHAPE, F32)] * 4
        + 2 * carry_buffers(),
        flops=50_000_000_000,
        moved=60_000_000,
        identity=0,
    )(
        info, zx, zx, zx, zx, taps, steps, spread_f, spread_r, sum_f, sum_r, skip, out_scale, w_out, d_branch, d_branch_t, hidden_t
    )

    def turned(grad):
        return grad.reshape(shard_rows, D // shard_rows, shard_rows).transpose(2, 1, 0).reshape(shard_rows, D)

    fits = total_fits(levels, shards, dp_count)
    if fits:
        split = (2, levels, shard_rows // (2 * levels), D)
        first_grad, gate_grad = first_grad.reshape(split), gate_grad.reshape(split)
    else:
        split = (1, 16, LANES)
    unused = jnp.zeros(split, F32)
    edge_buffers = [pltpu.VMEM((MB, HALO, CONV_COLS), F32)] * 3 + [pltpu.SemaphoreType.DMA((2, MB))]
    chunk_spec = pl.BlockSpec((PARTS,) + CARRY_SHAPE[1:], lambda m: (m, 0, 0))
    late, before, last, ending, d_taps, d_small, first_sum, gate_sum = call(
        partial(final_kernel, levels if fits else 0),
        (MB,),
        [SCALARS, zx_vals, zx_bc, zx_dt, taps_spec, steps_spec, wide_spec, lane_spec, lane_spec, lane_spec]
        + [chunk_spec, chunk_spec, state_spec, state_spec]
        + [dx_spec, chunk_spec, chunk_spec, per_micro((2, STATE, INNER)), per_micro((2, STATE, INNER))]
        + [wide_spec, lane_spec, lane_spec, lane_spec, spread_spec, spread_spec, sum_spec, sum_spec, once(split), once(split)],
        [per_micro((TOK_DEV, LATE)), per_micro((HALO, CONV_COLS)), per_micro((HALO, CONV_COLS)), once((MB, HALO, CONV_COLS)), once((8, CONV_COLS)), once((8, LANES))]
        + [once(split[1:])] * 2,
        [
            struct(MB, TOK_DEV, LATE, dtype=BF16),
            struct(MB, HALO, CONV_COLS),
            struct(MB, HALO, CONV_COLS),
            struct(MB, HALO, CONV_COLS),
            struct(8, CONV_COLS),
            struct(8, LANES),
            struct(*split[1:], dtype=BF16),
            struct(*split[1:], dtype=BF16),
        ],
        scratch=[pltpu.VMEM((TOK_DEV, CONV_COLS), F32)]
        + (2 * sum_buffers(*split[1:]) + sum_semaphores(levels, 2) + edge_buffers if fits else []),
        flops=2_000_000_000,
        moved=40_000_000,
        identity=3 if fits else None,
    )(
        info, zx, zx, zx, taps, steps, v, bc, fr, frp, enter_f, enter_r, kept_f, kept_r, dx, after_f, after_r, back_f, back_r,
        d_v, d_bc, sums, d_log, spread_f, spread_r, sum_f, sum_r, first_grad if fits else unused, gate_grad if fits else unused,
    )
    d_gate = d_gate.reshape(MB * TOK_DEV, INNER)
    normed = normed.reshape(MB * TOK_DEV, INNER)
    late = late.reshape(MB * TOK_DEV, LATE)
    if fits:
        flat = [part.reshape(MB * TOK_DEV, D) for part in (x, cot)]
        grads, first_sum = totals(
            (info, hidden_t, late, w_all, d_gate, *flat, w_back, normed, gain_in, first_sum, gate_sum, ending)
            + (d_taps, d_out_gain, d_skip, d_small, sum_f),
            2,
        )
        return (*grads, first_sum)

    ending = (last + shift(before, -1)).astype(BF16)
    late = lax.dynamic_update_slice(late.reshape(MB, TOK_DEV, LATE), ending, (0, TOK_DEV - HALO, 0)).reshape(MB * TOK_DEV, LATE)

    def owned(grad):
        return lax.psum_scatter(grad, "fsdp", scatter_dimension=0, tiled=True)

    places = base + jnp.arange(TOK_DEV, dtype=jnp.int32)
    first = lengths[:, :1]
    start = (first + BLOCK - 1) // BLOCK * BLOCK
    valid = (places[None] < first) | (places[None] >= start) & (places[None] < start + lengths[:, 1:])
    valid = valid[..., None]
    branch = dot(normed, w_back).reshape(MB, TOK_DEV, D)
    x_rows = x.astype(F32)
    layer_out = jnp.where(valid, x_rows + branch, 0.0).astype(BF16)
    late_grad = dot(hidden_t, late)
    d_hidden = dot(d_gate, w_all[:, :INNER], COLS) + dot(late, w_all[:, INNER:], COLS)
    d_hidden = d_hidden.reshape(MB, TOK_DEV, D)
    scale = rms(x_rows)
    d_norm_gain = jnp.sum(d_hidden * x_rows * scale, axis=(0, 1))
    pulled = d_hidden * gain_in
    d_x = scale * pulled - x_rows * (scale * scale * scale) * jnp.mean(x_rows * pulled, axis=-1, keepdims=True)
    tokens_grad = d_x + jnp.where(valid, cot.astype(F32), 0.0)
    d_skip_gain = jnp.sum(d_skip[0].reshape(HEADS, HEAD_DIM), axis=1)
    d_decay = d_small[1, :HEADS] + d_small[1, HEADS : 2 * HEADS]
    small = (d_norm_gain, d_taps[:CONV], d_taps[CONV], d_small[0, : 2 * HEADS], d_decay, d_skip_gain, d_out_gain[0])
    w_out_grad, gate_grad, late_grad = lax.psum((first_grad, gate_grad, owned(late_grad)), "dp")
    summed = lax.psum(scatter_small(small, shards), ("dp", "fsdp"))
    own = lax.dynamic_slice_in_dim(summed, lax.axis_index("fsdp"), 1, axis=0)[0]
    pieces = []
    at = 0
    for part in (norm_gain, conv_weight, conv_bias, step_bias, decay_log, skip_gain, out_gain):
        pieces.append(own[at : at + part.size].reshape(part.shape))
        at += part.size
    gate_grad = jnp.concatenate([gate_grad[: shard_rows // 2], gate_grad[shard_rows // 2 :]], axis=1)
    w_inner_grad = jnp.concatenate([gate_grad, late_grad[:, :INNER]], axis=1)
    w_state_grad = late_grad[:, INNER : INNER + 2 * STATE]
    w_step_grad = late_grad[:, INNER + LANES : INNER + LANES + 2 * HEADS]
    grads = pieces[:1] + [w_inner_grad, w_state_grad, w_step_grad] + pieces[1:] + [turned(w_out_grad)]
    return (layer_out[:, None], tokens_grad[:, None], *grads)


def solution(mesh):
    rows, vector, matrix = P(None, "fsdp", "dp", None), P("fsdp"), P("fsdp", None)
    weights = (vector, matrix, matrix, matrix, P(None, "fsdp"), vector, vector, vector, vector, vector, matrix)
    return jax.shard_map(
        on_device,
        mesh=mesh,
        in_specs=(rows, P(None, "fsdp", None)) + weights + (rows,),
        out_specs=(rows, rows) + weights,
        check_vma=False,
    )
```

```python
from functools import partial

import jax
import jax.numpy as jnp
from jax import lax
from jax.experimental import pallas as pl
from jax.experimental.pallas import tpu as pltpu
from jax.sharding import PartitionSpec as P

D = 768
INNER = 1536
HEADS = 24
HEAD_DIM = 64
STATE = 64
CONV = 4
BLOCK = 128
MB = 3
TOK_DEV = 256
HALO = 8
LANES = 128
CONV_COLS = INNER + 2 * STATE
WIDE = 2 * INNER + 2 * LANES
LATE = INNER + 2 * LANES
PAIRS = HEADS // 2
PARTS = 4
CHUNKS = MB * PARTS
LAG = 2
TURNS = 3
TURN_PAIRS = PAIRS // TURNS
CUTS = 3
EPSILON = 1e-05
HIGHEST = lax.Precision.HIGHEST
F32 = jnp.float32
BF16 = jnp.bfloat16
SENT = F32
ROWS = ((0,), (0,))
COLS = ((1,), (1,))
INNER_DIMS = ((1,), (0,))
VMEM_LIMIT = 60 * 1024 * 1024
SCALARS = pl.BlockSpec(memory_space=pltpu.SMEM)


def dot(left, right, dims=INNER_DIMS, precision=None):
    return lax.dot_general(left, right, (dims, ((), ())), precision=precision, preferred_element_type=F32)


def halves(value):
    high = value.astype(BF16)
    return high, (value - high.astype(F32)).astype(BF16)


def spread_operand(value):
    high, low = halves(value)
    return jnp.concatenate([high, low], axis=1)


def by_lane(first, second):
    low = iota(first.shape, 1) < STATE
    twice = jnp.where(low, first, second)
    high = twice.astype(BF16).astype(F32)
    return jnp.where(low, high, twice - high)


def twice(value, axis):
    return jnp.concatenate([value, value], axis=axis)


def fold(value):
    return value[:STATE] + value[STATE:]


def head_sums(value, selector):
    high, low = halves(value)
    return dot(high, selector) + dot(low, selector)


def sigmoid(value):
    return 1.0 / (1.0 + jnp.exp(-value))


def softplus(value):
    tail = jnp.exp(-jnp.abs(value))
    series = tail * (1.0 - tail * (0.5 - tail * (1.0 / 3.0 - 0.25 * tail)))
    return jnp.maximum(value, 0.0) + jnp.where(tail < 0.01, series, jnp.log(1.0 + tail))


def iota(shape, dim):
    return lax.broadcasted_iota(jnp.int32, shape, dim)


def span_scalars(info, m):
    first = info[2 * m]
    start = ((first + (BLOCK - 1)) >> 7) << 7
    return first, start, start + info[2 * m + 1], info[2 * MB], info[2 * MB + 1]


def keeps(info, m):
    _, start, _, base, span = span_scalars(info, m)

    def keep(position):
        begins = (position == 0) | (position == start) | (position >= span)
        return jnp.where(begins, 0.0, 1.0).astype(F32)

    forward = [keep(base), keep(base + BLOCK)]
    reverse = [keep(base + BLOCK), keep(base + 2 * BLOCK)]
    return forward, reverse


def row_masks(info, m, shape, offset=0):
    first, start, end, base, _ = span_scalars(info, m)
    place = iota(shape, 0) + (base + offset)
    inside = (place < first) | ((place >= start) & (place < end))
    offset = jnp.where(place >= start, place - start, place)
    return inside.astype(F32), [(offset >= k).astype(F32) for k in range(CONV)]


def conv_windows(ref, cols):
    main = ref[0, :TOK_DEV, cols]
    halo = ref[0, TOK_DEV:, cols]
    whole = jnp.concatenate([halo, main], axis=0)
    return [main] + [whole[HALO - k : HALO - k + TOK_DEV] for k in range(1, CONV)]


def conv_value(windows, masks, taps, cols):
    value = taps[CONV : CONV + 1, cols] + taps[0:1, cols] * windows[0]
    for k in range(1, CONV):
        value = value + taps[k : k + 1, cols] * (windows[k] * masks[k])
    return value


def gather_kernel(
    count, columns, info, x_hbm, cot_hbm, w_inner, w_state, w_step, mine,
    w_all_out, hidden_out, hidden_t_out, d_branch_out, d_branch_t_out, spread_f_out, spread_r_out, sum_f_out, sum_r_out,
    norm, taps, steps, skip, scale,
    x_in, cot_in, w_all, hidden, hidden_t, d_branch, d_branch_t, spread_f, spread_r, sum_f, sum_r, load_sems, keep_sems, row_sems,
    halo, small, skip_row, halo_sems, small_sems, x_sems, y_sems, mate_sems, own_sems,
):
    me, part = lax.axis_index("dp"), lax.axis_index("fsdp")
    side, core, column = lax.rem(me, 2), lax.rem(part, 2), part // 2
    partner, mate = me + 1 - 2 * side, part + 1 - 2 * core
    has_next, has_last = me < count - 1, me > 0
    shards = 2 * columns
    rows = w_inner.shape[0]
    chunk = rows // (2 * CUTS)
    here = pl.ds(pl.multiple_of(part * rows, 16), rows)
    results = (
        (hidden, hidden_out), (hidden_t, hidden_t_out), (d_branch, d_branch_out), (d_branch_t, d_branch_t_out),
        (spread_f, spread_f_out), (spread_r, spread_r_out), (sum_f, sum_f_out), (sum_r, sum_r_out),
    )

    def load(i):
        source = (w_inner, x_hbm, cot_hbm)[i]
        return pltpu.make_async_copy(source, (w_all.at[here, : 2 * INNER], x_in, cot_in)[i], load_sems.at[i])

    def keep(i):
        return pltpu.make_async_copy(*results[i], keep_sems.at[i])

    def keep_rows(owner):
        at = pl.ds(pl.multiple_of(owner * rows, 16), rows)
        return pltpu.make_async_copy(w_all.at[at], w_all_out.at[at], row_sems.at[owner])

    for i in range(3):
        load(i).start()

    barrier = pltpu.get_barrier_semaphore()

    @pl.when(has_next)
    def _():
        pl.semaphore_signal(barrier, inc=1, device_id={"dp": me + 1})

    @pl.when(has_last)
    def _():
        pl.semaphore_signal(barrier, inc=1, device_id={"dp": me - 1})

    def other(d):
        return lax.rem(part + d + shards, shards)

    def column_at(d):
        return lax.rem(column + d + columns, columns)

    for d in range(1, shards):
        pl.semaphore_signal(barrier, inc=1, device_id={"fsdp": other(d)})
    pl.semaphore_wait(barrier, shards - 1 + has_next.astype(jnp.int32) + has_last.astype(jnp.int32))

    def remote(source, target, sems, k, where):
        return pltpu.make_async_remote_copy(
            src_ref=source, dst_ref=target, send_sem=sems.at[0, k], recv_sem=sems.at[1, k], device_id=where
        )

    def rows_of(owner, half, k):
        return w_all.at[pl.ds(pl.multiple_of(owner * rows + half * (rows // 2) + k * chunk, 16), chunk)]

    edge = remote(x_in.at[:, pl.ds(TOK_DEV - 2 * HALO, 2 * HALO)], halo, halo_sems, 0, {"dp": me + 1})

    def small_copy(d, theirs):
        return remote(mine, small.at[other(-d) if theirs else part], small_sems, d, {"fsdp": other(d)})

    def x_copy(k, d):
        at = rows_of(part, side, k)
        return remote(at, at, x_sems, k * columns + d, {"fsdp": 2 * column_at(d) + core})

    def x_arrival(k, d):
        at = rows_of(2 * column_at(-d) + core, side, k)
        return remote(at, at, x_sems, k * columns + d, {"fsdp": part})

    def y_copy(k, d, theirs):
        at = rows_of(2 * column_at(-d) + core, 1 - side if theirs else side, k)
        return remote(at, at, y_sems, k * columns + d, {"dp": partner})

    def mate_copy(k, d, half, theirs):
        at = rows_of(2 * column_at(-d) + (1 - core if theirs else core), half, k)
        return remote(at, at, mate_sems, (k * columns + d) * 2 + half, {"fsdp": mate})

    def own_copy(owner):
        at = w_all.at[pl.ds(pl.multiple_of(owner * rows, 16), rows)]
        return remote(at, at, own_sems, 0, {"fsdp": mate})

    for d in range(1, shards):
        small_copy(d, False).start()
    w_all[here, 2 * INNER : 2 * INNER + 2 * STATE] = w_state[...]
    w_all[here, 2 * INNER + 2 * STATE :] = jnp.concatenate(
        [w_step[...].astype(F32), jnp.zeros((rows, LANES - 2 * HEADS), F32)], axis=1
    ).astype(BF16)
    load(0).wait()
    for k in range(2):
        for d in range(1, columns):
            x_copy(k, d).start()
    own_copy(part).start()
    keep_rows(part).start()
    load(1).wait()
    load(2).wait()

    @pl.when(has_next)
    def _():
        edge.start()

    @pl.when(me == 0)
    def _():
        halo[...] = jnp.zeros_like(halo)

    def chosen(mask):
        return jnp.where(mask, 1.0, 0.0).astype(BF16)

    shape = (2 * LANES, INNER)
    lane_of, head_of = iota(shape, 0) & (LANES - 1), iota(shape, 1) >> 6
    spread_f[...] = chosen(lane_of == head_of)
    spread_r[...] = chosen(lane_of == head_of + HEADS)
    shape = (INNER, LANES)
    lane_of, head_of = iota(shape, 1), iota(shape, 0) >> 6
    sum_f[...] = chosen(lane_of == head_of)
    sum_r[...] = chosen(lane_of == head_of + HEADS)
    for m in range(MB):
        valid = row_masks(info, m, (TOK_DEV, D))[0]
        value = jnp.where(valid > 0.0, cot_in[m].astype(F32), 0.0)
        d_branch[m] = value.astype(BF16)
        d_branch_t[:, m * TOK_DEV : (m + 1) * TOK_DEV] = jnp.transpose(value).astype(BF16)
    for i in range(2, 8):
        keep(i).start()

    for ref in (norm, taps, steps, skip_row):
        ref[...] = jnp.zeros_like(ref)
    for d in range(1, shards):
        small_copy(d, True).wait_recv()
    small[part] = mine[...]
    wide, heads = CONV_COLS // shards, HEADS // shards
    at = 0
    fields = [(taps, k, 1, wide) for k in range(CONV + 1)] + [(scale, 0, 8, INNER // shards), (norm, 0, 1, rows)]
    fields += [(steps, 0, 1, 2 * heads), (steps, 1, 1, heads), (skip_row, 0, 1, heads)]
    for ref, row, height, width in fields:
        done = 0
        while done < width:
            line, lane = divmod(at + done, LANES)
            size = min(width - done, LANES - lane)
            for f in range(shards):
                value = small[f, line : line + 1, lane : lane + size].astype(F32)
                if ref is steps and row == 1:
                    value = jnp.exp(value)
                    ref[row : row + 1, HEADS + f * width + done : HEADS + f * width + done + size] = value
                value = jnp.broadcast_to(value, (height, size))
                ref[row : row + height, f * width + done : f * width + done + size] = value
            done += size
        at += width
    skip[...] = dot(spread_operand(skip_row[...]), spread_f[...])

    @pl.when(has_last)
    def _():
        edge.wait_recv()

    def normalise(values):
        root = lax.rsqrt(jnp.mean(values * values, axis=1, keepdims=True) + EPSILON)
        return values * root * norm[...]

    def hide(m):
        value = normalise(x_in[m].astype(F32))
        hidden[m, :TOK_DEV] = value.astype(BF16)
        hidden_t[:, m * TOK_DEV : (m + 1) * TOK_DEV] = jnp.transpose(value).astype(BF16)
        hidden[m, TOK_DEV:] = normalise(halo[m].astype(F32)[HALO:]).astype(BF16)

    def pass_on(k):
        for d in range(1, columns):
            y_copy(k, d, True).wait_recv()

            @pl.when(side == 0)
            def _():
                mate_copy(k, d, 1, False).start()

            @pl.when(side == 1)
            def _():
                mate_copy(k, d, 0, False).start()

    for k in range(CUTS):
        if k < MB:
            hide(k)
        for d in range(1, columns):
            x_arrival(k, d).wait_recv()
            y_copy(k, d, False).start()

            @pl.when(side == 0)
            def _():
                mate_copy(k, d, 0, False).start()

            @pl.when(side == 1)
            def _():
                mate_copy(k, d, 1, False).start()

            if k + 2 < CUTS:
                x_copy(k + 2, d).start()
        if k > 0:
            pass_on(k - 1)
    for m in range(CUTS, MB):
        hide(m)
    keep(0).start()
    keep(1).start()
    own_copy(mate).wait_recv()
    keep_rows(mate).start()
    pass_on(CUTS - 1)
    for d in range(1, columns):
        keep_rows(2 * column_at(d) + core).start()
    own_copy(part).wait_send()
    for k in range(CUTS):
        for d in range(1, columns):
            for half in range(2):
                mate_copy(k, d, half, True).wait_recv()
                mate_copy(k, d, half, False).wait_send()
            x_copy(k, d).wait_send()
            y_copy(k, d, False).wait_send()
    for d in range(1, columns):
        keep_rows(2 * column_at(d) + 1 - core).start()
    for d in range(1, shards):
        small_copy(d, False).wait_send()
    for owner in range(shards):
        keep_rows(owner).wait()
    for i in range(8):
        keep(i).wait()

    @pl.when(has_next)
    def _():
        edge.wait_send()


def gather_weights(info, x, cot, w_inner, w_state, w_step, mine, identity):
    count, shards = lax.axis_size("dp"), lax.axis_size("fsdp")
    columns = shards // 2
    whole = pl.BlockSpec(memory_space=pltpu.VMEM)
    pairs = CUTS * columns
    anywhere = pl.BlockSpec(memory_space=pl.ANY)
    results = [
        struct(D, WIDE, dtype=BF16), struct(MB, TOK_DEV + HALO, D, dtype=BF16), struct(D, MB * TOK_DEV, dtype=BF16),
        struct(MB, TOK_DEV, D, dtype=BF16), struct(D, MB * TOK_DEV, dtype=BF16),
        struct(2 * LANES, INNER, dtype=BF16), struct(2 * LANES, INNER, dtype=BF16),
        struct(INNER, LANES, dtype=BF16), struct(INNER, LANES, dtype=BF16),
    ]
    rows = pltpu.VMEM((MB, TOK_DEV, D), BF16)
    outs = pl.pallas_call(
        partial(gather_kernel, count, columns),
        in_specs=[SCALARS, anywhere, anywhere, anywhere, whole, whole, whole],
        out_specs=[anywhere] * 9 + [whole] * 5,
        out_shape=results + [struct(1, D), struct(8, CONV_COLS), struct(8, LANES), struct(8, INNER), struct(8, INNER)],
        scratch_shapes=[rows, rows]
        + [pltpu.VMEM(result.shape, result.dtype) for result in results]
        + [pltpu.SemaphoreType.DMA((3,)), pltpu.SemaphoreType.DMA((8,)), pltpu.SemaphoreType.DMA((shards,))]
        + [
            pltpu.VMEM((MB, 2 * HALO, D), BF16), pltpu.VMEM((shards,) + mine.shape, BF16), pltpu.VMEM((8, LANES), F32),
            pltpu.SemaphoreType.DMA((2, 1)), pltpu.SemaphoreType.DMA((2, shards)), pltpu.SemaphoreType.DMA((2, pairs)),
            pltpu.SemaphoreType.DMA((2, pairs)), pltpu.SemaphoreType.DMA((2, 2 * pairs)), pltpu.SemaphoreType.DMA((2, 1)),
        ],
        compiler_params=pltpu.CompilerParams(vmem_limit_bytes=VMEM_LIMIT, collective_id=identity, has_side_effects=True),
    )(info, x, cot, w_inner, w_state, w_step, mine)
    return outs[:5] + outs[9:] + outs[5:9]


def front_body(m, info, vals, bc, dt, taps, steps, spread_f, spread_r, v_out, bc_out, fr_out, frp_out, tot_f, tot_r, kept_f, kept_r, dx_out):
    valid, masks = row_masks(info, m, (TOK_DEV, LANES))
    for chunk in range(PAIRS + 1):
        cols = pl.ds(chunk * LANES, LANES)
        source, own = (vals, cols) if chunk < PAIRS else (bc, pl.ds(0, LANES))
        value = conv_value(conv_windows(source, own), masks, taps, cols)
        value = valid * (value * sigmoid(value))
        if chunk < PAIRS:
            v_out[m, :, cols] = value.astype(BF16)
        else:
            bc_out[m] = value
    lane = iota((BLOCK, LANES), 1)
    rows = iota((BLOCK, BLOCK), 0)
    columns = iota((BLOCK, BLOCK), 1)
    lower = (rows >= columns).astype(F32)
    upper = (rows <= columns).astype(F32)
    forward, reverse = keeps(info, m)
    ends = []
    tails = []
    inputs = []
    for b in range(2):
        span = pl.ds(b * BLOCK, BLOCK)
        step = softplus(dt[0, span, :] + steps[0:1, :])
        log = -step * steps[1:2, :]
        summed = jnp.where(lane < HEADS, dot(lower, log, precision=HIGHEST), dot(upper, log, precision=HIGHEST))
        shifted = summed - jnp.log(step)
        fr_out[m, span, :] = summed
        frp_out[m, span, :] = shifted
        end = jnp.where(lane[:1] < HEADS, summed[BLOCK - 1 :], summed[:1])
        ends.append(jnp.exp(end))
        tails.append(spread_operand(jnp.where(lane < 2 * HEADS, jnp.exp(end - shifted), 0.0)))
        acts = bc_out[m, span, :]
        inputs.append(twice(jnp.transpose(by_lane(acts, swapped(acts))).astype(BF16), 1))
    ends = spread_operand(jnp.concatenate(ends + [jnp.zeros((6, LANES), F32)], axis=0))
    width = 2 * LANES
    for chunk in range(INNER // width):
        cols = pl.ds(chunk * width, width)
        decay_f = dot(ends, spread_f[:, cols])
        decay_r = dot(ends, spread_r[:, cols])
        parts_f = []
        parts_r = []
        for b in range(2):
            v = v_out[m, pl.ds(b * BLOCK, BLOCK), cols].astype(F32)
            parts_f.append(fold(dot(inputs[b], stacked(dot(tails[b], spread_f[:, cols]) * v))))
            parts_r.append(fold(dot(inputs[b], stacked(dot(tails[b], spread_r[:, cols]) * v))))
        kept_f[m, :, cols] = parts_f[0]
        kept_r[m, :, cols] = parts_r[1]
        total_f = parts_f[1] + (forward[1] * decay_f[1:2]) * parts_f[0]
        total_r = parts_r[0] + (reverse[0] * decay_r[0:1]) * parts_r[1]
        for k in range(PARTS):
            part = slice(k * STATE // PARTS, (k + 1) * STATE // PARTS)
            tot_f[PARTS * m + k, :, cols] = total_f[part]
            tot_r[PARTS * m + k, :, cols] = total_r[part]
        dx_out[m, 0:2, cols] = decay_f[0:2]
        dx_out[m, 2:4, cols] = decay_r[0:2]
        dx_out[m, 4:5, cols] = (forward[0] * forward[1]) * (decay_f[0:1] * decay_f[1:2])
        dx_out[m, 5:6, cols] = (reverse[0] * reverse[1]) * (decay_r[0:1] * decay_r[1:2])
        dx_out[m, 6:8, cols] = jnp.zeros((2, width), F32)


def stacked(value):
    return jnp.concatenate(halves(value), axis=0)


def doubled(value):
    high, low = halves(value)
    return jnp.concatenate([high, high, low, low], axis=0)


def pair_stack(value):
    lane = iota(value.shape, 1)
    zero = jnp.zeros_like(value)
    return jnp.concatenate([jnp.where(lane < HEAD_DIM, value, zero), jnp.where(lane < HEAD_DIM, zero, value)], axis=0)


def swapped(value):
    return pltpu.roll(value, STATE, axis=1)


def intra_body(m, b, v, bc, fr, frp, skip, y_out):
    span = pl.ds(pl.multiple_of(b * BLOCK, BLOCK), BLOCK)
    rows = iota((BLOCK, BLOCK), 0)
    columns = iota((BLOCK, BLOCK), 1)
    lower = rows > columns
    acts = bc[m, span, :]
    outs = jnp.where(columns < STATE, swapped(acts), 0.0)
    scores = jnp.where(rows == columns, 0.0, dot(outs, acts, COLS, HIGHEST))
    cum = fr[m, span, :]
    shifted = jnp.transpose(frp[m, span, :])
    for pair in range(PAIRS):
        mats = []
        for h in (2 * pair, 2 * pair + 1):
            r = HEADS + h
            gap = jnp.where(lower, cum[:, h : h + 1] - shifted[h : h + 1], cum[:, r : r + 1] - shifted[r : r + 1])
            mats.append((jnp.exp(gap) * scores).astype(BF16))
        cols = pl.ds(pair * LANES, LANES)
        value = v[m, span, cols]
        y = dot(jnp.concatenate(mats, axis=1), pair_stack(value))
        y_out[0, :, cols] = y + skip[0:1, cols] * value.astype(F32)


def entering(m, b, cols, forward, reverse, enter_f, enter_r, kept_f, kept_r, dx):
    first_f = forward[0] * jnp.concatenate([enter_f[PARTS * m + k, :, cols] for k in range(PARTS)], axis=0)
    last_r = reverse[1] * jnp.concatenate([enter_r[PARTS * m + k, :, cols] for k in range(PARTS)], axis=0)
    state_f = jnp.where(b == 0, first_f, forward[1] * (dx[m, 0:1, cols] * first_f + kept_f[m, :, cols]))
    state_r = jnp.where(b == 1, last_r, reverse[0] * (dx[m, 3:4, cols] * last_r + kept_r[m, :, cols]))
    return state_f, state_r


def middle_body(
    slot, info, y, gate, d_normed, v, bc, fr, enter_f, enter_r, kept_f, kept_r, dx, gain, spread_f, spread_r, sum_f, sum_r,
    normed, d_mixed, d_gate, back_f, back_r, leave_f, leave_r, d_outs, read_out, d_gain, d_skip, mixed_s, part_f, part_r, exp_f, exp_r,
):
    m, b = slot // 2, lax.rem(slot, 2)
    span = pl.ds(pl.multiple_of(b * BLOCK, BLOCK), BLOCK)
    forward, reverse = keeps(info, m)
    lane = iota((BLOCK, LANES), 1)
    acts = bc[m, span, :]
    outs = by_lane(swapped(acts), acts)
    outs_t = twice(jnp.transpose(outs).astype(BF16), 1)
    outs = twice(outs.astype(BF16), 1)
    grown = spread_operand(jnp.where(lane < 2 * HEADS, jnp.exp(fr[m, span, :]), 0.0))
    width = 2 * LANES
    chunks = INNER // width
    squares = jnp.zeros((BLOCK, 1), F32)
    cross = jnp.zeros((BLOCK, 1), F32)
    for chunk in range(chunks):
        cols = pl.ds(chunk * width, width)
        state_f, state_r = entering(m, b, cols, forward, reverse, enter_f, enter_r, kept_f, kept_r, dx)
        ef = dot(grown, spread_f[:, cols])
        er = dot(grown, spread_r[:, cols])
        carried_f = ef * dot(outs, doubled(state_f))
        carried_r = er * dot(outs, doubled(state_r))
        mixed = y[0, :, cols] + carried_f + carried_r
        exp_f[:, cols] = ef
        exp_r[:, cols] = er
        part_f[:, cols] = carried_f
        part_r[:, cols] = carried_r
        mixed_s[:, cols] = mixed
        g = gate[0, :, cols]
        gated = mixed * (g * sigmoid(g))
        squares = squares + jnp.sum(gated * gated, axis=1, keepdims=True)
        cross = cross + jnp.sum(gated * gain[0:1, cols] * d_normed[0, :, cols], axis=1, keepdims=True)
    scale = lax.rsqrt(squares * (1.0 / INNER) + EPSILON)
    pull = scale * scale * scale * (cross * (1.0 / INNER))
    d_o = jnp.zeros((BLOCK, LANES), F32)
    reads = jnp.zeros((BLOCK, LANES), F32)

    @pl.when((m == 0) & (b == 0))
    def _():
        d_gain[...] = jnp.zeros_like(d_gain)
        d_skip[...] = jnp.zeros_like(d_skip)

    @pl.when(b == 0)
    def _():
        for k in range(PARTS):
            leave_f[PARTS * m + k] = jnp.zeros(CARRY_SHAPE[1:], F32)
            leave_r[PARTS * m + k] = jnp.zeros(CARRY_SHAPE[1:], F32)

    for chunk in range(chunks):
        cols = pl.ds(chunk * width, width)
        g = gate[0, :, cols]
        sig = sigmoid(g)
        silu = g * sig
        mixed = mixed_s[:, cols]
        gated = mixed * silu
        dy = d_normed[0, :, cols]
        scaled = gated * scale
        normed[m, span, cols] = (scaled * gain[0:1, cols]).astype(BF16)
        d_gain[0:1, cols] += jnp.sum(dy * scaled, axis=0, keepdims=True)
        d_gated = scale * gain[0:1, cols] * dy - gated * pull
        dm = d_gated * silu
        d_gate[m, span, cols] = (d_gated * mixed * sig * (1.0 + g * (1.0 - sig))).astype(BF16)
        d_mixed[slot, :, cols] = dm.astype(BF16)
        d_skip[0:1, cols] += jnp.sum(dm * v[m, span, cols].astype(F32), axis=0, keepdims=True)
        state_f, state_r = entering(m, b, cols, forward, reverse, enter_f, enter_r, kept_f, kept_r, dx)
        grown_f = exp_f[:, cols] * dm
        grown_r = exp_r[:, cols] * dm
        local_f = fold(dot(outs_t, stacked(grown_f)))
        local_r = fold(dot(outs_t, stacked(grown_r)))
        back_f[0, 0, :, cols] = local_f
        back_r[0, 0, :, cols] = local_r
        weight_f = jnp.where(b == 0, forward[0], (forward[0] * forward[1]) * dx[m, 0:1, cols])
        weight_r = jnp.where(b == 0, (reverse[0] * reverse[1]) * dx[m, 3:4, cols], reverse[1])
        local_f = weight_f * local_f
        local_r = weight_r * local_r
        for k in range(PARTS):
            part = slice(k * STATE // PARTS, (k + 1) * STATE // PARTS)
            leave_f[PARTS * m + k, :, cols] += local_f[part]
            leave_r[PARTS * m + k, :, cols] += local_r[part]
        d_o = d_o + dot(spread_operand(grown_f), twice(stacked(state_f), 1), COLS)
        d_o = d_o + dot(spread_operand(grown_r), twice(stacked(state_r), 1), COLS)
        reads = reads + head_sums(dm * part_f[:, cols], sum_f[cols, :]) + head_sums(dm * part_r[:, cols], sum_r[cols, :])
    d_outs[slot] = jnp.where(lane < STATE, 0.0, d_o + swapped(d_o))
    read_out[slot] = reads


def intra_back_body(slot, v, d_mixed, bc, fr, frp, skip, d_outs, read_out, d_v, d_bc, sums, d_log, row_s, turn):
    m, b = slot // 2, lax.rem(slot, 2)
    span = pl.ds(pl.multiple_of(b * BLOCK, BLOCK), BLOCK)
    rows = iota((BLOCK, BLOCK), 0)
    columns = iota((BLOCK, BLOCK), 1)
    ahead = rows < columns
    acts = bc[m, span, :]
    low = columns < STATE
    turned = swapped(acts)
    outs = jnp.where(low, turned, 0.0)
    scores = jnp.where(rows == columns, 0.0, dot(acts, outs, COLS, HIGHEST))
    cum = jnp.transpose(fr[m, span, :])
    shifted = frp[m, span, :]
    d_scores = jnp.zeros((BLOCK, BLOCK), F32)
    gathered = jnp.zeros((BLOCK, LANES), F32)

    row_s[...] = jnp.zeros_like(row_s)
    for pair in range(PAIRS):
        cols = pl.ds(pair * LANES, LANES)
        value = v[m, span, cols]
        dm = d_mixed[slot, :, cols]
        products = dot(pair_stack(value), dm, COLS)
        mats = []
        for side in range(2):
            h = 2 * pair + side
            r = HEADS + h
            gap = jnp.where(ahead, cum[h : h + 1] - shifted[:, h : h + 1], cum[r : r + 1] - shifted[:, r : r + 1])
            weight = jnp.exp(gap)
            mats.append((weight * scores).astype(BF16))
            reach = products[side * BLOCK : (side + 1) * BLOCK] * weight
            d_scores = d_scores + reach
            both = reach * scores
            first = jnp.where(ahead, both, 0.0)
            second = both - first
            gathered = jnp.where(columns == h, jnp.sum(first, axis=1, keepdims=True), gathered)
            gathered = jnp.where(columns == r, jnp.sum(second, axis=1, keepdims=True), gathered)
            row_s[h : h + 1, :] = jnp.sum(first, axis=0, keepdims=True)
            row_s[r : r + 1, :] = jnp.sum(second, axis=0, keepdims=True)
        dmf = dm.astype(F32)
        d_v[0, :, cols] = dot(jnp.concatenate(mats, axis=1), pair_stack(dm)) + skip[0:1, cols] * dmf
        if pair % TURN_PAIRS == TURN_PAIRS - 1:
            turn(pair // TURN_PAIRS)
    d_scores = jnp.where(rows == columns, 0.0, d_scores)
    ins = jnp.where(low, 0.0, turned)
    d_bc[0] = dot(d_scores, outs, precision=HIGHEST) + dot(jnp.transpose(d_scores), ins, precision=HIGHEST) + d_outs[slot]
    sums[0] = gathered
    d_log[0] = jnp.transpose(row_s[...]) - gathered + read_out[slot]


def shard_steps(columns, normed, d_branch_t, hidden_t, d_gate, outs, buffers):
    put, gots, cross_puts, cross_gots, mate_sems, cross_sems = buffers
    part = lax.axis_index("fsdp")
    core, column = lax.rem(part, 2), part // 2
    mate = part + 1 - 2 * core
    rows = put.shape[1]

    def column_at(d):
        return lax.rem(column + d + columns, columns)

    def remote(source, target, sems, k, device):
        return pltpu.make_async_remote_copy(
            src_ref=source, dst_ref=target, send_sem=sems.at[0, k], recv_sem=sems.at[1, k], device_id={"fsdp": device}
        )

    def to_mate(which, x):
        return remote(put.at[x], gots[which].at[x], mate_sems, which * columns + x, mate)

    def across(which, d):
        target = 2 * column_at(d) + core
        return remote(cross_puts[which].at[d - 1], cross_gots[which].at[d - 1], cross_sems, which * columns + d, target)

    def piece(which, owner, h):
        half = rows // 2
        if which == 0:
            group = 1 if rows % LANES == 0 else 2
            at = pl.ds(pl.multiple_of((owner // group) * (group * rows), LANES), group * rows)
            total = sum(
                dot(d_branch_t[h * rows : (h + 1) * rows, m * TOK_DEV : (m + 1) * TOK_DEV], normed[m, :, at]) for m in range(MB)
            )
            return total if group == 1 else jnp.where(lax.rem(owner, 2) == 0, total[:, :rows], total[:, rows:])
        at = pl.ds(pl.multiple_of(owner * half, 16), half)
        return sum(
            dot(hidden_t[at, m * TOK_DEV : (m + 1) * TOK_DEV], d_gate[m, :, h * D : (h + 1) * D]) for m in range(MB)
        )

    def view(which, h):
        return (slice(None), slice(h * rows, (h + 1) * rows)) if which == 0 else (slice(h * rows // 2, (h + 1) * rows // 2),)

    def count(which):
        return D // rows if which == 0 else 2

    def greet(barrier):
        pl.semaphore_signal(barrier, inc=1, device_id={"fsdp": mate})
        for d in range(1, columns):
            pl.semaphore_signal(barrier, inc=1, device_id={"fsdp": 2 * column_at(d) + core})
        return columns

    def foreign(which):
        for x in range(columns):
            if which == 1:
                to_mate(0, x).wait_send()
            for h in range(count(which)):
                put[(x,) + view(which, h)] = piece(which, 2 * x + 1 - core, h).astype(BF16)
            to_mate(which, x).start()

    def local(which):
        for x in range(columns):
            to_mate(which, x).wait_recv()
        for d in list(range(1, columns)) + [0]:
            x = column_at(d)
            for h in range(count(which)):
                at = view(which, h)
                value = piece(which, 2 * x + core, h) + gots[which][(x,) + at].astype(F32)
                if d == 0:
                    outs[which][at] = value
                else:
                    cross_puts[which][(d - 1,) + at] = value.astype(BF16)
            if d > 0:
                across(which, d).start()

    def close():
        for which in range(2):
            for d in range(1, columns):
                across(which, d).wait()
                outs[which][...] += cross_gots[which][d - 1].astype(F32)
        for x in range(columns):
            to_mate(1, x).wait_send()

    return greet, foreign, local, close


def shard_buffers(shards):
    columns, shape = shards // 2, (INNER // shards, D)
    low, few = pltpu.VMEM((columns,) + shape, BF16), pltpu.VMEM((columns - 1,) + shape, BF16)
    return [low] * 3 + [few] * 4 + [pltpu.SemaphoreType.DMA((2, 2 * columns))] * 2


def gather_steps(columns, w_out, w_back, w_back_out, cross_sems, mate_sems, out_sems):
    part = lax.axis_index("fsdp")
    core, column = lax.rem(part, 2), part // 2
    mate = part + 1 - 2 * core
    rows = w_out.shape[0]

    def column_at(d):
        return lax.rem(column + d + columns, columns)

    def copy(sems, k, owner, device):
        at = w_back.at[pl.ds(pl.multiple_of(owner * rows, LANES // 2), rows)]
        return pltpu.make_async_remote_copy(
            src_ref=at, dst_ref=at, send_sem=sems.at[0, k], recv_sem=sems.at[1, k], device_id={"fsdp": device}
        )

    def across(d, theirs):
        return copy(cross_sems, d, 2 * column_at(-d) + core if theirs else part, 2 * column_at(d) + core)

    def to_mate(d, theirs):
        return copy(mate_sems, d, 2 * column_at(-d) + (1 - core if theirs else core), mate)

    def keep():
        return pltpu.make_async_copy(w_back, w_back_out, out_sems.at[0])

    def start():
        here = w_back.at[pl.ds(pl.multiple_of(part * rows, LANES // 2), rows)]
        own = pltpu.make_async_copy(w_out, here, out_sems.at[1])
        own.start()
        own.wait()
        for d in range(1, columns):
            across(d, False).start()
        to_mate(0, False).start()

    def forward():
        for d in range(1, columns):
            across(d, True).wait_recv()
            to_mate(d, False).start()

    def arrive():
        for d in range(columns):
            to_mate(d, True).wait_recv()
        keep().start()

    def close():
        keep().wait()
        for d in range(columns):
            to_mate(d, False).wait_send()
            if d > 0:
                across(d, False).wait_send()

    return start, forward, arrive, close


def mixer_kernel(
    levels, columns, info, vals, bc_in, dt, gate, taps, rates, spread_f, spread_r, sum_f, sum_r, skip, gain, w_out, d_branch_in, d_branch_t_in, hidden_t_in,
    v_out, bc_out, fr_out, frp_out, kept_f_out, kept_r_out, dx_out, normed_out, d_gate_out,
    back_f, back_r, d_gain, d_skip, d_v, d_bc, sums, d_log, first_out, second_out, enter_f, enter_r, after_f, after_r, w_back_out,
    v, bc, fr, frp, kept_f, kept_r, dx, normed, d_gate, d_branch, d_branch_t, hidden_t, load_sems, front_sems, middle_sems, y, d_normed, mixed_s, part_f, part_r, exp_f, exp_r, row_s, d_mixed, d_outs, read_out, w_back, w_cross, w_mate, w_kept,
    put, got_1, got_2, cross_put_1, cross_put_2, cross_got_1, cross_got_2, mate_sems, cross_sems,
    gains_other, gain_sems, tot_f, tot_r, leave_f, leave_r, *buffers,
):
    s = pl.program_id(0)
    half = len(buffers) // 2
    greet_dp, begin, send_gains, gains_here, send, run, end, total = carry_steps(
        levels, 4, 5, dx, gains_other, gain_sems, tot_f, tot_r, enter_f, enter_r, buffers[:half]
    )
    _, begin_back, _, _, send_back, run_back, end_back, _ = carry_steps(
        levels, 5, 4, dx, gains_other, gain_sems, leave_r, leave_f, after_r, after_f, buffers[half:]
    )
    greet, foreign, local, close = shard_steps(
        columns, normed, d_branch_t, hidden_t, d_gate, (first_out, second_out),
        (put, (got_1, got_2), (cross_put_1, cross_put_2), (cross_got_1, cross_got_2), mate_sems, cross_sems),
    )
    w_start, w_forward, w_arrive, w_close = gather_steps(columns, w_out, w_back, w_back_out, w_cross, w_mate, w_kept)
    entered_f, entered_r = buffers[0], buffers[1]
    fronts = ((v, v_out), (bc, bc_out), (fr, fr_out), (frp, frp_out), (kept_f, kept_f_out), (kept_r, kept_r_out), (dx, dx_out))

    def front_copy(i, m):
        return pltpu.make_async_copy(fronts[i][0].at[m], fronts[i][1].at[m], front_sems.at[i, m])

    def middle_copy(i, slot):
        ref, out = ((normed, normed_out), (d_gate, d_gate_out))[i]
        m, span = slot // 2, pl.ds(pl.multiple_of(lax.rem(slot, 2) * BLOCK, BLOCK), BLOCK)
        return pltpu.make_async_copy(ref.at[m, span], out.at[m, span], middle_sems.at[i, slot])

    def load(i):
        return pltpu.make_async_copy(*((d_branch_in, d_branch), (hidden_t_in, hidden_t), (d_branch_t_in, d_branch_t))[i], load_sems.at[i])

    middle, back = MB, 3 * MB
    window = 5

    @pl.when(s == 0)
    def _():
        barrier = pltpu.get_barrier_semaphore()
        pl.semaphore_wait(barrier, greet(barrier) + greet_dp(barrier))
        for i in range(3):
            load(i).start()
        begin()
        begin_back()
        w_start()

    @pl.when(s < middle)
    def _():
        front_body(s, info, vals, bc_in, dt, taps, rates, spread_f, spread_r, v, bc, fr, frp, tot_f, tot_r, kept_f, kept_r, dx)
        send_gains(s)
        for i in range(len(fronts)):
            front_copy(i, s).start()

        for m, (low, high) in enumerate(((0, 2), (2, 4), (4, window))):

            @pl.when(s == m)
            def _():
                send(low, high)

    done = 0
    for slot in range(2 * MB):
        need = min(PARTS + LAG * (levels - 1) + slot * (PARTS // 2), total)

        @pl.when(s == middle + slot)
        def _():
            if slot == 0:
                for m in range(MB):
                    gains_here(m)
                w_forward()
            run(done, need, window)
            if slot == 0:
                for i in range(3):
                    load(i).wait()
                w_arrive()

        done = need

    @pl.when((s >= middle) & (s < back))
    def _():
        slot = s - middle
        m, b = slot // 2, lax.rem(slot, 2)
        intra_body(m, b, v, bc, fr, frp, skip, y)
        d_normed[0] = dot(d_branch[m, pl.ds(pl.multiple_of(b * BLOCK, BLOCK), BLOCK), :], w_back[...], COLS)
        middle_body(
            slot, info, y, gate, d_normed, v, bc, fr, entered_f, entered_r, kept_f, kept_r, dx, gain, spread_f, spread_r, sum_f, sum_r,
            normed, d_mixed, d_gate, back_f, back_r, leave_f, leave_r, d_outs, read_out, d_gain, d_skip, mixed_s, part_f, part_r, exp_f, exp_r,
        )

        middle_copy(0, slot).start()
        middle_copy(1, slot).start()

        @pl.when(b == 1)
        def _():
            send_back(PARTS * m, PARTS * (m + 1))

    for k, step in enumerate((foreign, local)):
        for which in range(2):

            @pl.when(s == back + 2 * which + k)
            def _():
                step(which)

    @pl.when(s >= back)
    def _():
        slot = s - back
        each = -(-total // (2 * MB * TURNS))

        def turn(k):
            at = slot * TURNS + k
            run_back(at * each, (at + 1) * each, 0)

        intra_back_body(slot, v, d_mixed, bc, fr, frp, skip, d_outs, read_out, d_v, d_bc, sums, d_log, row_s, turn)

    @pl.when(s == 5 * MB - 1)
    def _():
        close()
        w_close()
        for m in range(MB):
            for i in range(len(fronts)):
                front_copy(i, m).wait()

        @pl.loop(0, 2 * MB)
        def _(slot):
            middle_copy(0, slot).wait()
            middle_copy(1, slot).wait()

        end(True)
        end_back(False)


def final_kernel(
    levels, info, vals, bc_in, dt, taps, rates, v, bc, fr, frp, enter_f, enter_r, kept_f, kept_r, dx, after_f, after_r, back_f, back_r,
    d_v, d_bc, sums, d_log, spread_f, spread_r, sum_f, sum_r, first_in, second_in,
    late, before, last, ending, d_taps, d_small, first_out, second_out, d_acts, *buffers,
):
    m = pl.program_id(0)
    forward, reverse = keeps(info, m)
    if levels:
        greet, steps = sum_steps(levels, (buffers[:6], buffers[6:12]), *buffers[12:14])
        leaving, arriving, kept, edge_sems = buffers[14:]
        me = lax.axis_index("dp")
        side = lax.rem(me, 2)
        neighbour = me - 1 + 2 * side
        paired = (neighbour >= 0) & (neighbour < 2 * levels)

        def edge_copy(k):
            return pltpu.make_async_remote_copy(
                src_ref=leaving.at[k], dst_ref=arriving.at[k], send_sem=edge_sems.at[0, k], recv_sem=edge_sems.at[1, k],
                device_id={"dp": me - 1},
            )

    def beside(at, *todo):
        if levels:

            @pl.when(m == at)
            def _():
                for stage, i in todo:
                    steps[stage](i)

    if levels:

        @pl.when(m == 0)
        def _():
            barrier = pltpu.get_barrier_semaphore()

            @pl.when(paired)
            def _():
                pl.semaphore_signal(barrier, inc=1, device_id={"dp": neighbour})

            pl.semaphore_wait(barrier, greet(barrier) + paired.astype(jnp.int32))

            @pl.when(me == 2 * levels - 1)
            def _():
                arriving[...] = jnp.zeros_like(arriving)

            buffers[0][...] = first_in[...]
            buffers[6][...] = second_in[...]

    beside(0, (0, 0))
    lane = iota((BLOCK, LANES), 1)
    row = iota((BLOCK, LANES), 0)
    rows = iota((BLOCK, BLOCK), 0)
    columns = iota((BLOCK, BLOCK), 1)
    lower = (rows >= columns).astype(F32)
    upper = (rows <= columns).astype(F32)
    width = 2 * LANES

    @pl.when(m == 0)
    def _():
        d_taps[...] = jnp.zeros_like(d_taps)
        d_small[...] = jnp.zeros_like(d_small)

    for b in range(2):
        span = pl.ds(b * BLOCK, BLOCK)
        summed = fr[0, span, :]
        end = jnp.where(lane[:1] < HEADS, summed[BLOCK - 1 :], summed[:1])
        tail = spread_operand(jnp.where(lane < 2 * HEADS, jnp.exp(end - frp[0, span, :]), 0.0))
        acts = bc[0, span, :]
        ins = twice(by_lane(acts, swapped(acts)).astype(BF16), 1)
        d_in = jnp.zeros((BLOCK, LANES), F32)
        used = jnp.zeros((BLOCK, LANES), F32)
        decays = jnp.zeros((8, LANES), F32)
        for chunk in range(INNER // width):
            cols = pl.ds(chunk * width, width)
            grad_f = jnp.concatenate([after_f[k, :, cols] for k in range(PARTS)], axis=0)
            grad_r = jnp.concatenate([after_r[k, :, cols] for k in range(PARTS)], axis=0)
            if b == 0:
                grad_f = forward[1] * (back_f[0, 1, :, cols] + dx[0, 1:2, cols] * grad_f)
            else:
                grad_r = reverse[0] * (back_r[0, 0, :, cols] + dx[0, 2:3, cols] * grad_r)
            state_f, state_r = entering(0, b, cols, forward, reverse, enter_f, enter_r, kept_f, kept_r, dx)
            tail_f = dot(tail, spread_f[:, cols])
            tail_r = dot(tail, spread_r[:, cols])
            value = v[0, span, cols].astype(F32)
            pulled_f = tail_f * dot(ins, doubled(grad_f))
            pulled_r = tail_r * dot(ins, doubled(grad_r))
            d_acts[span, cols] = d_v[0, span, cols] + pulled_f + pulled_r
            d_in = d_in + dot(spread_operand(tail_f * value), twice(stacked(grad_f), 1), COLS)
            d_in = d_in + dot(spread_operand(tail_r * value), twice(stacked(grad_r), 1), COLS)
            used = used + head_sums(pulled_f * value, sum_f[cols, :]) + head_sums(pulled_r * value, sum_r[cols, :])
            meet_f = jnp.sum(grad_f * state_f, axis=0, keepdims=True) * dx[0, b : b + 1, cols]
            meet_r = jnp.sum(grad_r * state_r, axis=0, keepdims=True) * dx[0, 2 + b : 3 + b, cols]
            zero = jnp.zeros((7, width), F32)
            decays = decays + head_sums(jnp.concatenate([meet_f, zero], axis=0), sum_f[cols, :])
            decays = decays + head_sums(jnp.concatenate([meet_r, zero], axis=0), sum_r[cols, :])
        d_acts[span, pl.ds(INNER, LANES)] = d_bc[0, span, :] + jnp.where(lane < STATE, d_in + swapped(d_in), 0.0)
        direct = sums[0, span, :] + used
        edge = decays[0:1] + jnp.sum(used, axis=0, keepdims=True)
        at_end = ((lane < HEADS) & (row == BLOCK - 1)) | ((lane >= HEADS) & (row == 0))
        grad = d_log[0, span, :] - used + jnp.where(at_end, edge, 0.0)
        grad = jnp.where(lane < HEADS, dot(upper, grad, precision=HIGHEST), dot(lower, grad, precision=HIGHEST))
        x = dt[0, span, :] + rates[0:1, :]
        step = softplus(x)
        sig = sigmoid(x)
        ratio = jnp.where(x < -17.0, 1.0, sig / step)
        d_x = direct * ratio - rates[1:2, :] * grad * sig
        d_x = jnp.where(lane < 2 * HEADS, d_x, 0.0)
        late[0, span, pl.ds(INNER + LANES, LANES)] = d_x.astype(BF16)
        d_small[0:1, :] += jnp.sum(d_x, axis=0, keepdims=True)
        d_small[1:2, :] -= rates[1:2, :] * jnp.sum(step * grad, axis=0, keepdims=True)
        if b == 0:
            beside(1, (1, 1))
        else:
            beside(0, (0, 1))
            beside(1, (2, 0))
    valid, masks = row_masks(info, m, (TOK_DEV, LANES))
    edge = jnp.zeros((HALO, LANES), F32)
    for chunk in range(PAIRS + 1):
        cols = pl.ds(chunk * LANES, LANES)
        source, own = (vals, cols) if chunk < PAIRS else (bc_in, pl.ds(0, LANES))
        windows = conv_windows(source, own)
        value = conv_value(windows, masks, taps, cols)
        sig = sigmoid(value)
        grad = valid * d_acts[:, cols] * (sig * (1.0 + value * (1.0 - sig)))
        total = jnp.zeros((HALO + TOK_DEV, LANES), F32)
        for k in range(CONV):
            masked = grad if k == 0 else grad * masks[k]
            d_taps[k : k + 1, cols] += jnp.sum(masked * windows[k], axis=0, keepdims=True)
            padded = jnp.concatenate([edge, masked, edge], axis=0)
            total = total + taps[k : k + 1, cols] * padded[k : k + HALO + TOK_DEV]
        d_taps[CONV : CONV + 1, cols] += jnp.sum(grad, axis=0, keepdims=True)
        before[0, :, cols] = total[:HALO]
        last[0, :, cols] = total[TOK_DEV:]
        if levels:
            leaving[m, :, cols] = total[:HALO]
            kept[m, :, cols] = total[TOK_DEV:]
        late[0, :, cols] = total[HALO:].astype(BF16)
    beside(0, (1, 0))
    beside(1, (2, 1))
    if levels:

        @pl.when(me > 0)
        def _():
            edge_copy(m).start()

        @pl.when(m == MB - 1)
        def _():
            for i, out in ((0, first_out), (1, second_out)):
                steps[3](i, False)
                out[...] = buffers[6 * i + 5][side]
            for i in range(2):
                steps[5](i, False)
            for k in range(MB):

                @pl.when(me < 2 * levels - 1)
                def _():
                    edge_copy(k).wait_recv()

                ending[k] = kept[k] + arriving[k]

                @pl.when(me > 0)
                def _():
                    edge_copy(k).wait_send()


def once(shape):
    return pl.BlockSpec(shape, lambda *grid: (0,) * len(shape), pipeline_mode=pl.Buffered(1))


def per_micro(shape, column=0):
    return pl.BlockSpec((1,) + shape, lambda m, *rest: (m,) + (0,) * (len(shape) - 1) + (column,))


def per_block(width, column=0):
    return pl.BlockSpec((1, BLOCK, width), lambda m, b: (m, b, column))


def struct(*shape, dtype=F32):
    return jax.ShapeDtypeStruct(shape, dtype)


def call(kernel, grid, in_specs, out_specs, out_shape, scratch=(), flops=0, moved=0, identity=None):
    return pl.pallas_call(
        kernel,
        grid=grid,
        in_specs=in_specs,
        out_specs=out_specs,
        out_shape=out_shape,
        scratch_shapes=list(scratch),
        compiler_params=pltpu.CompilerParams(
            vmem_limit_bytes=VMEM_LIMIT, collective_id=identity, has_side_effects=identity is not None
        ),
        cost_estimate=pl.CostEstimate(flops=flops, bytes_accessed=moved, transcendentals=0),
    )


def shift(value, distance):
    count = lax.axis_size("dp")
    route = [(i, i + distance) for i in range(count) if 0 <= i + distance < count]
    return lax.ppermute(value, "dp", route)


def carry_steps(levels, up_row, down_row, gains, gains_other, gain_sems, up_in, down_in, up_out, down_out, buffers):
    up_other, down_other, up_chain, down_chain, up_sems, down_sems, up_link, down_link, out_sems = buffers
    me = lax.axis_index("dp")
    side = lax.rem(me, 2)
    level = me // 2
    partner = me + 1 - 2 * side
    above, below = me + 2, me - 2
    has_above, has_below = level < levels - 1, level > 0
    first = side == 0

    def remote(source, target, sems, k, device):
        return pltpu.make_async_remote_copy(
            src_ref=source, dst_ref=target, send_sem=sems.at[0, k], recv_sem=sems.at[1, k], device_id={"dp": device}
        )

    def swap_gains(m):
        return remote(gains.at[m], gains_other.at[m], gain_sems, m, partner)

    def swap_up(k):
        return remote(up_in.at[k], up_other.at[k], up_sems, k, partner)

    def swap_down(k):
        return remote(down_in.at[k], down_other.at[k], down_sems, k, partner)

    def climb(k):
        return remote(up_in.at[k], up_chain.at[k], up_link, k, above)

    def descend(k):
        return remote(down_in.at[k], down_chain.at[k], down_link, k, below)

    def keep_up(k):
        return pltpu.make_async_copy(up_other.at[k], up_out.at[k], out_sems.at[0, k])

    def keep_down(k):
        return pltpu.make_async_copy(down_other.at[k], down_out.at[k], out_sems.at[1, k])

    def greet(barrier):
        pl.semaphore_signal(barrier, inc=1, device_id={"dp": partner})

        @pl.when(has_above)
        def _():
            pl.semaphore_signal(barrier, inc=1, device_id={"dp": above})

        @pl.when(has_below)
        def _():
            pl.semaphore_signal(barrier, inc=1, device_id={"dp": below})

        return 1 + has_above.astype(jnp.int32) + has_below.astype(jnp.int32)

    def begin():
        @pl.when(level == 0)
        def _():
            up_chain[...] = jnp.zeros_like(up_chain)

        @pl.when(level == levels - 1)
        def _():
            down_chain[...] = jnp.zeros_like(down_chain)

    total = CHUNKS + LAG * (levels - 1)

    def places(step):
        return step - LAG * level, step - LAG * (levels - 1 - level)

    def send(low, high):
        @pl.loop(low, high)
        def _(k):
            @pl.when(k < CHUNKS)
            def _():
                swap_up(k).start()
                swap_down(k).start()

    def advance(step):
        up, down = places(step)

        @pl.when((up >= 0) & (up < CHUNKS))
        def _():
            swap_up(up).wait_recv()

            @pl.when(has_below)
            def _():
                climb(up).wait_recv()

            m = up // PARTS
            own, other = gains[m, up_row : up_row + 1], gains_other[m, up_row : up_row + 1]
            near, far = jnp.where(first, own, other), jnp.where(first, other, own)
            mine, theirs = up_in[up], up_other[up]
            before = up_chain[up]
            middle = jnp.where(first, mine, theirs) + near * before
            up_other[up] = jnp.where(first, before, middle)
            keep_up(up).start()

            @pl.when(has_above)
            def _():
                swap_up(up).wait_send()
                up_in[up] = jnp.where(first, theirs, mine) + far * middle
                climb(up).start()

        @pl.when((down >= 0) & (down < CHUNKS))
        def _():
            swap_down(down).wait_recv()

            @pl.when(has_above)
            def _():
                descend(down).wait_recv()

            m = down // PARTS
            own, other = gains[m, down_row : down_row + 1], gains_other[m, down_row : down_row + 1]
            near, far = jnp.where(first, other, own), jnp.where(first, own, other)
            mine, theirs = down_in[down], down_other[down]
            before = down_chain[down]
            middle = jnp.where(first, theirs, mine) + near * before
            down_other[down] = jnp.where(first, middle, before)
            keep_down(down).start()

            @pl.when(has_below)
            def _():
                swap_down(down).wait_send()
                down_in[down] = jnp.where(first, mine, theirs) + far * middle
                descend(down).start()

    def run(low, high, window):
        @pl.loop(low, high)
        def _(step):
            advance(step)
            if window:
                send(step + window, step + window + 1)

    def gains_here(m):
        swap_gains(m).wait_recv()

    def end(last):
        if last:

            @pl.loop(0, MB)
            def _(m):
                swap_gains(m).wait_send()

        @pl.loop(0, CHUNKS)
        def _(k):
            keep_up(k).wait()
            keep_down(k).wait()

            @pl.when(has_above)
            def _():
                climb(k).wait_send()

            @pl.when(jnp.logical_not(has_above))
            def _():
                swap_up(k).wait_send()

            @pl.when(has_below)
            def _():
                descend(k).wait_send()

            @pl.when(jnp.logical_not(has_below))
            def _():
                swap_down(k).wait_send()

    return greet, begin, lambda m: swap_gains(m).start(), gains_here, send, run, end, total


CARRY_SHAPE = (CHUNKS, STATE // PARTS, INNER)


def carry_buffers():
    return [pltpu.VMEM(CARRY_SHAPE, F32)] * 4 + [pltpu.SemaphoreType.DMA((2, CHUNKS))] * 5


def sum_steps(levels, parts, side_sems, level_sems):
    me = lax.axis_index("dp")
    side, level = lax.rem(me, 2), me // 2
    partner = me + 1 - 2 * side

    def level_at(d):
        return lax.rem(level + d + levels, levels)

    def device(d):
        return {"dp": 2 * level_at(d) + side}

    def remote(source, target, sems, k, where):
        return pltpu.make_async_remote_copy(
            src_ref=source, dst_ref=target, send_sem=sems.at[0, k], recv_sem=sems.at[1, k], device_id=where
        )

    def greet(barrier):
        pl.semaphore_signal(barrier, inc=1, device_id={"dp": partner})
        for d in range(1, levels):
            pl.semaphore_signal(barrier, inc=1, device_id=device(d))
        return levels

    def halve(i):
        return remote(parts[i][1], parts[i][2], side_sems, 2 * i, {"dp": partner})

    def join(i, theirs):
        full = parts[i][5]
        return remote(full.at[side], full.at[1 - side if theirs else side], side_sems, 2 * i + 1, {"dp": partner})

    def scatter(i, d, theirs):
        put, got = parts[i][3:5]
        return remote(put.at[level_at(d)], got.at[level_at(-d) if theirs else level], level_sems, 2 * i * levels + d, device(d))

    def gather(i, d, theirs):
        full = parts[i][5]
        target = full.at[side, level_at(-d) if theirs else level]
        return remote(full.at[side, level], target, level_sems, (2 * i + 1) * levels + d, device(d))

    def step_0(i):
        total, put = parts[i][:2]
        put[...] = total[1 - side].astype(BF16)
        halve(i).start()

    def step_1(i):
        total, _, got, put = parts[i][:4]
        halve(i).wait_recv()
        total[side] = total[side] + got[...].astype(F32)
        for d in range(1, levels):
            target = level_at(d)
            put[target] = total[side, target].astype(BF16)
            scatter(i, d, False).start()

    def step_2(i):
        total, _, _, _, got, full = parts[i]
        value = total[side, level]
        for d in range(1, levels):
            scatter(i, d, True).wait_recv()
            value = value + got[level_at(-d)].astype(F32)
        full[side, level] = value.astype(BF16)
        for d in range(1, levels):
            gather(i, d, False).start()

    def step_3(i, joined=True):
        for d in range(1, levels):
            gather(i, d, True).wait_recv()
        if joined:
            join(i, False).start()

    def step_4(i):
        join(i, True).wait_recv()

    def close(i, joined=True):
        halve(i).wait_send()
        if joined:
            join(i, False).wait_send()
        for d in range(1, levels):
            scatter(i, d, False).wait_send()
            gather(i, d, False).wait_send()

    return greet, (step_0, step_1, step_2, step_3, step_4, close)


def sum_buffers(levels, piece, width):
    low = pltpu.VMEM((levels, piece, width), BF16)
    both = (2, levels, piece, width)
    return [pltpu.VMEM(both, F32), low, low, low, low, pltpu.VMEM(both, BF16)]


def sum_semaphores(levels, count):
    return [pltpu.SemaphoreType.DMA((2, 2 * count)), pltpu.SemaphoreType.DMA((2, 2 * count * levels))]


PIECES = ((0, 512), (512, 512), (1024, 384), (1408, 384))


def total_kernel(
    levels, columns, info, hidden_t_in, late_in, w_all_in, d_gate_in, x_hbm, cot_hbm, w_back_in, normed_in, gain_in,
    first_in, gate_in, ending, taps_in, scale_in, skip_in, small_in, selector,
    layer_hbm, tokens_hbm, first_out, inner_out, state_out, step_out, norm_out, taps_out, bias_out, steps_out, decay_out, skip_out, scale_out,
    hidden_t, late, w_all, d_gate, x_in, cot_in, w_back, normed, layer_out, tokens_out, first_sum, first_full, gate_full, load_sems, keep_sems, join_sems,
    third_in, norm_sum, mate_got, cross_put, cross_got, short_sum, short_got, short_sems, mate_sems, cross_sems, side_sems, level_sems, *buffers,
):
    me, part = lax.axis_index("dp"), lax.axis_index("fsdp")
    side, level = lax.rem(me, 2), me // 2
    core, column = lax.rem(part, 2), part // 2
    mate = part + 1 - 2 * core
    count = len(PIECES)
    parts = [buffers[6 * i : 6 * i + 6] for i in range(count)]
    sources = (hidden_t_in, late_in, w_all_in, d_gate_in, x_hbm, cot_hbm, w_back_in, normed_in)
    places = (hidden_t, late, w_all, d_gate, x_in, cot_in, w_back, normed)

    def load(i):
        return pltpu.make_async_copy(sources[i], places[i], load_sems.at[i])

    def keep(i, k):
        ref, out = ((layer_out, layer_hbm), (tokens_out, tokens_hbm))[i]
        at = pl.ds(k * BLOCK, BLOCK)
        return pltpu.make_async_copy(ref.at[at], out.at[at], keep_sems.at[i, k])

    for i in range(len(sources)):
        load(i).start()
    greet, steps = sum_steps(levels, parts, side_sems, level_sems)

    def column_at(d):
        return lax.rem(column + d + columns, columns)

    def remote(source, target, sems, k, where):
        return pltpu.make_async_remote_copy(
            src_ref=source, dst_ref=target, send_sem=sems.at[0, k], recv_sem=sems.at[1, k], device_id=where
        )

    barrier = pltpu.get_barrier_semaphore()
    pl.semaphore_signal(barrier, inc=1, device_id={"fsdp": mate})
    for d in range(1, columns):
        pl.semaphore_signal(barrier, inc=1, device_id={"fsdp": 2 * column_at(d) + core})
    pl.semaphore_wait(barrier, greet(barrier) + columns)

    def to_mate(i, x):
        at = pl.ds(*PIECES[i])
        return remote(third_in.at[2 * x + 1 - core, :, at], mate_got.at[x, :, at], mate_sems, i * columns + x, {"fsdp": mate})

    def across(i, d, theirs):
        at = pl.ds(*PIECES[i])
        where = {"fsdp": 2 * column_at(d) + core}
        slot = column_at(-d) if theirs else column
        return remote(cross_put.at[column_at(d), :, at], cross_got.at[slot, :, at], cross_sems, i * columns + d, where)

    joins = (first_full, gate_full)

    def join(i, theirs):
        full = joins[i]
        return remote(full.at[side], full.at[1 - side if theirs else side], join_sems, i, {"dp": me + 1 - 2 * side})

    for i, ref in enumerate((first_in, gate_in)):
        joins[i][side] = ref[...]
        join(i, False).start()
    load(0).wait()
    load(1).wait()
    for m in range(MB):
        late[(m + 1) * TOK_DEV - HALO : (m + 1) * TOK_DEV, :CONV_COLS] = ending[m].astype(BF16)

    block_rows = third_in.shape[1]

    def third(owner, i):
        at = pl.ds(pl.multiple_of(owner * block_rows, 16), block_rows)
        cols = pl.ds(*PIECES[i])
        third_in[owner, :, cols] = dot(hidden_t[at, :], late[:, cols])

    def d_hidden_block(k):
        m, b = divmod(k, 2)
        at = slice(k * BLOCK, (k + 1) * BLOCK)
        grad = dot(d_gate[at], w_all[:, :INNER], COLS) + dot(late[at], w_all[:, INNER:], COLS)
        rows = x_in[at].astype(F32)
        scale = lax.rsqrt(jnp.mean(rows * rows, axis=1, keepdims=True) + EPSILON)
        norm_sum[...] += jnp.sum(grad * rows * scale, axis=0, keepdims=True)
        pulled = grad * gain_in[...]
        pull = (scale * scale * scale) * jnp.mean(rows * pulled, axis=1, keepdims=True)
        valid = row_masks(info, m, (BLOCK, D), b * BLOCK)[0]
        tokens_out[at] = scale * pulled - rows * pull + valid * cot_in[at].astype(F32)
        keep(1, k).start()

    def layer_block(k):
        m, b = divmod(k, 2)
        at = slice(k * BLOCK, (k + 1) * BLOCK)
        branch = dot(normed[at], w_back[...])
        valid = row_masks(info, m, (BLOCK, D), b * BLOCK)[0]
        layer_out[at] = jnp.where(valid > 0.0, x_in[at].astype(F32) + branch, 0.0).astype(BF16)
        keep(0, k).start()

    norm_sum[...] = jnp.zeros_like(norm_sum)
    for i in range(count):
        for x in range(columns):
            third(2 * x + 1 - core, i)
            to_mate(i, x).start()
    for i in range(count):
        for x in range(columns):
            third(2 * x + core, i)

    def cross(i):
        at = pl.ds(*PIECES[i])
        for x in range(columns):
            to_mate(i, x).wait_recv()
        for d in range(1, columns):
            x = column_at(d)
            cross_put[x, :, at] = (third_in[2 * x + core, :, at] + mate_got[x, :, at]).astype(BF16)
            across(i, d, False).start()

    cross(0)
    cross(1)
    for i in range(2, 6):
        load(i).wait()
    for k in range(2 * MB - 2):
        d_hidden_block(k)

    lane = iota((8, LANES), 1)
    summed = jnp.where(lane < HEADS, head_sums(skip_in[...], selector[...]), 0.0)
    folded = small_in[...] + pltpu.roll(small_in[...], LANES - HEADS, axis=1)
    short_sum[0, 0:8, :] = taps_in[...]
    short_sum[0, 8:16, :] = jnp.zeros((8, CONV_COLS), F32)
    short_sum[0, 5:6, :INNER] = scale_in[0:1]
    short_sum[0, 8:9, :LANES] = small_in[0:1]
    short_sum[0, 9:10, :LANES] = folded[1:2]
    short_sum[0, 10:11, :LANES] = summed[0:1]
    routes = [{"fsdp": mate}, {"dp": me + 1 - 2 * side}]
    stride = 1
    while stride < columns:
        routes.append({"fsdp": part + 2 * stride - 4 * stride * lax.rem(column // stride, 2)})
        stride *= 2
    stride = 1
    while stride < levels:
        routes.append({"dp": me + 2 * stride - 4 * stride * lax.rem(level // stride, 2)})
        stride *= 2

    def short(k):
        return remote(short_sum.at[k], short_got.at[k], short_sems, k, routes[k])

    def short_step(k):
        if k > 0:
            short(k - 1).wait_recv()
            short_sum[k] = short_sum[k - 1] + short_got[k - 1]
        if k < len(routes):
            short(k).start()

    rows = parts[0][0].shape[2]

    def arrive(i):
        at = pl.ds(*PIECES[i])
        for d in range(1, columns):
            across(i, d, True).wait_recv()
        for x in range(2):
            for j in range(levels):
                here = pl.ds((x * levels + j) * rows, rows)
                value = third_in[part, here, at] + mate_got[column, here, at]
                for d in range(1, columns):
                    value = value + cross_got[column_at(-d), here, at].astype(F32)
                parts[i][0][x, j] = value
        steps[0](i)

    last = len(routes)
    for wave in range(count + 4):
        for stage in range(4, 0, -1):
            i = wave - stage
            if 0 <= i < count:
                steps[stage](i)
        if wave < count:
            arrive(wave)
        if wave + 2 < count:
            cross(wave + 2)
        if wave < 2:
            d_hidden_block(2 * MB - 2 + wave)
        elif wave < 2 + 2 * MB:
            if wave == 2:
                load(6).wait()
                load(7).wait()
            layer_block(wave - 2)
        if wave == 1:
            short_sum[0, 6:7, :D] = norm_sum[...]
        if 1 <= wave <= last + 1:
            short_step(wave - 1)
    for k in range(count + 3, last + 1):
        short_step(k)

    result = short_sum.at[last]
    for f in range(2 * columns):

        @pl.when(part == f)
        def _():
            def own(row, rows, width, ref):
                size = width // (2 * columns)
                ref[...] = result[row : row + rows, f * size : (f + 1) * size]

            own(0, CONV, CONV_COLS, taps_out)
            own(4, 1, CONV_COLS, bias_out)
            own(5, 1, INNER, scale_out)
            own(6, 1, D, norm_out)
            own(8, 1, 2 * HEADS, steps_out)
            own(9, 1, HEADS, decay_out)
            own(10, 1, HEADS, skip_out)

    for i in range(2):
        join(i, True).wait_recv()
    tall = gate_in.shape[1]
    for h in range(2):
        for j in range(levels):
            inner_out[j * tall : (j + 1) * tall, h * D : (h + 1) * D] = gate_full[h, j].astype(F32)
            at = (h * levels + j) * tall
            first_sum[at : at + tall] = first_full[h, j].astype(F32)
    tall = first_sum.shape[0]
    for g in range(D // tall):
        at = slice(g * tall, (g + 1) * tall)
        first_out[:, at] = jnp.transpose(first_sum[:, at])
    for i in range(count):
        start, width = PIECES[i]
        for x in range(2):
            for j in range(levels):
                here = pl.ds((x * levels + j) * rows, rows)
                value = parts[i][5][x, j].astype(F32)
                inside = min(width, INNER - start)
                inner_out[here, INNER + start : INNER + start + inside] = value[:, :inside]
                if inside < width:
                    state_out[here, :] = value[:, inside : inside + LANES]
                    step_out[here, :] = value[:, inside + LANES : inside + LANES + 2 * HEADS]
    for i in range(count):
        steps[5](i)
        for x in range(columns):
            to_mate(i, x).wait_send()
        for d in range(1, columns):
            across(i, d, False).wait_send()
    for k in range(last):
        short(k).wait_send()
    for i in range(2):
        join(i, False).wait_send()
        for k in range(2 * MB):
            keep(i, k).wait()


def total_fits(levels, shards, dp_count):
    rows = D // shards
    return dp_count == 2 * levels and shards % 2 == 0 and rows % (16 * levels) == 0 and 2 * rows % LANES == 0 and 24 % shards == 0


def totals(operands, identity):
    dp_count, shards = lax.axis_size("dp"), lax.axis_size("fsdp")
    levels, columns = dp_count // 2, shards // 2
    rows = D // shards
    small = rows // levels // 2
    steps = (dp_count * shards).bit_length() - 1
    count = len(PIECES)

    def low(*shape):
        return pltpu.VMEM(shape, BF16)

    def full(*shape):
        return pltpu.VMEM(shape, F32)

    outs = pl.pallas_call(
        partial(total_kernel, levels, columns),
        in_specs=[SCALARS] + [pl.BlockSpec(memory_space=pl.ANY)] * 8 + [pl.BlockSpec(memory_space=pltpu.VMEM)] * 9,
        out_specs=[pl.BlockSpec(memory_space=pl.ANY)] * 2 + [pl.BlockSpec(memory_space=pltpu.VMEM)] * 11,
        out_shape=[struct(MB * TOK_DEV, D, dtype=BF16), struct(MB * TOK_DEV, D), struct(2 * rows, D)]
        + [struct(rows, 2 * INNER), struct(rows, 2 * STATE), struct(rows, 2 * HEADS)]
        + [struct(1, D // shards), struct(CONV, CONV_COLS // shards), struct(1, CONV_COLS // shards)]
        + [struct(1, width // shards) for width in (2 * HEADS, HEADS, HEADS, INNER)],
        scratch_shapes=[pltpu.VMEM(operand.shape, BF16) for operand in operands[1:9]]
        + [low(MB * TOK_DEV, D), full(MB * TOK_DEV, D), full(2 * rows, D), low(2, levels, small * 2, D), low(2, levels, small * 2, D)]
        + [pltpu.SemaphoreType.DMA((8,)), pltpu.SemaphoreType.DMA((2, 2 * MB)), pltpu.SemaphoreType.DMA((2, 2))]
        + [full(shards, rows, LATE), full(1, D), full(columns, rows, LATE), low(columns, rows, LATE), low(columns, rows, LATE)]
        + [full(steps + 1, 16, CONV_COLS), full(steps, 16, CONV_COLS), pltpu.SemaphoreType.DMA((2, steps))]
        + [pltpu.SemaphoreType.DMA((2, count * columns))] * 2
        + sum_semaphores(levels, count)
        + [buffer for _, width in PIECES for buffer in sum_buffers(levels, small, width)],
        compiler_params=pltpu.CompilerParams(vmem_limit_bytes=VMEM_LIMIT, collective_id=identity, has_side_effects=True),
    )(*operands)
    heads = [out.reshape(MB, 1, TOK_DEV, D) for out in outs[:2]]
    flat = [out.reshape(-1) for out in outs[8:]]
    return heads + [outs[6].reshape(-1)] + list(outs[3:6]) + [outs[7]] + flat, outs[2]


def rms(values):
    return lax.rsqrt(jnp.mean(values * values, axis=-1, keepdims=True) + EPSILON)


def scatter_small(parts, shards):
    rows = []
    for part in parts:
        if part.ndim == 2:
            rows.append(part.reshape(part.shape[0], shards, -1).transpose(1, 0, 2).reshape(shards, -1))
        else:
            rows.append(part.reshape(shards, -1))
    flat = jnp.concatenate(rows, axis=1)
    size = flat.shape[1]
    padded = -(-size // LANES) * LANES
    return jnp.pad(flat, ((0, 0), (0, padded - size)))


def on_device(
    tokens, seq_lengths, norm_gain, w_inner, w_state, w_step, conv_weight, conv_bias, step_bias, decay_log, skip_gain, out_gain, w_out, cotangent,
):
    dp_count = lax.axis_size("dp")
    shards = lax.axis_size("fsdp")
    base = lax.axis_index("dp") * TOK_DEV
    lengths = seq_lengths[:, 0]
    info = jnp.concatenate([lengths.reshape(-1), jnp.stack([base, jnp.int32(dp_count * TOK_DEV)]).astype(jnp.int32)])
    small = [part.reshape(-1) for part in (conv_weight, conv_bias, out_gain, norm_gain, step_bias, decay_log, skip_gain)]
    flat = jnp.concatenate(small)
    mine = jnp.pad(flat, (0, 32 * LANES - flat.shape[0])).reshape(32, LANES)
    x, cot = tokens[:, 0], cotangent[:, 0]
    w_all, hidden, hidden_t, d_branch, d_branch_t, gain_in, taps, steps, skip, out_scale, spread_f, spread_r, sum_f, sum_r = gather_weights(
        info, x, cot, w_inner, w_state, w_step, mine, 4
    )
    rows = TOK_DEV + HALO
    zx = jnp.dot(hidden.reshape(MB * rows, D), w_all, preferred_element_type=F32).reshape(MB, rows, WIDE)

    levels = dp_count // 2
    zx_vals = per_micro((rows, INNER), 1)
    zx_bc = per_micro((rows, LANES), 2 * INNER // LANES)
    zx_dt = per_micro((rows, LANES), 2 * INNER // LANES + 1)
    taps_spec, steps_spec = once((8, CONV_COLS)), once((8, LANES))
    spread_spec, sum_spec = once((2 * LANES, INNER)), once((INNER, LANES))
    state_spec, dx_spec = per_micro((STATE, INNER)), per_micro((8, INNER))
    wide_spec, lane_spec = per_micro((TOK_DEV, INNER)), per_micro((TOK_DEV, LANES))
    row_spec, dx_all_spec, carry_spec = once((8, INNER)), once((MB, 8, INNER)), once(CARRY_SHAPE)

    def early(width, column):
        return pl.BlockSpec((1, rows, width), lambda s: (jnp.minimum(s, MB - 1), 0, column))

    def turning(s):
        return jnp.clip(s - MB, 0, 2 * MB - 1)

    def backing(s):
        return jnp.maximum(s - 3 * MB, 0)

    def block_at(pick, width):
        return pl.BlockSpec((1, BLOCK, width), lambda s: (pick(s) // 2, lax.rem(pick(s), 2), 0))

    back_spec = pl.BlockSpec((1, 1, STATE, INNER), lambda s: (turning(s) // 2, lax.rem(turning(s), 2), 0, 0))
    lanes_struct = struct(MB, TOK_DEV, LANES)
    lane_out, anywhere = block_at(backing, LANES), pl.BlockSpec(memory_space=pl.ANY)
    shard_rows = INNER // shards
    shard_spec = once((shard_rows, D))
    pairs = pltpu.SemaphoreType.DMA((2, shards // 2))
    block_scratch = pltpu.VMEM((BLOCK, INNER), F32)
    (
        v, bc, fr, frp, kept_f, kept_r, dx, normed, d_gate, back_f, back_r, d_out_gain, d_skip, d_v, d_bc, sums, d_log,
        first_grad, gate_grad, enter_f, enter_r, after_f, after_r, w_back,
    ) = call(
        partial(mixer_kernel, levels, shards // 2),
        (5 * MB,),
        [SCALARS, early(INNER, 1), early(LANES, 2 * INNER // LANES), early(LANES, 2 * INNER // LANES + 1), block_at(turning, INNER)]
        + [taps_spec, steps_spec, spread_spec, spread_spec, sum_spec, sum_spec, row_spec, row_spec]
        + [anywhere] * 4,
        [anywhere] * 9
        + [back_spec, back_spec]
        + [row_spec, row_spec, block_at(backing, INNER), lane_out, lane_out, lane_out, shard_spec, shard_spec]
        + [anywhere] * 5,
        [struct(MB, TOK_DEV, INNER, dtype=BF16)]
        + [lanes_struct] * 3
        + [struct(MB, STATE, INNER)] * 2
        + [struct(MB, 8, INNER)]
        + [struct(MB, TOK_DEV, INNER, dtype=BF16)] * 2
        + [struct(MB, 2, STATE, INNER)] * 2
        + [struct(8, INNER)] * 2
        + [struct(MB, TOK_DEV, INNER)]
        + [lanes_struct] * 3
        + [struct(shard_rows, D)] * 2
        + [struct(*CARRY_SHAPE)] * 4
        + [struct(INNER, D, dtype=BF16)],
        scratch=[pltpu.VMEM((MB, TOK_DEV, INNER), BF16)]
        + [pltpu.VMEM((MB, TOK_DEV, LANES), F32)] * 3
        + [pltpu.VMEM((MB, STATE, INNER), F32)] * 2
        + [pltpu.VMEM((MB, 8, INNER), F32)]
        + [pltpu.VMEM((MB, TOK_DEV, INNER), BF16)] * 2
        + [pltpu.VMEM((MB, TOK_DEV, D), BF16)]
        + [pltpu.VMEM((D, MB * TOK_DEV), BF16)] * 2
        + [pltpu.SemaphoreType.DMA((3,)), pltpu.SemaphoreType.DMA((7, MB)), pltpu.SemaphoreType.DMA((2, 2 * MB))]
        + [pltpu.VMEM((1, BLOCK, INNER), F32)] * 2
        + [block_scratch] * 5
        + [pltpu.VMEM((BLOCK, LANES), F32), pltpu.VMEM((2 * MB, BLOCK, INNER), BF16)]
        + [pltpu.VMEM((2 * MB, BLOCK, LANES), F32)] * 2
        + [pltpu.VMEM((INNER, D), BF16), pairs, pairs, pltpu.SemaphoreType.DMA((2,))]
        + shard_buffers(shards)
        + [pltpu.VMEM((MB, 8, INNER), F32), pltpu.SemaphoreType.DMA((2, MB))]
        + [pltpu.VMEM(CARRY_SHAPE, F32)] * 4
        + 2 * carry_buffers(),
        flops=50_000_000_000,
        moved=60_000_000,
        identity=0,
    )(
        info, zx, zx, zx, zx, taps, steps, spread_f, spread_r, sum_f, sum_r, skip, out_scale, w_out, d_branch, d_branch_t, hidden_t
    )

    def turned(grad):
        return grad.reshape(shard_rows, D // shard_rows, shard_rows).transpose(2, 1, 0).reshape(shard_rows, D)

    fits = total_fits(levels, shards, dp_count)
    if fits:
        split = (2, levels, shard_rows // (2 * levels), D)
        first_grad, gate_grad = first_grad.reshape(split), gate_grad.reshape(split)
    else:
        split = (1, 16, LANES)
    unused = jnp.zeros(split, F32)
    edge_buffers = [pltpu.VMEM((MB, HALO, CONV_COLS), F32)] * 3 + [pltpu.SemaphoreType.DMA((2, MB))]
    chunk_spec = pl.BlockSpec((PARTS,) + CARRY_SHAPE[1:], lambda m: (m, 0, 0))
    late, before, last, ending, d_taps, d_small, first_sum, gate_sum = call(
        partial(final_kernel, levels if fits else 0),
        (MB,),
        [SCALARS, zx_vals, zx_bc, zx_dt, taps_spec, steps_spec, wide_spec, lane_spec, lane_spec, lane_spec]
        + [chunk_spec, chunk_spec, state_spec, state_spec]
        + [dx_spec, chunk_spec, chunk_spec, per_micro((2, STATE, INNER)), per_micro((2, STATE, INNER))]
        + [wide_spec, lane_spec, lane_spec, lane_spec, spread_spec, spread_spec, sum_spec, sum_spec, once(split), once(split)],
        [per_micro((TOK_DEV, LATE)), per_micro((HALO, CONV_COLS)), per_micro((HALO, CONV_COLS)), once((MB, HALO, CONV_COLS)), once((8, CONV_COLS)), once((8, LANES))]
        + [once(split[1:])] * 2,
        [
            struct(MB, TOK_DEV, LATE, dtype=BF16),
            struct(MB, HALO, CONV_COLS),
            struct(MB, HALO, CONV_COLS),
            struct(MB, HALO, CONV_COLS),
            struct(8, CONV_COLS),
            struct(8, LANES),
            struct(*split[1:], dtype=BF16),
            struct(*split[1:], dtype=BF16),
        ],
        scratch=[pltpu.VMEM((TOK_DEV, CONV_COLS), F32)]
        + (2 * sum_buffers(*split[1:]) + sum_semaphores(levels, 2) + edge_buffers if fits else []),
        flops=2_000_000_000,
        moved=40_000_000,
        identity=3 if fits else None,
    )(
        info, zx, zx, zx, taps, steps, v, bc, fr, frp, enter_f, enter_r, kept_f, kept_r, dx, after_f, after_r, back_f, back_r,
        d_v, d_bc, sums, d_log, spread_f, spread_r, sum_f, sum_r, first_grad if fits else unused, gate_grad if fits else unused,
    )
    d_gate = d_gate.reshape(MB * TOK_DEV, INNER)
    normed = normed.reshape(MB * TOK_DEV, INNER)
    late = late.reshape(MB * TOK_DEV, LATE)
    if fits:
        flat = [part.reshape(MB * TOK_DEV, D) for part in (x, cot)]
        grads, first_sum = totals(
            (info, hidden_t, late, w_all, d_gate, *flat, w_back, normed, gain_in, first_sum, gate_sum, ending)
            + (d_taps, d_out_gain, d_skip, d_small, sum_f),
            2,
        )
        return (*grads, first_sum)

    ending = (last + shift(before, -1)).astype(BF16)
    late = lax.dynamic_update_slice(late.reshape(MB, TOK_DEV, LATE), ending, (0, TOK_DEV - HALO, 0)).reshape(MB * TOK_DEV, LATE)

    def owned(grad):
        return lax.psum_scatter(grad, "fsdp", scatter_dimension=0, tiled=True)

    places = base + jnp.arange(TOK_DEV, dtype=jnp.int32)
    first = lengths[:, :1]
    start = (first + BLOCK - 1) // BLOCK * BLOCK
    valid = (places[None] < first) | (places[None] >= start) & (places[None] < start + lengths[:, 1:])
    valid = valid[..., None]
    branch = dot(normed, w_back).reshape(MB, TOK_DEV, D)
    x_rows = x.astype(F32)
    layer_out = jnp.where(valid, x_rows + branch, 0.0).astype(BF16)
    late_grad = dot(hidden_t, late)
    d_hidden = dot(d_gate, w_all[:, :INNER], COLS) + dot(late, w_all[:, INNER:], COLS)
    d_hidden = d_hidden.reshape(MB, TOK_DEV, D)
    scale = rms(x_rows)
    d_norm_gain = jnp.sum(d_hidden * x_rows * scale, axis=(0, 1))
    pulled = d_hidden * gain_in
    d_x = scale * pulled - x_rows * (scale * scale * scale) * jnp.mean(x_rows * pulled, axis=-1, keepdims=True)
    tokens_grad = d_x + jnp.where(valid, cot.astype(F32), 0.0)
    d_skip_gain = jnp.sum(d_skip[0].reshape(HEADS, HEAD_DIM), axis=1)
    d_decay = d_small[1, :HEADS] + d_small[1, HEADS : 2 * HEADS]
    small = (d_norm_gain, d_taps[:CONV], d_taps[CONV], d_small[0, : 2 * HEADS], d_decay, d_skip_gain, d_out_gain[0])
    w_out_grad, gate_grad, late_grad = lax.psum((first_grad, gate_grad, owned(late_grad)), "dp")
    summed = lax.psum(scatter_small(small, shards), ("dp", "fsdp"))
    own = lax.dynamic_slice_in_dim(summed, lax.axis_index("fsdp"), 1, axis=0)[0]
    pieces = []
    at = 0
    for part in (norm_gain, conv_weight, conv_bias, step_bias, decay_log, skip_gain, out_gain):
        pieces.append(own[at : at + part.size].reshape(part.shape))
        at += part.size
    gate_grad = jnp.concatenate([gate_grad[: shard_rows // 2], gate_grad[shard_rows // 2 :]], axis=1)
    w_inner_grad = jnp.concatenate([gate_grad, late_grad[:, :INNER]], axis=1)
    w_state_grad = late_grad[:, INNER : INNER + 2 * STATE]
    w_step_grad = late_grad[:, INNER + LANES : INNER + LANES + 2 * HEADS]
    grads = pieces[:1] + [w_inner_grad, w_state_grad, w_step_grad] + pieces[1:] + [turned(w_out_grad)]
    return (layer_out[:, None], tokens_grad[:, None], *grads)


def solution(mesh):
    rows, vector, matrix = P(None, "fsdp", "dp", None), P("fsdp"), P("fsdp", None)
    weights = (vector, matrix, matrix, matrix, P(None, "fsdp"), vector, vector, vector, vector, vector, matrix)
    return jax.shard_map(
        on_device,
        mesh=mesh,
        in_specs=(rows, P(None, "fsdp", None)) + weights + (rows,),
        out_specs=(rows, rows) + weights,
        check_vma=False,
    )
```
